32 devices in a mesh: batch: 4 (over z), seq: 2 (over core), ch: 4 (over y, x).
Axes of the slice: x: 2, y: 2, z: 4, core: 2. Of those that a mesh axis runs over, the one named last changes fastest.
Arguments:
- inputs: bfloat16 [16, 1280, 2048], P('batch', 'ch', 'seq'), may hold values from -6 to 6
- segment_ids: int32 [16, 2048], P('batch', 'seq'), may hold values from 0 to 7, never falling along the last dimension, each value on 1 to 512 neighbouring positions
- norm0_gain: float32 [1280], P('ch'), may hold values from 0.1 to 1.9
- norm0_shift: float32 [1280], P('ch'), may hold values from -3 to 3
- w_inner: bfloat16 [1280, 640], P('ch'), may hold values from -0.15625 to 0.15625
- b_inner: float32 [640], P('ch'), may hold values from -3 to 3
- norm1_gain: float32 [640], P('ch'), may hold values from 0.1 to 1.9
- norm1_shift: float32 [640], P('ch'), may hold values from -3 to 3
- w_conv: bfloat16 [5, 640, 640], P(None, 'ch'), may hold values from -0.109375 to 0.109375
- b_conv: float32 [640], P('ch'), may hold values from -3 to 3
- norm2_gain: float32 [640], P('ch'), may hold values from 0.1 to 1.9
- norm2_shift: float32 [640], P('ch'), may hold values from -3 to 3
- w_outer: bfloat16 [640, 1280], P('ch'), may hold values from -0.25 to 0.25
- b_outer: float32 [1280], P('ch'), may hold values from -3 to 3
- cotangent: bfloat16 [16, 1280, 2048], P('batch', 'ch', 'seq'), may hold values from -6 to 6
Outputs:
- output: bfloat16 [16, 1280, 2048], P('batch', 'ch', 'seq')
- input_grad: bfloat16 [16, 1280, 2048], P('batch', 'ch', 'seq')
- grad_norm0_gain: float32 [1280], P('ch')
- grad_norm0_shift: float32 [1280], P('ch')
- grad_w_inner: float32 [1280, 640], P('ch')
- grad_b_inner: float32 [640], P('ch')
- grad_norm1_gain: float32 [640], P('ch')
- grad_norm1_shift: float32 [640], P('ch')
- grad_w_conv: float32 [5, 640, 640], P(None, 'ch')
- grad_b_conv: float32 [640], P('ch')
- grad_norm2_gain: float32 [640], P('ch')
- grad_norm2_shift: float32 [640], P('ch')
- grad_w_outer: float32 [640, 1280], P('ch')
- grad_b_outer: float32 [1280], P('ch')
The draws below stay inside these ranges and needn't reach their ends.
Inputs may be any that keep to these rules, and one draw needn't show every extreme that they name: `segment_ids`: along a row the ids never fall; each protein is one run of 1 to 512 residues, one run of each row has exactly 512, and every row holds all 8 ids.
All inputs are finite; a program needn't handle non-finite values.
Results may differ from the reference program's by a relative error of at most 0.0065.
Values may be sent and summed in bfloat16 or wider, within the bound.
A program may use at most 192 MiB of HBM per device.

```python
import math
import jax
import jax.numpy as jnp
import numpy as np
from jax import lax

D = 1280
HID = 640
KERNEL_TAPS = 5
DILATION_SPACING = 32
LEN = 2048
SEGS = 8
SEG_MOST = 512
ROWS = 16


def levels(key, dims, pieces, least, top_value):
    loudness = 1.0
    for axis_at, blocks in pieces:
        draws = jax.random.uniform(jax.random.fold_in(jax.random.fold_in(key, 6), axis_at), (blocks,), jnp.float32, least / len(pieces), top_value / len(pieces))
        loudness = loudness * jnp.repeat(jnp.exp(draws), dims[axis_at] // blocks).reshape((-1,) + (1,) * (len(dims) - 1 - axis_at))
    return loudness


def length_profile(count, total, reach, slope):
    portions = [(1 << 20) // math.isqrt(standing ** slope) + 1 for standing in range(2, count + 1)]
    surplus, counts = total - reach - (count - 1), [1] * (count - 1)
    while surplus > 0:
        free = [i for i in range(count - 1) if counts[i] < reach]
        mass, budget = sum([portions[i] for i in free]), surplus
        for i in free:
            more = min(reach - counts[i], max(1, budget * portions[i] // mass), surplus)
            counts[i] = counts[i] + more
            surplus = surplus - more
    return np.array([reach] + counts)


def uneven(rng, amount, total, reach, skew):
    if amount == 2:
        one = jax.random.randint(rng, (), max(1, total - reach), min(reach, total - 1) + 1)
        return jnp.stack([one, total - one])
    tallies = jnp.asarray(length_profile(amount, total, reach, skew), jnp.int32)
    twos = (amount - 1) // 2
    donor, taker = tallies[1:1 + 2 * twos:2], tallies[2:2 + 2 * twos:2]
    room = jnp.minimum(donor - 1, reach - taker)
    passed = jax.random.randint(jax.random.fold_in(rng, 1), (twos,), 0, 1 << 20) % (room + 1)
    tallies = tallies.at[1:1 + 2 * twos:2].set(donor - passed).at[2:2 + 2 * twos:2].set(taker + passed)
    return tallies[jax.random.permutation(jax.random.fold_in(rng, 2), amount)]


def noise(rng, shape, width, reach, cuts=(), kind=jnp.bfloat16):
    entries = jax.random.normal(rng, shape, jnp.float32) * width
    if len(cuts) > 0:
        entries = levels(rng, shape, cuts, -0.22, 0.18) * entries
    return jnp.clip(entries, min=-reach, max=reach).astype(kind)


def setup_inputs(seed: int = 0) -> dict:
    seeds = jax.random.split(jax.random.key(seed), 16)
    return {
        "inputs": noise(seeds[0], (ROWS, D, LEN), 1.0, 6.0, ((0, 4), (1, 4), (2, 2))),
        "segment_ids": jax.vmap(lambda own: jnp.searchsorted(jnp.cumsum(uneven(own, SEGS, LEN, SEG_MOST, 1)), jnp.arange(LEN), side="right"))(jax.random.split(seeds[1], ROWS)).reshape((ROWS, LEN)).astype(jnp.int32),
        "norm0_gain": jnp.clip(1.0 + 0.18 * jax.random.normal(seeds[2], (D,), jnp.float32), 0.1, 1.9),
        "norm0_shift": noise(seeds[3], (D,), 0.5, 3.0, ((0, 4),), jnp.float32),
        "w_inner": noise(seeds[4], (D, HID), D ** -0.5, 0.15625, ((0, 4),)),
        "b_inner": noise(seeds[5], (HID,), 0.5, 3.0, ((0, 4),), jnp.float32),
        "norm1_gain": jnp.clip(1.0 + 0.18 * jax.random.normal(seeds[6], (HID,), jnp.float32), 0.1, 1.9),
        "norm1_shift": noise(seeds[7], (HID,), 0.5, 3.0, ((0, 4),), jnp.float32),
        "w_conv": noise(seeds[8], (KERNEL_TAPS, HID, HID), (KERNEL_TAPS * HID) ** -0.5, 0.109375, ((1, 4),)),
        "b_conv": noise(seeds[9], (HID,), 0.5, 3.0, ((0, 4),), jnp.float32),
        "norm2_gain": jnp.clip(1.0 + 0.18 * jax.random.normal(seeds[10], (HID,), jnp.float32), 0.1, 1.9),
        "norm2_shift": noise(seeds[11], (HID,), 0.5, 3.0, ((0, 4),), jnp.float32),
        "w_outer": noise(seeds[12], (HID, D), HID ** -0.5, 0.25, ((0, 4),)),
        "b_outer": noise(seeds[13], (D,), 0.5, 3.0, ((0, 4),), jnp.float32),
        "cotangent": noise(seeds[14], (ROWS, D, LEN), 1.0, 6.0, ((0, 4), (1, 4), (2, 2))),
    }


@jax.custom_vjp
def low(v):
    return lax.optimization_barrier(v.astype(jnp.bfloat16)).astype(jnp.float32)

@jax.custom_vjp
def low_back(v):
    return v

def low_keep(v):
    return (low(v), None)

def low_pass(kept, grad):
    return (grad,)

def back_keep(v):
    return (v, None)

def back_low(kept, grad):
    return (low(grad),)
low.defvjp(low_keep, low_pass)
low_back.defvjp(back_keep, back_low)
EPSILON = 1e-05
HIGHEST = lax.Precision.HIGHEST

def layer_norm(values, gain, shift):
    center = lax.optimization_barrier(jnp.mean(values, axis=-1, keepdims=True))
    tap_displacement = values - center
    spread = lax.optimization_barrier(jnp.mean(tap_displacement * tap_displacement, axis=-1, keepdims=True))
    return tap_displacement * lax.rsqrt(spread + EPSILON) * gain + shift

def gelu_exact(values):
    return jax.nn.gelu(values, approximate=False)

def forward_block(residual, seg_rows, g0, s0, w_in, b_in, g1, s1, w_cv, b_cv, g2, s2, w_out, b_out):
    hidden0 = low(gelu_exact(layer_norm(residual, g0, s0)))
    inner = low_back(jnp.einsum('rld,dh->rlh', hidden0, w_in, precision=HIGHEST) + b_in)
    hidden1 = low(gelu_exact(layer_norm(inner, g1, s1)))
    length = seg_rows.shape[1]
    border_extent = 2 * DILATION_SPACING
    padded = jnp.pad(hidden1, ((0, 0), (border_extent, border_extent), (0, 0)))
    padded_ids = jnp.pad(seg_rows, ((0, 0), (border_extent, border_extent)), constant_values=-1)
    total = b_cv
    for tap_stride in range(KERNEL_TAPS):
        tap_displacement = (tap_stride - KERNEL_TAPS // 2) * DILATION_SPACING
        lower = border_extent + tap_displacement
        shifted = padded[:, lower:lower + length]
        matching = (padded_ids[:, lower:lower + length] == seg_rows)[:, :, None]
        tapped = jnp.where(matching, shifted, jnp.zeros_like(shifted))
        total = total + jnp.einsum('rlh,hg->rlg', tapped, w_cv[tap_stride], precision=HIGHEST)
    mixed = low_back(total)
    hidden2 = low(gelu_exact(layer_norm(mixed, g2, s2)))
    branch = jnp.einsum('rlh,hd->rld', hidden2, w_out, precision=HIGHEST) + b_out
    return residual + branch

def reference(inputs, segment_ids, norm0_gain, norm0_shift, w_inner, b_inner, norm1_gain, norm1_shift, w_conv, b_conv, norm2_gain, norm2_shift, w_outer, b_outer, cotangent):
    params = tuple((p.astype(jnp.float32) for p in (norm0_gain, norm0_shift, w_inner, b_inner, norm1_gain, norm1_shift, w_conv, b_conv, norm2_gain, norm2_shift, w_outer, b_outer)))
    groups = ROWS
    rows_x = jnp.transpose(inputs.astype(jnp.float32), (0, 2, 1)).reshape(groups, 1, LEN, D)
    row_segment_index = segment_ids.reshape(groups, 1, LEN)
    rows_cot = jnp.transpose(cotangent.astype(jnp.float32), (0, 2, 1)).reshape(groups, 1, LEN, D)

    def one_group(totals, group):
        group_x, group_ids, group_cot = group

        def run(values, *weights):
            return forward_block(values, group_ids, *weights)
        result, pull = jax.vjp(run, group_x, *params)
        grads = pull(group_cot)
        totals = tuple((t + g for t, g in zip(totals, grads[1:])))
        return (totals, (result.astype(jnp.bfloat16), grads[0].astype(jnp.bfloat16)))
    start_totals = tuple((jnp.zeros_like(p) for p in params))
    totals, (outputs, input_grads) = lax.scan(one_group, start_totals, (rows_x, row_segment_index, rows_cot))
    output = jnp.transpose(outputs.reshape(ROWS, LEN, D), (0, 2, 1))
    input_grad = jnp.transpose(input_grads.reshape(ROWS, LEN, D), (0, 2, 1))
    return (output, input_grad, totals[0], totals[1], totals[2], totals[3], totals[4], totals[5], totals[6], totals[7], totals[8], totals[9], totals[10], totals[11])
```

```python
import jax
import jax.numpy as jnp
from jax import lax
from jax.sharding import PartitionSpec as P

KERNEL_TAPS = 5
DILATION_SPACING = 32


EPSILON = 1e-05


def gelu_exact(values):
    return jax.nn.gelu(values, approximate=False)


def gelu_back(point, grad):
    return jax.vjp(gelu_exact, point)[1](grad)[0]


def normalize(values, gain, shift):
    center = jnp.mean(values, axis=1, keepdims=True)
    offset = values - center
    spread = jnp.mean(offset * offset, axis=1, keepdims=True)
    scale = lax.rsqrt(spread + EPSILON)
    unit = offset * scale
    return (unit * gain[:, None] + shift[:, None], unit, scale)


def normalize_back(grad, unit, scale, gain):
    scaled = grad * gain[:, None]
    first = jnp.mean(scaled, axis=1, keepdims=True)
    second = jnp.mean(scaled * unit, axis=1, keepdims=True)
    return scale * (scaled - first - unit * second)


def neighbour_pairs(seqs, nch, q_count):
    pairs = []
    for s in range(seqs):
        for c in range(nch):
            q = c % q_count
            if q < q_count - 1:
                pairs.append((s * nch + c, s * nch + c + 1))
            elif s < seqs - 1:
                pairs.append((s * nch + c, (s + 1) * nch + c - (q_count - 1)))
    return pairs


def extended(x, width, pairs):
    down = [(j, i) for i, j in pairs]
    length = x.shape[-1]
    before = lax.ppermute(x[..., length - width :], ("seq", "ch"), pairs)
    after = lax.ppermute(x[..., :width], ("seq", "ch"), down)
    return jnp.concatenate([before, x, after], axis=-1)


def shifted_taps(wide, wide_ids, own_ids, offsets, border):
    length = own_ids.shape[-1]
    pieces = []
    for offset in offsets:
        lower = border + offset
        shifted = wide[:, :, lower : lower + length]
        matching = wide_ids[:, lower : lower + length] == own_ids
        pieces.append(jnp.where(matching[:, None, :], shifted, jnp.zeros_like(shifted)))
    return jnp.concatenate(pieces, axis=1)


def to_positions(x, nch, q_count):
    rows, width, length = x.shape
    if q_count > 1:
        x = x.reshape(rows, width, q_count, length // q_count).transpose(0, 2, 1, 3)
        x = x.reshape(rows * q_count, width, length // q_count)
    return lax.all_to_all(x, "ch", 0, 1, tiled=True)


def to_channels(x, nch, q_count, rows):
    x = lax.all_to_all(x, "ch", 1, 0, tiled=True)
    if q_count > 1:
        _, width, part = x.shape
        x = x.reshape(rows, q_count, width, part).transpose(0, 2, 1, 3).reshape(rows, width, q_count * part)
    return x


def local(
    inputs,
    segment_ids,
    norm0_gain,
    norm0_shift,
    w_inner,
    b_inner,
    norm1_gain,
    norm1_shift,
    w_conv,
    b_conv,
    norm2_gain,
    norm2_shift,
    w_outer,
    b_outer,
    cotangent,
):
    nch = lax.axis_size("ch")
    seqs = lax.axis_size("seq")
    batches = lax.axis_size("batch")
    rows, dloc, length = inputs.shape
    hloc = w_conv.shape[1]
    hid = hloc * nch
    dim = dloc * nch
    if rows % nch == 0:
        q_count = 1
    else:
        q_count = nch // rows
    part = length // q_count
    border = 2 * DILATION_SPACING
    offsets = [(k - KERNEL_TAPS // 2) * DILATION_SPACING for k in range(KERNEL_TAPS)]
    back_offsets = [-o for o in offsets]
    pairs = neighbour_pairs(seqs, nch, q_count)
    me = lax.axis_index("ch")

    smalls = [norm0_gain, norm0_shift, b_inner, norm1_gain, norm1_shift, b_conv, norm2_gain, norm2_shift, b_outer]
    small_all = lax.all_gather(jnp.concatenate(smalls), "ch", axis=0, tiled=False)
    cut = 0
    full = []
    for s in smalls:
        n = s.shape[0]
        full.append(small_all[:, cut : cut + n].reshape(n * nch))
        cut += n
    g0, s0, b_in, g1, s1, b_cv, g2, s2, b_out = full
    packed = jnp.concatenate([w_inner.reshape(-1), w_conv.reshape(-1), w_outer.reshape(-1)])
    packed_all = lax.all_gather(packed.reshape(1, -1, 128), "ch", axis=0, tiled=True).reshape(nch, -1)
    n_in, n_cv = w_inner.size, w_conv.size
    w_in = packed_all[:, :n_in].reshape(dim, hid)
    w_cv = (
        packed_all[:, n_in : n_in + n_cv]
        .reshape(nch, KERNEL_TAPS, hloc, hid)
        .transpose(1, 0, 2, 3)
        .reshape(KERNEL_TAPS, hid, hid)
    )
    w_out = packed_all[:, n_in + n_cv :].reshape(hid, dim)

    x = to_positions(inputs, nch, q_count)
    cot = to_positions(cotangent, nch, q_count)
    prow = x.shape[0]
    if q_count == 1:
        ids = lax.dynamic_slice_in_dim(segment_ids, me * prow, prow, axis=0)
    else:
        ids = lax.dynamic_slice_in_dim(segment_ids, me // q_count, 1, axis=0)
        ids = lax.dynamic_slice_in_dim(ids, (me % q_count) * part, part, axis=1)
    own_ids = ids + 1
    wide_ids = extended(own_ids, border, pairs)

    residual = x.astype(jnp.float32)
    normed0, unit0, scale0 = normalize(residual, g0, s0)
    hidden0 = gelu_exact(normed0).astype(jnp.bfloat16)
    inner = jnp.einsum("dh,rdl->rhl", w_in, hidden0, preferred_element_type=jnp.float32) + b_in[:, None]
    normed1, unit1, scale1 = normalize(inner, g1, s1)
    hidden1 = gelu_exact(normed1).astype(jnp.bfloat16)
    wide_hidden = extended(hidden1, border, pairs)
    taps = shifted_taps(wide_hidden, wide_ids, own_ids, offsets, border)
    kernel_flat = w_cv.reshape(KERNEL_TAPS * hid, hid)
    mixed = jnp.einsum("co,rcl->rol", kernel_flat, taps, preferred_element_type=jnp.float32) + b_cv[:, None]
    normed2, unit2, scale2 = normalize(mixed, g2, s2)
    hidden2 = gelu_exact(normed2).astype(jnp.bfloat16)
    branch = jnp.einsum("hd,rhl->rdl", w_out, hidden2, preferred_element_type=jnp.float32)
    output = (residual + branch + b_out[:, None]).astype(jnp.bfloat16)

    grad_b_outer = jnp.sum(cot.astype(jnp.float32), axis=(0, 2))
    grad_w_outer = jnp.einsum("rhl,rdl->hd", hidden2, cot, preferred_element_type=jnp.float32)
    grad_hidden2 = jnp.einsum("hd,rdl->rhl", w_out, cot, preferred_element_type=jnp.float32)
    grad_normed2 = gelu_back(normed2, grad_hidden2)
    grad_norm2_gain = jnp.sum(grad_normed2 * unit2, axis=(0, 2))
    grad_norm2_shift = jnp.sum(grad_normed2, axis=(0, 2))
    grad_mixed = normalize_back(grad_normed2, unit2, scale2, g2).astype(jnp.bfloat16)
    grad_b_conv = jnp.sum(grad_mixed.astype(jnp.float32), axis=(0, 2))
    grad_w_conv = jnp.einsum("rcl,rol->co", taps, grad_mixed, preferred_element_type=jnp.float32).reshape(
        KERNEL_TAPS, hid, hid
    )
    wide_grad = extended(grad_mixed, border, pairs)
    back_taps = shifted_taps(wide_grad, wide_ids, own_ids, back_offsets, border)
    kernel_back = jnp.transpose(w_cv, (0, 2, 1)).reshape(KERNEL_TAPS * hid, hid)
    grad_hidden1 = jnp.einsum("oc,rol->rcl", kernel_back, back_taps, preferred_element_type=jnp.float32)
    grad_normed1 = gelu_back(normed1, grad_hidden1)
    grad_norm1_gain = jnp.sum(grad_normed1 * unit1, axis=(0, 2))
    grad_norm1_shift = jnp.sum(grad_normed1, axis=(0, 2))
    grad_inner = normalize_back(grad_normed1, unit1, scale1, g1).astype(jnp.bfloat16)
    grad_b_inner = jnp.sum(grad_inner.astype(jnp.float32), axis=(0, 2))
    grad_w_inner = jnp.einsum("rdl,rhl->dh", hidden0, grad_inner, preferred_element_type=jnp.float32)
    grad_hidden0 = jnp.einsum("dh,rhl->rdl", w_in, grad_inner, preferred_element_type=jnp.float32)
    grad_normed0 = gelu_back(normed0, grad_hidden0)
    grad_norm0_gain = jnp.sum(grad_normed0 * unit0, axis=(0, 2))
    grad_norm0_shift = jnp.sum(grad_normed0, axis=(0, 2))
    input_grad = (cot.astype(jnp.float32) + normalize_back(grad_normed0, unit0, scale0, g0)).astype(jnp.bfloat16)

    output = to_channels(output, nch, q_count, rows)
    input_grad = to_channels(input_grad, nch, q_count, rows)

    grads = [
        grad_norm0_gain,
        grad_norm0_shift,
        grad_w_inner,
        grad_b_inner,
        grad_norm1_gain,
        grad_norm1_shift,
        grad_w_conv.transpose(1, 0, 2),
        grad_b_conv,
        grad_norm2_gain,
        grad_norm2_shift,
        grad_w_outer,
        grad_b_outer,
    ]
    flat = [g.reshape(nch, -1) for g in grads]
    sizes = [f.shape[1] for f in flat]
    stack = jnp.concatenate(flat, axis=1)
    total = stack.shape[1]
    lanes = 128
    spread = seqs * batches * 8 * lanes
    padded = -(-total // spread) * spread
    if padded != total:
        stack = jnp.pad(stack, ((0, 0), (0, padded - total)))
    stack = stack.reshape(nch, padded // lanes, lanes)
    stack = lax.psum_scatter(stack, "seq", scatter_dimension=1, tiled=True)
    stack = lax.psum_scatter(stack, "batch", scatter_dimension=1, tiled=True)
    stack = lax.psum_scatter(stack, "ch", scatter_dimension=0, tiled=True)
    stack = lax.all_gather(stack, ("seq", "batch"), axis=1, tiled=True).reshape(padded)[:total]
    shard_shapes = [
        norm0_gain.shape,
        norm0_shift.shape,
        w_inner.shape,
        b_inner.shape,
        norm1_gain.shape,
        norm1_shift.shape,
        (hloc, KERNEL_TAPS, hid),
        b_conv.shape,
        norm2_gain.shape,
        norm2_shift.shape,
        w_outer.shape,
        b_outer.shape,
    ]
    outs = []
    cut = 0
    for n, shape in zip(sizes, shard_shapes):
        outs.append(stack[cut : cut + n].reshape(shape))
        cut += n
    outs[6] = outs[6].transpose(1, 0, 2)
    return (output, input_grad, *outs)


def solution(mesh):
    return jax.shard_map(
        local,
        mesh=mesh,
        in_specs=(
            P("batch", "ch", "seq"),
            P("batch", "seq"),
            P("ch"),
            P("ch"),
            P("ch", None),
            P("ch"),
            P("ch"),
            P("ch"),
            P(None, "ch", None),
            P("ch"),
            P("ch"),
            P("ch"),
            P("ch", None),
            P("ch"),
            P("batch", "ch", "seq"),
        ),
        out_specs=(
            P("batch", "ch", "seq"),
            P("batch", "ch", "seq"),
            P("ch"),
            P("ch"),
            P("ch", None),
            P("ch"),
            P("ch"),
            P("ch"),
            P(None, "ch", None),
            P("ch"),
            P("ch"),
            P("ch"),
            P("ch", None),
            P("ch"),
        ),
        check_vma=False,
    )
```

```python
import jax
import jax.numpy as jnp
from jax import lax
from jax.sharding import PartitionSpec as P

KERNEL_TAPS = 5
DILATION_SPACING = 32


EPSILON = 1e-05


def gelu_exact(values):
    return jax.nn.gelu(values, approximate=False)


def gelu_back(point, grad):
    return jax.vjp(gelu_exact, point)[1](grad)[0]


def normalize(values, gain, shift):
    center = jnp.mean(values, axis=1, keepdims=True)
    offset = values - center
    spread = jnp.mean(offset * offset, axis=1, keepdims=True)
    scale = lax.rsqrt(spread + EPSILON)
    unit = offset * scale
    return (unit * gain[:, None] + shift[:, None], unit, scale)


def normalize_back(grad, unit, scale, gain):
    scaled = grad * gain[:, None]
    first = jnp.mean(scaled, axis=1, keepdims=True)
    second = jnp.mean(scaled * unit, axis=1, keepdims=True)
    return scale * (scaled - first - unit * second)


def neighbour_pairs(seqs, nch, q_count):
    pairs = []
    for s in range(seqs):
        for c in range(nch):
            q = c % q_count
            if q < q_count - 1:
                pairs.append((s * nch + c, s * nch + c + 1))
            elif s < seqs - 1:
                pairs.append((s * nch + c, (s + 1) * nch + c - (q_count - 1)))
    return pairs


def extended(x, width, pairs):
    down = [(j, i) for i, j in pairs]
    length = x.shape[-1]
    before = lax.ppermute(x[..., length - width :], ("seq", "ch"), pairs)
    after = lax.ppermute(x[..., :width], ("seq", "ch"), down)
    return jnp.concatenate([before, x, after], axis=-1)


def shifted_taps(wide, wide_ids, own_ids, offsets, border):
    length = own_ids.shape[-1]
    pieces = []
    for offset in offsets:
        lower = border + offset
        shifted = wide[:, :, lower : lower + length]
        matching = wide_ids[:, lower : lower + length] == own_ids
        pieces.append(jnp.where(matching[:, None, :], shifted, jnp.zeros_like(shifted)))
    return jnp.concatenate(pieces, axis=1)


def to_positions(x, nch, q_count):
    rows, width, length = x.shape
    if q_count > 1:
        x = x.reshape(rows, width, q_count, length // q_count).transpose(0, 2, 1, 3)
        x = x.reshape(rows * q_count, width, length // q_count)
    x = lax.all_to_all(x, "ch", 0, 0, tiled=True)
    return _join(x, nch)


def _join(x, nch):
    total, width, length = x.shape
    p = total // nch
    return x.reshape(nch, p, width, length).transpose(1, 0, 2, 3).reshape(p, nch * width, length)


def to_channels(x, nch, q_count, rows):
    p, width, length = x.shape
    x = x.reshape(p, nch, width // nch, length).transpose(1, 0, 2, 3).reshape(nch * p, width // nch, length)
    x = lax.all_to_all(x, "ch", 0, 0, tiled=True)
    if q_count > 1:
        _, width, part = x.shape
        x = x.reshape(rows, q_count, width, part).transpose(0, 2, 1, 3).reshape(rows, width, q_count * part)
    return x


def local(
    inputs,
    segment_ids,
    norm0_gain,
    norm0_shift,
    w_inner,
    b_inner,
    norm1_gain,
    norm1_shift,
    w_conv,
    b_conv,
    norm2_gain,
    norm2_shift,
    w_outer,
    b_outer,
    cotangent,
):
    nch = lax.axis_size("ch")
    seqs = lax.axis_size("seq")
    batches = lax.axis_size("batch")
    rows, dloc, length = inputs.shape
    hloc = w_conv.shape[1]
    hid = hloc * nch
    dim = dloc * nch
    if rows % nch == 0:
        q_count = 1
    else:
        q_count = nch // rows
    part = length // q_count
    border = 2 * DILATION_SPACING
    offsets = [(k - KERNEL_TAPS // 2) * DILATION_SPACING for k in range(KERNEL_TAPS)]
    back_offsets = [-o for o in offsets]
    pairs = neighbour_pairs(seqs, nch, q_count)
    me = lax.axis_index("ch")

    smalls = [norm0_gain, norm0_shift, b_inner, norm1_gain, norm1_shift, b_conv, norm2_gain, norm2_shift, b_outer]
    small_cat = jnp.concatenate(smalls)
    small_len = small_cat.shape[0]
    small_pad = -(-small_len // 1024) * 1024
    small_cat = jnp.pad(small_cat, (0, small_pad - small_len)).reshape(1, small_pad // 128, 128)
    small_all = lax.all_gather(small_cat, "ch", axis=0, tiled=True).reshape(nch, small_pad)
    cut = 0
    full = []
    for s in smalls:
        n = s.shape[0]
        full.append(small_all[:, cut : cut + n].reshape(n * nch))
        cut += n
    g0, s0, b_in, g1, s1, b_cv, g2, s2, b_out = full
    sidx = lax.axis_index("seq")
    w_in = lax.dynamic_slice_in_dim(w_inner, sidx * (dloc // seqs), dloc // seqs, 0)
    w_cv = lax.dynamic_slice_in_dim(w_conv, sidx * (hloc // seqs), hloc // seqs, 1)
    w_out = lax.dynamic_slice_in_dim(w_outer, sidx * (hloc // seqs), hloc // seqs, 0)
    w_in = lax.all_gather(w_in, "ch", axis=0)
    w_cv = lax.all_gather(w_cv, "ch", axis=1)
    w_out = lax.all_gather(w_out, "ch", axis=0)
    w_in = lax.all_gather(w_in, "seq", axis=1, tiled=True).reshape(dim, hid)
    w_cv = lax.all_gather(w_cv, "seq", axis=2, tiled=True).reshape(KERNEL_TAPS, hid, hid)
    w_out = lax.all_gather(w_out, "seq", axis=1, tiled=True).reshape(hid, dim)

    x = to_positions(inputs, nch, q_count)
    cot = to_positions(cotangent, nch, q_count)
    prow = x.shape[0]
    if q_count == 1:
        ids = lax.dynamic_slice_in_dim(segment_ids, me * prow, prow, axis=0)
    else:
        ids = lax.dynamic_slice_in_dim(segment_ids, me // q_count, 1, axis=0)
        ids = lax.dynamic_slice_in_dim(ids, (me % q_count) * part, part, axis=1)
    own_ids = ids + 1
    wide_ids = extended(own_ids, border, pairs)

    residual = x.astype(jnp.float32)
    normed0, unit0, scale0 = normalize(residual, g0, s0)
    hidden0 = gelu_exact(normed0).astype(jnp.bfloat16)
    inner = jnp.einsum("dh,rdl->rhl", w_in, hidden0, preferred_element_type=jnp.float32) + b_in[:, None]
    normed1, unit1, scale1 = normalize(inner, g1, s1)
    hidden1 = gelu_exact(normed1).astype(jnp.bfloat16)
    wide_hidden = extended(hidden1, border, pairs)
    taps = shifted_taps(wide_hidden, wide_ids, own_ids, offsets, border)
    kernel_flat = w_cv.reshape(KERNEL_TAPS * hid, hid)
    mixed = jnp.einsum("co,rcl->rol", kernel_flat, taps, preferred_element_type=jnp.float32) + b_cv[:, None]
    normed2, unit2, scale2 = normalize(mixed, g2, s2)
    hidden2 = gelu_exact(normed2).astype(jnp.bfloat16)
    branch = jnp.einsum("hd,rhl->rdl", w_out, hidden2, preferred_element_type=jnp.float32)
    output = (residual + branch + b_out[:, None]).astype(jnp.bfloat16)

    grad_b_outer = jnp.sum(cot.astype(jnp.float32), axis=(0, 2))
    grad_w_outer = jnp.einsum("rhl,rdl->hd", hidden2, cot, preferred_element_type=jnp.float32)
    grad_hidden2 = jnp.einsum("hd,rdl->rhl", w_out, cot, preferred_element_type=jnp.float32)
    grad_normed2 = gelu_back(normed2, grad_hidden2)
    grad_norm2_gain = jnp.sum(grad_normed2 * unit2, axis=(0, 2))
    grad_norm2_shift = jnp.sum(grad_normed2, axis=(0, 2))
    grad_mixed = normalize_back(grad_normed2, unit2, scale2, g2).astype(jnp.bfloat16)
    grad_b_conv = jnp.sum(grad_mixed.astype(jnp.float32), axis=(0, 2))
    grad_w_conv = jnp.einsum("rcl,rol->co", taps, grad_mixed, preferred_element_type=jnp.float32).reshape(
        KERNEL_TAPS, hid, hid
    )
    wide_grad = extended(grad_mixed, border, pairs)
    back_taps = shifted_taps(wide_grad, wide_ids, own_ids, back_offsets, border)
    kernel_back = jnp.transpose(w_cv, (0, 2, 1)).reshape(KERNEL_TAPS * hid, hid)
    grad_hidden1 = jnp.einsum("oc,rol->rcl", kernel_back, back_taps, preferred_element_type=jnp.float32)
    grad_normed1 = gelu_back(normed1, grad_hidden1)
    grad_norm1_gain = jnp.sum(grad_normed1 * unit1, axis=(0, 2))
    grad_norm1_shift = jnp.sum(grad_normed1, axis=(0, 2))
    grad_inner = normalize_back(grad_normed1, unit1, scale1, g1).astype(jnp.bfloat16)
    grad_b_inner = jnp.sum(grad_inner.astype(jnp.float32), axis=(0, 2))
    grad_w_inner = jnp.einsum("rdl,rhl->dh", hidden0, grad_inner, preferred_element_type=jnp.float32)
    grad_hidden0 = jnp.einsum("dh,rhl->rdl", w_in, grad_inner, preferred_element_type=jnp.float32)
    grad_normed0 = gelu_back(normed0, grad_hidden0)
    grad_norm0_gain = jnp.sum(grad_normed0 * unit0, axis=(0, 2))
    grad_norm0_shift = jnp.sum(grad_normed0, axis=(0, 2))
    input_grad = (cot.astype(jnp.float32) + normalize_back(grad_normed0, unit0, scale0, g0)).astype(jnp.bfloat16)

    output = to_channels(output, nch, q_count, rows)
    input_grad = to_channels(input_grad, nch, q_count, rows)

    def reduce_weight(g, shard_dim, split_dim):
        g = lax.psum_scatter(g, "seq", scatter_dimension=split_dim, tiled=True)
        g = lax.psum_scatter(g, "batch", scatter_dimension=split_dim, tiled=True)
        g = lax.psum_scatter(g, "ch", scatter_dimension=shard_dim, tiled=True)
        return lax.all_gather(g, ("seq", "batch"), axis=split_dim, tiled=True)

    red_w_outer = reduce_weight(grad_w_outer.reshape(nch, hloc, dim), 0, 2).reshape(hloc, dim)
    red_w_conv = reduce_weight(grad_w_conv, 1, 2)
    red_w_inner = reduce_weight(grad_w_inner.reshape(nch, dloc, hid), 0, 1).reshape(dloc, hid)
    vectors = [
        grad_norm0_gain,
        grad_norm0_shift,
        grad_b_inner,
        grad_norm1_gain,
        grad_norm1_shift,
        grad_b_conv,
        grad_norm2_gain,
        grad_norm2_shift,
        grad_b_outer,
    ]
    flat = jnp.concatenate([v.reshape(nch, -1) for v in vectors], axis=1)
    flat = lax.psum(flat, ("seq", "batch", "ch"))
    mine = lax.dynamic_index_in_dim(flat, me, 0, keepdims=False)
    reds = []
    cut = 0
    for v in vectors:
        n = v.shape[0] // nch
        reds.append(mine[cut : cut + n])
        cut += n
    return (
        output,
        input_grad,
        reds[0],
        reds[1],
        red_w_inner,
        reds[2],
        reds[3],
        reds[4],
        red_w_conv,
        reds[5],
        reds[6],
        reds[7],
        red_w_outer,
        reds[8],
    )


def solution(mesh):
    return jax.shard_map(
        local,
        mesh=mesh,
        in_specs=(
            P("batch", "ch", "seq"),
            P("batch", "seq"),
            P("ch"),
            P("ch"),
            P("ch", None),
            P("ch"),
            P("ch"),
            P("ch"),
            P(None, "ch", None),
            P("ch"),
            P("ch"),
            P("ch"),
            P("ch", None),
            P("ch"),
            P("batch", "ch", "seq"),
        ),
        out_specs=(
            P("batch", "ch", "seq"),
            P("batch", "ch", "seq"),
            P("ch"),
            P("ch"),
            P("ch", None),
            P("ch"),
            P("ch"),
            P("ch"),
            P(None, "ch", None),
            P("ch"),
            P("ch"),
            P("ch"),
            P("ch", None),
            P("ch"),
        ),
        check_vma=False,
    )
```

```python
import functools
import math

import jax
import jax.numpy as jnp
from jax import lax
from jax.experimental import pallas as pl
from jax.experimental.pallas import tpu as pltpu
from jax.sharding import PartitionSpec as P

KERNEL_TAPS = 5
DILATION_SPACING = 32


EPSILON = 1e-05


MESH_AXES = ("batch", "seq", "ch")
MESH_ID = pl.DeviceIdType.MESH


def _exchange_kernel(sizes, group, gather, x_ref, o_ref, send_sem, recv_sem, own_sem):
    coords = {a: lax.axis_index(a) for a in MESH_AXES}
    me = 0
    for a in group:
        me = me * sizes[a] + coords[a]
    count = math.prod(sizes[a] for a in group)

    def device(index):
        where = dict(coords)
        rest = index
        for a in reversed(group):
            where[a] = lax.rem(rest, sizes[a])
            rest = rest // sizes[a]
        return tuple(where[a] for a in MESH_AXES)

    barrier = pltpu.get_barrier_semaphore()
    for j in range(1, count):
        pl.semaphore_signal(barrier, 1, device_id=device(lax.rem(me + j, count)), device_id_type=MESH_ID)
    pl.semaphore_wait(barrier, count - 1)
    copies = []
    for j in range(1, count):
        peer = lax.rem(me + j, count)
        copy = pltpu.make_async_remote_copy(
            src_ref=x_ref if gather else x_ref.at[peer],
            dst_ref=o_ref.at[me],
            send_sem=send_sem.at[j - 1],
            recv_sem=recv_sem.at[j - 1],
            device_id=device(peer),
            device_id_type=MESH_ID,
        )
        copy.start()
        copies.append(copy)
    own = pltpu.make_async_copy(x_ref if gather else x_ref.at[me], o_ref.at[me], own_sem)
    own.start()
    own.wait()
    for copy in copies:
        copy.wait()


def exchange(x, group, collective_id, gather=False):
    sizes = {a: lax.axis_size(a) for a in MESH_AXES}
    count = math.prod(sizes[a] for a in group)
    if count == 1:
        return x[None] if gather else x
    out_shape = (count,) + x.shape if gather else x.shape
    moved = x.size * x.dtype.itemsize * (count if gather else 1)
    return pl.pallas_call(
        functools.partial(_exchange_kernel, sizes, group, gather),
        out_shape=jax.ShapeDtypeStruct(out_shape, x.dtype),
        in_specs=[pl.BlockSpec(memory_space=pl.ANY)],
        out_specs=pl.BlockSpec(memory_space=pl.ANY),
        scratch_shapes=[
            pltpu.SemaphoreType.DMA((count - 1,)),
            pltpu.SemaphoreType.DMA((count - 1,)),
            pltpu.SemaphoreType.DMA(()),
        ],
        compiler_params=pltpu.CompilerParams(collective_id=collective_id, has_side_effects=True),
        cost_estimate=pl.CostEstimate(flops=0, transcendentals=0, bytes_accessed=2 * moved),
    )(x)


def gelu_exact(values):
    return jax.nn.gelu(values, approximate=False)


def gelu_back(point, grad):
    return jax.vjp(gelu_exact, point)[1](grad)[0]


def normalize(values, gain, shift):
    center = jnp.mean(values, axis=1, keepdims=True)
    offset = values - center
    spread = jnp.mean(offset * offset, axis=1, keepdims=True)
    scale = lax.rsqrt(spread + EPSILON)
    unit = offset * scale
    return (unit * gain[:, None] + shift[:, None], unit, scale)


def normalize_back(grad, unit, scale, gain):
    scaled = grad * gain[:, None]
    first = jnp.mean(scaled, axis=1, keepdims=True)
    second = jnp.mean(scaled * unit, axis=1, keepdims=True)
    return scale * (scaled - first - unit * second)


def neighbour_pairs(seqs, nch, q_count):
    pairs = []
    for s in range(seqs):
        for c in range(nch):
            q = c % q_count
            if q < q_count - 1:
                pairs.append((s * nch + c, s * nch + c + 1))
            elif s < seqs - 1:
                pairs.append((s * nch + c, (s + 1) * nch + c - (q_count - 1)))
    return pairs


def extended(x, width, pairs):
    down = [(j, i) for i, j in pairs]
    length = x.shape[-1]
    before = lax.ppermute(x[..., length - width :], ("seq", "ch"), pairs)
    after = lax.ppermute(x[..., :width], ("seq", "ch"), down)
    return jnp.concatenate([before, x, after], axis=-1)


def shifted_taps(wide, wide_ids, own_ids, offsets, border):
    length = own_ids.shape[-1]
    pieces = []
    for offset in offsets:
        lower = border + offset
        shifted = wide[:, :, lower : lower + length]
        matching = wide_ids[:, lower : lower + length] == own_ids
        pieces.append(jnp.where(matching[:, None, :], shifted, jnp.zeros_like(shifted)))
    return jnp.concatenate(pieces, axis=1)


def to_positions(x, nch, q_count):
    rows, width, length = x.shape
    if q_count > 1:
        x = x.reshape(rows, width, q_count, length // q_count).transpose(0, 2, 1, 3)
        x = x.reshape(rows * q_count, width, length // q_count)
    x = lax.all_to_all(x, "ch", 0, 0, tiled=True)
    return _join(x, nch)


def _join(x, nch):
    total, width, length = x.shape
    p = total // nch
    return x.reshape(nch, p, width, length).transpose(1, 0, 2, 3).reshape(p, nch * width, length)


def to_channels(x, nch, q_count, rows):
    p, width, length = x.shape
    x = x.reshape(p, nch, width // nch, length).transpose(1, 0, 2, 3).reshape(nch * p, width // nch, length)
    x = lax.all_to_all(x, "ch", 0, 0, tiled=True)
    if q_count > 1:
        _, width, part = x.shape
        x = x.reshape(rows, q_count, width, part).transpose(0, 2, 1, 3).reshape(rows, width, q_count * part)
    return x


def local(
    inputs,
    segment_ids,
    norm0_gain,
    norm0_shift,
    w_inner,
    b_inner,
    norm1_gain,
    norm1_shift,
    w_conv,
    b_conv,
    norm2_gain,
    norm2_shift,
    w_outer,
    b_outer,
    cotangent,
):
    nch = lax.axis_size("ch")
    seqs = lax.axis_size("seq")
    batches = lax.axis_size("batch")
    rows, dloc, length = inputs.shape
    hloc = w_conv.shape[1]
    hid = hloc * nch
    dim = dloc * nch
    if rows % nch == 0:
        q_count = 1
    else:
        q_count = nch // rows
    part = length // q_count
    border = 2 * DILATION_SPACING
    offsets = [(k - KERNEL_TAPS // 2) * DILATION_SPACING for k in range(KERNEL_TAPS)]
    back_offsets = [-o for o in offsets]
    pairs = neighbour_pairs(seqs, nch, q_count)
    me = lax.axis_index("ch")

    smalls = [norm0_gain, norm0_shift, b_inner, norm1_gain, norm1_shift, b_conv, norm2_gain, norm2_shift, b_outer]
    small_all = exchange(jnp.concatenate(smalls), ("ch",), 0, gather=True)
    cut = 0
    full = []
    for v in smalls:
        n = v.shape[0]
        full.append(small_all[:, cut : cut + n].reshape(n * nch))
        cut += n
    g0, s0, b_in, g1, s1, b_cv, g2, s2, b_out = full
    sidx = lax.axis_index("seq")
    w_in = lax.dynamic_slice_in_dim(w_inner, sidx * (dloc // seqs), dloc // seqs, 0)
    w_cv = lax.dynamic_slice_in_dim(w_conv, sidx * (hloc // seqs), hloc // seqs, 1)
    w_out = lax.dynamic_slice_in_dim(w_outer, sidx * (hloc // seqs), hloc // seqs, 0)
    w_in = exchange(exchange(w_in, ("ch",), 1, gather=True), ("seq",), 2, gather=True)
    w_cv = exchange(exchange(w_cv, ("ch",), 3, gather=True), ("seq",), 4, gather=True)
    w_out = exchange(exchange(w_out, ("ch",), 5, gather=True), ("seq",), 6, gather=True)
    w_in = w_in.transpose(1, 0, 2, 3).reshape(dim, hid)
    w_cv = w_cv.transpose(2, 1, 0, 3, 4).reshape(KERNEL_TAPS, hid, hid)
    w_out = w_out.transpose(1, 0, 2, 3).reshape(hid, dim)

    x = to_positions(inputs, nch, q_count)
    cot = to_positions(cotangent, nch, q_count)
    prow = x.shape[0]
    if q_count == 1:
        ids = lax.dynamic_slice_in_dim(segment_ids, me * prow, prow, axis=0)
    else:
        ids = lax.dynamic_slice_in_dim(segment_ids, me // q_count, 1, axis=0)
        ids = lax.dynamic_slice_in_dim(ids, (me % q_count) * part, part, axis=1)
    own_ids = ids + 1
    wide_ids = extended(own_ids, border, pairs)

    residual = x.astype(jnp.float32)
    normed0, unit0, scale0 = normalize(residual, g0, s0)
    hidden0 = gelu_exact(normed0).astype(jnp.bfloat16)
    inner = jnp.einsum("dh,rdl->rhl", w_in, hidden0, preferred_element_type=jnp.float32) + b_in[:, None]
    normed1, unit1, scale1 = normalize(inner, g1, s1)
    hidden1 = gelu_exact(normed1).astype(jnp.bfloat16)
    wide_hidden = extended(hidden1, border, pairs)
    taps = shifted_taps(wide_hidden, wide_ids, own_ids, offsets, border)
    kernel_flat = w_cv.reshape(KERNEL_TAPS * hid, hid)
    mixed = jnp.einsum("co,rcl->rol", kernel_flat, taps, preferred_element_type=jnp.float32) + b_cv[:, None]
    normed2, unit2, scale2 = normalize(mixed, g2, s2)
    hidden2 = gelu_exact(normed2).astype(jnp.bfloat16)
    branch = jnp.einsum("hd,rhl->rdl", w_out, hidden2, preferred_element_type=jnp.float32)
    output = (residual + branch + b_out[:, None]).astype(jnp.bfloat16)

    grad_b_outer = jnp.sum(cot.astype(jnp.float32), axis=(0, 2))
    grad_w_outer = jnp.einsum("rhl,rdl->hd", hidden2, cot, preferred_element_type=jnp.float32)
    grad_hidden2 = jnp.einsum("hd,rdl->rhl", w_out, cot, preferred_element_type=jnp.float32)
    grad_normed2 = gelu_back(normed2, grad_hidden2)
    grad_norm2_gain = jnp.sum(grad_normed2 * unit2, axis=(0, 2))
    grad_norm2_shift = jnp.sum(grad_normed2, axis=(0, 2))
    grad_mixed = normalize_back(grad_normed2, unit2, scale2, g2).astype(jnp.bfloat16)
    grad_b_conv = jnp.sum(grad_mixed.astype(jnp.float32), axis=(0, 2))
    grad_w_conv = jnp.einsum(
        "rkcil,rol->ckio",
        taps.reshape(prow, KERNEL_TAPS, nch, hloc, part),
        grad_mixed,
        preferred_element_type=jnp.float32,
    )
    wide_grad = extended(grad_mixed, border, pairs)
    back_taps = shifted_taps(wide_grad, wide_ids, own_ids, back_offsets, border)
    kernel_back = jnp.transpose(w_cv, (0, 2, 1)).reshape(KERNEL_TAPS * hid, hid)
    grad_hidden1 = jnp.einsum("oc,rol->rcl", kernel_back, back_taps, preferred_element_type=jnp.float32)
    grad_normed1 = gelu_back(normed1, grad_hidden1)
    grad_norm1_gain = jnp.sum(grad_normed1 * unit1, axis=(0, 2))
    grad_norm1_shift = jnp.sum(grad_normed1, axis=(0, 2))
    grad_inner = normalize_back(grad_normed1, unit1, scale1, g1).astype(jnp.bfloat16)
    grad_b_inner = jnp.sum(grad_inner.astype(jnp.float32), axis=(0, 2))
    grad_w_inner = jnp.einsum("rdl,rhl->dh", hidden0, grad_inner, preferred_element_type=jnp.float32)
    grad_hidden0 = jnp.einsum("dh,rhl->rdl", w_in, grad_inner, preferred_element_type=jnp.float32)
    grad_normed0 = gelu_back(normed0, grad_hidden0)
    grad_norm0_gain = jnp.sum(grad_normed0 * unit0, axis=(0, 2))
    grad_norm0_shift = jnp.sum(grad_normed0, axis=(0, 2))
    input_grad = (cot.astype(jnp.float32) + normalize_back(grad_normed0, unit0, scale0, g0)).astype(jnp.bfloat16)

    output = to_channels(output, nch, q_count, rows)
    input_grad = to_channels(input_grad, nch, q_count, rows)

    vectors = [
        grad_norm0_gain,
        grad_norm0_shift,
        grad_b_inner,
        grad_norm1_gain,
        grad_norm1_shift,
        grad_b_conv,
        grad_norm2_gain,
        grad_norm2_shift,
        grad_b_outer,
    ]
    flat = jnp.concatenate([v.reshape(nch, -1) for v in vectors], axis=1)
    vec_len = flat.shape[1]
    vec_rows = -(-vec_len // dim)
    flat = jnp.pad(flat, ((0, 0), (0, vec_rows * dim - vec_len))).reshape(nch, vec_rows, dim)
    outer_plus = jnp.concatenate([grad_w_outer.reshape(nch, hloc, dim), flat], axis=1)

    def reduce_weight(g, split_dim, cid):
        g = lax.psum_scatter(g, "seq", scatter_dimension=split_dim, tiled=True)
        g = lax.psum_scatter(g, "batch", scatter_dimension=split_dim, tiled=True)
        g = jnp.sum(exchange(g, ("ch",), cid), axis=0)
        g = exchange(g, ("seq", "batch"), cid + 1, gather=True)
        return jnp.moveaxis(g, 0, split_dim - 1)

    red_outer = reduce_weight(outer_plus, 2, 7)
    red_outer = red_outer.reshape(hloc + vec_rows, dim)
    red_w_outer = red_outer[:hloc]
    mine = red_outer[hloc:].reshape(-1)[:vec_len]
    red_w_conv = reduce_weight(grad_w_conv, 3, 9)
    red_w_conv = red_w_conv.reshape(KERNEL_TAPS, hloc, hid)
    red_w_inner = reduce_weight(grad_w_inner.reshape(nch, dloc, hid), 1, 11).reshape(dloc, hid)
    reds = []
    cut = 0
    for v in vectors:
        n = v.shape[0] // nch
        reds.append(mine[cut : cut + n])
        cut += n
    return (
        output,
        input_grad,
        reds[0],
        reds[1],
        red_w_inner,
        reds[2],
        reds[3],
        reds[4],
        red_w_conv,
        reds[5],
        reds[6],
        reds[7],
        red_w_outer,
        reds[8],
    )


def solution(mesh):
    return jax.shard_map(
        local,
        mesh=mesh,
        in_specs=(
            P("batch", "ch", "seq"),
            P("batch", "seq"),
            P("ch"),
            P("ch"),
            P("ch", None),
            P("ch"),
            P("ch"),
            P("ch"),
            P(None, "ch", None),
            P("ch"),
            P("ch"),
            P("ch"),
            P("ch", None),
            P("ch"),
            P("batch", "ch", "seq"),
        ),
        out_specs=(
            P("batch", "ch", "seq"),
            P("batch", "ch", "seq"),
            P("ch"),
            P("ch"),
            P("ch", None),
            P("ch"),
            P("ch"),
            P("ch"),
            P(None, "ch", None),
            P("ch"),
            P("ch"),
            P("ch"),
            P("ch", None),
            P("ch"),
        ),
        check_vma=False,
    )
```

```python
import functools
import math

import jax
import jax.numpy as jnp
from jax import lax
from jax.experimental import pallas as pl
from jax.experimental.pallas import tpu as pltpu
from jax.sharding import PartitionSpec as P

KERNEL_TAPS = 5
DILATION_SPACING = 32


EPSILON = 1e-05


MESH_AXES = ("batch", "seq", "ch")
MESH_ID = pl.DeviceIdType.MESH


def _exchange_kernel(sizes, group, gather, x_ref, o_ref, send_sem, recv_sem):
    coords = {a: lax.axis_index(a) for a in MESH_AXES}
    me = 0
    for a in group:
        me = me * sizes[a] + coords[a]
    count = math.prod(sizes[a] for a in group)

    def device(index):
        where = dict(coords)
        rest = index
        for a in reversed(group):
            where[a] = lax.rem(rest, sizes[a])
            rest = rest // sizes[a]
        return tuple(where[a] for a in MESH_AXES)

    barrier = pltpu.get_barrier_semaphore()
    for j in range(1, count):
        pl.semaphore_signal(barrier, 1, device_id=device(lax.rem(me + j, count)), device_id_type=MESH_ID)
    pl.semaphore_wait(barrier, count - 1)
    copies = []
    for j in range(1, count):
        peer = lax.rem(me + j, count)
        copy = pltpu.make_async_remote_copy(
            src_ref=x_ref if gather else x_ref.at[peer],
            dst_ref=o_ref.at[me],
            send_sem=send_sem.at[j - 1],
            recv_sem=recv_sem.at[j - 1],
            device_id=device(peer),
            device_id_type=MESH_ID,
        )
        copy.start()
        copies.append(copy)
    for copy in copies:
        copy.wait()


def exchange(x, group, collective_id, gather=False):
    sizes = {a: lax.axis_size(a) for a in MESH_AXES}
    count = math.prod(sizes[a] for a in group)
    if count == 1:
        return x[None] if gather else x
    out_shape = (count,) + x.shape if gather else x.shape
    moved = x.size * x.dtype.itemsize * (count if gather else 1)
    out = pl.pallas_call(
        functools.partial(_exchange_kernel, sizes, group, gather),
        out_shape=jax.ShapeDtypeStruct(out_shape, x.dtype),
        in_specs=[pl.BlockSpec(memory_space=pl.ANY)],
        out_specs=pl.BlockSpec(memory_space=pl.ANY),
        scratch_shapes=[
            pltpu.SemaphoreType.DMA((count - 1,)),
            pltpu.SemaphoreType.DMA((count - 1,)),
        ],
        compiler_params=pltpu.CompilerParams(collective_id=collective_id, has_side_effects=True),
        cost_estimate=pl.CostEstimate(flops=0, transcendentals=0, bytes_accessed=2 * moved),
    )(x)
    me = 0
    for a in group:
        me = me * sizes[a] + lax.axis_index(a)
    own = x if gather else lax.dynamic_index_in_dim(x, me, 0, keepdims=False)
    return lax.dynamic_update_index_in_dim(out, own, me, 0)


def gelu_exact(values):
    return jax.nn.gelu(values, approximate=False)


def gelu_back(point, grad):
    return jax.vjp(gelu_exact, point)[1](grad)[0]


def normalize(values, gain, shift):
    center = jnp.mean(values, axis=1, keepdims=True)
    offset = values - center
    spread = jnp.mean(offset * offset, axis=1, keepdims=True)
    scale = lax.rsqrt(spread + EPSILON)
    unit = offset * scale
    return (unit * gain[:, None] + shift[:, None], unit, scale)


def normalize_back(grad, unit, scale, gain):
    scaled = grad * gain[:, None]
    first = jnp.mean(scaled, axis=1, keepdims=True)
    second = jnp.mean(scaled * unit, axis=1, keepdims=True)
    return scale * (scaled - first - unit * second)


def neighbour_pairs(seqs, nch, q_count):
    pairs = []
    for s in range(seqs):
        for c in range(nch):
            q = c % q_count
            if q < q_count - 1:
                pairs.append((s * nch + c, s * nch + c + 1))
            elif s < seqs - 1:
                pairs.append((s * nch + c, (s + 1) * nch + c - (q_count - 1)))
    return pairs


def extended(x, width, pairs):
    down = [(j, i) for i, j in pairs]
    length = x.shape[-1]
    before = lax.ppermute(x[..., length - width :], ("seq", "ch"), pairs)
    after = lax.ppermute(x[..., :width], ("seq", "ch"), down)
    return jnp.concatenate([before, x, after], axis=-1)


def shifted_taps(wide, wide_ids, own_ids, offsets, border):
    length = own_ids.shape[-1]
    pieces = []
    for offset in offsets:
        lower = border + offset
        shifted = wide[:, :, lower : lower + length]
        matching = wide_ids[:, lower : lower + length] == own_ids
        pieces.append(jnp.where(matching[:, None, :], shifted, jnp.zeros_like(shifted)))
    return jnp.concatenate(pieces, axis=1)


def to_positions(x, nch, q_count):
    rows, width, length = x.shape
    if q_count > 1:
        x = x.reshape(rows, width, q_count, length // q_count).transpose(0, 2, 1, 3)
        x = x.reshape(rows * q_count, width, length // q_count)
    x = lax.all_to_all(x, "ch", 0, 0, tiled=True)
    return _join(x, nch)


def _join(x, nch):
    total, width, length = x.shape
    p = total // nch
    return x.reshape(nch, p, width, length).transpose(1, 0, 2, 3).reshape(p, nch * width, length)


def to_channels(x, nch, q_count, rows):
    p, width, length = x.shape
    x = x.reshape(p, nch, width // nch, length).transpose(1, 0, 2, 3).reshape(nch * p, width // nch, length)
    x = lax.all_to_all(x, "ch", 0, 0, tiled=True)
    if q_count > 1:
        _, width, part = x.shape
        x = x.reshape(rows, q_count, width, part).transpose(0, 2, 1, 3).reshape(rows, width, q_count * part)
    return x


def local(
    inputs,
    segment_ids,
    norm0_gain,
    norm0_shift,
    w_inner,
    b_inner,
    norm1_gain,
    norm1_shift,
    w_conv,
    b_conv,
    norm2_gain,
    norm2_shift,
    w_outer,
    b_outer,
    cotangent,
):
    nch = lax.axis_size("ch")
    seqs = lax.axis_size("seq")
    batches = lax.axis_size("batch")
    rows, dloc, length = inputs.shape
    hloc = w_conv.shape[1]
    hid = hloc * nch
    dim = dloc * nch
    if rows % nch == 0:
        q_count = 1
    else:
        q_count = nch // rows
    part = length // q_count
    border = 2 * DILATION_SPACING
    offsets = [(k - KERNEL_TAPS // 2) * DILATION_SPACING for k in range(KERNEL_TAPS)]
    back_offsets = [-o for o in offsets]
    pairs = neighbour_pairs(seqs, nch, q_count)
    me = lax.axis_index("ch")

    smalls = [norm0_gain, norm0_shift, b_inner, norm1_gain, norm1_shift, b_conv, norm2_gain, norm2_shift, b_outer]
    small_all = exchange(jnp.concatenate(smalls), ("ch",), 0, gather=True)
    cut = 0
    full = []
    for v in smalls:
        n = v.shape[0]
        full.append(small_all[:, cut : cut + n].reshape(n * nch))
        cut += n
    g0, s0, b_in, g1, s1, b_cv, g2, s2, b_out = full
    sidx = lax.axis_index("seq")
    halves = [
        lax.dynamic_slice_in_dim(w_inner, sidx * (dloc // seqs), dloc // seqs, 0),
        lax.dynamic_slice_in_dim(w_conv, sidx * (hloc // seqs), hloc // seqs, 1),
        lax.dynamic_slice_in_dim(w_outer, sidx * (hloc // seqs), hloc // seqs, 0),
    ]
    packed = jnp.concatenate([h.reshape(-1) for h in halves])
    packed = exchange(packed.reshape(-1, 128), ("ch",), 1, gather=True)
    packed = lax.all_gather(packed, "seq", axis=0, tiled=False).reshape(seqs, nch, -1)
    cut = 0
    parts = []
    for h in halves:
        parts.append(packed[:, :, cut : cut + h.size].reshape((seqs, nch) + h.shape))
        cut += h.size
    w_in = parts[0].transpose(1, 0, 2, 3).reshape(dim, hid)
    w_cv = parts[1].transpose(2, 1, 0, 3, 4).reshape(KERNEL_TAPS, hid, hid)
    w_out = parts[2].transpose(1, 0, 2, 3).reshape(hid, dim)

    x = to_positions(inputs, nch, q_count)
    cot = to_positions(cotangent, nch, q_count)
    prow = x.shape[0]
    if q_count == 1:
        ids = lax.dynamic_slice_in_dim(segment_ids, me * prow, prow, axis=0)
    else:
        ids = lax.dynamic_slice_in_dim(segment_ids, me // q_count, 1, axis=0)
        ids = lax.dynamic_slice_in_dim(ids, (me % q_count) * part, part, axis=1)
    own_ids = ids + 1
    wide_ids = extended(own_ids, border, pairs)

    residual = x.astype(jnp.float32)
    normed0, unit0, scale0 = normalize(residual, g0, s0)
    hidden0 = gelu_exact(normed0).astype(jnp.bfloat16)
    inner = jnp.einsum("dh,rdl->rhl", w_in, hidden0, preferred_element_type=jnp.float32) + b_in[:, None]
    normed1, unit1, scale1 = normalize(inner, g1, s1)
    hidden1 = gelu_exact(normed1).astype(jnp.bfloat16)
    wide_hidden = extended(hidden1, border, pairs)
    taps = shifted_taps(wide_hidden, wide_ids, own_ids, offsets, border)
    kernel_flat = w_cv.reshape(KERNEL_TAPS * hid, hid)
    mixed = jnp.einsum("co,rcl->rol", kernel_flat, taps, preferred_element_type=jnp.float32) + b_cv[:, None]
    normed2, unit2, scale2 = normalize(mixed, g2, s2)
    hidden2 = gelu_exact(normed2).astype(jnp.bfloat16)
    branch = jnp.einsum("hd,rhl->rdl", w_out, hidden2, preferred_element_type=jnp.float32)
    output = (residual + branch + b_out[:, None]).astype(jnp.bfloat16)

    grad_b_outer = jnp.sum(cot.astype(jnp.float32), axis=(0, 2))
    grad_w_outer = jnp.einsum("rhl,rdl->hd", hidden2, cot, preferred_element_type=jnp.float32)
    grad_hidden2 = jnp.einsum("hd,rdl->rhl", w_out, cot, preferred_element_type=jnp.float32)
    grad_normed2 = gelu_back(normed2, grad_hidden2)
    grad_norm2_gain = jnp.sum(grad_normed2 * unit2, axis=(0, 2))
    grad_norm2_shift = jnp.sum(grad_normed2, axis=(0, 2))
    grad_mixed = normalize_back(grad_normed2, unit2, scale2, g2).astype(jnp.bfloat16)
    grad_b_conv = jnp.sum(grad_mixed.astype(jnp.float32), axis=(0, 2))
    grad_w_conv = jnp.einsum(
        "rkcil,rol->ckio",
        taps.reshape(prow, KERNEL_TAPS, nch, hloc, part),
        grad_mixed,
        preferred_element_type=jnp.float32,
    )
    wide_grad = extended(grad_mixed, border, pairs)
    back_taps = shifted_taps(wide_grad, wide_ids, own_ids, back_offsets, border)
    kernel_back = jnp.transpose(w_cv, (0, 2, 1)).reshape(KERNEL_TAPS * hid, hid)
    grad_hidden1 = jnp.einsum("oc,rol->rcl", kernel_back, back_taps, preferred_element_type=jnp.float32)
    grad_normed1 = gelu_back(normed1, grad_hidden1)
    grad_norm1_gain = jnp.sum(grad_normed1 * unit1, axis=(0, 2))
    grad_norm1_shift = jnp.sum(grad_normed1, axis=(0, 2))
    grad_inner = normalize_back(grad_normed1, unit1, scale1, g1).astype(jnp.bfloat16)
    grad_b_inner = jnp.sum(grad_inner.astype(jnp.float32), axis=(0, 2))
    grad_w_inner = jnp.einsum("rdl,rhl->dh", hidden0, grad_inner, preferred_element_type=jnp.float32)
    grad_hidden0 = jnp.einsum("dh,rhl->rdl", w_in, grad_inner, preferred_element_type=jnp.float32)
    grad_normed0 = gelu_back(normed0, grad_hidden0)
    grad_norm0_gain = jnp.sum(grad_normed0 * unit0, axis=(0, 2))
    grad_norm0_shift = jnp.sum(grad_normed0, axis=(0, 2))
    input_grad = (cot.astype(jnp.float32) + normalize_back(grad_normed0, unit0, scale0, g0)).astype(jnp.bfloat16)

    output = to_channels(output, nch, q_count, rows)
    input_grad = to_channels(input_grad, nch, q_count, rows)

    vectors = [
        grad_norm0_gain,
        grad_norm0_shift,
        grad_b_inner,
        grad_norm1_gain,
        grad_norm1_shift,
        grad_b_conv,
        grad_norm2_gain,
        grad_norm2_shift,
        grad_b_outer,
    ]
    flat = jnp.concatenate([v.reshape(nch, -1) for v in vectors], axis=1)
    vec_len = flat.shape[1]
    vec_rows = -(-vec_len // dim)
    flat = jnp.pad(flat, ((0, 0), (0, vec_rows * dim - vec_len))).reshape(nch, vec_rows, dim)
    outer_plus = jnp.concatenate([grad_w_outer.reshape(nch, hloc, dim), flat], axis=1)

    def reduce_weight(g, split_dim, cid):
        g = lax.psum_scatter(g, "seq", scatter_dimension=split_dim, tiled=True)
        g = lax.psum_scatter(g, "batch", scatter_dimension=split_dim, tiled=True)
        g = lax.psum_scatter(g, "ch", scatter_dimension=0, tiled=True)
        spread = seqs * batches
        g = jnp.broadcast_to(g, (spread,) + g.shape[1:])
        g = lax.all_to_all(g, ("seq", "batch"), 0, 0, tiled=True)
        return jnp.moveaxis(g, 0, split_dim - 1)

    red_outer = reduce_weight(outer_plus, 2, 7)
    red_outer = red_outer.reshape(hloc + vec_rows, dim)
    red_w_outer = red_outer[:hloc]
    mine = red_outer[hloc:].reshape(-1)[:vec_len]
    red_w_conv = reduce_weight(grad_w_conv, 3, 9)
    red_w_conv = red_w_conv.reshape(KERNEL_TAPS, hloc, hid)
    red_w_inner = reduce_weight(grad_w_inner.reshape(nch, dloc, hid), 1, 11).reshape(dloc, hid)
    reds = []
    cut = 0
    for v in vectors:
        n = v.shape[0] // nch
        reds.append(mine[cut : cut + n])
        cut += n
    return (
        output,
        input_grad,
        reds[0],
        reds[1],
        red_w_inner,
        reds[2],
        reds[3],
        reds[4],
        red_w_conv,
        reds[5],
        reds[6],
        reds[7],
        red_w_outer,
        reds[8],
    )


def solution(mesh):
    return jax.shard_map(
        local,
        mesh=mesh,
        in_specs=(
            P("batch", "ch", "seq"),
            P("batch", "seq"),
            P("ch"),
            P("ch"),
            P("ch", None),
            P("ch"),
            P("ch"),
            P("ch"),
            P(None, "ch", None),
            P("ch"),
            P("ch"),
            P("ch"),
            P("ch", None),
            P("ch"),
            P("batch", "ch", "seq"),
        ),
        out_specs=(
            P("batch", "ch", "seq"),
            P("batch", "ch", "seq"),
            P("ch"),
            P("ch"),
            P("ch", None),
            P("ch"),
            P("ch"),
            P("ch"),
            P(None, "ch", None),
            P("ch"),
            P("ch"),
            P("ch"),
            P("ch", None),
            P("ch"),
        ),
        check_vma=False,
    )
```

```python
import functools
import math

import jax
import jax.numpy as jnp
from jax import lax
from jax.experimental import pallas as pl
from jax.experimental.pallas import tpu as pltpu
from jax.sharding import PartitionSpec as P

KERNEL_TAPS = 5
DILATION_SPACING = 32


EPSILON = 1e-05


MESH_AXES = ("batch", "seq", "ch")
MESH_ID = pl.DeviceIdType.MESH


def _group_index(group, sizes, coords):
    me = 0
    for a in group:
        me = me * sizes[a] + coords[a]
    return me


def _exchange_kernel(sizes, group, gather, count_arrays, *refs):
    x_refs = refs[:count_arrays]
    o_refs = refs[count_arrays : 2 * count_arrays]
    send_sem, recv_sem = refs[2 * count_arrays :]
    coords = {a: lax.axis_index(a) for a in MESH_AXES}
    me = _group_index(group, sizes, coords)
    count = math.prod(sizes[a] for a in group)

    def device(index):
        where = dict(coords)
        rest = index
        for a in reversed(group):
            where[a] = lax.rem(rest, sizes[a])
            rest = rest // sizes[a]
        return tuple(where[a] for a in MESH_AXES)

    barrier = pltpu.get_barrier_semaphore()
    for j in range(1, count):
        pl.semaphore_signal(barrier, 1, device_id=device(lax.rem(me + j, count)), device_id_type=MESH_ID)
    pl.semaphore_wait(barrier, count - 1)
    copies = []
    for j in range(1, count):
        peer = lax.rem(me + j, count)
        for i in range(count_arrays):
            copy = pltpu.make_async_remote_copy(
                src_ref=x_refs[i] if gather else x_refs[i].at[peer],
                dst_ref=o_refs[i].at[me],
                send_sem=send_sem.at[i, j - 1],
                recv_sem=recv_sem.at[i, j - 1],
                device_id=device(peer),
                device_id_type=MESH_ID,
            )
            copy.start()
            copies.append(copy)
    for copy in copies:
        copy.wait()


def exchange(xs, group, collective_id, gather=False):
    sizes = {a: lax.axis_size(a) for a in MESH_AXES}
    count = math.prod(sizes[a] for a in group)
    if count == 1:
        return [x[None] if gather else x for x in xs]
    shapes = [jax.ShapeDtypeStruct((count,) + x.shape if gather else x.shape, x.dtype) for x in xs]
    moved = sum(x.size * x.dtype.itemsize * (count if gather else 1) for x in xs)
    outs = pl.pallas_call(
        functools.partial(_exchange_kernel, sizes, group, gather, len(xs)),
        out_shape=shapes,
        in_specs=[pl.BlockSpec(memory_space=pl.ANY)] * len(xs),
        out_specs=[pl.BlockSpec(memory_space=pl.ANY)] * len(xs),
        scratch_shapes=[
            pltpu.SemaphoreType.DMA((len(xs), count - 1)),
            pltpu.SemaphoreType.DMA((len(xs), count - 1)),
        ],
        compiler_params=pltpu.CompilerParams(collective_id=collective_id, has_side_effects=True),
        cost_estimate=pl.CostEstimate(flops=0, transcendentals=0, bytes_accessed=2 * moved),
    )(*xs)
    me = _group_index(group, sizes, {a: lax.axis_index(a) for a in group})
    placed = []
    for x, out in zip(xs, outs):
        own = x if gather else lax.dynamic_index_in_dim(x, me, 0, keepdims=False)
        placed.append(lax.dynamic_update_index_in_dim(out, own, me, 0))
    return placed


def gelu_exact(values):
    return jax.nn.gelu(values, approximate=False)


def gelu_back(point, grad):
    return jax.vjp(gelu_exact, point)[1](grad)[0]


def normalize(values, gain, shift):
    center = jnp.mean(values, axis=1, keepdims=True)
    offset = values - center
    spread = jnp.mean(offset * offset, axis=1, keepdims=True)
    scale = lax.rsqrt(spread + EPSILON)
    unit = offset * scale
    return (unit * gain[:, None] + shift[:, None], unit, scale)


def normalize_back(grad, unit, scale, gain):
    scaled = grad * gain[:, None]
    first = jnp.mean(scaled, axis=1, keepdims=True)
    second = jnp.mean(scaled * unit, axis=1, keepdims=True)
    return scale * (scaled - first - unit * second)


def neighbour_pairs(seqs, nch, q_count):
    pairs = []
    for s in range(seqs):
        for c in range(nch):
            q = c % q_count
            if q < q_count - 1:
                pairs.append((s * nch + c, s * nch + c + 1))
            elif s < seqs - 1:
                pairs.append((s * nch + c, (s + 1) * nch + c - (q_count - 1)))
    return pairs


def extended(x, width, pairs):
    down = [(j, i) for i, j in pairs]
    length = x.shape[-1]
    before = lax.ppermute(x[..., length - width :], ("seq", "ch"), pairs)
    after = lax.ppermute(x[..., :width], ("seq", "ch"), down)
    return jnp.concatenate([before, x, after], axis=-1)


def shifted_taps(wide, wide_ids, own_ids, offsets, border):
    length = own_ids.shape[-1]
    pieces = []
    for offset in offsets:
        lower = border + offset
        shifted = wide[:, :, lower : lower + length]
        matching = wide_ids[:, lower : lower + length] == own_ids
        pieces.append(jnp.where(matching[:, None, :], shifted, jnp.zeros_like(shifted)))
    return jnp.concatenate(pieces, axis=1)


def to_positions(x, nch, q_count):
    rows, width, length = x.shape
    if q_count > 1:
        x = x.reshape(rows, width, q_count, length // q_count).transpose(0, 2, 1, 3)
        x = x.reshape(rows * q_count, width, length // q_count)
    x = lax.all_to_all(x, "ch", 0, 0, tiled=True)
    return _join(x, nch)


def _join(x, nch):
    total, width, length = x.shape
    p = total // nch
    return x.reshape(nch, p, width, length).transpose(1, 0, 2, 3).reshape(p, nch * width, length)


def to_channels(x, nch, q_count, rows):
    p, width, length = x.shape
    x = x.reshape(p, nch, width // nch, length).transpose(1, 0, 2, 3).reshape(nch * p, width // nch, length)
    x = lax.all_to_all(x, "ch", 0, 0, tiled=True)
    if q_count > 1:
        _, width, part = x.shape
        x = x.reshape(rows, q_count, width, part).transpose(0, 2, 1, 3).reshape(rows, width, q_count * part)
    return x


def local(
    inputs,
    segment_ids,
    norm0_gain,
    norm0_shift,
    w_inner,
    b_inner,
    norm1_gain,
    norm1_shift,
    w_conv,
    b_conv,
    norm2_gain,
    norm2_shift,
    w_outer,
    b_outer,
    cotangent,
):
    nch = lax.axis_size("ch")
    seqs = lax.axis_size("seq")
    batches = lax.axis_size("batch")
    rows, dloc, length = inputs.shape
    hloc = w_conv.shape[1]
    hid = hloc * nch
    dim = dloc * nch
    if rows % nch == 0:
        q_count = 1
    else:
        q_count = nch // rows
    part = length // q_count
    border = 2 * DILATION_SPACING
    offsets = [(k - KERNEL_TAPS // 2) * DILATION_SPACING for k in range(KERNEL_TAPS)]
    back_offsets = [-o for o in offsets]
    pairs = neighbour_pairs(seqs, nch, q_count)
    me = lax.axis_index("ch")

    smalls = [norm0_gain, norm0_shift, b_inner, norm1_gain, norm1_shift, b_conv, norm2_gain, norm2_shift, b_outer]
    sidx = lax.axis_index("seq")
    halves = [
        lax.dynamic_slice_in_dim(w_inner, sidx * (dloc // seqs), dloc // seqs, 0),
        lax.dynamic_slice_in_dim(w_conv, sidx * (hloc // seqs), hloc // seqs, 1),
        lax.dynamic_slice_in_dim(w_outer, sidx * (hloc // seqs), hloc // seqs, 0),
    ]
    small_all, w_in, w_cv, w_out = exchange([jnp.concatenate(smalls)] + halves, ("ch",), 0, gather=True)
    cut = 0
    full = []
    for v in smalls:
        n = v.shape[0]
        full.append(small_all[:, cut : cut + n].reshape(n * nch))
        cut += n
    g0, s0, b_in, g1, s1, b_cv, g2, s2, b_out = full
    w_in = lax.all_gather(w_in, "seq", axis=1, tiled=True).reshape(dim, hid)
    w_cv = lax.all_gather(w_cv, "seq", axis=2, tiled=True).transpose(1, 0, 2, 3).reshape(KERNEL_TAPS, hid, hid)
    w_out = lax.all_gather(w_out, "seq", axis=1, tiled=True).reshape(hid, dim)

    x = to_positions(inputs, nch, q_count)
    cot = to_positions(cotangent, nch, q_count)
    prow = x.shape[0]
    if q_count == 1:
        ids = lax.dynamic_slice_in_dim(segment_ids, me * prow, prow, axis=0)
    else:
        ids = lax.dynamic_slice_in_dim(segment_ids, me // q_count, 1, axis=0)
        ids = lax.dynamic_slice_in_dim(ids, (me % q_count) * part, part, axis=1)
    own_ids = ids + 1
    wide_ids = extended(own_ids, border, pairs)

    residual = x.astype(jnp.float32)
    normed0, unit0, scale0 = normalize(residual, g0, s0)
    hidden0 = gelu_exact(normed0).astype(jnp.bfloat16)
    inner = jnp.einsum("dh,rdl->rhl", w_in, hidden0, preferred_element_type=jnp.float32) + b_in[:, None]
    normed1, unit1, scale1 = normalize(inner, g1, s1)
    hidden1 = gelu_exact(normed1).astype(jnp.bfloat16)
    wide_hidden = extended(hidden1, border, pairs)
    taps = shifted_taps(wide_hidden, wide_ids, own_ids, offsets, border)
    kernel_flat = w_cv.reshape(KERNEL_TAPS * hid, hid)
    mixed = jnp.einsum("co,rcl->rol", kernel_flat, taps, preferred_element_type=jnp.float32) + b_cv[:, None]
    normed2, unit2, scale2 = normalize(mixed, g2, s2)
    hidden2 = gelu_exact(normed2).astype(jnp.bfloat16)
    branch = jnp.einsum("hd,rhl->rdl", w_out, hidden2, preferred_element_type=jnp.float32)
    output = (residual + branch + b_out[:, None]).astype(jnp.bfloat16)

    grad_b_outer = jnp.sum(cot.astype(jnp.float32), axis=(0, 2))
    grad_w_outer = jnp.einsum("rhl,rdl->hd", hidden2, cot, preferred_element_type=jnp.float32)
    grad_hidden2 = jnp.einsum("hd,rdl->rhl", w_out, cot, preferred_element_type=jnp.float32)
    grad_normed2 = gelu_back(normed2, grad_hidden2)
    grad_norm2_gain = jnp.sum(grad_normed2 * unit2, axis=(0, 2))
    grad_norm2_shift = jnp.sum(grad_normed2, axis=(0, 2))
    grad_mixed = normalize_back(grad_normed2, unit2, scale2, g2).astype(jnp.bfloat16)
    grad_b_conv = jnp.sum(grad_mixed.astype(jnp.float32), axis=(0, 2))
    grad_w_conv = jnp.einsum(
        "rkcil,rol->ckio",
        taps.reshape(prow, KERNEL_TAPS, nch, hloc, part),
        grad_mixed,
        preferred_element_type=jnp.float32,
    )
    wide_grad = extended(grad_mixed, border, pairs)
    back_taps = shifted_taps(wide_grad, wide_ids, own_ids, back_offsets, border)
    kernel_back = jnp.transpose(w_cv, (0, 2, 1)).reshape(KERNEL_TAPS * hid, hid)
    grad_hidden1 = jnp.einsum("oc,rol->rcl", kernel_back, back_taps, preferred_element_type=jnp.float32)
    grad_normed1 = gelu_back(normed1, grad_hidden1)
    grad_norm1_gain = jnp.sum(grad_normed1 * unit1, axis=(0, 2))
    grad_norm1_shift = jnp.sum(grad_normed1, axis=(0, 2))
    grad_inner = normalize_back(grad_normed1, unit1, scale1, g1).astype(jnp.bfloat16)
    grad_b_inner = jnp.sum(grad_inner.astype(jnp.float32), axis=(0, 2))
    grad_w_inner = jnp.einsum("rdl,rhl->dh", hidden0, grad_inner, preferred_element_type=jnp.float32)
    grad_hidden0 = jnp.einsum("dh,rhl->rdl", w_in, grad_inner, preferred_element_type=jnp.float32)
    grad_normed0 = gelu_back(normed0, grad_hidden0)
    grad_norm0_gain = jnp.sum(grad_normed0 * unit0, axis=(0, 2))
    grad_norm0_shift = jnp.sum(grad_normed0, axis=(0, 2))
    input_grad = (cot.astype(jnp.float32) + normalize_back(grad_normed0, unit0, scale0, g0)).astype(jnp.bfloat16)

    output = to_channels(output, nch, q_count, rows)
    input_grad = to_channels(input_grad, nch, q_count, rows)

    vectors = [
        grad_norm0_gain,
        grad_norm0_shift,
        grad_b_inner,
        grad_norm1_gain,
        grad_norm1_shift,
        grad_b_conv,
        grad_norm2_gain,
        grad_norm2_shift,
        grad_b_outer,
    ]
    flat = jnp.concatenate([v.reshape(nch, -1) for v in vectors], axis=1)
    vec_len = flat.shape[1]
    vec_rows = -(-vec_len // dim)
    vec_rows = -(-(hloc + vec_rows) // 32) * 32 - hloc
    flat = jnp.pad(flat, ((0, 0), (0, vec_rows * dim - vec_len))).reshape(nch, vec_rows, dim)
    outer_plus = jnp.concatenate([grad_w_outer.reshape(nch, hloc, dim), flat], axis=1)
    outer_plus = outer_plus.reshape(nch, (hloc + vec_rows) * dim // 128, 128)

    def reduce_seq_batch(g, split_dim):
        g = lax.psum_scatter(g, "seq", scatter_dimension=split_dim, tiled=True)
        return lax.psum_scatter(g, "batch", scatter_dimension=split_dim, tiled=True)

    parts = [
        reduce_seq_batch(outer_plus, 1),
        reduce_seq_batch(grad_w_conv, 3),
        reduce_seq_batch(grad_w_inner.reshape(nch, dloc, hid), 1),
    ]
    parts = [jnp.sum(p, axis=0) for p in exchange(parts, ("ch",), 1)]
    parts = exchange(parts, ("seq", "batch"), 2, gather=True)
    red_outer = parts[0].reshape(hloc + vec_rows, dim)
    red_w_outer = red_outer[:hloc]
    mine = red_outer[hloc:].reshape(-1)[:vec_len]
    red_w_conv = jnp.moveaxis(parts[1], 0, 2).reshape(KERNEL_TAPS, hloc, hid)
    red_w_inner = parts[2].reshape(dloc, hid)
    reds = []
    cut = 0
    for v in vectors:
        n = v.shape[0] // nch
        reds.append(mine[cut : cut + n])
        cut += n
    return (
        output,
        input_grad,
        reds[0],
        reds[1],
        red_w_inner,
        reds[2],
        reds[3],
        reds[4],
        red_w_conv,
        reds[5],
        reds[6],
        reds[7],
        red_w_outer,
        reds[8],
    )


def solution(mesh):
    return jax.shard_map(
        local,
        mesh=mesh,
        in_specs=(
            P("batch", "ch", "seq"),
            P("batch", "seq"),
            P("ch"),
            P("ch"),
            P("ch", None),
            P("ch"),
            P("ch"),
            P("ch"),
            P(None, "ch", None),
            P("ch"),
            P("ch"),
            P("ch"),
            P("ch", None),
            P("ch"),
            P("batch", "ch", "seq"),
        ),
        out_specs=(
            P("batch", "ch", "seq"),
            P("batch", "ch", "seq"),
            P("ch"),
            P("ch"),
            P("ch", None),
            P("ch"),
            P("ch"),
            P("ch"),
            P(None, "ch", None),
            P("ch"),
            P("ch"),
            P("ch"),
            P("ch", None),
            P("ch"),
        ),
        check_vma=False,
    )
```

```python
import functools
import math

import jax
import jax.numpy as jnp
from jax import lax
from jax.experimental import pallas as pl
from jax.experimental.pallas import tpu as pltpu
from jax.sharding import PartitionSpec as P

KERNEL_TAPS = 5
DILATION_SPACING = 32


EPSILON = 1e-05


MESH_AXES = ("batch", "seq", "ch")
MESH_ID = pl.DeviceIdType.MESH


def _group_index(group, sizes, coords):
    me = 0
    for a in group:
        me = me * sizes[a] + coords[a]
    return me


def _exchange_kernel(sizes, group, gather, count_arrays, *refs):
    x_refs = refs[:count_arrays]
    o_refs = refs[count_arrays : 2 * count_arrays]
    send_sem, recv_sem = refs[2 * count_arrays :]
    coords = {a: lax.axis_index(a) for a in MESH_AXES}
    me = _group_index(group, sizes, coords)
    count = math.prod(sizes[a] for a in group)

    def device(index):
        where = dict(coords)
        rest = index
        for a in reversed(group):
            where[a] = lax.rem(rest, sizes[a])
            rest = rest // sizes[a]
        return tuple(where[a] for a in MESH_AXES)

    barrier = pltpu.get_barrier_semaphore()
    for j in range(1, count):
        pl.semaphore_signal(barrier, 1, device_id=device(lax.rem(me + j, count)), device_id_type=MESH_ID)
    pl.semaphore_wait(barrier, count - 1)
    copies = []
    for j in range(1, count):
        peer = lax.rem(me + j, count)
        for i in range(count_arrays):
            copy = pltpu.make_async_remote_copy(
                src_ref=x_refs[i] if gather else x_refs[i].at[peer],
                dst_ref=o_refs[i].at[me],
                send_sem=send_sem.at[i, j - 1],
                recv_sem=recv_sem.at[i, j - 1],
                device_id=device(peer),
                device_id_type=MESH_ID,
            )
            copy.start()
            copies.append(copy)
    for copy in copies:
        copy.wait()


def exchange(xs, group, collective_id, gather=False):
    sizes = {a: lax.axis_size(a) for a in MESH_AXES}
    count = math.prod(sizes[a] for a in group)
    if count == 1:
        return [x[None] if gather else x for x in xs]
    shapes = [jax.ShapeDtypeStruct((count,) + x.shape if gather else x.shape, x.dtype) for x in xs]
    moved = sum(x.size * x.dtype.itemsize * (count if gather else 1) for x in xs)
    outs = pl.pallas_call(
        functools.partial(_exchange_kernel, sizes, group, gather, len(xs)),
        out_shape=shapes,
        in_specs=[pl.BlockSpec(memory_space=pl.ANY)] * len(xs),
        out_specs=[pl.BlockSpec(memory_space=pl.ANY)] * len(xs),
        scratch_shapes=[
            pltpu.SemaphoreType.DMA((len(xs), count - 1)),
            pltpu.SemaphoreType.DMA((len(xs), count - 1)),
        ],
        compiler_params=pltpu.CompilerParams(collective_id=collective_id, has_side_effects=True),
        cost_estimate=pl.CostEstimate(flops=0, transcendentals=0, bytes_accessed=2 * moved),
    )(*xs)
    me = _group_index(group, sizes, {a: lax.axis_index(a) for a in group})
    placed = []
    for x, out in zip(xs, outs):
        own = x if gather else lax.dynamic_index_in_dim(x, me, 0, keepdims=False)
        placed.append(lax.dynamic_update_index_in_dim(out, own, me, 0))
    return placed


def gelu_exact(values):
    return jax.nn.gelu(values, approximate=False)


def gelu_back(point, grad):
    return jax.vjp(gelu_exact, point)[1](grad)[0]


def normalize(values, gain, shift):
    center = jnp.mean(values, axis=1, keepdims=True)
    offset = values - center
    spread = jnp.mean(offset * offset, axis=1, keepdims=True)
    scale = lax.rsqrt(spread + EPSILON)
    unit = offset * scale
    return (unit * gain[:, None] + shift[:, None], unit, scale)


def normalize_back(grad, unit, scale, gain):
    scaled = grad * gain[:, None]
    first = jnp.mean(scaled, axis=1, keepdims=True)
    second = jnp.mean(scaled * unit, axis=1, keepdims=True)
    return scale * (scaled - first - unit * second)


def neighbour_pairs(seqs, nch, q_count):
    pairs = []
    for s in range(seqs):
        for c in range(nch):
            q = c % q_count
            if q < q_count - 1:
                pairs.append((s * nch + c, s * nch + c + 1))
            elif s < seqs - 1:
                pairs.append((s * nch + c, (s + 1) * nch + c - (q_count - 1)))
    return pairs


def extended(x, width, pairs):
    down = [(j, i) for i, j in pairs]
    length = x.shape[-1]
    before = lax.ppermute(x[..., length - width :], ("seq", "ch"), pairs)
    after = lax.ppermute(x[..., :width], ("seq", "ch"), down)
    return jnp.concatenate([before, x, after], axis=-1)


def shifted_taps(wide, wide_ids, own_ids, offsets, border):
    length = own_ids.shape[-1]
    pieces = []
    for offset in offsets:
        lower = border + offset
        shifted = wide[:, :, lower : lower + length]
        matching = wide_ids[:, lower : lower + length] == own_ids
        pieces.append(jnp.where(matching[:, None, :], shifted, jnp.zeros_like(shifted)))
    return jnp.concatenate(pieces, axis=1)


def to_positions(x, nch, q_count):
    rows, width, length = x.shape
    if q_count > 1:
        x = x.reshape(rows, width, q_count, length // q_count).transpose(0, 2, 1, 3)
        x = x.reshape(rows * q_count, width, length // q_count)
    x = lax.all_to_all(x, "ch", 0, 0, tiled=True)
    return _join(x, nch)


def _join(x, nch):
    total, width, length = x.shape
    p = total // nch
    return x.reshape(nch, p, width, length).transpose(1, 0, 2, 3).reshape(p, nch * width, length)


def to_channels(x, nch, q_count, rows):
    p, width, length = x.shape
    x = x.reshape(p, nch, width // nch, length).transpose(1, 0, 2, 3).reshape(nch * p, width // nch, length)
    x = lax.all_to_all(x, "ch", 0, 0, tiled=True)
    if q_count > 1:
        _, width, part = x.shape
        x = x.reshape(rows, q_count, width, part).transpose(0, 2, 1, 3).reshape(rows, width, q_count * part)
    return x


def local(
    inputs,
    segment_ids,
    norm0_gain,
    norm0_shift,
    w_inner,
    b_inner,
    norm1_gain,
    norm1_shift,
    w_conv,
    b_conv,
    norm2_gain,
    norm2_shift,
    w_outer,
    b_outer,
    cotangent,
):
    nch = lax.axis_size("ch")
    seqs = lax.axis_size("seq")
    batches = lax.axis_size("batch")
    rows, dloc, length = inputs.shape
    hloc = w_conv.shape[1]
    hid = hloc * nch
    dim = dloc * nch
    if rows % nch == 0:
        q_count = 1
    else:
        q_count = nch // rows
    part = length // q_count
    border = 2 * DILATION_SPACING
    offsets = [(k - KERNEL_TAPS // 2) * DILATION_SPACING for k in range(KERNEL_TAPS)]
    back_offsets = [-o for o in offsets]
    pairs = neighbour_pairs(seqs, nch, q_count)
    me = lax.axis_index("ch")

    smalls = [norm0_gain, norm0_shift, b_inner, norm1_gain, norm1_shift, b_conv, norm2_gain, norm2_shift, b_outer]
    sidx = lax.axis_index("seq")
    halves = [
        lax.dynamic_slice_in_dim(w_inner, sidx * (dloc // seqs), dloc // seqs, 0),
        lax.dynamic_slice_in_dim(w_conv, sidx * (hloc // seqs), hloc // seqs, 1),
        lax.dynamic_slice_in_dim(w_outer, sidx * (hloc // seqs), hloc // seqs, 0),
    ]
    small_all, w_in, w_cv, w_out = exchange([jnp.concatenate(smalls)] + halves, ("ch",), 0, gather=True)
    cut = 0
    full = []
    for v in smalls:
        n = v.shape[0]
        full.append(small_all[:, cut : cut + n].reshape(n * nch))
        cut += n
    g0, s0, b_in, g1, s1, b_cv, g2, s2, b_out = full
    w_in = lax.all_gather(w_in, "seq", axis=1, tiled=True).reshape(dim, hid)
    w_cv = lax.all_gather(w_cv, "seq", axis=2, tiled=True).transpose(1, 0, 2, 3).reshape(KERNEL_TAPS, hid, hid)
    w_out = lax.all_gather(w_out, "seq", axis=1, tiled=True).reshape(hid, dim)

    x = to_positions(inputs, nch, q_count)
    cot = to_positions(cotangent, nch, q_count)
    prow = x.shape[0]
    if q_count == 1:
        ids = lax.dynamic_slice_in_dim(segment_ids, me * prow, prow, axis=0)
    else:
        ids = lax.dynamic_slice_in_dim(segment_ids, me // q_count, 1, axis=0)
        ids = lax.dynamic_slice_in_dim(ids, (me % q_count) * part, part, axis=1)
    own_ids = ids + 1
    wide_ids = extended(own_ids, border, pairs)

    residual = x.astype(jnp.float32)
    normed0, unit0, scale0 = normalize(residual, g0, s0)
    hidden0 = gelu_exact(normed0).astype(jnp.bfloat16)
    inner = jnp.einsum("dh,rdl->rhl", w_in, hidden0, preferred_element_type=jnp.float32) + b_in[:, None]
    normed1, unit1, scale1 = normalize(inner, g1, s1)
    hidden1 = gelu_exact(normed1).astype(jnp.bfloat16)
    wide_hidden = extended(hidden1, border, pairs)
    taps = shifted_taps(wide_hidden, wide_ids, own_ids, offsets, border)
    kernel_flat = w_cv.reshape(KERNEL_TAPS * hid, hid)
    mixed = jnp.einsum("co,rcl->rol", kernel_flat, taps, preferred_element_type=jnp.float32) + b_cv[:, None]
    normed2, unit2, scale2 = normalize(mixed, g2, s2)
    hidden2 = gelu_exact(normed2).astype(jnp.bfloat16)
    branch = jnp.einsum("hd,rhl->rdl", w_out, hidden2, preferred_element_type=jnp.float32)
    output = (residual + branch + b_out[:, None]).astype(jnp.bfloat16)

    grad_b_outer = jnp.sum(cot.astype(jnp.float32), axis=(0, 2))
    grad_w_outer = jnp.einsum("rhl,rdl->hd", hidden2, cot, preferred_element_type=jnp.float32)
    grad_hidden2 = jnp.einsum("hd,rdl->rhl", w_out, cot, preferred_element_type=jnp.float32)
    grad_normed2 = gelu_back(normed2, grad_hidden2)
    grad_norm2_gain = jnp.sum(grad_normed2 * unit2, axis=(0, 2))
    grad_norm2_shift = jnp.sum(grad_normed2, axis=(0, 2))
    grad_mixed = normalize_back(grad_normed2, unit2, scale2, g2).astype(jnp.bfloat16)
    grad_b_conv = jnp.sum(grad_mixed.astype(jnp.float32), axis=(0, 2))
    grad_w_conv = jnp.einsum(
        "rkcil,rol->ckio",
        taps.reshape(prow, KERNEL_TAPS, nch, hloc, part),
        grad_mixed,
        preferred_element_type=jnp.float32,
    )
    wide_grad = extended(grad_mixed, border, pairs)
    back_taps = shifted_taps(wide_grad, wide_ids, own_ids, back_offsets, border)
    kernel_back = jnp.transpose(w_cv, (0, 2, 1)).reshape(KERNEL_TAPS * hid, hid)
    grad_hidden1 = jnp.einsum("oc,rol->rcl", kernel_back, back_taps, preferred_element_type=jnp.float32)
    grad_normed1 = gelu_back(normed1, grad_hidden1)
    grad_norm1_gain = jnp.sum(grad_normed1 * unit1, axis=(0, 2))
    grad_norm1_shift = jnp.sum(grad_normed1, axis=(0, 2))
    grad_inner = normalize_back(grad_normed1, unit1, scale1, g1).astype(jnp.bfloat16)
    grad_b_inner = jnp.sum(grad_inner.astype(jnp.float32), axis=(0, 2))
    grad_w_inner = jnp.einsum("rdl,rhl->dh", hidden0, grad_inner, preferred_element_type=jnp.float32)
    grad_hidden0 = jnp.einsum("dh,rhl->rdl", w_in, grad_inner, preferred_element_type=jnp.float32)
    grad_normed0 = gelu_back(normed0, grad_hidden0)
    grad_norm0_gain = jnp.sum(grad_normed0 * unit0, axis=(0, 2))
    grad_norm0_shift = jnp.sum(grad_normed0, axis=(0, 2))
    input_grad = (cot.astype(jnp.float32) + normalize_back(grad_normed0, unit0, scale0, g0)).astype(jnp.bfloat16)

    output = to_channels(output, nch, q_count, rows)
    input_grad = to_channels(input_grad, nch, q_count, rows)

    vectors = [
        grad_norm0_gain,
        grad_norm0_shift,
        grad_b_inner,
        grad_norm1_gain,
        grad_norm1_shift,
        grad_b_conv,
        grad_norm2_gain,
        grad_norm2_shift,
        grad_b_outer,
    ]
    flat = jnp.concatenate([v.reshape(nch, -1) for v in vectors], axis=1)
    vec_len = flat.shape[1]
    vec_rows = -(-vec_len // dim)
    vec_rows = -(-(hloc + vec_rows) // 32) * 32 - hloc
    flat = jnp.pad(flat, ((0, 0), (0, vec_rows * dim - vec_len))).reshape(nch, vec_rows, dim)
    outer_plus = jnp.concatenate([grad_w_outer.reshape(nch, hloc, dim), flat], axis=1)
    outer_plus = outer_plus.reshape(nch, (hloc + vec_rows) * dim // 128, 128)

    def reduce_seq_batch(g, split_dim):
        return lax.psum_scatter(g, ("seq", "batch"), scatter_dimension=split_dim, tiled=True)

    parts = [
        reduce_seq_batch(outer_plus, 1),
        reduce_seq_batch(grad_w_conv, 3),
        reduce_seq_batch(grad_w_inner.reshape(nch, dloc, hid), 1),
    ]
    parts = [jnp.sum(p, axis=0) for p in exchange(parts, ("ch",), 1)]
    parts = exchange(parts, ("batch",), 2, gather=True)
    parts = [p.reshape((seqs * batches,) + p.shape[2:]) for p in exchange(parts, ("seq",), 3, gather=True)]
    red_outer = parts[0].reshape(hloc + vec_rows, dim)
    red_w_outer = red_outer[:hloc]
    mine = red_outer[hloc:].reshape(-1)[:vec_len]
    red_w_conv = jnp.moveaxis(parts[1], 0, 2).reshape(KERNEL_TAPS, hloc, hid)
    red_w_inner = parts[2].reshape(dloc, hid)
    reds = []
    cut = 0
    for v in vectors:
        n = v.shape[0] // nch
        reds.append(mine[cut : cut + n])
        cut += n
    return (
        output,
        input_grad,
        reds[0],
        reds[1],
        red_w_inner,
        reds[2],
        reds[3],
        reds[4],
        red_w_conv,
        reds[5],
        reds[6],
        reds[7],
        red_w_outer,
        reds[8],
    )


def solution(mesh):
    return jax.shard_map(
        local,
        mesh=mesh,
        in_specs=(
            P("batch", "ch", "seq"),
            P("batch", "seq"),
            P("ch"),
            P("ch"),
            P("ch", None),
            P("ch"),
            P("ch"),
            P("ch"),
            P(None, "ch", None),
            P("ch"),
            P("ch"),
            P("ch"),
            P("ch", None),
            P("ch"),
            P("batch", "ch", "seq"),
        ),
        out_specs=(
            P("batch", "ch", "seq"),
            P("batch", "ch", "seq"),
            P("ch"),
            P("ch"),
            P("ch", None),
            P("ch"),
            P("ch"),
            P("ch"),
            P(None, "ch", None),
            P("ch"),
            P("ch"),
            P("ch"),
            P("ch", None),
            P("ch"),
        ),
        check_vma=False,
    )
```

```python
import functools
import math

import jax
import jax.numpy as jnp
from jax import lax
from jax.experimental import pallas as pl
from jax.experimental.pallas import tpu as pltpu
from jax.sharding import PartitionSpec as P

KERNEL_TAPS = 5
DILATION_SPACING = 32


EPSILON = 1e-05


MESH_AXES = ("batch", "seq", "ch")
MESH_ID = pl.DeviceIdType.MESH


def _group_index(group, sizes, coords):
    me = 0
    for a in group:
        me = me * sizes[a] + coords[a]
    return me


def _exchange_kernel(sizes, group, gather, count_arrays, *refs):
    x_refs = refs[:count_arrays]
    o_refs = refs[count_arrays : 2 * count_arrays]
    send_sem, recv_sem = refs[2 * count_arrays :]
    coords = {a: lax.axis_index(a) for a in MESH_AXES}
    me = _group_index(group, sizes, coords)
    count = math.prod(sizes[a] for a in group)

    def device(index):
        where = dict(coords)
        rest = index
        for a in reversed(group):
            where[a] = lax.rem(rest, sizes[a])
            rest = rest // sizes[a]
        return tuple(where[a] for a in MESH_AXES)

    barrier = pltpu.get_barrier_semaphore()
    for j in range(1, count):
        pl.semaphore_signal(barrier, 1, device_id=device(lax.rem(me + j, count)), device_id_type=MESH_ID)
    pl.semaphore_wait(barrier, count - 1)
    copies = []
    for j in range(1, count):
        peer = lax.rem(me + j, count)
        for i in range(count_arrays):
            copy = pltpu.make_async_remote_copy(
                src_ref=x_refs[i] if gather else x_refs[i].at[peer],
                dst_ref=o_refs[i].at[me],
                send_sem=send_sem.at[i, j - 1],
                recv_sem=recv_sem.at[i, j - 1],
                device_id=device(peer),
                device_id_type=MESH_ID,
            )
            copy.start()
            copies.append(copy)
    for copy in copies:
        copy.wait()


def exchange(xs, group, collective_id, gather=False):
    sizes = {a: lax.axis_size(a) for a in MESH_AXES}
    count = math.prod(sizes[a] for a in group)
    if count == 1:
        return [x[None] if gather else x for x in xs]
    shapes = [jax.ShapeDtypeStruct((count,) + x.shape if gather else x.shape, x.dtype) for x in xs]
    moved = sum(x.size * x.dtype.itemsize * (count if gather else 1) for x in xs)
    outs = pl.pallas_call(
        functools.partial(_exchange_kernel, sizes, group, gather, len(xs)),
        out_shape=shapes,
        in_specs=[pl.BlockSpec(memory_space=pl.ANY)] * len(xs),
        out_specs=[pl.BlockSpec(memory_space=pl.ANY)] * len(xs),
        scratch_shapes=[
            pltpu.SemaphoreType.DMA((len(xs), count - 1)),
            pltpu.SemaphoreType.DMA((len(xs), count - 1)),
        ],
        compiler_params=pltpu.CompilerParams(collective_id=collective_id, has_side_effects=True),
        cost_estimate=pl.CostEstimate(flops=0, transcendentals=0, bytes_accessed=2 * moved),
    )(*xs)
    me = _group_index(group, sizes, {a: lax.axis_index(a) for a in group})
    placed = []
    for x, out in zip(xs, outs):
        own = x if gather else lax.dynamic_index_in_dim(x, me, 0, keepdims=False)
        placed.append(lax.dynamic_update_index_in_dim(out, own, me, 0))
    return placed


def gelu_exact(values):
    return jax.nn.gelu(values, approximate=False)


def gelu_back(point, grad):
    return jax.vjp(gelu_exact, point)[1](grad)[0]


def normalize(values, gain, shift):
    center = jnp.mean(values, axis=1, keepdims=True)
    offset = values - center
    spread = jnp.mean(offset * offset, axis=1, keepdims=True)
    scale = lax.rsqrt(spread + EPSILON)
    unit = offset * scale
    return (unit * gain[:, None] + shift[:, None], unit, scale)


def normalize_back(grad, unit, scale, gain):
    scaled = grad * gain[:, None]
    first = jnp.mean(scaled, axis=1, keepdims=True)
    second = jnp.mean(scaled * unit, axis=1, keepdims=True)
    return scale * (scaled - first - unit * second)


def neighbour_pairs(seqs, nch, q_count):
    pairs = []
    for s in range(seqs):
        for c in range(nch):
            q = c % q_count
            if q < q_count - 1:
                pairs.append((s * nch + c, s * nch + c + 1))
            elif s < seqs - 1:
                pairs.append((s * nch + c, (s + 1) * nch + c - (q_count - 1)))
    return pairs


def extended(x, width, pairs):
    down = [(j, i) for i, j in pairs]
    length = x.shape[-1]
    before = lax.ppermute(x[..., length - width :], ("seq", "ch"), pairs)
    after = lax.ppermute(x[..., :width], ("seq", "ch"), down)
    return jnp.concatenate([before, x, after], axis=-1)


def shifted_taps(wide, wide_ids, own_ids, offsets, border):
    length = own_ids.shape[-1]
    pieces = []
    for offset in offsets:
        lower = border + offset
        shifted = wide[:, :, lower : lower + length]
        matching = wide_ids[:, lower : lower + length] == own_ids
        pieces.append(jnp.where(matching[:, None, :], shifted, jnp.zeros_like(shifted)))
    return jnp.concatenate(pieces, axis=1)


def to_positions(x, nch, q_count):
    rows, width, length = x.shape
    if q_count > 1:
        x = x.reshape(rows, width, q_count, length // q_count).transpose(0, 2, 1, 3)
        x = x.reshape(rows * q_count, width, length // q_count)
    x = lax.all_to_all(x, "ch", 0, 0, tiled=True)
    return _join(x, nch)


def _join(x, nch):
    total, width, length = x.shape
    p = total // nch
    return x.reshape(nch, p, width, length).transpose(1, 0, 2, 3).reshape(p, nch * width, length)


def to_channels(x, nch, q_count, rows):
    p, width, length = x.shape
    x = x.reshape(p, nch, width // nch, length).transpose(1, 0, 2, 3).reshape(nch * p, width // nch, length)
    x = lax.all_to_all(x, "ch", 0, 0, tiled=True)
    if q_count > 1:
        _, width, part = x.shape
        x = x.reshape(rows, q_count, width, part).transpose(0, 2, 1, 3).reshape(rows, width, q_count * part)
    return x


def local(
    inputs,
    segment_ids,
    norm0_gain,
    norm0_shift,
    w_inner,
    b_inner,
    norm1_gain,
    norm1_shift,
    w_conv,
    b_conv,
    norm2_gain,
    norm2_shift,
    w_outer,
    b_outer,
    cotangent,
):
    nch = lax.axis_size("ch")
    seqs = lax.axis_size("seq")
    batches = lax.axis_size("batch")
    rows, dloc, length = inputs.shape
    hloc = w_conv.shape[1]
    hid = hloc * nch
    dim = dloc * nch
    if rows % nch == 0:
        q_count = 1
    else:
        q_count = nch // rows
    part = length // q_count
    border = 2 * DILATION_SPACING
    offsets = [(k - KERNEL_TAPS // 2) * DILATION_SPACING for k in range(KERNEL_TAPS)]
    back_offsets = [-o for o in offsets]
    pairs = neighbour_pairs(seqs, nch, q_count)
    me = lax.axis_index("ch")

    smalls = [norm0_gain, norm0_shift, b_inner, norm1_gain, norm1_shift, b_conv, norm2_gain, norm2_shift, b_outer]
    sidx = lax.axis_index("seq")
    halves = [
        lax.dynamic_slice_in_dim(w_inner, sidx * (dloc // seqs), dloc // seqs, 0),
        lax.dynamic_slice_in_dim(w_conv, sidx * (hloc // seqs), hloc // seqs, 1),
        lax.dynamic_slice_in_dim(w_outer, sidx * (hloc // seqs), hloc // seqs, 0),
    ]
    small_all, w_in, w_cv, w_out = exchange([jnp.concatenate(smalls)] + halves, ("ch",), 0, gather=True)
    cut = 0
    full = []
    for v in smalls:
        n = v.shape[0]
        full.append(small_all[:, cut : cut + n].reshape(n * nch))
        cut += n
    g0, s0, b_in, g1, s1, b_cv, g2, s2, b_out = full
    w_in = lax.all_gather(w_in, "seq", axis=1, tiled=True).reshape(dim, hid)
    w_cv = lax.all_gather(w_cv, "seq", axis=2, tiled=True).transpose(1, 0, 2, 3).reshape(KERNEL_TAPS, hid, hid)
    w_out = lax.all_gather(w_out, "seq", axis=1, tiled=True).reshape(hid, dim)

    x = to_positions(inputs, nch, q_count)
    cot = to_positions(cotangent, nch, q_count)
    prow = x.shape[0]
    if q_count == 1:
        ids = lax.dynamic_slice_in_dim(segment_ids, me * prow, prow, axis=0)
    else:
        ids = lax.dynamic_slice_in_dim(segment_ids, me // q_count, 1, axis=0)
        ids = lax.dynamic_slice_in_dim(ids, (me % q_count) * part, part, axis=1)
    own_ids = ids + 1
    wide_ids = extended(own_ids, border, pairs)

    residual = x.astype(jnp.float32)
    normed0, unit0, scale0 = normalize(residual, g0, s0)
    hidden0 = gelu_exact(normed0).astype(jnp.bfloat16)
    inner = jnp.einsum("dh,rdl->rhl", w_in, hidden0, preferred_element_type=jnp.float32) + b_in[:, None]
    normed1, unit1, scale1 = normalize(inner, g1, s1)
    hidden1 = gelu_exact(normed1).astype(jnp.bfloat16)
    wide_hidden = extended(hidden1, border, pairs)
    taps = shifted_taps(wide_hidden, wide_ids, own_ids, offsets, border)
    kernel_flat = w_cv.reshape(KERNEL_TAPS * hid, hid)
    mixed = jnp.einsum("co,rcl->rol", kernel_flat, taps, preferred_element_type=jnp.float32) + b_cv[:, None]
    normed2, unit2, scale2 = normalize(mixed, g2, s2)
    hidden2 = gelu_exact(normed2).astype(jnp.bfloat16)
    branch = jnp.einsum("hd,rhl->rdl", w_out, hidden2, preferred_element_type=jnp.float32)
    output = (residual + branch + b_out[:, None]).astype(jnp.bfloat16)

    grad_b_outer = jnp.sum(cot.astype(jnp.float32), axis=(0, 2))
    grad_w_outer = jnp.einsum("rhl,rdl->hd", hidden2, cot, preferred_element_type=jnp.float32)
    grad_hidden2 = jnp.einsum("hd,rdl->rhl", w_out, cot, preferred_element_type=jnp.float32)
    grad_normed2 = gelu_back(normed2, grad_hidden2)
    grad_norm2_gain = jnp.sum(grad_normed2 * unit2, axis=(0, 2))
    grad_norm2_shift = jnp.sum(grad_normed2, axis=(0, 2))
    grad_mixed = normalize_back(grad_normed2, unit2, scale2, g2).astype(jnp.bfloat16)
    grad_b_conv = jnp.sum(grad_mixed.astype(jnp.float32), axis=(0, 2))
    grad_w_conv = jnp.einsum(
        "rkcil,rol->ckio",
        taps.reshape(prow, KERNEL_TAPS, nch, hloc, part),
        grad_mixed,
        preferred_element_type=jnp.float32,
    )
    wide_grad = extended(grad_mixed, border, pairs)
    back_taps = shifted_taps(wide_grad, wide_ids, own_ids, back_offsets, border)
    kernel_back = jnp.transpose(w_cv, (0, 2, 1)).reshape(KERNEL_TAPS * hid, hid)
    grad_hidden1 = jnp.einsum("oc,rol->rcl", kernel_back, back_taps, preferred_element_type=jnp.float32)
    grad_normed1 = gelu_back(normed1, grad_hidden1)
    grad_norm1_gain = jnp.sum(grad_normed1 * unit1, axis=(0, 2))
    grad_norm1_shift = jnp.sum(grad_normed1, axis=(0, 2))
    grad_inner = normalize_back(grad_normed1, unit1, scale1, g1).astype(jnp.bfloat16)
    grad_b_inner = jnp.sum(grad_inner.astype(jnp.float32), axis=(0, 2))
    grad_w_inner = jnp.einsum("rdl,rhl->dh", hidden0, grad_inner, preferred_element_type=jnp.float32)
    grad_hidden0 = jnp.einsum("dh,rhl->rdl", w_in, grad_inner, preferred_element_type=jnp.float32)
    grad_normed0 = gelu_back(normed0, grad_hidden0)
    grad_norm0_gain = jnp.sum(grad_normed0 * unit0, axis=(0, 2))
    grad_norm0_shift = jnp.sum(grad_normed0, axis=(0, 2))
    input_grad = (cot.astype(jnp.float32) + normalize_back(grad_normed0, unit0, scale0, g0)).astype(jnp.bfloat16)

    output = to_channels(output, nch, q_count, rows)
    input_grad = to_channels(input_grad, nch, q_count, rows)

    vectors = [
        grad_norm0_gain,
        grad_norm0_shift,
        grad_b_inner,
        grad_norm1_gain,
        grad_norm1_shift,
        grad_b_conv,
        grad_norm2_gain,
        grad_norm2_shift,
        grad_b_outer,
    ]
    flat = jnp.concatenate([v.reshape(nch, -1) for v in vectors], axis=1)
    vec_len = flat.shape[1]
    vec_rows = -(-vec_len // dim)
    vec_rows = -(-(hloc + vec_rows) // 32) * 32 - hloc
    flat = jnp.pad(flat, ((0, 0), (0, vec_rows * dim - vec_len))).reshape(nch, vec_rows, dim)
    outer_plus = jnp.concatenate([grad_w_outer.reshape(nch, hloc, dim), flat], axis=1)
    outer_plus = outer_plus.reshape(nch, (hloc + vec_rows) * dim // 128, 128)

    def reduce_seq_batch(g, split_dim, after=None):
        if after is not None:
            g, _ = lax.optimization_barrier((g, after))
        g = lax.psum_scatter(g, "seq", scatter_dimension=split_dim, tiled=True)
        return lax.psum_scatter(g, "batch", scatter_dimension=split_dim, tiled=True)

    part_conv = reduce_seq_batch(grad_w_conv, 3)
    part_outer = reduce_seq_batch(outer_plus, 1, part_conv)
    part_inner = reduce_seq_batch(grad_w_inner.reshape(nch, dloc, hid), 1, part_outer)
    parts = [part_outer, part_conv, part_inner]
    parts = [jnp.sum(p, axis=0) for p in exchange(parts, ("ch",), 1)]
    parts = exchange(parts, ("batch",), 2, gather=True)
    parts = [p.reshape((seqs * batches,) + p.shape[2:]) for p in exchange(parts, ("seq",), 3, gather=True)]
    red_outer = parts[0].reshape(hloc + vec_rows, dim)
    red_w_outer = red_outer[:hloc]
    mine = red_outer[hloc:].reshape(-1)[:vec_len]
    red_w_conv = jnp.moveaxis(parts[1], 0, 2).reshape(KERNEL_TAPS, hloc, hid)
    red_w_inner = parts[2].reshape(dloc, hid)
    reds = []
    cut = 0
    for v in vectors:
        n = v.shape[0] // nch
        reds.append(mine[cut : cut + n])
        cut += n
    return (
        output,
        input_grad,
        reds[0],
        reds[1],
        red_w_inner,
        reds[2],
        reds[3],
        reds[4],
        red_w_conv,
        reds[5],
        reds[6],
        reds[7],
        red_w_outer,
        reds[8],
    )


def solution(mesh):
    return jax.shard_map(
        local,
        mesh=mesh,
        in_specs=(
            P("batch", "ch", "seq"),
            P("batch", "seq"),
            P("ch"),
            P("ch"),
            P("ch", None),
            P("ch"),
            P("ch"),
            P("ch"),
            P(None, "ch", None),
            P("ch"),
            P("ch"),
            P("ch"),
            P("ch", None),
            P("ch"),
            P("batch", "ch", "seq"),
        ),
        out_specs=(
            P("batch", "ch", "seq"),
            P("batch", "ch", "seq"),
            P("ch"),
            P("ch"),
            P("ch", None),
            P("ch"),
            P("ch"),
            P("ch"),
            P(None, "ch", None),
            P("ch"),
            P("ch"),
            P("ch"),
            P("ch", None),
            P("ch"),
        ),
        check_vma=False,
    )
```

```python
import functools
import math

import jax
import jax.numpy as jnp
from jax import lax
from jax.experimental import pallas as pl
from jax.experimental.pallas import tpu as pltpu
from jax.sharding import PartitionSpec as P

KERNEL_TAPS = 5
DILATION_SPACING = 32


EPSILON = 1e-05


MESH_AXES = ("batch", "seq", "ch")
MESH_ID = pl.DeviceIdType.MESH


def _group_index(group, sizes, coords):
    me = 0
    for a in group:
        me = me * sizes[a] + coords[a]
    return me


def _exchange_kernel(sizes, group, gather, count_arrays, *refs):
    x_refs = refs[:count_arrays]
    o_refs = refs[count_arrays : 2 * count_arrays]
    send_sem, recv_sem = refs[2 * count_arrays :]
    coords = {a: lax.axis_index(a) for a in MESH_AXES}
    me = _group_index(group, sizes, coords)
    count = math.prod(sizes[a] for a in group)

    def device(index):
        where = dict(coords)
        rest = index
        for a in reversed(group):
            where[a] = lax.rem(rest, sizes[a])
            rest = rest // sizes[a]
        return tuple(where[a] for a in MESH_AXES)

    barrier = pltpu.get_barrier_semaphore()
    for j in range(1, count):
        pl.semaphore_signal(barrier, 1, device_id=device(lax.rem(me + j, count)), device_id_type=MESH_ID)
    pl.semaphore_wait(barrier, count - 1)
    copies = []
    for j in range(1, count):
        peer = lax.rem(me + j, count)
        for i in range(count_arrays):
            copy = pltpu.make_async_remote_copy(
                src_ref=x_refs[i] if gather else x_refs[i].at[peer],
                dst_ref=o_refs[i].at[me],
                send_sem=send_sem.at[i, j - 1],
                recv_sem=recv_sem.at[i, j - 1],
                device_id=device(peer),
                device_id_type=MESH_ID,
            )
            copy.start()
            copies.append(copy)
    for copy in copies:
        copy.wait()


def exchange(xs, group, collective_id, gather=False):
    sizes = {a: lax.axis_size(a) for a in MESH_AXES}
    count = math.prod(sizes[a] for a in group)
    if count == 1:
        return [x[None] if gather else x for x in xs]
    shapes = [jax.ShapeDtypeStruct((count,) + x.shape if gather else x.shape, x.dtype) for x in xs]
    moved = sum(x.size * x.dtype.itemsize * (count if gather else 1) for x in xs)
    outs = pl.pallas_call(
        functools.partial(_exchange_kernel, sizes, group, gather, len(xs)),
        out_shape=shapes,
        in_specs=[pl.BlockSpec(memory_space=pl.ANY)] * len(xs),
        out_specs=[pl.BlockSpec(memory_space=pl.ANY)] * len(xs),
        scratch_shapes=[
            pltpu.SemaphoreType.DMA((len(xs), count - 1)),
            pltpu.SemaphoreType.DMA((len(xs), count - 1)),
        ],
        compiler_params=pltpu.CompilerParams(collective_id=collective_id, has_side_effects=True),
        cost_estimate=pl.CostEstimate(flops=0, transcendentals=0, bytes_accessed=2 * moved),
    )(*xs)
    me = _group_index(group, sizes, {a: lax.axis_index(a) for a in group})
    placed = []
    for x, out in zip(xs, outs):
        own = x if gather else lax.dynamic_index_in_dim(x, me, 0, keepdims=False)
        placed.append(lax.dynamic_update_index_in_dim(out, own, me, 0))
    return placed


def gelu_exact(values):
    return jax.nn.gelu(values, approximate=False)


def gelu_back(point, grad):
    return jax.vjp(gelu_exact, point)[1](grad)[0]


def normalize(values, gain, shift):
    center = jnp.mean(values, axis=1, keepdims=True)
    offset = values - center
    spread = jnp.mean(offset * offset, axis=1, keepdims=True)
    scale = lax.rsqrt(spread + EPSILON)
    unit = offset * scale
    return (unit * gain[:, None] + shift[:, None], unit, scale)


def normalize_back(grad, unit, scale, gain):
    scaled = grad * gain[:, None]
    first = jnp.mean(scaled, axis=1, keepdims=True)
    second = jnp.mean(scaled * unit, axis=1, keepdims=True)
    return scale * (scaled - first - unit * second)


def neighbour_pairs(seqs, nch, q_count):
    pairs = []
    for s in range(seqs):
        for c in range(nch):
            q = c % q_count
            if q < q_count - 1:
                pairs.append((s * nch + c, s * nch + c + 1))
            elif s < seqs - 1:
                pairs.append((s * nch + c, (s + 1) * nch + c - (q_count - 1)))
    return pairs


def extended(x, width, pairs):
    down = [(j, i) for i, j in pairs]
    length = x.shape[-1]
    before = lax.ppermute(x[..., length - width :], ("seq", "ch"), pairs)
    after = lax.ppermute(x[..., :width], ("seq", "ch"), down)
    return jnp.concatenate([before, x, after], axis=-1)


def shifted_taps(wide, wide_ids, own_ids, offsets, border):
    length = own_ids.shape[-1]
    pieces = []
    for offset in offsets:
        lower = border + offset
        shifted = wide[:, :, lower : lower + length]
        matching = wide_ids[:, lower : lower + length] == own_ids
        pieces.append(jnp.where(matching[:, None, :], shifted, jnp.zeros_like(shifted)))
    return jnp.concatenate(pieces, axis=1)


def to_positions(x, nch, q_count):
    rows, width, length = x.shape
    if q_count > 1:
        x = x.reshape(rows, width, q_count, length // q_count).transpose(0, 2, 1, 3)
        x = x.reshape(rows * q_count, width, length // q_count)
    x = lax.all_to_all(x, "ch", 0, 0, tiled=True)
    return _join(x, nch)


def _join(x, nch):
    total, width, length = x.shape
    p = total // nch
    return x.reshape(nch, p, width, length).transpose(1, 0, 2, 3).reshape(p, nch * width, length)


def to_channels(x, nch, q_count, rows):
    p, width, length = x.shape
    x = x.reshape(p, nch, width // nch, length).transpose(1, 0, 2, 3).reshape(nch * p, width // nch, length)
    x = lax.all_to_all(x, "ch", 0, 0, tiled=True)
    if q_count > 1:
        _, width, part = x.shape
        x = x.reshape(rows, q_count, width, part).transpose(0, 2, 1, 3).reshape(rows, width, q_count * part)
    return x


def local(
    inputs,
    segment_ids,
    norm0_gain,
    norm0_shift,
    w_inner,
    b_inner,
    norm1_gain,
    norm1_shift,
    w_conv,
    b_conv,
    norm2_gain,
    norm2_shift,
    w_outer,
    b_outer,
    cotangent,
):
    nch = lax.axis_size("ch")
    seqs = lax.axis_size("seq")
    batches = lax.axis_size("batch")
    rows, dloc, length = inputs.shape
    hloc = w_conv.shape[1]
    hid = hloc * nch
    dim = dloc * nch
    if rows % nch == 0:
        q_count = 1
    else:
        q_count = nch // rows
    part = length // q_count
    border = 2 * DILATION_SPACING
    offsets = [(k - KERNEL_TAPS // 2) * DILATION_SPACING for k in range(KERNEL_TAPS)]
    back_offsets = [-o for o in offsets]
    pairs = neighbour_pairs(seqs, nch, q_count)
    me = lax.axis_index("ch")

    smalls = [norm0_gain, norm0_shift, b_inner, norm1_gain, norm1_shift, b_conv, norm2_gain, norm2_shift, b_outer]
    sidx = lax.axis_index("seq")
    halves = [
        lax.dynamic_slice_in_dim(w_inner, sidx * (dloc // seqs), dloc // seqs, 0),
        lax.dynamic_slice_in_dim(w_conv, sidx * (hloc // seqs), hloc // seqs, 1),
        lax.dynamic_slice_in_dim(w_outer, sidx * (hloc // seqs), hloc // seqs, 0),
    ]
    small_all, w_in, w_cv, w_out = exchange([jnp.concatenate(smalls)] + halves, ("ch",), 0, gather=True)
    cut = 0
    full = []
    for v in smalls:
        n = v.shape[0]
        full.append(small_all[:, cut : cut + n].reshape(n * nch))
        cut += n
    g0, s0, b_in, g1, s1, b_cv, g2, s2, b_out = full
    w_in = lax.all_gather(w_in, "seq", axis=1, tiled=True).reshape(dim, hid)
    w_cv = lax.all_gather(w_cv, "seq", axis=2, tiled=True).transpose(1, 0, 2, 3).reshape(KERNEL_TAPS, hid, hid)
    w_out = lax.all_gather(w_out, "seq", axis=1, tiled=True).reshape(hid, dim)

    x = to_positions(inputs, nch, q_count)
    cot = to_positions(cotangent, nch, q_count)
    prow = x.shape[0]
    if q_count == 1:
        ids = lax.dynamic_slice_in_dim(segment_ids, me * prow, prow, axis=0)
    else:
        ids = lax.dynamic_slice_in_dim(segment_ids, me // q_count, 1, axis=0)
        ids = lax.dynamic_slice_in_dim(ids, (me % q_count) * part, part, axis=1)
    own_ids = ids + 1
    wide_ids = extended(own_ids, border, pairs)

    residual = x.astype(jnp.float32)
    normed0, unit0, scale0 = normalize(residual, g0, s0)
    hidden0 = gelu_exact(normed0).astype(jnp.bfloat16)
    inner = jnp.einsum("dh,rdl->rhl", w_in, hidden0, preferred_element_type=jnp.float32) + b_in[:, None]
    normed1, unit1, scale1 = normalize(inner, g1, s1)
    hidden1 = gelu_exact(normed1).astype(jnp.bfloat16)
    wide_hidden = extended(hidden1, border, pairs)
    taps = shifted_taps(wide_hidden, wide_ids, own_ids, offsets, border)
    kernel_flat = w_cv.reshape(KERNEL_TAPS * hid, hid)
    mixed = jnp.einsum("co,rcl->rol", kernel_flat, taps, preferred_element_type=jnp.float32) + b_cv[:, None]
    normed2, unit2, scale2 = normalize(mixed, g2, s2)
    hidden2 = gelu_exact(normed2).astype(jnp.bfloat16)
    branch = jnp.einsum("hd,rhl->rdl", w_out, hidden2, preferred_element_type=jnp.float32)
    output = (residual + branch + b_out[:, None]).astype(jnp.bfloat16)

    grad_b_outer = jnp.sum(cot.astype(jnp.float32), axis=(0, 2))
    grad_w_outer = jnp.einsum("rhl,rdl->hd", hidden2, cot, preferred_element_type=jnp.float32)
    grad_hidden2 = jnp.einsum("hd,rdl->rhl", w_out, cot, preferred_element_type=jnp.float32)
    grad_normed2 = gelu_back(normed2, grad_hidden2)
    grad_norm2_gain = jnp.sum(grad_normed2 * unit2, axis=(0, 2))
    grad_norm2_shift = jnp.sum(grad_normed2, axis=(0, 2))
    grad_mixed = normalize_back(grad_normed2, unit2, scale2, g2).astype(jnp.bfloat16)
    grad_b_conv = jnp.sum(grad_mixed.astype(jnp.float32), axis=(0, 2))
    grad_w_conv = jnp.einsum(
        "rkcil,rol->ckio",
        taps.reshape(prow, KERNEL_TAPS, nch, hloc, part),
        grad_mixed,
        preferred_element_type=jnp.float32,
    )
    wide_grad = extended(grad_mixed, border, pairs)
    back_taps = shifted_taps(wide_grad, wide_ids, own_ids, back_offsets, border)
    kernel_back = jnp.transpose(w_cv, (0, 2, 1)).reshape(KERNEL_TAPS * hid, hid)
    grad_hidden1 = jnp.einsum("oc,rol->rcl", kernel_back, back_taps, preferred_element_type=jnp.float32)
    grad_normed1 = gelu_back(normed1, grad_hidden1)
    grad_norm1_gain = jnp.sum(grad_normed1 * unit1, axis=(0, 2))
    grad_norm1_shift = jnp.sum(grad_normed1, axis=(0, 2))
    grad_inner = normalize_back(grad_normed1, unit1, scale1, g1).astype(jnp.bfloat16)
    grad_b_inner = jnp.sum(grad_inner.astype(jnp.float32), axis=(0, 2))
    grad_w_inner = jnp.einsum("rdl,rhl->dh", hidden0, grad_inner, preferred_element_type=jnp.float32)
    grad_hidden0 = jnp.einsum("dh,rhl->rdl", w_in, grad_inner, preferred_element_type=jnp.float32)
    grad_normed0 = gelu_back(normed0, grad_hidden0)
    grad_norm0_gain = jnp.sum(grad_normed0 * unit0, axis=(0, 2))
    grad_norm0_shift = jnp.sum(grad_normed0, axis=(0, 2))
    input_grad = (cot.astype(jnp.float32) + normalize_back(grad_normed0, unit0, scale0, g0)).astype(jnp.bfloat16)

    output = to_channels(output, nch, q_count, rows)
    input_grad = to_channels(input_grad, nch, q_count, rows)

    vectors = [
        grad_norm0_gain,
        grad_norm0_shift,
        grad_b_inner,
        grad_norm1_gain,
        grad_norm1_shift,
        grad_b_conv,
        grad_norm2_gain,
        grad_norm2_shift,
        grad_b_outer,
    ]
    flat = jnp.concatenate([v.reshape(nch, -1) for v in vectors], axis=1)
    vec_len = flat.shape[1]
    vec_rows = -(-vec_len // dim)
    vec_rows = -(-(hloc + vec_rows) // 32) * 32 - hloc
    flat = jnp.pad(flat, ((0, 0), (0, vec_rows * dim - vec_len))).reshape(nch, vec_rows, dim)
    outer_plus = jnp.concatenate([grad_w_outer.reshape(nch, hloc, dim), flat], axis=1)
    outer_plus = outer_plus.reshape(nch, (hloc + vec_rows) * dim // 128, 128)

    def reduce_seq_batch(g, split_dim, after=None):
        if after is not None:
            g, _ = lax.optimization_barrier((g, after))
        g = lax.psum_scatter(g, "seq", scatter_dimension=split_dim, tiled=True)
        return lax.psum_scatter(g, "batch", scatter_dimension=split_dim, tiled=True)

    part_outer = reduce_seq_batch(outer_plus, 1)
    part_conv = reduce_seq_batch(grad_w_conv, 3, part_outer)
    part_inner = reduce_seq_batch(grad_w_inner.reshape(nch, dloc, hid), 1, part_conv)
    parts = [part_outer, part_conv, part_inner]
    parts = [jnp.sum(p, axis=0) for p in exchange(parts, ("ch",), 1)]
    parts = exchange(parts, ("batch",), 2, gather=True)
    parts = [p.reshape((seqs * batches,) + p.shape[2:]) for p in exchange(parts, ("seq",), 3, gather=True)]
    red_outer = parts[0].reshape(hloc + vec_rows, dim)
    red_w_outer = red_outer[:hloc]
    mine = red_outer[hloc:].reshape(-1)[:vec_len]
    red_w_conv = jnp.moveaxis(parts[1], 0, 2).reshape(KERNEL_TAPS, hloc, hid)
    red_w_inner = parts[2].reshape(dloc, hid)
    reds = []
    cut = 0
    for v in vectors:
        n = v.shape[0] // nch
        reds.append(mine[cut : cut + n])
        cut += n
    return (
        output,
        input_grad,
        reds[0],
        reds[1],
        red_w_inner,
        reds[2],
        reds[3],
        reds[4],
        red_w_conv,
        reds[5],
        reds[6],
        reds[7],
        red_w_outer,
        reds[8],
    )


def solution(mesh):
    return jax.shard_map(
        local,
        mesh=mesh,
        in_specs=(
            P("batch", "ch", "seq"),
            P("batch", "seq"),
            P("ch"),
            P("ch"),
            P("ch", None),
            P("ch"),
            P("ch"),
            P("ch"),
            P(None, "ch", None),
            P("ch"),
            P("ch"),
            P("ch"),
            P("ch", None),
            P("ch"),
            P("batch", "ch", "seq"),
        ),
        out_specs=(
            P("batch", "ch", "seq"),
            P("batch", "ch", "seq"),
            P("ch"),
            P("ch"),
            P("ch", None),
            P("ch"),
            P("ch"),
            P("ch"),
            P(None, "ch", None),
            P("ch"),
            P("ch"),
            P("ch"),
            P("ch", None),
            P("ch"),
        ),
        check_vma=False,
    )
```

```python
import functools
import math

import jax
import jax.numpy as jnp
from jax import lax
from jax.experimental import pallas as pl
from jax.experimental.pallas import tpu as pltpu
from jax.sharding import PartitionSpec as P

KERNEL_TAPS = 5
DILATION_SPACING = 32


EPSILON = 1e-05


MESH_AXES = ("batch", "seq", "ch")
MESH_ID = pl.DeviceIdType.MESH


def _group_index(group, sizes, coords):
    me = 0
    for a in group:
        me = me * sizes[a] + coords[a]
    return me


def _exchange_kernel(sizes, group, gather, count_arrays, *refs):
    x_refs = refs[:count_arrays]
    o_refs = refs[count_arrays : 2 * count_arrays]
    send_sem, recv_sem = refs[2 * count_arrays :]
    coords = {a: lax.axis_index(a) for a in MESH_AXES}
    me = _group_index(group, sizes, coords)
    count = math.prod(sizes[a] for a in group)

    def device(index):
        where = dict(coords)
        rest = index
        for a in reversed(group):
            where[a] = lax.rem(rest, sizes[a])
            rest = rest // sizes[a]
        return tuple(where[a] for a in MESH_AXES)

    barrier = pltpu.get_barrier_semaphore()
    for j in range(1, count):
        pl.semaphore_signal(barrier, 1, device_id=device(lax.rem(me + j, count)), device_id_type=MESH_ID)
    pl.semaphore_wait(barrier, count - 1)
    copies = []
    for j in range(1, count):
        peer = lax.rem(me + j, count)
        for i in range(count_arrays):
            copy = pltpu.make_async_remote_copy(
                src_ref=x_refs[i] if gather else x_refs[i].at[peer],
                dst_ref=o_refs[i].at[me],
                send_sem=send_sem.at[i, j - 1],
                recv_sem=recv_sem.at[i, j - 1],
                device_id=device(peer),
                device_id_type=MESH_ID,
            )
            copy.start()
            copies.append(copy)
    for copy in copies:
        copy.wait()


def exchange(xs, group, collective_id, gather=False):
    sizes = {a: lax.axis_size(a) for a in MESH_AXES}
    count = math.prod(sizes[a] for a in group)
    if count == 1:
        return [x[None] if gather else x for x in xs]
    shapes = [jax.ShapeDtypeStruct((count,) + x.shape if gather else x.shape, x.dtype) for x in xs]
    moved = sum(x.size * x.dtype.itemsize * (count if gather else 1) for x in xs)
    outs = pl.pallas_call(
        functools.partial(_exchange_kernel, sizes, group, gather, len(xs)),
        out_shape=shapes,
        in_specs=[pl.BlockSpec(memory_space=pl.ANY)] * len(xs),
        out_specs=[pl.BlockSpec(memory_space=pl.ANY)] * len(xs),
        scratch_shapes=[
            pltpu.SemaphoreType.DMA((len(xs), count - 1)),
            pltpu.SemaphoreType.DMA((len(xs), count - 1)),
        ],
        compiler_params=pltpu.CompilerParams(collective_id=collective_id, has_side_effects=True),
        cost_estimate=pl.CostEstimate(flops=0, transcendentals=0, bytes_accessed=2 * moved),
    )(*xs)
    me = _group_index(group, sizes, {a: lax.axis_index(a) for a in group})
    placed = []
    for x, out in zip(xs, outs):
        own = x if gather else lax.dynamic_index_in_dim(x, me, 0, keepdims=False)
        placed.append(lax.dynamic_update_index_in_dim(out, own, me, 0))
    return placed


def gelu_exact(values):
    return jax.nn.gelu(values, approximate=False)


def gelu_back(point, grad):
    return jax.vjp(gelu_exact, point)[1](grad)[0]


def normalize(values, gain, shift):
    center = jnp.mean(values, axis=1, keepdims=True)
    offset = values - center
    spread = jnp.mean(offset * offset, axis=1, keepdims=True)
    scale = lax.rsqrt(spread + EPSILON)
    unit = offset * scale
    return (unit * gain[:, None] + shift[:, None], unit, scale)


def normalize_back(grad, unit, scale, gain):
    scaled = grad * gain[:, None]
    first = jnp.mean(scaled, axis=1, keepdims=True)
    second = jnp.mean(scaled * unit, axis=1, keepdims=True)
    return scale * (scaled - first - unit * second)


def neighbour_pairs(seqs, nch, q_count):
    pairs = []
    for s in range(seqs):
        for c in range(nch):
            q = c % q_count
            if q < q_count - 1:
                pairs.append((s * nch + c, s * nch + c + 1))
            elif s < seqs - 1:
                pairs.append((s * nch + c, (s + 1) * nch + c - (q_count - 1)))
    return pairs


def extended(x, width, pairs):
    down = [(j, i) for i, j in pairs]
    length = x.shape[-1]
    before = lax.ppermute(x[..., length - width :], ("seq", "ch"), pairs)
    after = lax.ppermute(x[..., :width], ("seq", "ch"), down)
    return jnp.concatenate([before, x, after], axis=-1)


def shifted_taps(wide, wide_ids, own_ids, offsets, border):
    length = own_ids.shape[-1]
    pieces = []
    for offset in offsets:
        lower = border + offset
        shifted = wide[:, :, lower : lower + length]
        matching = wide_ids[:, lower : lower + length] == own_ids
        pieces.append(jnp.where(matching[:, None, :], shifted, jnp.zeros_like(shifted)))
    return jnp.concatenate(pieces, axis=1)


def to_positions(x, nch, q_count):
    rows, width, length = x.shape
    if q_count > 1:
        x = x.reshape(rows, width, q_count, length // q_count).transpose(0, 2, 1, 3)
        x = x.reshape(rows * q_count, width, length // q_count)
    x = lax.all_to_all(x, "ch", 0, 0, tiled=True)
    return _join(x, nch)


def _join(x, nch):
    total, width, length = x.shape
    p = total // nch
    return x.reshape(nch, p, width, length).transpose(1, 0, 2, 3).reshape(p, nch * width, length)


def to_channels(x, nch, q_count, rows):
    p, width, length = x.shape
    x = x.reshape(p, nch, width // nch, length).transpose(1, 0, 2, 3).reshape(nch * p, width // nch, length)
    x = lax.all_to_all(x, "ch", 0, 0, tiled=True)
    if q_count > 1:
        _, width, part = x.shape
        x = x.reshape(rows, q_count, width, part).transpose(0, 2, 1, 3).reshape(rows, width, q_count * part)
    return x


def local(
    inputs,
    segment_ids,
    norm0_gain,
    norm0_shift,
    w_inner,
    b_inner,
    norm1_gain,
    norm1_shift,
    w_conv,
    b_conv,
    norm2_gain,
    norm2_shift,
    w_outer,
    b_outer,
    cotangent,
):
    nch = lax.axis_size("ch")
    seqs = lax.axis_size("seq")
    batches = lax.axis_size("batch")
    rows, dloc, length = inputs.shape
    hloc = w_conv.shape[1]
    hid = hloc * nch
    dim = dloc * nch
    if rows % nch == 0:
        q_count = 1
    else:
        q_count = nch // rows
    part = length // q_count
    border = 2 * DILATION_SPACING
    offsets = [(k - KERNEL_TAPS // 2) * DILATION_SPACING for k in range(KERNEL_TAPS)]
    back_offsets = [-o for o in offsets]
    pairs = neighbour_pairs(seqs, nch, q_count)
    me = lax.axis_index("ch")

    smalls = [norm0_gain, norm0_shift, b_inner, norm1_gain, norm1_shift, b_conv, norm2_gain, norm2_shift, b_outer]
    sidx = lax.axis_index("seq")
    halves = [
        lax.dynamic_slice_in_dim(w_inner, sidx * (dloc // seqs), dloc // seqs, 0),
        lax.dynamic_slice_in_dim(w_conv, sidx * (hloc // seqs), hloc // seqs, 1),
        lax.dynamic_slice_in_dim(w_outer, sidx * (hloc // seqs), hloc // seqs, 0),
    ]
    small_all, w_in, w_cv, w_out = exchange([jnp.concatenate(smalls)] + halves, ("ch",), 0, gather=True)
    cut = 0
    full = []
    for v in smalls:
        n = v.shape[0]
        full.append(small_all[:, cut : cut + n].reshape(n * nch))
        cut += n
    g0, s0, b_in, g1, s1, b_cv, g2, s2, b_out = full
    w_in = lax.all_gather(w_in, "seq", axis=1, tiled=True).reshape(dim, hid)
    w_cv = lax.all_gather(w_cv, "seq", axis=2, tiled=True).transpose(1, 0, 2, 3).reshape(KERNEL_TAPS, hid, hid)
    w_out = lax.all_gather(w_out, "seq", axis=1, tiled=True).reshape(hid, dim)

    x = to_positions(inputs, nch, q_count)
    cot = to_positions(cotangent, nch, q_count)
    prow = x.shape[0]
    if q_count == 1:
        ids = lax.dynamic_slice_in_dim(segment_ids, me * prow, prow, axis=0)
    else:
        ids = lax.dynamic_slice_in_dim(segment_ids, me // q_count, 1, axis=0)
        ids = lax.dynamic_slice_in_dim(ids, (me % q_count) * part, part, axis=1)
    own_ids = ids + 1
    wide_ids = extended(own_ids, border, pairs)

    residual = x.astype(jnp.float32)
    normed0, unit0, scale0 = normalize(residual, g0, s0)
    hidden0 = gelu_exact(normed0).astype(jnp.bfloat16)
    inner = jnp.einsum("dh,rdl->rhl", w_in, hidden0, preferred_element_type=jnp.float32) + b_in[:, None]
    normed1, unit1, scale1 = normalize(inner, g1, s1)
    hidden1 = gelu_exact(normed1).astype(jnp.bfloat16)
    wide_hidden = extended(hidden1, border, pairs)
    taps = shifted_taps(wide_hidden, wide_ids, own_ids, offsets, border)
    kernel_flat = w_cv.reshape(KERNEL_TAPS * hid, hid)
    mixed = jnp.einsum("co,rcl->rol", kernel_flat, taps, preferred_element_type=jnp.float32) + b_cv[:, None]
    normed2, unit2, scale2 = normalize(mixed, g2, s2)
    hidden2 = gelu_exact(normed2).astype(jnp.bfloat16)
    branch = jnp.einsum("hd,rhl->rdl", w_out, hidden2, preferred_element_type=jnp.float32)
    output = (residual + branch + b_out[:, None]).astype(jnp.bfloat16)

    grad_b_outer = jnp.sum(cot.astype(jnp.float32), axis=(0, 2))
    grad_w_outer = jnp.einsum("rhl,rdl->hd", hidden2, cot, preferred_element_type=jnp.float32)
    def reduce_seq_batch(g, split_dim, after=None):
        if after is not None:
            g, _ = lax.optimization_barrier((g, after))
        g = lax.psum_scatter(g, "seq", scatter_dimension=split_dim, tiled=True)
        return lax.psum_scatter(g, "batch", scatter_dimension=split_dim, tiled=True)

    part_outer = reduce_seq_batch(grad_w_outer.reshape(nch, hloc * dim // 128, 128), 1)
    grad_hidden2 = jnp.einsum("hd,rdl->rhl", w_out, cot, preferred_element_type=jnp.float32)
    grad_normed2 = gelu_back(normed2, grad_hidden2)
    grad_norm2_gain = jnp.sum(grad_normed2 * unit2, axis=(0, 2))
    grad_norm2_shift = jnp.sum(grad_normed2, axis=(0, 2))
    grad_mixed = normalize_back(grad_normed2, unit2, scale2, g2).astype(jnp.bfloat16)
    grad_b_conv = jnp.sum(grad_mixed.astype(jnp.float32), axis=(0, 2))
    grad_w_conv = jnp.einsum(
        "rkcil,rol->ckio",
        taps.reshape(prow, KERNEL_TAPS, nch, hloc, part),
        grad_mixed,
        preferred_element_type=jnp.float32,
    )
    wide_grad = extended(grad_mixed, border, pairs)
    back_taps = shifted_taps(wide_grad, wide_ids, own_ids, back_offsets, border)
    kernel_back = jnp.transpose(w_cv, (0, 2, 1)).reshape(KERNEL_TAPS * hid, hid)
    grad_hidden1 = jnp.einsum("oc,rol->rcl", kernel_back, back_taps, preferred_element_type=jnp.float32)
    grad_normed1 = gelu_back(normed1, grad_hidden1)
    grad_norm1_gain = jnp.sum(grad_normed1 * unit1, axis=(0, 2))
    grad_norm1_shift = jnp.sum(grad_normed1, axis=(0, 2))
    grad_inner = normalize_back(grad_normed1, unit1, scale1, g1).astype(jnp.bfloat16)
    grad_inner, _ = lax.optimization_barrier((grad_inner, part_outer))
    grad_b_inner = jnp.sum(grad_inner.astype(jnp.float32), axis=(0, 2))
    grad_w_inner = jnp.einsum("rdl,rhl->dh", hidden0, grad_inner, preferred_element_type=jnp.float32)
    grad_hidden0 = jnp.einsum("dh,rhl->rdl", w_in, grad_inner, preferred_element_type=jnp.float32)
    grad_normed0 = gelu_back(normed0, grad_hidden0)
    grad_norm0_gain = jnp.sum(grad_normed0 * unit0, axis=(0, 2))
    grad_norm0_shift = jnp.sum(grad_normed0, axis=(0, 2))
    input_grad = (cot.astype(jnp.float32) + normalize_back(grad_normed0, unit0, scale0, g0)).astype(jnp.bfloat16)

    output = to_channels(output, nch, q_count, rows)
    input_grad = to_channels(input_grad, nch, q_count, rows)

    vectors = [
        grad_norm0_gain,
        grad_norm0_shift,
        grad_b_inner,
        grad_norm1_gain,
        grad_norm1_shift,
        grad_b_conv,
        grad_norm2_gain,
        grad_norm2_shift,
        grad_b_outer,
    ]
    flat = jnp.concatenate([v.reshape(nch, -1) for v in vectors], axis=1)
    vec_len = flat.shape[1]
    vec_rows = -(-vec_len // hid)
    vec_rows = -(-(dloc + vec_rows) // 64) * 64 - dloc
    flat = jnp.pad(flat, ((0, 0), (0, vec_rows * hid - vec_len))).reshape(nch, vec_rows, hid)
    inner_plus = jnp.concatenate([grad_w_inner.reshape(nch, dloc, hid), flat], axis=1)
    inner_plus = inner_plus.reshape(nch, (dloc + vec_rows) * hid // 128, 128)

    part_conv = reduce_seq_batch(grad_w_conv, 3, part_outer)
    part_inner = reduce_seq_batch(inner_plus, 1, part_conv)
    parts = [part_outer, part_conv, part_inner]
    parts = [jnp.sum(p, axis=0) for p in exchange(parts, ("ch",), 1)]
    parts = exchange(parts, ("batch",), 2, gather=True)
    parts = [p.reshape((seqs * batches,) + p.shape[2:]) for p in exchange(parts, ("seq",), 3, gather=True)]
    red_w_outer = parts[0].reshape(hloc, dim)
    red_w_conv = jnp.moveaxis(parts[1], 0, 2).reshape(KERNEL_TAPS, hloc, hid)
    red_inner = parts[2].reshape(dloc + vec_rows, hid)
    red_w_inner = red_inner[:dloc]
    mine = red_inner[dloc:].reshape(-1)[:vec_len]
    reds = []
    cut = 0
    for v in vectors:
        n = v.shape[0] // nch
        reds.append(mine[cut : cut + n])
        cut += n
    return (
        output,
        input_grad,
        reds[0],
        reds[1],
        red_w_inner,
        reds[2],
        reds[3],
        reds[4],
        red_w_conv,
        reds[5],
        reds[6],
        reds[7],
        red_w_outer,
        reds[8],
    )


def solution(mesh):
    return jax.shard_map(
        local,
        mesh=mesh,
        in_specs=(
            P("batch", "ch", "seq"),
            P("batch", "seq"),
            P("ch"),
            P("ch"),
            P("ch", None),
            P("ch"),
            P("ch"),
            P("ch"),
            P(None, "ch", None),
            P("ch"),
            P("ch"),
            P("ch"),
            P("ch", None),
            P("ch"),
            P("batch", "ch", "seq"),
        ),
        out_specs=(
            P("batch", "ch", "seq"),
            P("batch", "ch", "seq"),
            P("ch"),
            P("ch"),
            P("ch", None),
            P("ch"),
            P("ch"),
            P("ch"),
            P(None, "ch", None),
            P("ch"),
            P("ch"),
            P("ch"),
            P("ch", None),
            P("ch"),
        ),
        check_vma=False,
    )
```

```python
import functools
import math

import jax
import jax.numpy as jnp
from jax import lax
from jax.experimental import pallas as pl
from jax.experimental.pallas import tpu as pltpu
from jax.sharding import PartitionSpec as P

KERNEL_TAPS = 5
DILATION_SPACING = 32


EPSILON = 1e-05


MESH_AXES = ("batch", "seq", "ch")
MESH_ID = pl.DeviceIdType.MESH


def _group_index(group, sizes, coords):
    me = 0
    for a in group:
        me = me * sizes[a] + coords[a]
    return me


def _exchange_kernel(sizes, group, gather, axes, *refs):
    count_arrays = len(axes)
    x_refs = refs[:count_arrays]
    o_refs = refs[count_arrays : 2 * count_arrays]
    send_sem, recv_sem = refs[2 * count_arrays :]
    coords = {a: lax.axis_index(a) for a in MESH_AXES}
    me = _group_index(group, sizes, coords)
    count = math.prod(sizes[a] for a in group)

    def device(index):
        where = dict(coords)
        rest = index
        for a in reversed(group):
            where[a] = lax.rem(rest, sizes[a])
            rest = rest // sizes[a]
        return tuple(where[a] for a in MESH_AXES)

    barrier = pltpu.get_barrier_semaphore()
    for j in range(1, count):
        pl.semaphore_signal(barrier, 1, device_id=device(lax.rem(me + j, count)), device_id_type=MESH_ID)
    pl.semaphore_wait(barrier, count - 1)
    copies = []
    for j in range(1, count):
        peer = lax.rem(me + j, count)
        for i in range(count_arrays):
            lead = (slice(None),) * axes[i]
            copy = pltpu.make_async_remote_copy(
                src_ref=x_refs[i] if gather else x_refs[i].at[lead + (peer,)],
                dst_ref=o_refs[i].at[lead + (me,)],
                send_sem=send_sem.at[i, j - 1],
                recv_sem=recv_sem.at[i, j - 1],
                device_id=device(peer),
                device_id_type=MESH_ID,
            )
            copy.start()
            copies.append(copy)
    for copy in copies:
        copy.wait()


def exchange(xs, group, collective_id, gather=False, axes=None):
    sizes = {a: lax.axis_size(a) for a in MESH_AXES}
    count = math.prod(sizes[a] for a in group)
    axes = tuple(axes or (0,) * len(xs))
    if count == 1:
        return [x[None] if gather else x for x in xs]
    shapes = [jax.ShapeDtypeStruct((count,) + x.shape if gather else x.shape, x.dtype) for x in xs]
    moved = sum(x.size * x.dtype.itemsize * (count if gather else 1) for x in xs)
    outs = pl.pallas_call(
        functools.partial(_exchange_kernel, sizes, group, gather, axes),
        out_shape=shapes,
        in_specs=[pl.BlockSpec(memory_space=pl.ANY)] * len(xs),
        out_specs=[pl.BlockSpec(memory_space=pl.ANY)] * len(xs),
        scratch_shapes=[
            pltpu.SemaphoreType.DMA((len(xs), count - 1)),
            pltpu.SemaphoreType.DMA((len(xs), count - 1)),
        ],
        compiler_params=pltpu.CompilerParams(collective_id=collective_id, has_side_effects=True),
        cost_estimate=pl.CostEstimate(flops=0, transcendentals=0, bytes_accessed=2 * moved),
    )(*xs)
    me = _group_index(group, sizes, {a: lax.axis_index(a) for a in group})
    placed = []
    for x, out, axis in zip(xs, outs, axes):
        own = x if gather else lax.dynamic_index_in_dim(x, me, axis, keepdims=False)
        placed.append(lax.dynamic_update_index_in_dim(out, own, me, axis))
    return placed


def gelu_exact(values):
    return jax.nn.gelu(values, approximate=False)


def gelu_back(point, grad):
    return jax.vjp(gelu_exact, point)[1](grad)[0]


def normalize(values, gain, shift):
    center = jnp.mean(values, axis=1, keepdims=True)
    offset = values - center
    spread = jnp.mean(offset * offset, axis=1, keepdims=True)
    scale = lax.rsqrt(spread + EPSILON)
    unit = offset * scale
    return (unit * gain[:, None] + shift[:, None], unit, scale)


def normalize_back(grad, unit, scale, gain):
    scaled = grad * gain[:, None]
    first = jnp.mean(scaled, axis=1, keepdims=True)
    second = jnp.mean(scaled * unit, axis=1, keepdims=True)
    return scale * (scaled - first - unit * second)


def neighbour_pairs(seqs, nch, q_count):
    pairs = []
    for s in range(seqs):
        for c in range(nch):
            q = c % q_count
            if q < q_count - 1:
                pairs.append((s * nch + c, s * nch + c + 1))
            elif s < seqs - 1:
                pairs.append((s * nch + c, (s + 1) * nch + c - (q_count - 1)))
    return pairs


def extended(x, width, pairs):
    down = [(j, i) for i, j in pairs]
    length = x.shape[-1]
    before = lax.ppermute(x[..., length - width :], ("seq", "ch"), pairs)
    after = lax.ppermute(x[..., :width], ("seq", "ch"), down)
    return jnp.concatenate([before, x, after], axis=-1)


def shifted_taps(wide, wide_ids, own_ids, offsets, border):
    length = own_ids.shape[-1]
    pieces = []
    for offset in offsets:
        lower = border + offset
        shifted = wide[:, :, lower : lower + length]
        matching = wide_ids[:, lower : lower + length] == own_ids
        pieces.append(jnp.where(matching[:, None, :], shifted, jnp.zeros_like(shifted)))
    return jnp.concatenate(pieces, axis=1)


def to_positions(x, nch, q_count):
    rows, width, length = x.shape
    if q_count > 1:
        x = x.reshape(rows, width, q_count, length // q_count).transpose(0, 2, 1, 3)
        x = x.reshape(rows * q_count, width, length // q_count)
    x = lax.all_to_all(x, "ch", 0, 0, tiled=True)
    return _join(x, nch)


def _join(x, nch):
    total, width, length = x.shape
    p = total // nch
    return x.reshape(nch, p, width, length).transpose(1, 0, 2, 3).reshape(p, nch * width, length)


def to_channels(x, nch, q_count, rows):
    p, width, length = x.shape
    x = x.reshape(p, nch, width // nch, length).transpose(1, 0, 2, 3).reshape(nch * p, width // nch, length)
    x = lax.all_to_all(x, "ch", 0, 0, tiled=True)
    if q_count > 1:
        _, width, part = x.shape
        x = x.reshape(rows, q_count, width, part).transpose(0, 2, 1, 3).reshape(rows, width, q_count * part)
    return x


def local(
    inputs,
    segment_ids,
    norm0_gain,
    norm0_shift,
    w_inner,
    b_inner,
    norm1_gain,
    norm1_shift,
    w_conv,
    b_conv,
    norm2_gain,
    norm2_shift,
    w_outer,
    b_outer,
    cotangent,
):
    nch = lax.axis_size("ch")
    seqs = lax.axis_size("seq")
    batches = lax.axis_size("batch")
    rows, dloc, length = inputs.shape
    hloc = w_conv.shape[1]
    hid = hloc * nch
    dim = dloc * nch
    if rows % nch == 0:
        q_count = 1
    else:
        q_count = nch // rows
    part = length // q_count
    border = 2 * DILATION_SPACING
    offsets = [(k - KERNEL_TAPS // 2) * DILATION_SPACING for k in range(KERNEL_TAPS)]
    back_offsets = [-o for o in offsets]
    pairs = neighbour_pairs(seqs, nch, q_count)
    me = lax.axis_index("ch")

    smalls = [norm0_gain, norm0_shift, b_inner, norm1_gain, norm1_shift, b_conv, norm2_gain, norm2_shift, b_outer]
    sidx = lax.axis_index("seq")
    halves = [
        lax.dynamic_slice_in_dim(w_inner, sidx * (dloc // seqs), dloc // seqs, 0),
        lax.dynamic_slice_in_dim(w_conv, sidx * (hloc // seqs), hloc // seqs, 1),
        lax.dynamic_slice_in_dim(w_outer, sidx * (hloc // seqs), hloc // seqs, 0),
    ]
    small_all, w_in, w_cv, w_out = exchange([jnp.concatenate(smalls)] + halves, ("ch",), 0, gather=True)
    cut = 0
    full = []
    for v in smalls:
        n = v.shape[0]
        full.append(small_all[:, cut : cut + n].reshape(n * nch))
        cut += n
    g0, s0, b_in, g1, s1, b_cv, g2, s2, b_out = full
    w_in = lax.all_gather(w_in, "seq", axis=1, tiled=True).reshape(dim, hid)
    w_cv = lax.all_gather(w_cv, "seq", axis=2, tiled=True).transpose(1, 0, 2, 3).reshape(KERNEL_TAPS, hid, hid)
    w_out = lax.all_gather(w_out, "seq", axis=1, tiled=True).reshape(hid, dim)

    x = to_positions(inputs, nch, q_count)
    cot = to_positions(cotangent, nch, q_count)
    prow = x.shape[0]
    if q_count == 1:
        ids = lax.dynamic_slice_in_dim(segment_ids, me * prow, prow, axis=0)
    else:
        ids = lax.dynamic_slice_in_dim(segment_ids, me // q_count, 1, axis=0)
        ids = lax.dynamic_slice_in_dim(ids, (me % q_count) * part, part, axis=1)
    own_ids = ids + 1
    wide_ids = extended(own_ids, border, pairs)

    residual = x.astype(jnp.float32)
    normed0, unit0, scale0 = normalize(residual, g0, s0)
    hidden0 = gelu_exact(normed0).astype(jnp.bfloat16)
    inner = jnp.einsum("dh,rdl->rhl", w_in, hidden0, preferred_element_type=jnp.float32) + b_in[:, None]
    normed1, unit1, scale1 = normalize(inner, g1, s1)
    hidden1 = gelu_exact(normed1).astype(jnp.bfloat16)
    wide_hidden = extended(hidden1, border, pairs)
    taps = shifted_taps(wide_hidden, wide_ids, own_ids, offsets, border)
    kernel_flat = w_cv.reshape(KERNEL_TAPS * hid, hid)
    mixed = jnp.einsum("co,rcl->rol", kernel_flat, taps, preferred_element_type=jnp.float32) + b_cv[:, None]
    normed2, unit2, scale2 = normalize(mixed, g2, s2)
    hidden2 = gelu_exact(normed2).astype(jnp.bfloat16)
    branch = jnp.einsum("hd,rhl->rdl", w_out, hidden2, preferred_element_type=jnp.float32)
    output = (residual + branch + b_out[:, None]).astype(jnp.bfloat16)

    grad_b_outer = jnp.sum(cot.astype(jnp.float32), axis=(0, 2))
    grad_w_outer = jnp.einsum("rhl,rdl->hd", hidden2, cot, preferred_element_type=jnp.float32)
    def reduce_seq_batch(g, split_dim, after=None):
        if after is not None:
            g, _ = lax.optimization_barrier((g, after))
        g = lax.psum_scatter(g, "seq", scatter_dimension=split_dim, tiled=True)
        return lax.psum_scatter(g, "batch", scatter_dimension=split_dim, tiled=True)

    part_outer = reduce_seq_batch(grad_w_outer.reshape(nch, hloc * dim // 128, 128), 1)
    grad_hidden2 = jnp.einsum("hd,rdl->rhl", w_out, cot, preferred_element_type=jnp.float32)
    grad_normed2 = gelu_back(normed2, grad_hidden2)
    grad_norm2_gain = jnp.sum(grad_normed2 * unit2, axis=(0, 2))
    grad_norm2_shift = jnp.sum(grad_normed2, axis=(0, 2))
    grad_mixed = normalize_back(grad_normed2, unit2, scale2, g2).astype(jnp.bfloat16)
    grad_b_conv = jnp.sum(grad_mixed.astype(jnp.float32), axis=(0, 2))
    grad_w_conv = jnp.einsum(
        "rol,rkcil->okci",
        grad_mixed,
        taps.reshape(prow, KERNEL_TAPS, nch, hloc, part),
        preferred_element_type=jnp.float32,
    )
    wide_grad = extended(grad_mixed, border, pairs)
    back_taps = shifted_taps(wide_grad, wide_ids, own_ids, back_offsets, border)
    kernel_back = jnp.transpose(w_cv, (0, 2, 1)).reshape(KERNEL_TAPS * hid, hid)
    grad_hidden1 = jnp.einsum("oc,rol->rcl", kernel_back, back_taps, preferred_element_type=jnp.float32)
    grad_normed1 = gelu_back(normed1, grad_hidden1)
    grad_norm1_gain = jnp.sum(grad_normed1 * unit1, axis=(0, 2))
    grad_norm1_shift = jnp.sum(grad_normed1, axis=(0, 2))
    grad_inner = normalize_back(grad_normed1, unit1, scale1, g1).astype(jnp.bfloat16)
    grad_inner, _ = lax.optimization_barrier((grad_inner, part_outer))
    grad_b_inner = jnp.sum(grad_inner.astype(jnp.float32), axis=(0, 2))
    grad_w_inner = jnp.einsum("rdl,rhl->dh", hidden0, grad_inner, preferred_element_type=jnp.float32)
    grad_hidden0 = jnp.einsum("dh,rhl->rdl", w_in, grad_inner, preferred_element_type=jnp.float32)
    grad_normed0 = gelu_back(normed0, grad_hidden0)
    grad_norm0_gain = jnp.sum(grad_normed0 * unit0, axis=(0, 2))
    grad_norm0_shift = jnp.sum(grad_normed0, axis=(0, 2))
    input_grad = (cot.astype(jnp.float32) + normalize_back(grad_normed0, unit0, scale0, g0)).astype(jnp.bfloat16)

    output = to_channels(output, nch, q_count, rows)
    input_grad = to_channels(input_grad, nch, q_count, rows)

    vectors = [
        grad_norm0_gain,
        grad_norm0_shift,
        grad_b_inner,
        grad_norm1_gain,
        grad_norm1_shift,
        grad_b_conv,
        grad_norm2_gain,
        grad_norm2_shift,
        grad_b_outer,
    ]
    flat = jnp.concatenate([v.reshape(nch, -1) for v in vectors], axis=1)
    vec_len = flat.shape[1]
    vec_rows = -(-vec_len // hid)
    vec_rows = -(-(dloc + vec_rows) // 64) * 64 - dloc
    flat = jnp.pad(flat, ((0, 0), (0, vec_rows * hid - vec_len))).reshape(nch, vec_rows, hid)
    inner_plus = jnp.concatenate([grad_w_inner.reshape(nch, dloc, hid), flat], axis=1)
    inner_plus = inner_plus.reshape(nch, (dloc + vec_rows) * hid // 128, 128)

    conv_tail = grad_w_conv.shape[1:]
    part_conv = reduce_seq_batch(grad_w_conv.reshape(hid, math.prod(conv_tail) // 128, 128), 0, part_outer)
    part_conv = part_conv.reshape((part_conv.shape[0],) + conv_tail)
    part_inner = reduce_seq_batch(inner_plus, 1, part_conv)
    parts = [part_outer, part_conv, part_inner]
    parts = exchange(parts, ("ch",), 1, axes=(0, 2, 0))
    parts = [jnp.sum(p, axis=a) for p, a in zip(parts, (0, 2, 0))]
    parts = exchange(parts, ("batch",), 2, gather=True)
    parts = [p.reshape((seqs * batches,) + p.shape[2:]) for p in exchange(parts, ("seq",), 3, gather=True)]
    red_w_outer = parts[0].reshape(hloc, dim)
    red_w_conv = parts[1].reshape(hid, KERNEL_TAPS, hloc).transpose(1, 2, 0)
    red_inner = parts[2].reshape(dloc + vec_rows, hid)
    red_w_inner = red_inner[:dloc]
    mine = red_inner[dloc:].reshape(-1)[:vec_len]
    reds = []
    cut = 0
    for v in vectors:
        n = v.shape[0] // nch
        reds.append(mine[cut : cut + n])
        cut += n
    return (
        output,
        input_grad,
        reds[0],
        reds[1],
        red_w_inner,
        reds[2],
        reds[3],
        reds[4],
        red_w_conv,
        reds[5],
        reds[6],
        reds[7],
        red_w_outer,
        reds[8],
    )


def solution(mesh):
    return jax.shard_map(
        local,
        mesh=mesh,
        in_specs=(
            P("batch", "ch", "seq"),
            P("batch", "seq"),
            P("ch"),
            P("ch"),
            P("ch", None),
            P("ch"),
            P("ch"),
            P("ch"),
            P(None, "ch", None),
            P("ch"),
            P("ch"),
            P("ch"),
            P("ch", None),
            P("ch"),
            P("batch", "ch", "seq"),
        ),
        out_specs=(
            P("batch", "ch", "seq"),
            P("batch", "ch", "seq"),
            P("ch"),
            P("ch"),
            P("ch", None),
            P("ch"),
            P("ch"),
            P("ch"),
            P(None, "ch", None),
            P("ch"),
            P("ch"),
            P("ch"),
            P("ch", None),
            P("ch"),
        ),
        check_vma=False,
    )
```

```python
import functools
import math

import jax
import jax.numpy as jnp
from jax import lax
from jax.experimental import pallas as pl
from jax.experimental.pallas import tpu as pltpu
from jax.sharding import PartitionSpec as P

KERNEL_TAPS = 5
DILATION_SPACING = 32


EPSILON = 1e-05


MESH_AXES = ("batch", "seq", "ch")
MESH_ID = pl.DeviceIdType.MESH


def _group_index(group, sizes, coords):
    me = 0
    for a in group:
        me = me * sizes[a] + coords[a]
    return me


def _exchange_kernel(sizes, group, gather, axes, *refs):
    count_arrays = len(axes)
    x_refs = refs[:count_arrays]
    o_refs = refs[count_arrays : 2 * count_arrays]
    send_sem, recv_sem = refs[2 * count_arrays :]
    coords = {a: lax.axis_index(a) for a in MESH_AXES}
    me = _group_index(group, sizes, coords)
    count = math.prod(sizes[a] for a in group)

    def device(index):
        where = dict(coords)
        rest = index
        for a in reversed(group):
            where[a] = lax.rem(rest, sizes[a])
            rest = rest // sizes[a]
        return tuple(where[a] for a in MESH_AXES)

    barrier = pltpu.get_barrier_semaphore()
    for j in range(1, count):
        pl.semaphore_signal(barrier, 1, device_id=device(lax.rem(me + j, count)), device_id_type=MESH_ID)
    pl.semaphore_wait(barrier, count - 1)
    copies = []
    for j in range(1, count):
        peer = lax.rem(me + j, count)
        for i in range(count_arrays):
            lead = (slice(None),) * axes[i]
            copy = pltpu.make_async_remote_copy(
                src_ref=x_refs[i] if gather else x_refs[i].at[lead + (peer,)],
                dst_ref=o_refs[i].at[lead + (me,)],
                send_sem=send_sem.at[i, j - 1],
                recv_sem=recv_sem.at[i, j - 1],
                device_id=device(peer),
                device_id_type=MESH_ID,
            )
            copy.start()
            copies.append(copy)
    for copy in copies:
        copy.wait()


def exchange(xs, group, collective_id, gather=False, axes=None):
    sizes = {a: lax.axis_size(a) for a in MESH_AXES}
    count = math.prod(sizes[a] for a in group)
    axes = tuple(axes or (0,) * len(xs))
    if count == 1:
        return [x[None] if gather else x for x in xs]
    shapes = [jax.ShapeDtypeStruct((count,) + x.shape if gather else x.shape, x.dtype) for x in xs]
    moved = sum(x.size * x.dtype.itemsize * (count if gather else 1) for x in xs)
    outs = pl.pallas_call(
        functools.partial(_exchange_kernel, sizes, group, gather, axes),
        out_shape=shapes,
        in_specs=[pl.BlockSpec(memory_space=pl.ANY)] * len(xs),
        out_specs=[pl.BlockSpec(memory_space=pl.ANY)] * len(xs),
        scratch_shapes=[
            pltpu.SemaphoreType.DMA((len(xs), count - 1)),
            pltpu.SemaphoreType.DMA((len(xs), count - 1)),
        ],
        compiler_params=pltpu.CompilerParams(collective_id=collective_id, has_side_effects=True),
        cost_estimate=pl.CostEstimate(flops=0, transcendentals=0, bytes_accessed=2 * moved),
    )(*xs)
    me = _group_index(group, sizes, {a: lax.axis_index(a) for a in group})
    placed = []
    for x, out, axis in zip(xs, outs, axes):
        own = x if gather else lax.dynamic_index_in_dim(x, me, axis, keepdims=False)
        placed.append(lax.dynamic_update_index_in_dim(out, own, me, axis))
    return placed


def gelu_exact(values):
    return jax.nn.gelu(values, approximate=False)


def gelu_back(point, grad):
    return jax.vjp(gelu_exact, point)[1](grad)[0]


def normalize(values, gain, shift):
    center = jnp.mean(values, axis=1, keepdims=True)
    offset = values - center
    spread = jnp.mean(offset * offset, axis=1, keepdims=True)
    scale = lax.rsqrt(spread + EPSILON)
    unit = offset * scale
    return (unit * gain[:, None] + shift[:, None], unit, scale)


def normalize_back(grad, unit, scale, gain):
    scaled = grad * gain[:, None]
    first = jnp.mean(scaled, axis=1, keepdims=True)
    second = jnp.mean(scaled * unit, axis=1, keepdims=True)
    return scale * (scaled - first - unit * second)


def neighbour_pairs(seqs, nch, q_count):
    pairs = []
    for s in range(seqs):
        for c in range(nch):
            q = c % q_count
            if q < q_count - 1:
                pairs.append((s * nch + c, s * nch + c + 1))
            elif s < seqs - 1:
                pairs.append((s * nch + c, (s + 1) * nch + c - (q_count - 1)))
    return pairs


def extended(x, width, pairs):
    down = [(j, i) for i, j in pairs]
    length = x.shape[-1]
    before = lax.ppermute(x[..., length - width :], ("seq", "ch"), pairs)
    after = lax.ppermute(x[..., :width], ("seq", "ch"), down)
    return jnp.concatenate([before, x, after], axis=-1)


def shifted_taps(wide, wide_ids, own_ids, offsets, border):
    length = own_ids.shape[-1]
    pieces = []
    for offset in offsets:
        lower = border + offset
        shifted = wide[:, :, lower : lower + length]
        matching = wide_ids[:, lower : lower + length] == own_ids
        pieces.append(jnp.where(matching[:, None, :], shifted, jnp.zeros_like(shifted)))
    return jnp.concatenate(pieces, axis=1)


def to_positions(x, nch, q_count):
    rows, width, length = x.shape
    if q_count > 1:
        x = x.reshape(rows, width, q_count, length // q_count).transpose(0, 2, 1, 3)
        x = x.reshape(rows * q_count, width, length // q_count)
    x = lax.all_to_all(x, "ch", 0, 0, tiled=True)
    return _join(x, nch)


def _join(x, nch):
    total, width, length = x.shape
    p = total // nch
    return x.reshape(nch, p, width, length).transpose(1, 0, 2, 3).reshape(p, nch * width, length)


def to_channels(x, nch, q_count, rows):
    p, width, length = x.shape
    x = x.reshape(p, nch, width // nch, length).transpose(1, 0, 2, 3).reshape(nch * p, width // nch, length)
    x = lax.all_to_all(x, "ch", 0, 0, tiled=True)
    if q_count > 1:
        _, width, part = x.shape
        x = x.reshape(rows, q_count, width, part).transpose(0, 2, 1, 3).reshape(rows, width, q_count * part)
    return x


def local(
    inputs,
    segment_ids,
    norm0_gain,
    norm0_shift,
    w_inner,
    b_inner,
    norm1_gain,
    norm1_shift,
    w_conv,
    b_conv,
    norm2_gain,
    norm2_shift,
    w_outer,
    b_outer,
    cotangent,
):
    nch = lax.axis_size("ch")
    seqs = lax.axis_size("seq")
    batches = lax.axis_size("batch")
    rows, dloc, length = inputs.shape
    hloc = w_conv.shape[1]
    hid = hloc * nch
    dim = dloc * nch
    if rows % nch == 0:
        q_count = 1
    else:
        q_count = nch // rows
    part = length // q_count
    border = 2 * DILATION_SPACING
    offsets = [(k - KERNEL_TAPS // 2) * DILATION_SPACING for k in range(KERNEL_TAPS)]
    back_offsets = [-o for o in offsets]
    pairs = neighbour_pairs(seqs, nch, q_count)
    me = lax.axis_index("ch")

    smalls = [norm0_gain, norm0_shift, b_inner, norm1_gain, norm1_shift, b_conv, norm2_gain, norm2_shift, b_outer]
    sidx = lax.axis_index("seq")
    halves = [
        lax.dynamic_slice_in_dim(w_inner, sidx * (dloc // seqs), dloc // seqs, 0),
        lax.dynamic_slice_in_dim(w_conv, sidx * (hloc // seqs), hloc // seqs, 1),
        lax.dynamic_slice_in_dim(w_outer, sidx * (hloc // seqs), hloc // seqs, 0),
    ]
    small_all, w_in, w_cv, w_out = exchange([jnp.concatenate(smalls)] + halves, ("ch",), 0, gather=True)
    cut = 0
    full = []
    for v in smalls:
        n = v.shape[0]
        full.append(small_all[:, cut : cut + n].reshape(n * nch))
        cut += n
    g0, s0, b_in, g1, s1, b_cv, g2, s2, b_out = full
    w_in = lax.all_gather(w_in, "seq", axis=1, tiled=True).reshape(dim, hid)
    w_cv = lax.all_gather(w_cv, "seq", axis=2, tiled=True).transpose(1, 0, 2, 3).reshape(KERNEL_TAPS, hid, hid)
    w_out = lax.all_gather(w_out, "seq", axis=1, tiled=True).reshape(hid, dim)

    x = to_positions(inputs, nch, q_count)
    cot = to_positions(cotangent, nch, q_count)
    prow = x.shape[0]
    if q_count == 1:
        ids = lax.dynamic_slice_in_dim(segment_ids, me * prow, prow, axis=0)
    else:
        ids = lax.dynamic_slice_in_dim(segment_ids, me // q_count, 1, axis=0)
        ids = lax.dynamic_slice_in_dim(ids, (me % q_count) * part, part, axis=1)
    own_ids = ids + 1
    wide_ids = extended(own_ids, border, pairs)

    residual = x.astype(jnp.float32)
    normed0, unit0, scale0 = normalize(residual, g0, s0)
    hidden0 = gelu_exact(normed0).astype(jnp.bfloat16)
    inner = jnp.einsum("dh,rdl->rhl", w_in, hidden0, preferred_element_type=jnp.float32) + b_in[:, None]
    normed1, unit1, scale1 = normalize(inner, g1, s1)
    hidden1 = gelu_exact(normed1).astype(jnp.bfloat16)
    wide_hidden = extended(hidden1, border, pairs)
    taps = shifted_taps(wide_hidden, wide_ids, own_ids, offsets, border)
    kernel_flat = w_cv.reshape(KERNEL_TAPS * hid, hid)
    mixed = jnp.einsum("co,rcl->rol", kernel_flat, taps, preferred_element_type=jnp.float32) + b_cv[:, None]
    normed2, unit2, scale2 = normalize(mixed, g2, s2)
    hidden2 = gelu_exact(normed2).astype(jnp.bfloat16)
    branch = jnp.einsum("hd,rhl->rdl", w_out, hidden2, preferred_element_type=jnp.float32)
    output = (residual + branch + b_out[:, None]).astype(jnp.bfloat16)
    output = to_channels(output, nch, q_count, rows)

    grad_b_outer = jnp.sum(cot.astype(jnp.float32), axis=(0, 2))
    grad_w_outer = jnp.einsum("rhl,rdl->hd", hidden2, cot, preferred_element_type=jnp.float32)
    def reduce_seq_batch(g, split_dim, after=None):
        if after is not None:
            g, _ = lax.optimization_barrier((g, after))
        g = lax.psum_scatter(g, "seq", scatter_dimension=split_dim, tiled=True)
        return lax.psum_scatter(g, "batch", scatter_dimension=split_dim, tiled=True)

    part_outer = reduce_seq_batch(grad_w_outer.reshape(nch, hloc * dim // 128, 128), 1)
    grad_hidden2 = jnp.einsum("hd,rdl->rhl", w_out, cot, preferred_element_type=jnp.float32)
    grad_normed2 = gelu_back(normed2, grad_hidden2)
    grad_norm2_gain = jnp.sum(grad_normed2 * unit2, axis=(0, 2))
    grad_norm2_shift = jnp.sum(grad_normed2, axis=(0, 2))
    grad_mixed = normalize_back(grad_normed2, unit2, scale2, g2).astype(jnp.bfloat16)
    grad_b_conv = jnp.sum(grad_mixed.astype(jnp.float32), axis=(0, 2))
    grad_w_conv = jnp.einsum(
        "rol,rkcil->okci",
        grad_mixed,
        taps.reshape(prow, KERNEL_TAPS, nch, hloc, part),
        preferred_element_type=jnp.float32,
    )
    wide_grad = extended(grad_mixed, border, pairs)
    back_taps = shifted_taps(wide_grad, wide_ids, own_ids, back_offsets, border)
    kernel_back = jnp.transpose(w_cv, (0, 2, 1)).reshape(KERNEL_TAPS * hid, hid)
    grad_hidden1 = jnp.einsum("oc,rol->rcl", kernel_back, back_taps, preferred_element_type=jnp.float32)
    grad_normed1 = gelu_back(normed1, grad_hidden1)
    grad_norm1_gain = jnp.sum(grad_normed1 * unit1, axis=(0, 2))
    grad_norm1_shift = jnp.sum(grad_normed1, axis=(0, 2))
    grad_inner = normalize_back(grad_normed1, unit1, scale1, g1).astype(jnp.bfloat16)
    grad_inner, _, output = lax.optimization_barrier((grad_inner, part_outer, output))
    grad_b_inner = jnp.sum(grad_inner.astype(jnp.float32), axis=(0, 2))
    grad_w_inner = jnp.einsum("rdl,rhl->dh", hidden0, grad_inner, preferred_element_type=jnp.float32)
    grad_hidden0 = jnp.einsum("dh,rhl->rdl", w_in, grad_inner, preferred_element_type=jnp.float32)
    grad_normed0 = gelu_back(normed0, grad_hidden0)
    grad_norm0_gain = jnp.sum(grad_normed0 * unit0, axis=(0, 2))
    grad_norm0_shift = jnp.sum(grad_normed0, axis=(0, 2))
    input_grad = (cot.astype(jnp.float32) + normalize_back(grad_normed0, unit0, scale0, g0)).astype(jnp.bfloat16)

    input_grad = to_channels(input_grad, nch, q_count, rows)

    vectors = [
        grad_norm0_gain,
        grad_norm0_shift,
        grad_b_inner,
        grad_norm1_gain,
        grad_norm1_shift,
        grad_b_conv,
        grad_norm2_gain,
        grad_norm2_shift,
        grad_b_outer,
    ]
    flat = jnp.concatenate([v.reshape(nch, -1) for v in vectors], axis=1)
    vec_len = flat.shape[1]
    vec_rows = -(-vec_len // hid)
    vec_rows = -(-(dloc + vec_rows) // 64) * 64 - dloc
    flat = jnp.pad(flat, ((0, 0), (0, vec_rows * hid - vec_len))).reshape(nch, vec_rows, hid)
    inner_plus = jnp.concatenate([grad_w_inner.reshape(nch, dloc, hid), flat], axis=1)
    inner_plus = inner_plus.reshape(nch, (dloc + vec_rows) * hid // 128, 128)

    conv_tail = grad_w_conv.shape[1:]
    def finish(part, axis, cid):
        part = exchange([part], ("ch",), cid, axes=(axis,))[0]
        part = jnp.sum(part, axis=axis)
        shape = part.shape
        if part.size % 128 == 0:
            part = part.reshape(part.size // 128, 128)
        part = exchange([part], ("batch",), cid + 1, gather=True)[0]
        part = exchange([part], ("seq",), cid + 2, gather=True)[0]
        return part.reshape((seqs * batches,) + shape)

    conv_tail = grad_w_conv.shape[1:]
    part_conv = reduce_seq_batch(grad_w_conv.reshape(hid, math.prod(conv_tail) // 128, 128), 0, part_outer)
    part_conv = part_conv.reshape((part_conv.shape[0],) + conv_tail)
    part_outer, _ = lax.optimization_barrier((part_outer, grad_w_conv))
    red_w_outer = finish(part_outer, 0, 1).reshape(hloc, dim)
    part_inner = reduce_seq_batch(inner_plus, 1, part_conv)
    part_conv, _ = lax.optimization_barrier((part_conv, inner_plus))
    red_w_conv = finish(part_conv, 2, 4).reshape(hid, KERNEL_TAPS, hloc).transpose(1, 2, 0)
    red_inner = finish(part_inner, 0, 7).reshape(dloc + vec_rows, hid)
    red_w_inner = red_inner[:dloc]
    mine = red_inner[dloc:].reshape(-1)[:vec_len]
    reds = []
    cut = 0
    for v in vectors:
        n = v.shape[0] // nch
        reds.append(mine[cut : cut + n])
        cut += n
    return (
        output,
        input_grad,
        reds[0],
        reds[1],
        red_w_inner,
        reds[2],
        reds[3],
        reds[4],
        red_w_conv,
        reds[5],
        reds[6],
        reds[7],
        red_w_outer,
        reds[8],
    )


def solution(mesh):
    return jax.shard_map(
        local,
        mesh=mesh,
        in_specs=(
            P("batch", "ch", "seq"),
            P("batch", "seq"),
            P("ch"),
            P("ch"),
            P("ch", None),
            P("ch"),
            P("ch"),
            P("ch"),
            P(None, "ch", None),
            P("ch"),
            P("ch"),
            P("ch"),
            P("ch", None),
            P("ch"),
            P("batch", "ch", "seq"),
        ),
        out_specs=(
            P("batch", "ch", "seq"),
            P("batch", "ch", "seq"),
            P("ch"),
            P("ch"),
            P("ch", None),
            P("ch"),
            P("ch"),
            P("ch"),
            P(None, "ch", None),
            P("ch"),
            P("ch"),
            P("ch"),
            P("ch", None),
            P("ch"),
        ),
        check_vma=False,
    )
```

```python
import functools
import math

import jax
import jax.numpy as jnp
from jax import lax
from jax.experimental import pallas as pl
from jax.experimental.pallas import tpu as pltpu
from jax.sharding import PartitionSpec as P

KERNEL_TAPS = 5
DILATION_SPACING = 32


EPSILON = 1e-05


MESH_AXES = ("batch", "seq", "ch")
MESH_ID = pl.DeviceIdType.MESH


def _group_index(group, sizes, coords):
    me = 0
    for a in group:
        me = me * sizes[a] + coords[a]
    return me


def _exchange_kernel(sizes, group, gather, axes, *refs):
    count_arrays = len(axes)
    x_refs = refs[:count_arrays]
    o_refs = refs[count_arrays : 2 * count_arrays]
    send_sem, recv_sem = refs[2 * count_arrays :]
    coords = {a: lax.axis_index(a) for a in MESH_AXES}
    me = _group_index(group, sizes, coords)
    count = math.prod(sizes[a] for a in group)

    def device(index):
        where = dict(coords)
        rest = index
        for a in reversed(group):
            where[a] = lax.rem(rest, sizes[a])
            rest = rest // sizes[a]
        return tuple(where[a] for a in MESH_AXES)

    barrier = pltpu.get_barrier_semaphore()
    for j in range(1, count):
        pl.semaphore_signal(barrier, 1, device_id=device(lax.rem(me + j, count)), device_id_type=MESH_ID)
    pl.semaphore_wait(barrier, count - 1)
    copies = []
    for j in range(1, count):
        peer = lax.rem(me + j, count)
        for i in range(count_arrays):
            lead = (slice(None),) * axes[i]
            copy = pltpu.make_async_remote_copy(
                src_ref=x_refs[i] if gather else x_refs[i].at[lead + (peer,)],
                dst_ref=o_refs[i].at[lead + (me,)],
                send_sem=send_sem.at[i, j - 1],
                recv_sem=recv_sem.at[i, j - 1],
                device_id=device(peer),
                device_id_type=MESH_ID,
            )
            copy.start()
            copies.append(copy)
    for copy in copies:
        copy.wait()


def exchange(xs, group, collective_id, gather=False, axes=None):
    sizes = {a: lax.axis_size(a) for a in MESH_AXES}
    count = math.prod(sizes[a] for a in group)
    axes = tuple(axes or (0,) * len(xs))
    if count == 1:
        return [x[None] if gather else x for x in xs]
    shapes = [jax.ShapeDtypeStruct((count,) + x.shape if gather else x.shape, x.dtype) for x in xs]
    moved = sum(x.size * x.dtype.itemsize * (count if gather else 1) for x in xs)
    outs = pl.pallas_call(
        functools.partial(_exchange_kernel, sizes, group, gather, axes),
        out_shape=shapes,
        in_specs=[pl.BlockSpec(memory_space=pl.ANY)] * len(xs),
        out_specs=[pl.BlockSpec(memory_space=pl.ANY)] * len(xs),
        scratch_shapes=[
            pltpu.SemaphoreType.DMA((len(xs), count - 1)),
            pltpu.SemaphoreType.DMA((len(xs), count - 1)),
        ],
        compiler_params=pltpu.CompilerParams(collective_id=collective_id, has_side_effects=True),
        cost_estimate=pl.CostEstimate(flops=0, transcendentals=0, bytes_accessed=2 * moved),
    )(*xs)
    me = _group_index(group, sizes, {a: lax.axis_index(a) for a in group})
    placed = []
    for x, out, axis in zip(xs, outs, axes):
        own = x if gather else lax.dynamic_index_in_dim(x, me, axis, keepdims=False)
        placed.append(lax.dynamic_update_index_in_dim(out, own, me, axis))
    return placed


def gelu_exact(values):
    return jax.nn.gelu(values, approximate=False)


def gelu_back(point, grad):
    return jax.vjp(gelu_exact, point)[1](grad)[0]


def normalize(values, gain, shift):
    center = jnp.mean(values, axis=1, keepdims=True)
    offset = values - center
    spread = jnp.mean(offset * offset, axis=1, keepdims=True)
    scale = lax.rsqrt(spread + EPSILON)
    unit = offset * scale
    return (unit * gain[:, None] + shift[:, None], unit, scale)


def normalize_back(grad, unit, scale, gain):
    scaled = grad * gain[:, None]
    first = jnp.mean(scaled, axis=1, keepdims=True)
    second = jnp.mean(scaled * unit, axis=1, keepdims=True)
    return scale * (scaled - first - unit * second)


def neighbour_pairs(seqs, nch, q_count):
    pairs = []
    for s in range(seqs):
        for c in range(nch):
            q = c % q_count
            if q < q_count - 1:
                pairs.append((s * nch + c, s * nch + c + 1))
            elif s < seqs - 1:
                pairs.append((s * nch + c, (s + 1) * nch + c - (q_count - 1)))
    return pairs


def extended(x, width, pairs):
    down = [(j, i) for i, j in pairs]
    length = x.shape[-1]
    before = lax.ppermute(x[..., length - width :], ("seq", "ch"), pairs)
    after = lax.ppermute(x[..., :width], ("seq", "ch"), down)
    return jnp.concatenate([before, x, after], axis=-1)


def shifted_taps(wide, wide_ids, own_ids, offsets, border):
    length = own_ids.shape[-1]
    pieces = []
    for offset in offsets:
        lower = border + offset
        shifted = wide[:, :, lower : lower + length]
        matching = wide_ids[:, lower : lower + length] == own_ids
        pieces.append(jnp.where(matching[:, None, :], shifted, jnp.zeros_like(shifted)))
    return jnp.concatenate(pieces, axis=1)


def to_positions(x, nch, q_count):
    rows, width, length = x.shape
    if q_count > 1:
        x = x.reshape(rows, width, q_count, length // q_count).transpose(0, 2, 1, 3)
        x = x.reshape(rows * q_count, width, length // q_count)
    x = lax.all_to_all(x, "ch", 0, 0, tiled=True)
    return _join(x, nch)


def _join(x, nch):
    total, width, length = x.shape
    p = total // nch
    return x.reshape(nch, p, width, length).transpose(1, 0, 2, 3).reshape(p, nch * width, length)


def to_channels(x, nch, q_count, rows):
    p, width, length = x.shape
    x = x.reshape(p, nch, width // nch, length).transpose(1, 0, 2, 3).reshape(nch * p, width // nch, length)
    x = lax.all_to_all(x, "ch", 0, 0, tiled=True)
    if q_count > 1:
        _, width, part = x.shape
        x = x.reshape(rows, q_count, width, part).transpose(0, 2, 1, 3).reshape(rows, width, q_count * part)
    return x


def local(
    inputs,
    segment_ids,
    norm0_gain,
    norm0_shift,
    w_inner,
    b_inner,
    norm1_gain,
    norm1_shift,
    w_conv,
    b_conv,
    norm2_gain,
    norm2_shift,
    w_outer,
    b_outer,
    cotangent,
):
    nch = lax.axis_size("ch")
    seqs = lax.axis_size("seq")
    batches = lax.axis_size("batch")
    rows, dloc, length = inputs.shape
    hloc = w_conv.shape[1]
    hid = hloc * nch
    dim = dloc * nch
    if rows % nch == 0:
        q_count = 1
    else:
        q_count = nch // rows
    part = length // q_count
    border = 2 * DILATION_SPACING
    offsets = [(k - KERNEL_TAPS // 2) * DILATION_SPACING for k in range(KERNEL_TAPS)]
    back_offsets = [-o for o in offsets]
    pairs = neighbour_pairs(seqs, nch, q_count)
    me = lax.axis_index("ch")

    smalls = [norm0_gain, norm0_shift, b_inner, norm1_gain, norm1_shift, b_conv, norm2_gain, norm2_shift, b_outer]
    sidx = lax.axis_index("seq")
    halves = [
        lax.dynamic_slice_in_dim(w_inner, sidx * (dloc // seqs), dloc // seqs, 0),
        lax.dynamic_slice_in_dim(w_conv, sidx * (hloc // seqs), hloc // seqs, 1),
        lax.dynamic_slice_in_dim(w_outer, sidx * (hloc // seqs), hloc // seqs, 0),
    ]
    small_all, w_in, w_cv, w_out = exchange([jnp.concatenate(smalls)] + halves, ("ch",), 0, gather=True)
    cut = 0
    full = []
    for v in smalls:
        n = v.shape[0]
        full.append(small_all[:, cut : cut + n].reshape(n * nch))
        cut += n
    g0, s0, b_in, g1, s1, b_cv, g2, s2, b_out = full
    w_in = lax.all_gather(w_in, "seq", axis=1, tiled=True).reshape(dim, hid)
    w_cv = lax.all_gather(w_cv, "seq", axis=2, tiled=True).transpose(1, 0, 2, 3).reshape(KERNEL_TAPS, hid, hid)
    w_out = lax.all_gather(w_out, "seq", axis=1, tiled=True).reshape(hid, dim)

    x = to_positions(inputs, nch, q_count)
    cot = to_positions(cotangent, nch, q_count)
    prow = x.shape[0]
    if q_count == 1:
        ids = lax.dynamic_slice_in_dim(segment_ids, me * prow, prow, axis=0)
    else:
        ids = lax.dynamic_slice_in_dim(segment_ids, me // q_count, 1, axis=0)
        ids = lax.dynamic_slice_in_dim(ids, (me % q_count) * part, part, axis=1)
    own_ids = ids + 1
    wide_ids = extended(own_ids, border, pairs)

    residual = x.astype(jnp.float32)
    normed0, unit0, scale0 = normalize(residual, g0, s0)
    hidden0 = gelu_exact(normed0).astype(jnp.bfloat16)
    inner = jnp.einsum("dh,rdl->rhl", w_in, hidden0, preferred_element_type=jnp.float32) + b_in[:, None]
    normed1, unit1, scale1 = normalize(inner, g1, s1)
    hidden1 = gelu_exact(normed1).astype(jnp.bfloat16)
    wide_hidden = extended(hidden1, border, pairs)
    taps = shifted_taps(wide_hidden, wide_ids, own_ids, offsets, border)
    kernel_flat = w_cv.reshape(KERNEL_TAPS * hid, hid)
    mixed = jnp.einsum("co,rcl->rol", kernel_flat, taps, preferred_element_type=jnp.float32) + b_cv[:, None]
    normed2, unit2, scale2 = normalize(mixed, g2, s2)
    hidden2 = gelu_exact(normed2).astype(jnp.bfloat16)
    branch = jnp.einsum("hd,rhl->rdl", w_out, hidden2, preferred_element_type=jnp.float32)
    output = (residual + branch + b_out[:, None]).astype(jnp.bfloat16)

    grad_b_outer = jnp.sum(cot.astype(jnp.float32), axis=(0, 2))
    grad_w_outer = jnp.einsum("rhl,rdl->hd", hidden2, cot, preferred_element_type=jnp.float32)
    def reduce_seq_batch(g, split_dim, after=None):
        if after is not None:
            g, _ = lax.optimization_barrier((g, after))
        g = lax.psum_scatter(g, "seq", scatter_dimension=split_dim, tiled=True)
        return lax.psum_scatter(g, "batch", scatter_dimension=split_dim, tiled=True)

    part_outer = reduce_seq_batch(grad_w_outer.reshape(nch, hloc, dim), 2)
    grad_hidden2 = jnp.einsum("hd,rdl->rhl", w_out, cot, preferred_element_type=jnp.float32)
    grad_normed2 = gelu_back(normed2, grad_hidden2)
    grad_norm2_gain = jnp.sum(grad_normed2 * unit2, axis=(0, 2))
    grad_norm2_shift = jnp.sum(grad_normed2, axis=(0, 2))
    grad_mixed = normalize_back(grad_normed2, unit2, scale2, g2).astype(jnp.bfloat16)
    grad_b_conv = jnp.sum(grad_mixed.astype(jnp.float32), axis=(0, 2))
    grad_w_conv = jnp.einsum(
        "rol,rkcil->okci",
        grad_mixed,
        taps.reshape(prow, KERNEL_TAPS, nch, hloc, part),
        preferred_element_type=jnp.float32,
    )
    wide_grad = extended(grad_mixed, border, pairs)
    back_taps = shifted_taps(wide_grad, wide_ids, own_ids, back_offsets, border)
    grad_hidden1 = jnp.einsum(
        "kco,rkol->rcl",
        w_cv,
        back_taps.reshape(prow, KERNEL_TAPS, hid, part),
        preferred_element_type=jnp.float32,
    )
    grad_normed1 = gelu_back(normed1, grad_hidden1)
    grad_norm1_gain = jnp.sum(grad_normed1 * unit1, axis=(0, 2))
    grad_norm1_shift = jnp.sum(grad_normed1, axis=(0, 2))
    grad_inner = normalize_back(grad_normed1, unit1, scale1, g1).astype(jnp.bfloat16)
    grad_inner, _ = lax.optimization_barrier((grad_inner, part_outer))
    grad_b_inner = jnp.sum(grad_inner.astype(jnp.float32), axis=(0, 2))
    grad_w_inner = jnp.einsum("rdl,rhl->dh", hidden0, grad_inner, preferred_element_type=jnp.float32)
    grad_hidden0 = jnp.einsum("dh,rhl->rdl", w_in, grad_inner, preferred_element_type=jnp.float32)
    grad_normed0 = gelu_back(normed0, grad_hidden0)
    grad_norm0_gain = jnp.sum(grad_normed0 * unit0, axis=(0, 2))
    grad_norm0_shift = jnp.sum(grad_normed0, axis=(0, 2))
    input_grad = (cot.astype(jnp.float32) + normalize_back(grad_normed0, unit0, scale0, g0)).astype(jnp.bfloat16)

    output = to_channels(output, nch, q_count, rows)
    input_grad = to_channels(input_grad, nch, q_count, rows)

    vectors = [
        grad_norm0_gain,
        grad_norm0_shift,
        grad_b_inner,
        grad_norm1_gain,
        grad_norm1_shift,
        grad_b_conv,
        grad_norm2_gain,
        grad_norm2_shift,
        grad_b_outer,
    ]
    flat = jnp.concatenate([v.reshape(nch, -1) for v in vectors], axis=1)
    vec_len = flat.shape[1]
    vec_rows = -(-vec_len // hid)
    vec_rows = -(-(dloc + vec_rows) // 64) * 64 - dloc
    flat = jnp.pad(flat, ((0, 0), (0, vec_rows * hid - vec_len))).reshape(nch, vec_rows, hid)
    inner_plus = jnp.concatenate([grad_w_inner.reshape(nch, dloc, hid), flat], axis=1)
    inner_plus = inner_plus.reshape(nch, (dloc + vec_rows) * hid // 128, 128)

    conv_tail = grad_w_conv.shape[1:]
    part_conv = reduce_seq_batch(grad_w_conv.reshape(hid, math.prod(conv_tail) // 128, 128), 0, part_outer)
    part_conv = part_conv.reshape((part_conv.shape[0],) + conv_tail)
    part_inner = reduce_seq_batch(inner_plus, 1, part_conv)
    parts = [part_outer, part_conv, part_inner]
    parts = exchange(parts, ("ch",), 1, axes=(0, 2, 0))
    parts = [jnp.sum(p, axis=a) for p, a in zip(parts, (0, 2, 0))]
    outer_shape = parts[0].shape
    parts = exchange(parts, ("batch",), 2, gather=True)
    parts = [p.reshape((seqs * batches,) + p.shape[2:]) for p in exchange(parts, ("seq",), 3, gather=True)]
    red_w_outer = jnp.moveaxis(parts[0].reshape((seqs * batches,) + outer_shape), 0, 1).reshape(hloc, dim)
    red_w_conv = parts[1].reshape(hid, KERNEL_TAPS, hloc).transpose(1, 2, 0)
    red_inner = parts[2].reshape(dloc + vec_rows, hid)
    red_w_inner = red_inner[:dloc]
    mine = red_inner[dloc:].reshape(-1)[:vec_len]
    reds = []
    cut = 0
    for v in vectors:
        n = v.shape[0] // nch
        reds.append(mine[cut : cut + n])
        cut += n
    return (
        output,
        input_grad,
        reds[0],
        reds[1],
        red_w_inner,
        reds[2],
        reds[3],
        reds[4],
        red_w_conv,
        reds[5],
        reds[6],
        reds[7],
        red_w_outer,
        reds[8],
    )


def solution(mesh):
    return jax.shard_map(
        local,
        mesh=mesh,
        in_specs=(
            P("batch", "ch", "seq"),
            P("batch", "seq"),
            P("ch"),
            P("ch"),
            P("ch", None),
            P("ch"),
            P("ch"),
            P("ch"),
            P(None, "ch", None),
            P("ch"),
            P("ch"),
            P("ch"),
            P("ch", None),
            P("ch"),
            P("batch", "ch", "seq"),
        ),
        out_specs=(
            P("batch", "ch", "seq"),
            P("batch", "ch", "seq"),
            P("ch"),
            P("ch"),
            P("ch", None),
            P("ch"),
            P("ch"),
            P("ch"),
            P(None, "ch", None),
            P("ch"),
            P("ch"),
            P("ch"),
            P("ch", None),
            P("ch"),
        ),
        check_vma=False,
    )
```

```python
import functools
import math

import jax
import jax.numpy as jnp
from jax import lax
from jax.experimental import pallas as pl
from jax.experimental.pallas import tpu as pltpu
from jax.sharding import PartitionSpec as P

KERNEL_TAPS = 5
DILATION_SPACING = 32


EPSILON = 1e-05


MESH_AXES = ("batch", "seq", "ch")
MESH_ID = pl.DeviceIdType.MESH


def _group_index(group, sizes, coords):
    me = 0
    for a in group:
        me = me * sizes[a] + coords[a]
    return me


def _exchange_kernel(sizes, group, gather, axes, *refs):
    count_arrays = len(axes)
    x_refs = refs[:count_arrays]
    o_refs = refs[count_arrays : 2 * count_arrays]
    send_sem, recv_sem = refs[2 * count_arrays :]
    coords = {a: lax.axis_index(a) for a in MESH_AXES}
    me = _group_index(group, sizes, coords)
    count = math.prod(sizes[a] for a in group)

    def device(index):
        where = dict(coords)
        rest = index
        for a in reversed(group):
            where[a] = lax.rem(rest, sizes[a])
            rest = rest // sizes[a]
        return tuple(where[a] for a in MESH_AXES)

    barrier = pltpu.get_barrier_semaphore()
    for j in range(1, count):
        pl.semaphore_signal(barrier, 1, device_id=device(lax.rem(me + j, count)), device_id_type=MESH_ID)
    pl.semaphore_wait(barrier, count - 1)
    copies = []
    for j in range(1, count):
        peer = lax.rem(me + j, count)
        for i in range(count_arrays):
            lead = (slice(None),) * axes[i]
            copy = pltpu.make_async_remote_copy(
                src_ref=x_refs[i] if gather else x_refs[i].at[lead + (peer,)],
                dst_ref=o_refs[i].at[lead + (me,)],
                send_sem=send_sem.at[i, j - 1],
                recv_sem=recv_sem.at[i, j - 1],
                device_id=device(peer),
                device_id_type=MESH_ID,
            )
            copy.start()
            copies.append(copy)
    for copy in copies:
        copy.wait()


def exchange(xs, group, collective_id, gather=False, axes=None):
    sizes = {a: lax.axis_size(a) for a in MESH_AXES}
    count = math.prod(sizes[a] for a in group)
    axes = tuple(axes or (0,) * len(xs))
    if count == 1:
        return [x[None] if gather else x for x in xs]
    shapes = [jax.ShapeDtypeStruct((count,) + x.shape if gather else x.shape, x.dtype) for x in xs]
    moved = sum(x.size * x.dtype.itemsize * (count if gather else 1) for x in xs)
    outs = pl.pallas_call(
        functools.partial(_exchange_kernel, sizes, group, gather, axes),
        out_shape=shapes,
        in_specs=[pl.BlockSpec(memory_space=pl.ANY)] * len(xs),
        out_specs=[pl.BlockSpec(memory_space=pl.ANY)] * len(xs),
        scratch_shapes=[
            pltpu.SemaphoreType.DMA((len(xs), count - 1)),
            pltpu.SemaphoreType.DMA((len(xs), count - 1)),
        ],
        compiler_params=pltpu.CompilerParams(collective_id=collective_id, has_side_effects=True),
        cost_estimate=pl.CostEstimate(flops=0, transcendentals=0, bytes_accessed=2 * moved),
    )(*xs)
    me = _group_index(group, sizes, {a: lax.axis_index(a) for a in group})
    placed = []
    for x, out, axis in zip(xs, outs, axes):
        own = x if gather else lax.dynamic_index_in_dim(x, me, axis, keepdims=False)
        placed.append(lax.dynamic_update_index_in_dim(out, own, me, axis))
    return placed


def gelu_exact(values):
    return jax.nn.gelu(values, approximate=False)


def gelu_back(point, grad):
    return jax.vjp(gelu_exact, point)[1](grad)[0]


def normalize(values, gain, shift):
    center = jnp.mean(values, axis=1, keepdims=True)
    offset = values - center
    spread = jnp.mean(offset * offset, axis=1, keepdims=True)
    scale = lax.rsqrt(spread + EPSILON)
    unit = offset * scale
    return (unit * gain[:, None] + shift[:, None], unit, scale)


def normalize_back(grad, unit, scale, gain):
    scaled = grad * gain[:, None]
    first = jnp.mean(scaled, axis=1, keepdims=True)
    second = jnp.mean(scaled * unit, axis=1, keepdims=True)
    return scale * (scaled - first - unit * second)


def neighbour_pairs(seqs, nch, q_count):
    pairs = []
    for s in range(seqs):
        for c in range(nch):
            q = c % q_count
            if q < q_count - 1:
                pairs.append((s * nch + c, s * nch + c + 1))
            elif s < seqs - 1:
                pairs.append((s * nch + c, (s + 1) * nch + c - (q_count - 1)))
    return pairs


def extended(x, width, pairs):
    down = [(j, i) for i, j in pairs]
    length = x.shape[-1]
    before = lax.ppermute(x[..., length - width :], ("seq", "ch"), pairs)
    after = lax.ppermute(x[..., :width], ("seq", "ch"), down)
    return jnp.concatenate([before, x, after], axis=-1)


def shifted_taps(wide, wide_ids, own_ids, offsets, border):
    length = own_ids.shape[-1]
    pieces = []
    for offset in offsets:
        lower = border + offset
        shifted = wide[:, :, lower : lower + length]
        matching = wide_ids[:, lower : lower + length] == own_ids
        pieces.append(jnp.where(matching[:, None, :], shifted, jnp.zeros_like(shifted)))
    return jnp.concatenate(pieces, axis=1)


def to_positions(x, nch, q_count):
    rows, width, length = x.shape
    if q_count > 1:
        x = x.reshape(rows, width, q_count, length // q_count).transpose(0, 2, 1, 3)
        x = x.reshape(rows * q_count, width, length // q_count)
    x = lax.all_to_all(x, "ch", 0, 0, tiled=True)
    return _join(x, nch)


def _join(x, nch):
    total, width, length = x.shape
    p = total // nch
    return x.reshape(nch, p, width, length).transpose(1, 0, 2, 3).reshape(p, nch * width, length)


def to_channels(x, nch, q_count, rows):
    p, width, length = x.shape
    x = x.reshape(p, nch, width // nch, length).transpose(1, 0, 2, 3).reshape(nch * p, width // nch, length)
    x = lax.all_to_all(x, "ch", 0, 0, tiled=True)
    if q_count > 1:
        _, width, part = x.shape
        x = x.reshape(rows, q_count, width, part).transpose(0, 2, 1, 3).reshape(rows, width, q_count * part)
    return x


def local(
    inputs,
    segment_ids,
    norm0_gain,
    norm0_shift,
    w_inner,
    b_inner,
    norm1_gain,
    norm1_shift,
    w_conv,
    b_conv,
    norm2_gain,
    norm2_shift,
    w_outer,
    b_outer,
    cotangent,
):
    nch = lax.axis_size("ch")
    seqs = lax.axis_size("seq")
    batches = lax.axis_size("batch")
    rows, dloc, length = inputs.shape
    hloc = w_conv.shape[1]
    hid = hloc * nch
    dim = dloc * nch
    if rows % nch == 0:
        q_count = 1
    else:
        q_count = nch // rows
    part = length // q_count
    border = 2 * DILATION_SPACING
    offsets = [(k - KERNEL_TAPS // 2) * DILATION_SPACING for k in range(KERNEL_TAPS)]
    back_offsets = [-o for o in offsets]
    pairs = neighbour_pairs(seqs, nch, q_count)
    me = lax.axis_index("ch")

    smalls = [norm0_gain, norm0_shift, b_inner, norm1_gain, norm1_shift, b_conv, norm2_gain, norm2_shift, b_outer]
    sidx = lax.axis_index("seq")
    halves = [
        lax.dynamic_slice_in_dim(w_inner, sidx * (dloc // seqs), dloc // seqs, 0),
        lax.dynamic_slice_in_dim(w_conv, sidx * (hloc // seqs), hloc // seqs, 1),
        lax.dynamic_slice_in_dim(w_outer, sidx * (hloc // seqs), hloc // seqs, 0),
    ]
    small_all, w_in, w_cv, w_out = exchange([jnp.concatenate(smalls)] + halves, ("ch",), 0, gather=True)
    cut = 0
    full = []
    for v in smalls:
        n = v.shape[0]
        full.append(small_all[:, cut : cut + n].reshape(n * nch))
        cut += n
    g0, s0, b_in, g1, s1, b_cv, g2, s2, b_out = full
    w_in = lax.all_gather(w_in, "seq", axis=1, tiled=True).reshape(dim, hid)
    w_cv = lax.all_gather(w_cv, "seq", axis=2, tiled=True).transpose(1, 0, 2, 3).reshape(KERNEL_TAPS, hid, hid)
    w_out = lax.all_gather(w_out, "seq", axis=1, tiled=True).reshape(hid, dim)

    x = to_positions(inputs, nch, q_count)
    cot = to_positions(cotangent, nch, q_count)
    prow = x.shape[0]
    if q_count == 1:
        ids = lax.dynamic_slice_in_dim(segment_ids, me * prow, prow, axis=0)
    else:
        ids = lax.dynamic_slice_in_dim(segment_ids, me // q_count, 1, axis=0)
        ids = lax.dynamic_slice_in_dim(ids, (me % q_count) * part, part, axis=1)
    own_ids = ids + 1
    wide_ids = extended(own_ids, border, pairs)

    residual = x.astype(jnp.float32)
    normed0, unit0, scale0 = normalize(residual, g0, s0)
    hidden0 = gelu_exact(normed0).astype(jnp.bfloat16)
    inner = jnp.einsum("dh,rdl->rhl", w_in, hidden0, preferred_element_type=jnp.float32) + b_in[:, None]
    normed1, unit1, scale1 = normalize(inner, g1, s1)
    hidden1 = gelu_exact(normed1).astype(jnp.bfloat16)
    wide_hidden = extended(hidden1, border, pairs)
    taps = shifted_taps(wide_hidden, wide_ids, own_ids, offsets, border)
    kernel_flat = w_cv.reshape(KERNEL_TAPS * hid, hid)
    mixed = jnp.einsum("co,rcl->rol", kernel_flat, taps, preferred_element_type=jnp.float32) + b_cv[:, None]
    normed2, unit2, scale2 = normalize(mixed, g2, s2)
    hidden2 = gelu_exact(normed2).astype(jnp.bfloat16)
    branch = jnp.einsum("hd,rhl->rdl", w_out, hidden2, preferred_element_type=jnp.float32)
    output = (residual + branch + b_out[:, None]).astype(jnp.bfloat16)

    grad_b_outer = jnp.sum(cot.astype(jnp.float32), axis=(0, 2))
    grad_w_outer = jnp.einsum("rhl,rdl->hd", hidden2, cot, preferred_element_type=jnp.float32)
    def reduce_seq_batch(g, split_dim, after=None):
        if after is not None:
            g, _ = lax.optimization_barrier((g, after))
        g = lax.psum_scatter(g, "seq", scatter_dimension=split_dim, tiled=True)
        return lax.psum_scatter(g, "batch", scatter_dimension=split_dim, tiled=True)

    part_outer = reduce_seq_batch(grad_w_outer.reshape(nch, hloc * dim // 128, 128), 1)
    grad_hidden2 = jnp.einsum("hd,rdl->rhl", w_out, cot, preferred_element_type=jnp.float32)
    grad_normed2 = gelu_back(normed2, grad_hidden2)
    grad_norm2_gain = jnp.sum(grad_normed2 * unit2, axis=(0, 2))
    grad_norm2_shift = jnp.sum(grad_normed2, axis=(0, 2))
    grad_mixed = normalize_back(grad_normed2, unit2, scale2, g2).astype(jnp.bfloat16)
    grad_b_conv = jnp.sum(grad_mixed.astype(jnp.float32), axis=(0, 2))
    grad_w_conv = jnp.einsum(
        "rol,rkcil->okci",
        grad_mixed,
        taps.reshape(prow, KERNEL_TAPS, nch, hloc, part),
        preferred_element_type=jnp.float32,
    )
    wide_grad = extended(grad_mixed, border, pairs)
    back_taps = shifted_taps(wide_grad, wide_ids, own_ids, back_offsets, border)
    kernel_back = jnp.transpose(w_cv, (0, 2, 1)).reshape(KERNEL_TAPS * hid, hid)
    grad_hidden1 = jnp.einsum("oc,rol->rcl", kernel_back, back_taps, preferred_element_type=jnp.float32)
    grad_normed1 = gelu_back(normed1, grad_hidden1)
    grad_norm1_gain = jnp.sum(grad_normed1 * unit1, axis=(0, 2))
    grad_norm1_shift = jnp.sum(grad_normed1, axis=(0, 2))
    grad_inner = normalize_back(grad_normed1, unit1, scale1, g1).astype(jnp.bfloat16)
    grad_inner, _ = lax.optimization_barrier((grad_inner, part_outer))
    grad_b_inner = jnp.sum(grad_inner.astype(jnp.float32), axis=(0, 2))
    grad_w_inner = jnp.einsum("rdl,rhl->dh", hidden0, grad_inner, preferred_element_type=jnp.float32)
    grad_hidden0 = jnp.einsum("dh,rhl->rdl", w_in, grad_inner, preferred_element_type=jnp.float32)
    grad_normed0 = gelu_back(normed0, grad_hidden0)
    grad_norm0_gain = jnp.sum(grad_normed0 * unit0, axis=(0, 2))
    grad_norm0_shift = jnp.sum(grad_normed0, axis=(0, 2))
    input_grad = (cot.astype(jnp.float32) + normalize_back(grad_normed0, unit0, scale0, g0)).astype(jnp.bfloat16)

    output = to_channels(output, nch, q_count, rows)
    input_grad = to_channels(input_grad, nch, q_count, rows)

    vectors = [
        grad_norm0_gain,
        grad_norm0_shift,
        grad_b_inner,
        grad_norm1_gain,
        grad_norm1_shift,
        grad_b_conv,
        grad_norm2_gain,
        grad_norm2_shift,
        grad_b_outer,
    ]
    flat = jnp.concatenate([v.reshape(nch, -1) for v in vectors], axis=1)
    vec_len = flat.shape[1]
    vec_rows = -(-vec_len // hid)
    vec_rows = -(-(dloc + vec_rows) // 64) * 64 - dloc
    flat = jnp.pad(flat, ((0, 0), (0, vec_rows * hid - vec_len))).reshape(nch, vec_rows, hid)
    inner_plus = jnp.concatenate([grad_w_inner.reshape(nch, dloc, hid), flat], axis=1)
    inner_plus = inner_plus.reshape(nch, (dloc + vec_rows) * hid // 128, 128)

    conv_tail = grad_w_conv.shape[1:]
    part_conv = reduce_seq_batch(grad_w_conv.reshape(hid, math.prod(conv_tail) // 128, 128), 0, part_outer)
    part_conv = part_conv.reshape((part_conv.shape[0],) + conv_tail)
    part_inner = reduce_seq_batch(inner_plus, 1, part_conv)
    parts = [part_outer, part_conv, part_inner]
    parts = exchange(parts, ("ch",), 1, axes=(0, 2, 0))
    parts = [jnp.sum(p, axis=a) for p, a in zip(parts, (0, 2, 0))]
    parts = [lax.all_gather(p, "batch", axis=0) for p in parts]
    parts = [lax.all_gather(p, "seq", axis=0, tiled=True).reshape((seqs * batches,) + p.shape[1:]) for p in parts]
    red_w_outer = parts[0].reshape(hloc, dim)
    red_w_conv = parts[1].reshape(hid, KERNEL_TAPS, hloc).transpose(1, 2, 0)
    red_inner = parts[2].reshape(dloc + vec_rows, hid)
    red_w_inner = red_inner[:dloc]
    mine = red_inner[dloc:].reshape(-1)[:vec_len]
    reds = []
    cut = 0
    for v in vectors:
        n = v.shape[0] // nch
        reds.append(mine[cut : cut + n])
        cut += n
    return (
        output,
        input_grad,
        reds[0],
        reds[1],
        red_w_inner,
        reds[2],
        reds[3],
        reds[4],
        red_w_conv,
        reds[5],
        reds[6],
        reds[7],
        red_w_outer,
        reds[8],
    )


def solution(mesh):
    return jax.shard_map(
        local,
        mesh=mesh,
        in_specs=(
            P("batch", "ch", "seq"),
            P("batch", "seq"),
            P("ch"),
            P("ch"),
            P("ch", None),
            P("ch"),
            P("ch"),
            P("ch"),
            P(None, "ch", None),
            P("ch"),
            P("ch"),
            P("ch"),
            P("ch", None),
            P("ch"),
            P("batch", "ch", "seq"),
        ),
        out_specs=(
            P("batch", "ch", "seq"),
            P("batch", "ch", "seq"),
            P("ch"),
            P("ch"),
            P("ch", None),
            P("ch"),
            P("ch"),
            P("ch"),
            P(None, "ch", None),
            P("ch"),
            P("ch"),
            P("ch"),
            P("ch", None),
            P("ch"),
        ),
        check_vma=False,
    )
```

```python
import functools
import math

import jax
import jax.numpy as jnp
from jax import lax
from jax.experimental import pallas as pl
from jax.experimental.pallas import tpu as pltpu
from jax.sharding import PartitionSpec as P

KERNEL_TAPS = 5
DILATION_SPACING = 32


EPSILON = 1e-05


MESH_AXES = ("batch", "seq", "ch")
MESH_ID = pl.DeviceIdType.MESH


def _group_index(group, sizes, coords):
    me = 0
    for a in group:
        me = me * sizes[a] + coords[a]
    return me


def _exchange_kernel(sizes, group, gather, reduce, axes, *refs):
    count_arrays = len(axes)
    x_refs = refs[:count_arrays]
    o_refs = refs[count_arrays : 2 * count_arrays]
    send_sem, recv_sem = refs[2 * count_arrays :]
    coords = {a: lax.axis_index(a) for a in MESH_AXES}
    me = _group_index(group, sizes, coords)
    count = math.prod(sizes[a] for a in group)

    def device(index):
        where = dict(coords)
        rest = index
        for a in reversed(group):
            where[a] = lax.rem(rest, sizes[a])
            rest = rest // sizes[a]
        return tuple(where[a] for a in MESH_AXES)

    barrier = pltpu.get_barrier_semaphore()
    for j in range(1, count):
        pl.semaphore_signal(barrier, 1, device_id=device(lax.rem(me + j, count)), device_id_type=MESH_ID)
    pl.semaphore_wait(barrier, count - 1)
    copies = []
    for j in range(1, count):
        peer = lax.rem(me + j, count)
        for i in range(count_arrays):
            lead = (slice(None),) * axes[i]
            if gather:
                src, dst = x_refs[i], o_refs[i].at[me]
            else:
                slot = (j - 1) if reduce else me
                src = x_refs[i].at[lead + (pl.ds(peer, 1),)]
                dst = o_refs[i].at[lead + (pl.ds(slot, 1),)]
            copy = pltpu.make_async_remote_copy(
                src_ref=src,
                dst_ref=dst,
                send_sem=send_sem.at[i, j - 1],
                recv_sem=recv_sem.at[i, j - 1],
                device_id=device(peer),
                device_id_type=MESH_ID,
            )
            copy.start()
            copies.append(copy)
    for copy in copies:
        copy.wait()


def exchange(xs, group, collective_id, gather=False, axes=None, reduce=False):
    sizes = {a: lax.axis_size(a) for a in MESH_AXES}
    count = math.prod(sizes[a] for a in group)
    axes = tuple(axes or (0,) * len(xs))
    if count == 1:
        return [x[None] if gather else x for x in xs]
    shapes = [jax.ShapeDtypeStruct((count,) + x.shape if gather else x.shape, x.dtype) for x in xs]
    if reduce:
        shapes = [
            jax.ShapeDtypeStruct(x.shape[:a] + (count - 1,) + x.shape[a + 1 :], x.dtype) for x, a in zip(xs, axes)
        ]
    moved = sum(x.size * x.dtype.itemsize * (count if gather else 1) for x in xs)
    outs = pl.pallas_call(
        functools.partial(_exchange_kernel, sizes, group, gather, reduce, axes),
        out_shape=shapes,
        in_specs=[pl.BlockSpec(memory_space=pl.ANY)] * len(xs),
        out_specs=[pl.BlockSpec(memory_space=pl.ANY)] * len(xs),
        scratch_shapes=[
            pltpu.SemaphoreType.DMA((len(xs), count - 1)),
            pltpu.SemaphoreType.DMA((len(xs), count - 1)),
        ],
        compiler_params=pltpu.CompilerParams(collective_id=collective_id, has_side_effects=True),
        cost_estimate=pl.CostEstimate(flops=0, transcendentals=0, bytes_accessed=2 * moved),
    )(*xs)
    me = _group_index(group, sizes, {a: lax.axis_index(a) for a in group})
    placed = []
    if reduce:
        for x, out, axis in zip(xs, outs, axes):
            own = lax.dynamic_index_in_dim(x, me, axis, keepdims=False)
            placed.append(own + jnp.sum(out, axis=axis))
        return placed
    for x, out, axis in zip(xs, outs, axes):
        own = x if gather else lax.dynamic_index_in_dim(x, me, axis, keepdims=False)
        placed.append(lax.dynamic_update_index_in_dim(out, own, me, axis))
    return placed


def gelu_exact(values):
    return jax.nn.gelu(values, approximate=False)


def gelu_back(point, grad):
    return jax.vjp(gelu_exact, point)[1](grad)[0]


def normalize(values, gain, shift):
    center = jnp.mean(values, axis=1, keepdims=True)
    offset = values - center
    spread = jnp.mean(offset * offset, axis=1, keepdims=True)
    scale = lax.rsqrt(spread + EPSILON)
    unit = offset * scale
    return (unit * gain[:, None] + shift[:, None], unit, scale)


def normalize_back(grad, unit, scale, gain):
    scaled = grad * gain[:, None]
    first = jnp.mean(scaled, axis=1, keepdims=True)
    second = jnp.mean(scaled * unit, axis=1, keepdims=True)
    return scale * (scaled - first - unit * second)


def neighbour_pairs(seqs, nch, q_count):
    pairs = []
    for s in range(seqs):
        for c in range(nch):
            q = c % q_count
            if q < q_count - 1:
                pairs.append((s * nch + c, s * nch + c + 1))
            elif s < seqs - 1:
                pairs.append((s * nch + c, (s + 1) * nch + c - (q_count - 1)))
    return pairs


def extended(x, width, pairs):
    down = [(j, i) for i, j in pairs]
    length = x.shape[-1]
    before = lax.ppermute(x[..., length - width :], ("seq", "ch"), pairs)
    after = lax.ppermute(x[..., :width], ("seq", "ch"), down)
    return jnp.concatenate([before, x, after], axis=-1)


def shifted_taps(wide, wide_ids, own_ids, offsets, border):
    length = own_ids.shape[-1]
    pieces = []
    for offset in offsets:
        lower = border + offset
        shifted = wide[:, :, lower : lower + length]
        matching = wide_ids[:, lower : lower + length] == own_ids
        pieces.append(jnp.where(matching[:, None, :], shifted, jnp.zeros_like(shifted)))
    return jnp.concatenate(pieces, axis=1)


def to_positions(x, nch, q_count):
    rows, width, length = x.shape
    if q_count > 1:
        x = x.reshape(rows, width, q_count, length // q_count).transpose(0, 2, 1, 3)
        x = x.reshape(rows * q_count, width, length // q_count)
    x = lax.all_to_all(x, "ch", 0, 0, tiled=True)
    return _join(x, nch)


def _join(x, nch):
    total, width, length = x.shape
    p = total // nch
    return x.reshape(nch, p, width, length).transpose(1, 0, 2, 3).reshape(p, nch * width, length)


def to_channels(x, nch, q_count, rows):
    p, width, length = x.shape
    x = x.reshape(p, nch, width // nch, length).transpose(1, 0, 2, 3).reshape(nch * p, width // nch, length)
    x = lax.all_to_all(x, "ch", 0, 0, tiled=True)
    if q_count > 1:
        _, width, part = x.shape
        x = x.reshape(rows, q_count, width, part).transpose(0, 2, 1, 3).reshape(rows, width, q_count * part)
    return x


def local(
    inputs,
    segment_ids,
    norm0_gain,
    norm0_shift,
    w_inner,
    b_inner,
    norm1_gain,
    norm1_shift,
    w_conv,
    b_conv,
    norm2_gain,
    norm2_shift,
    w_outer,
    b_outer,
    cotangent,
):
    nch = lax.axis_size("ch")
    seqs = lax.axis_size("seq")
    batches = lax.axis_size("batch")
    rows, dloc, length = inputs.shape
    hloc = w_conv.shape[1]
    hid = hloc * nch
    dim = dloc * nch
    if rows % nch == 0:
        q_count = 1
    else:
        q_count = nch // rows
    part = length // q_count
    border = 2 * DILATION_SPACING
    offsets = [(k - KERNEL_TAPS // 2) * DILATION_SPACING for k in range(KERNEL_TAPS)]
    back_offsets = [-o for o in offsets]
    pairs = neighbour_pairs(seqs, nch, q_count)
    me = lax.axis_index("ch")

    smalls = [norm0_gain, norm0_shift, b_inner, norm1_gain, norm1_shift, b_conv, norm2_gain, norm2_shift, b_outer]
    sidx = lax.axis_index("seq")
    halves = [
        lax.dynamic_slice_in_dim(w_inner, sidx * (dloc // seqs), dloc // seqs, 0),
        lax.dynamic_slice_in_dim(w_conv, sidx * (hloc // seqs), hloc // seqs, 1),
        lax.dynamic_slice_in_dim(w_outer, sidx * (hloc // seqs), hloc // seqs, 0),
    ]
    small_all, w_in, w_cv, w_out = exchange([jnp.concatenate(smalls)] + halves, ("ch",), 0, gather=True)
    cut = 0
    full = []
    for v in smalls:
        n = v.shape[0]
        full.append(small_all[:, cut : cut + n].reshape(n * nch))
        cut += n
    g0, s0, b_in, g1, s1, b_cv, g2, s2, b_out = full
    w_in = lax.all_gather(w_in, "seq", axis=1, tiled=True).reshape(dim, hid)
    w_cv = lax.all_gather(w_cv, "seq", axis=2, tiled=True).transpose(1, 0, 2, 3).reshape(KERNEL_TAPS, hid, hid)
    w_out = lax.all_gather(w_out, "seq", axis=1, tiled=True).reshape(hid, dim)

    x = to_positions(inputs, nch, q_count)
    cot = to_positions(cotangent, nch, q_count)
    prow = x.shape[0]
    if q_count == 1:
        ids = lax.dynamic_slice_in_dim(segment_ids, me * prow, prow, axis=0)
    else:
        ids = lax.dynamic_slice_in_dim(segment_ids, me // q_count, 1, axis=0)
        ids = lax.dynamic_slice_in_dim(ids, (me % q_count) * part, part, axis=1)
    own_ids = ids + 1
    wide_ids = extended(own_ids, border, pairs)

    residual = x.astype(jnp.float32)
    normed0, unit0, scale0 = normalize(residual, g0, s0)
    hidden0 = gelu_exact(normed0).astype(jnp.bfloat16)
    inner = jnp.einsum("dh,rdl->rhl", w_in, hidden0, preferred_element_type=jnp.float32) + b_in[:, None]
    normed1, unit1, scale1 = normalize(inner, g1, s1)
    hidden1 = gelu_exact(normed1).astype(jnp.bfloat16)
    wide_hidden = extended(hidden1, border, pairs)
    taps = shifted_taps(wide_hidden, wide_ids, own_ids, offsets, border)
    kernel_flat = w_cv.reshape(KERNEL_TAPS * hid, hid)
    mixed = jnp.einsum("co,rcl->rol", kernel_flat, taps, preferred_element_type=jnp.float32) + b_cv[:, None]
    normed2, unit2, scale2 = normalize(mixed, g2, s2)
    hidden2 = gelu_exact(normed2).astype(jnp.bfloat16)
    branch = jnp.einsum("hd,rhl->rdl", w_out, hidden2, preferred_element_type=jnp.float32)
    output = (residual + branch + b_out[:, None]).astype(jnp.bfloat16)

    grad_b_outer = jnp.sum(cot.astype(jnp.float32), axis=(0, 2))
    grad_w_outer = jnp.einsum("rhl,rdl->hd", hidden2, cot, preferred_element_type=jnp.float32)
    def reduce_seq_batch(g, split_dim, after=None):
        if after is not None:
            g, _ = lax.optimization_barrier((g, after))
        g = lax.psum_scatter(g, "seq", scatter_dimension=split_dim, tiled=True)
        return lax.psum_scatter(g, "batch", scatter_dimension=split_dim, tiled=True)

    part_outer = reduce_seq_batch(grad_w_outer.reshape(nch, hloc * dim // 128, 128), 1)
    grad_hidden2 = jnp.einsum("hd,rdl->rhl", w_out, cot, preferred_element_type=jnp.float32)
    grad_normed2 = gelu_back(normed2, grad_hidden2)
    grad_norm2_gain = jnp.sum(grad_normed2 * unit2, axis=(0, 2))
    grad_norm2_shift = jnp.sum(grad_normed2, axis=(0, 2))
    grad_mixed = normalize_back(grad_normed2, unit2, scale2, g2).astype(jnp.bfloat16)
    grad_b_conv = jnp.sum(grad_mixed.astype(jnp.float32), axis=(0, 2))
    grad_w_conv = jnp.einsum(
        "rol,rkcil->okci",
        grad_mixed,
        taps.reshape(prow, KERNEL_TAPS, nch, hloc, part),
        preferred_element_type=jnp.float32,
    )
    wide_grad = extended(grad_mixed, border, pairs)
    back_taps = shifted_taps(wide_grad, wide_ids, own_ids, back_offsets, border)
    kernel_back = jnp.transpose(w_cv, (0, 2, 1)).reshape(KERNEL_TAPS * hid, hid)
    grad_hidden1 = jnp.einsum("oc,rol->rcl", kernel_back, back_taps, preferred_element_type=jnp.float32)
    grad_normed1 = gelu_back(normed1, grad_hidden1)
    grad_norm1_gain = jnp.sum(grad_normed1 * unit1, axis=(0, 2))
    grad_norm1_shift = jnp.sum(grad_normed1, axis=(0, 2))
    grad_inner = normalize_back(grad_normed1, unit1, scale1, g1).astype(jnp.bfloat16)
    grad_inner, _ = lax.optimization_barrier((grad_inner, part_outer))
    grad_b_inner = jnp.sum(grad_inner.astype(jnp.float32), axis=(0, 2))
    grad_w_inner = jnp.einsum("rdl,rhl->dh", hidden0, grad_inner, preferred_element_type=jnp.float32)
    grad_hidden0 = jnp.einsum("dh,rhl->rdl", w_in, grad_inner, preferred_element_type=jnp.float32)
    grad_normed0 = gelu_back(normed0, grad_hidden0)
    grad_norm0_gain = jnp.sum(grad_normed0 * unit0, axis=(0, 2))
    grad_norm0_shift = jnp.sum(grad_normed0, axis=(0, 2))
    input_grad = (cot.astype(jnp.float32) + normalize_back(grad_normed0, unit0, scale0, g0)).astype(jnp.bfloat16)

    output = to_channels(output, nch, q_count, rows)
    input_grad = to_channels(input_grad, nch, q_count, rows)

    vectors = [
        grad_norm0_gain,
        grad_norm0_shift,
        grad_b_inner,
        grad_norm1_gain,
        grad_norm1_shift,
        grad_b_conv,
        grad_norm2_gain,
        grad_norm2_shift,
        grad_b_outer,
    ]
    flat = jnp.concatenate([v.reshape(nch, -1) for v in vectors], axis=1)
    vec_len = flat.shape[1]
    vec_rows = -(-vec_len // hid)
    vec_rows = -(-(dloc + vec_rows) // 64) * 64 - dloc
    flat = jnp.pad(flat, ((0, 0), (0, vec_rows * hid - vec_len))).reshape(nch, vec_rows, hid)
    inner_plus = jnp.concatenate([grad_w_inner.reshape(nch, dloc, hid), flat], axis=1)
    inner_plus = inner_plus.reshape(nch, (dloc + vec_rows) * hid // 128, 128)

    conv_tail = grad_w_conv.shape[1:]
    part_conv = reduce_seq_batch(grad_w_conv.reshape(hid, math.prod(conv_tail) // 128, 128), 0, part_outer)
    part_conv = part_conv.reshape((part_conv.shape[0],) + conv_tail)
    part_inner = reduce_seq_batch(inner_plus, 1, part_conv)
    parts = [part_outer, part_conv, part_inner]
    parts = exchange(parts, ("ch",), 1, axes=(0, 2, 0), reduce=True)
    piece_shapes = [p.shape for p in parts]
    parts = [p.reshape(p.size // 128, 128) if p.size % 128 == 0 else p for p in parts]
    parts = [lax.all_gather(p, "batch", axis=0) for p in parts]
    parts = [
        lax.all_gather(p, "seq", axis=0, tiled=True).reshape((seqs * batches,) + shape)
        for p, shape in zip(parts, piece_shapes)
    ]
    red_w_outer = parts[0].reshape(hloc, dim)
    red_w_conv = parts[1].reshape(hid, KERNEL_TAPS, hloc).transpose(1, 2, 0)
    red_inner = parts[2].reshape(dloc + vec_rows, hid)
    red_w_inner = red_inner[:dloc]
    mine = red_inner[dloc:].reshape(-1)[:vec_len]
    reds = []
    cut = 0
    for v in vectors:
        n = v.shape[0] // nch
        reds.append(mine[cut : cut + n])
        cut += n
    return (
        output,
        input_grad,
        reds[0],
        reds[1],
        red_w_inner,
        reds[2],
        reds[3],
        reds[4],
        red_w_conv,
        reds[5],
        reds[6],
        reds[7],
        red_w_outer,
        reds[8],
    )


def solution(mesh):
    return jax.shard_map(
        local,
        mesh=mesh,
        in_specs=(
            P("batch", "ch", "seq"),
            P("batch", "seq"),
            P("ch"),
            P("ch"),
            P("ch", None),
            P("ch"),
            P("ch"),
            P("ch"),
            P(None, "ch", None),
            P("ch"),
            P("ch"),
            P("ch"),
            P("ch", None),
            P("ch"),
            P("batch", "ch", "seq"),
        ),
        out_specs=(
            P("batch", "ch", "seq"),
            P("batch", "ch", "seq"),
            P("ch"),
            P("ch"),
            P("ch", None),
            P("ch"),
            P("ch"),
            P("ch"),
            P(None, "ch", None),
            P("ch"),
            P("ch"),
            P("ch"),
            P("ch", None),
            P("ch"),
        ),
        check_vma=False,
    )
```

```python
import functools
import math

import jax
import jax.numpy as jnp
from jax import lax
from jax.experimental import pallas as pl
from jax.experimental.pallas import tpu as pltpu
from jax.sharding import PartitionSpec as P

KERNEL_TAPS = 5
DILATION_SPACING = 32


EPSILON = 1e-05


MESH_AXES = ("batch", "seq", "ch")
MESH_ID = pl.DeviceIdType.MESH


def _group_index(group, sizes, coords):
    me = 0
    for a in group:
        me = me * sizes[a] + coords[a]
    return me


def _exchange_kernel(sizes, group, gather, reduce, axes, *refs):
    count_arrays = len(axes)
    x_refs = refs[:count_arrays]
    o_refs = refs[count_arrays : 2 * count_arrays]
    send_sem, recv_sem = refs[2 * count_arrays :]
    coords = {a: lax.axis_index(a) for a in MESH_AXES}
    me = _group_index(group, sizes, coords)
    count = math.prod(sizes[a] for a in group)

    def device(index):
        where = dict(coords)
        rest = index
        for a in reversed(group):
            where[a] = lax.rem(rest, sizes[a])
            rest = rest // sizes[a]
        return tuple(where[a] for a in MESH_AXES)

    barrier = pltpu.get_barrier_semaphore()
    for j in range(1, count):
        pl.semaphore_signal(barrier, 1, device_id=device(lax.rem(me + j, count)), device_id_type=MESH_ID)
    pl.semaphore_wait(barrier, count - 1)
    copies = []
    for j in range(1, count):
        peer = lax.rem(me + j, count)
        for i in range(count_arrays):
            lead = (slice(None),) * axes[i]
            if gather:
                src, dst = x_refs[i], o_refs[i].at[me]
            else:
                slot = (j - 1) if reduce else me
                src = x_refs[i].at[lead + (pl.ds(peer, 1),)]
                dst = o_refs[i].at[lead + (pl.ds(slot, 1),)]
            copy = pltpu.make_async_remote_copy(
                src_ref=src,
                dst_ref=dst,
                send_sem=send_sem.at[i, j - 1],
                recv_sem=recv_sem.at[i, j - 1],
                device_id=device(peer),
                device_id_type=MESH_ID,
            )
            copy.start()
            copies.append(copy)
    for copy in copies:
        copy.wait()


def exchange(xs, group, collective_id, gather=False, axes=None, reduce=False):
    sizes = {a: lax.axis_size(a) for a in MESH_AXES}
    count = math.prod(sizes[a] for a in group)
    axes = tuple(axes or (0,) * len(xs))
    if count == 1:
        return [x[None] if gather else x for x in xs]
    shapes = [jax.ShapeDtypeStruct((count,) + x.shape if gather else x.shape, x.dtype) for x in xs]
    if reduce:
        shapes = [
            jax.ShapeDtypeStruct(x.shape[:a] + (count - 1,) + x.shape[a + 1 :], x.dtype) for x, a in zip(xs, axes)
        ]
    moved = sum(x.size * x.dtype.itemsize * (count if gather else 1) for x in xs)
    outs = pl.pallas_call(
        functools.partial(_exchange_kernel, sizes, group, gather, reduce, axes),
        out_shape=shapes,
        in_specs=[pl.BlockSpec(memory_space=pl.ANY)] * len(xs),
        out_specs=[pl.BlockSpec(memory_space=pl.ANY)] * len(xs),
        scratch_shapes=[
            pltpu.SemaphoreType.DMA((len(xs), count - 1)),
            pltpu.SemaphoreType.DMA((len(xs), count - 1)),
        ],
        compiler_params=pltpu.CompilerParams(collective_id=collective_id, has_side_effects=True),
        cost_estimate=pl.CostEstimate(flops=0, transcendentals=0, bytes_accessed=2 * moved),
    )(*xs)
    me = _group_index(group, sizes, {a: lax.axis_index(a) for a in group})
    placed = []
    if reduce:
        for x, out, axis in zip(xs, outs, axes):
            own = lax.dynamic_index_in_dim(x, me, axis, keepdims=False)
            placed.append(own + jnp.sum(out, axis=axis))
        return placed
    for x, out, axis in zip(xs, outs, axes):
        own = x if gather else lax.dynamic_index_in_dim(x, me, axis, keepdims=False)
        placed.append(lax.dynamic_update_index_in_dim(out, own, me, axis))
    return placed


def gelu_exact(values):
    return jax.nn.gelu(values, approximate=False)


def gelu_back(point, grad):
    return jax.vjp(gelu_exact, point)[1](grad)[0]


def normalize(values, gain, shift):
    center = jnp.mean(values, axis=1, keepdims=True)
    offset = values - center
    spread = jnp.mean(offset * offset, axis=1, keepdims=True)
    scale = lax.rsqrt(spread + EPSILON)
    unit = offset * scale
    return (unit * gain[:, None] + shift[:, None], unit, scale)


def normalize_back(grad, unit, scale, gain):
    scaled = grad * gain[:, None]
    first = jnp.mean(scaled, axis=1, keepdims=True)
    second = jnp.mean(scaled * unit, axis=1, keepdims=True)
    return scale * (scaled - first - unit * second)


def neighbour_pairs(seqs, nch, q_count):
    pairs = []
    for s in range(seqs):
        for c in range(nch):
            q = c % q_count
            if q < q_count - 1:
                pairs.append((s * nch + c, s * nch + c + 1))
            elif s < seqs - 1:
                pairs.append((s * nch + c, (s + 1) * nch + c - (q_count - 1)))
    return pairs


def extended(x, width, pairs):
    down = [(j, i) for i, j in pairs]
    length = x.shape[-1]
    before = lax.ppermute(x[..., length - width :], ("seq", "ch"), pairs)
    after = lax.ppermute(x[..., :width], ("seq", "ch"), down)
    return jnp.concatenate([before, x, after], axis=-1)


def shifted_taps(wide, wide_ids, own_ids, offsets, border):
    length = own_ids.shape[-1]
    pieces = []
    for offset in offsets:
        lower = border + offset
        shifted = wide[:, :, lower : lower + length]
        matching = wide_ids[:, lower : lower + length] == own_ids
        pieces.append(jnp.where(matching[:, None, :], shifted, jnp.zeros_like(shifted)))
    return jnp.concatenate(pieces, axis=1)


def to_positions(x, nch, q_count):
    rows, width, length = x.shape
    if q_count > 1:
        x = x.reshape(rows, width, q_count, length // q_count).transpose(0, 2, 1, 3)
        x = x.reshape(rows * q_count, width, length // q_count)
    x = lax.all_to_all(x, "ch", 0, 0, tiled=True)
    return _join(x, nch)


def _join(x, nch):
    total, width, length = x.shape
    p = total // nch
    return x.reshape(nch, p, width, length).transpose(1, 0, 2, 3).reshape(p, nch * width, length)


def to_channels(x, nch, q_count, rows):
    p, width, length = x.shape
    x = x.reshape(p, nch, width // nch, length).transpose(1, 0, 2, 3).reshape(nch * p, width // nch, length)
    x = lax.all_to_all(x, "ch", 0, 0, tiled=True)
    if q_count > 1:
        _, width, part = x.shape
        x = x.reshape(rows, q_count, width, part).transpose(0, 2, 1, 3).reshape(rows, width, q_count * part)
    return x


def local(
    inputs,
    segment_ids,
    norm0_gain,
    norm0_shift,
    w_inner,
    b_inner,
    norm1_gain,
    norm1_shift,
    w_conv,
    b_conv,
    norm2_gain,
    norm2_shift,
    w_outer,
    b_outer,
    cotangent,
):
    nch = lax.axis_size("ch")
    seqs = lax.axis_size("seq")
    batches = lax.axis_size("batch")
    rows, dloc, length = inputs.shape
    hloc = w_conv.shape[1]
    hid = hloc * nch
    dim = dloc * nch
    if rows % nch == 0:
        q_count = 1
    else:
        q_count = nch // rows
    part = length // q_count
    border = 2 * DILATION_SPACING
    offsets = [(k - KERNEL_TAPS // 2) * DILATION_SPACING for k in range(KERNEL_TAPS)]
    back_offsets = [-o for o in offsets]
    pairs = neighbour_pairs(seqs, nch, q_count)
    me = lax.axis_index("ch")

    smalls = [norm0_gain, norm0_shift, b_inner, norm1_gain, norm1_shift, b_conv, norm2_gain, norm2_shift, b_outer]
    sidx = lax.axis_index("seq")
    halves = [
        lax.dynamic_slice_in_dim(w_inner, sidx * (dloc // seqs), dloc // seqs, 0),
        lax.dynamic_slice_in_dim(w_conv, sidx * (hloc // seqs), hloc // seqs, 1),
        lax.dynamic_slice_in_dim(w_outer, sidx * (hloc // seqs), hloc // seqs, 0),
    ]
    small_all, w_in, w_out = exchange([jnp.concatenate(smalls), halves[0], halves[2]], ("ch",), 0, gather=True)
    w_cv = lax.all_gather(halves[1], "ch", axis=0)
    cut = 0
    full = []
    for v in smalls:
        n = v.shape[0]
        full.append(small_all[:, cut : cut + n].reshape(n * nch))
        cut += n
    g0, s0, b_in, g1, s1, b_cv, g2, s2, b_out = full
    w_in = lax.all_gather(w_in, "seq", axis=1, tiled=True).reshape(dim, hid)
    w_cv = lax.all_gather(w_cv, "seq", axis=2, tiled=True).transpose(1, 0, 2, 3).reshape(KERNEL_TAPS, hid, hid)
    w_out = lax.all_gather(w_out, "seq", axis=1, tiled=True).reshape(hid, dim)

    x = to_positions(inputs, nch, q_count)
    cot = to_positions(cotangent, nch, q_count)
    prow = x.shape[0]
    if q_count == 1:
        ids = lax.dynamic_slice_in_dim(segment_ids, me * prow, prow, axis=0)
    else:
        ids = lax.dynamic_slice_in_dim(segment_ids, me // q_count, 1, axis=0)
        ids = lax.dynamic_slice_in_dim(ids, (me % q_count) * part, part, axis=1)
    own_ids = ids + 1
    wide_ids = extended(own_ids, border, pairs)

    residual = x.astype(jnp.float32)
    normed0, unit0, scale0 = normalize(residual, g0, s0)
    hidden0 = gelu_exact(normed0).astype(jnp.bfloat16)
    inner = jnp.einsum("dh,rdl->rhl", w_in, hidden0, preferred_element_type=jnp.float32) + b_in[:, None]
    normed1, unit1, scale1 = normalize(inner, g1, s1)
    hidden1 = gelu_exact(normed1).astype(jnp.bfloat16)
    wide_hidden = extended(hidden1, border, pairs)
    taps = shifted_taps(wide_hidden, wide_ids, own_ids, offsets, border)
    kernel_flat = w_cv.reshape(KERNEL_TAPS * hid, hid)
    mixed = jnp.einsum("co,rcl->rol", kernel_flat, taps, preferred_element_type=jnp.float32) + b_cv[:, None]
    normed2, unit2, scale2 = normalize(mixed, g2, s2)
    hidden2 = gelu_exact(normed2).astype(jnp.bfloat16)
    branch = jnp.einsum("hd,rhl->rdl", w_out, hidden2, preferred_element_type=jnp.float32)
    output = (residual + branch + b_out[:, None]).astype(jnp.bfloat16)

    grad_b_outer = jnp.sum(cot.astype(jnp.float32), axis=(0, 2))
    grad_w_outer = jnp.einsum("rhl,rdl->hd", hidden2, cot, preferred_element_type=jnp.float32)
    def reduce_seq_batch(g, split_dim, after=None):
        if after is not None:
            g, _ = lax.optimization_barrier((g, after))
        g = lax.psum_scatter(g, "seq", scatter_dimension=split_dim, tiled=True)
        return lax.psum_scatter(g, "batch", scatter_dimension=split_dim, tiled=True)

    part_outer = reduce_seq_batch(grad_w_outer.reshape(nch, hloc * dim // 128, 128), 1)
    grad_hidden2 = jnp.einsum("hd,rdl->rhl", w_out, cot, preferred_element_type=jnp.float32)
    grad_normed2 = gelu_back(normed2, grad_hidden2)
    grad_norm2_gain = jnp.sum(grad_normed2 * unit2, axis=(0, 2))
    grad_norm2_shift = jnp.sum(grad_normed2, axis=(0, 2))
    grad_mixed = normalize_back(grad_normed2, unit2, scale2, g2).astype(jnp.bfloat16)
    grad_b_conv = jnp.sum(grad_mixed.astype(jnp.float32), axis=(0, 2))
    grad_w_conv = jnp.einsum(
        "rol,rkcil->okci",
        grad_mixed,
        taps.reshape(prow, KERNEL_TAPS, nch, hloc, part),
        preferred_element_type=jnp.float32,
    )
    wide_grad = extended(grad_mixed, border, pairs)
    back_taps = shifted_taps(wide_grad, wide_ids, own_ids, back_offsets, border)
    kernel_back = jnp.transpose(w_cv, (0, 2, 1)).reshape(KERNEL_TAPS * hid, hid)
    grad_hidden1 = jnp.einsum("oc,rol->rcl", kernel_back, back_taps, preferred_element_type=jnp.float32)
    grad_normed1 = gelu_back(normed1, grad_hidden1)
    grad_norm1_gain = jnp.sum(grad_normed1 * unit1, axis=(0, 2))
    grad_norm1_shift = jnp.sum(grad_normed1, axis=(0, 2))
    grad_inner = normalize_back(grad_normed1, unit1, scale1, g1).astype(jnp.bfloat16)
    grad_inner, _ = lax.optimization_barrier((grad_inner, part_outer))
    grad_b_inner = jnp.sum(grad_inner.astype(jnp.float32), axis=(0, 2))
    grad_w_inner = jnp.einsum("rdl,rhl->dh", hidden0, grad_inner, preferred_element_type=jnp.float32)
    grad_hidden0 = jnp.einsum("dh,rhl->rdl", w_in, grad_inner, preferred_element_type=jnp.float32)
    grad_normed0 = gelu_back(normed0, grad_hidden0)
    grad_norm0_gain = jnp.sum(grad_normed0 * unit0, axis=(0, 2))
    grad_norm0_shift = jnp.sum(grad_normed0, axis=(0, 2))
    input_grad = (cot.astype(jnp.float32) + normalize_back(grad_normed0, unit0, scale0, g0)).astype(jnp.bfloat16)

    output = to_channels(output, nch, q_count, rows)
    input_grad = to_channels(input_grad, nch, q_count, rows)

    vectors = [
        grad_norm0_gain,
        grad_norm0_shift,
        grad_b_inner,
        grad_norm1_gain,
        grad_norm1_shift,
        grad_b_conv,
        grad_norm2_gain,
        grad_norm2_shift,
        grad_b_outer,
    ]
    flat = jnp.concatenate([v.reshape(nch, -1) for v in vectors], axis=1)
    vec_len = flat.shape[1]
    vec_rows = -(-vec_len // hid)
    vec_rows = -(-(dloc + vec_rows) // 64) * 64 - dloc
    flat = jnp.pad(flat, ((0, 0), (0, vec_rows * hid - vec_len))).reshape(nch, vec_rows, hid)
    inner_plus = jnp.concatenate([grad_w_inner.reshape(nch, dloc, hid), flat], axis=1)
    inner_plus = inner_plus.reshape(nch, (dloc + vec_rows) * hid // 128, 128)

    conv_tail = grad_w_conv.shape[1:]
    part_conv = reduce_seq_batch(grad_w_conv.reshape(hid, math.prod(conv_tail) // 128, 128), 0, part_outer)
    part_conv = part_conv.reshape((part_conv.shape[0],) + conv_tail)
    part_inner = reduce_seq_batch(inner_plus, 1, part_conv)
    parts = [part_outer, part_conv, part_inner]
    parts = exchange(parts, ("ch",), 1, axes=(0, 2, 0), reduce=True)
    piece_shapes = [p.shape for p in parts]
    parts = [p.reshape(p.size // 128, 128) if p.size % 128 == 0 else p for p in parts]
    parts = [lax.all_gather(p, "batch", axis=0) for p in parts]
    parts = [
        lax.all_gather(p, "seq", axis=0, tiled=True).reshape((seqs * batches,) + shape)
        for p, shape in zip(parts, piece_shapes)
    ]
    red_w_outer = parts[0].reshape(hloc, dim)
    red_w_conv = parts[1].reshape(hid, KERNEL_TAPS, hloc).transpose(1, 2, 0)
    red_inner = parts[2].reshape(dloc + vec_rows, hid)
    red_w_inner = red_inner[:dloc]
    mine = red_inner[dloc:].reshape(-1)[:vec_len]
    reds = []
    cut = 0
    for v in vectors:
        n = v.shape[0] // nch
        reds.append(mine[cut : cut + n])
        cut += n
    return (
        output,
        input_grad,
        reds[0],
        reds[1],
        red_w_inner,
        reds[2],
        reds[3],
        reds[4],
        red_w_conv,
        reds[5],
        reds[6],
        reds[7],
        red_w_outer,
        reds[8],
    )


def solution(mesh):
    return jax.shard_map(
        local,
        mesh=mesh,
        in_specs=(
            P("batch", "ch", "seq"),
            P("batch", "seq"),
            P("ch"),
            P("ch"),
            P("ch", None),
            P("ch"),
            P("ch"),
            P("ch"),
            P(None, "ch", None),
            P("ch"),
            P("ch"),
            P("ch"),
            P("ch", None),
            P("ch"),
            P("batch", "ch", "seq"),
        ),
        out_specs=(
            P("batch", "ch", "seq"),
            P("batch", "ch", "seq"),
            P("ch"),
            P("ch"),
            P("ch", None),
            P("ch"),
            P("ch"),
            P("ch"),
            P(None, "ch", None),
            P("ch"),
            P("ch"),
            P("ch"),
            P("ch", None),
            P("ch"),
        ),
        check_vma=False,
    )
```

```python
import functools
import math

import jax
import jax.numpy as jnp
from jax import lax
from jax.experimental import pallas as pl
from jax.experimental.pallas import tpu as pltpu
from jax.sharding import PartitionSpec as P

KERNEL_TAPS = 5
DILATION_SPACING = 32


EPSILON = 1e-05


MESH_AXES = ("batch", "seq", "ch")
MESH_ID = pl.DeviceIdType.MESH


def _group_index(group, sizes, coords):
    me = 0
    for a in group:
        me = me * sizes[a] + coords[a]
    return me


def _exchange_kernel(sizes, group, gather, reduce, axes, *refs):
    count_arrays = len(axes)
    x_refs = refs[:count_arrays]
    o_refs = refs[count_arrays : 2 * count_arrays]
    send_sem, recv_sem = refs[2 * count_arrays :]
    coords = {a: lax.axis_index(a) for a in MESH_AXES}
    me = _group_index(group, sizes, coords)
    count = math.prod(sizes[a] for a in group)

    def device(index):
        where = dict(coords)
        rest = index
        for a in reversed(group):
            where[a] = lax.rem(rest, sizes[a])
            rest = rest // sizes[a]
        return tuple(where[a] for a in MESH_AXES)

    barrier = pltpu.get_barrier_semaphore()
    for j in range(1, count):
        pl.semaphore_signal(barrier, 1, device_id=device(lax.rem(me + j, count)), device_id_type=MESH_ID)
    pl.semaphore_wait(barrier, count - 1)
    copies = []
    for j in range(1, count):
        peer = lax.rem(me + j, count)
        for i in range(count_arrays):
            lead = (slice(None),) * axes[i]
            if gather[i]:
                src, dst = x_refs[i], o_refs[i].at[me]
            else:
                slot = (j - 1) if reduce else me
                src = x_refs[i].at[lead + (pl.ds(peer, 1),)]
                dst = o_refs[i].at[lead + (pl.ds(slot, 1),)]
            copy = pltpu.make_async_remote_copy(
                src_ref=src,
                dst_ref=dst,
                send_sem=send_sem.at[i, j - 1],
                recv_sem=recv_sem.at[i, j - 1],
                device_id=device(peer),
                device_id_type=MESH_ID,
            )
            copy.start()
            copies.append(copy)
    for copy in copies:
        copy.wait()


def exchange(xs, group, collective_id, gather=False, axes=None, reduce=False):
    sizes = {a: lax.axis_size(a) for a in MESH_AXES}
    count = math.prod(sizes[a] for a in group)
    axes = tuple(axes or (0,) * len(xs))
    if isinstance(gather, bool):
        gather = (gather,) * len(xs)
    gather = tuple(gather)
    if count == 1:
        return [x[None] if g else x for x, g in zip(xs, gather)]
    shapes = [jax.ShapeDtypeStruct((count,) + x.shape if g else x.shape, x.dtype) for x, g in zip(xs, gather)]
    if reduce:
        shapes = [
            jax.ShapeDtypeStruct(x.shape[:a] + (count - 1,) + x.shape[a + 1 :], x.dtype) for x, a in zip(xs, axes)
        ]
    moved = sum(x.size * x.dtype.itemsize * (count if g else 1) for x, g in zip(xs, gather))
    outs = pl.pallas_call(
        functools.partial(_exchange_kernel, sizes, group, gather, reduce, axes),
        out_shape=shapes,
        in_specs=[pl.BlockSpec(memory_space=pl.ANY)] * len(xs),
        out_specs=[pl.BlockSpec(memory_space=pl.ANY)] * len(xs),
        scratch_shapes=[
            pltpu.SemaphoreType.DMA((len(xs), count - 1)),
            pltpu.SemaphoreType.DMA((len(xs), count - 1)),
        ],
        compiler_params=pltpu.CompilerParams(collective_id=collective_id, has_side_effects=True),
        cost_estimate=pl.CostEstimate(flops=0, transcendentals=0, bytes_accessed=2 * moved),
    )(*xs)
    me = _group_index(group, sizes, {a: lax.axis_index(a) for a in group})
    placed = []
    if reduce:
        for x, out, axis in zip(xs, outs, axes):
            own = lax.dynamic_index_in_dim(x, me, axis, keepdims=False)
            placed.append(own + jnp.sum(out, axis=axis))
        return placed
    for x, out, axis, g in zip(xs, outs, axes, gather):
        own = x if g else lax.dynamic_index_in_dim(x, me, axis, keepdims=False)
        placed.append(lax.dynamic_update_index_in_dim(out, own, me, axis))
    return placed


def gelu_exact(values):
    return jax.nn.gelu(values, approximate=False)


def gelu_back(point, grad):
    return jax.vjp(gelu_exact, point)[1](grad)[0]


def normalize(values, gain, shift):
    center = jnp.mean(values, axis=1, keepdims=True)
    offset = values - center
    spread = jnp.mean(offset * offset, axis=1, keepdims=True)
    scale = lax.rsqrt(spread + EPSILON)
    unit = offset * scale
    return (unit * gain[:, None] + shift[:, None], unit, scale)


def normalize_back(grad, unit, scale, gain):
    scaled = grad * gain[:, None]
    first = jnp.mean(scaled, axis=1, keepdims=True)
    second = jnp.mean(scaled * unit, axis=1, keepdims=True)
    return scale * (scaled - first - unit * second)


def neighbour_pairs(seqs, nch, q_count):
    pairs = []
    for s in range(seqs):
        for c in range(nch):
            q = c % q_count
            if q < q_count - 1:
                pairs.append((s * nch + c, s * nch + c + 1))
            elif s < seqs - 1:
                pairs.append((s * nch + c, (s + 1) * nch + c - (q_count - 1)))
    return pairs


def extended(x, width, pairs):
    down = [(j, i) for i, j in pairs]
    length = x.shape[-1]
    before = lax.ppermute(x[..., length - width :], ("seq", "ch"), pairs)
    after = lax.ppermute(x[..., :width], ("seq", "ch"), down)
    return jnp.concatenate([before, x, after], axis=-1)


def shifted_taps(wide, wide_ids, own_ids, offsets, border):
    length = own_ids.shape[-1]
    pieces = []
    for offset in offsets:
        lower = border + offset
        shifted = wide[:, :, lower : lower + length]
        matching = wide_ids[:, lower : lower + length] == own_ids
        pieces.append(jnp.where(matching[:, None, :], shifted, jnp.zeros_like(shifted)))
    return jnp.concatenate(pieces, axis=1)


def to_positions(x, nch, q_count):
    rows, width, length = x.shape
    if q_count > 1:
        x = x.reshape(rows, width, q_count, length // q_count).transpose(0, 2, 1, 3)
        x = x.reshape(rows * q_count, width, length // q_count)
    x = lax.all_to_all(x, "ch", 0, 0, tiled=True)
    return _join(x, nch)


def _join(x, nch):
    total, width, length = x.shape
    p = total // nch
    return x.reshape(nch, p, width, length).transpose(1, 0, 2, 3).reshape(p, nch * width, length)


def to_channels(x, nch, q_count, rows):
    p, width, length = x.shape
    x = x.reshape(p, nch, width // nch, length).transpose(1, 0, 2, 3).reshape(nch * p, width // nch, length)
    x = lax.all_to_all(x, "ch", 0, 0, tiled=True)
    if q_count > 1:
        _, width, part = x.shape
        x = x.reshape(rows, q_count, width, part).transpose(0, 2, 1, 3).reshape(rows, width, q_count * part)
    return x


def local(
    inputs,
    segment_ids,
    norm0_gain,
    norm0_shift,
    w_inner,
    b_inner,
    norm1_gain,
    norm1_shift,
    w_conv,
    b_conv,
    norm2_gain,
    norm2_shift,
    w_outer,
    b_outer,
    cotangent,
):
    nch = lax.axis_size("ch")
    seqs = lax.axis_size("seq")
    batches = lax.axis_size("batch")
    rows, dloc, length = inputs.shape
    hloc = w_conv.shape[1]
    hid = hloc * nch
    dim = dloc * nch
    if rows % nch == 0:
        q_count = 1
    else:
        q_count = nch // rows
    part = length // q_count
    border = 2 * DILATION_SPACING
    offsets = [(k - KERNEL_TAPS // 2) * DILATION_SPACING for k in range(KERNEL_TAPS)]
    back_offsets = [-o for o in offsets]
    pairs = neighbour_pairs(seqs, nch, q_count)
    me = lax.axis_index("ch")

    smalls = [norm0_gain, norm0_shift, b_inner, norm1_gain, norm1_shift, b_conv, norm2_gain, norm2_shift, b_outer]
    sidx = lax.axis_index("seq")
    halves = [
        lax.dynamic_slice_in_dim(w_inner, sidx * (dloc // seqs), dloc // seqs, 0),
        lax.dynamic_slice_in_dim(w_conv, sidx * (hloc // seqs), hloc // seqs, 1),
        lax.dynamic_slice_in_dim(w_outer, sidx * (hloc // seqs), hloc // seqs, 0),
    ]
    if q_count == 1:
        small_all, w_in, w_out, x = exchange(
            [jnp.concatenate(smalls), halves[0], halves[2], inputs], ("ch",), 0, gather=(True, True, True, False)
        )
        x = _join(x, nch)
    else:
        small_all, w_in, w_out = exchange([jnp.concatenate(smalls), halves[0], halves[2]], ("ch",), 0, gather=True)
        x = to_positions(inputs, nch, q_count)
    w_cv = lax.all_gather(halves[1], "ch", axis=0)
    cut = 0
    full = []
    for v in smalls:
        n = v.shape[0]
        full.append(small_all[:, cut : cut + n].reshape(n * nch))
        cut += n
    g0, s0, b_in, g1, s1, b_cv, g2, s2, b_out = full
    w_in = lax.all_gather(w_in, "seq", axis=1, tiled=True).reshape(dim, hid)
    w_cv = lax.all_gather(w_cv, "seq", axis=2, tiled=True).transpose(1, 0, 2, 3).reshape(KERNEL_TAPS, hid, hid)
    w_out = lax.all_gather(w_out, "seq", axis=1, tiled=True).reshape(hid, dim)

    cot = to_positions(cotangent, nch, q_count)
    prow = x.shape[0]
    if q_count == 1:
        ids = lax.dynamic_slice_in_dim(segment_ids, me * prow, prow, axis=0)
    else:
        ids = lax.dynamic_slice_in_dim(segment_ids, me // q_count, 1, axis=0)
        ids = lax.dynamic_slice_in_dim(ids, (me % q_count) * part, part, axis=1)
    own_ids = ids + 1
    wide_ids = extended(own_ids, border, pairs)

    residual = x.astype(jnp.float32)
    normed0, unit0, scale0 = normalize(residual, g0, s0)
    hidden0 = gelu_exact(normed0).astype(jnp.bfloat16)
    inner = jnp.einsum("dh,rdl->rhl", w_in, hidden0, preferred_element_type=jnp.float32) + b_in[:, None]
    normed1, unit1, scale1 = normalize(inner, g1, s1)
    hidden1 = gelu_exact(normed1).astype(jnp.bfloat16)
    wide_hidden = extended(hidden1, border, pairs)
    taps = shifted_taps(wide_hidden, wide_ids, own_ids, offsets, border)
    kernel_flat = w_cv.reshape(KERNEL_TAPS * hid, hid)
    mixed = jnp.einsum("co,rcl->rol", kernel_flat, taps, preferred_element_type=jnp.float32) + b_cv[:, None]
    normed2, unit2, scale2 = normalize(mixed, g2, s2)
    hidden2 = gelu_exact(normed2).astype(jnp.bfloat16)
    branch = jnp.einsum("hd,rhl->rdl", w_out, hidden2, preferred_element_type=jnp.float32)
    output = (residual + branch + b_out[:, None]).astype(jnp.bfloat16)

    grad_b_outer = jnp.sum(cot.astype(jnp.float32), axis=(0, 2))
    grad_w_outer = jnp.einsum("rhl,rdl->hd", hidden2, cot, preferred_element_type=jnp.float32)
    def reduce_seq_batch(g, split_dim, after=None):
        if after is not None:
            g, _ = lax.optimization_barrier((g, after))
        g = lax.psum_scatter(g, "seq", scatter_dimension=split_dim, tiled=True)
        return lax.psum_scatter(g, "batch", scatter_dimension=split_dim, tiled=True)

    part_outer = reduce_seq_batch(grad_w_outer.reshape(nch, hloc * dim // 128, 128), 1)
    grad_hidden2 = jnp.einsum("hd,rdl->rhl", w_out, cot, preferred_element_type=jnp.float32)
    grad_normed2 = gelu_back(normed2, grad_hidden2)
    grad_norm2_gain = jnp.sum(grad_normed2 * unit2, axis=(0, 2))
    grad_norm2_shift = jnp.sum(grad_normed2, axis=(0, 2))
    grad_mixed = normalize_back(grad_normed2, unit2, scale2, g2).astype(jnp.bfloat16)
    grad_b_conv = jnp.sum(grad_mixed.astype(jnp.float32), axis=(0, 2))
    grad_w_conv = jnp.einsum(
        "rol,rkcil->okci",
        grad_mixed,
        taps.reshape(prow, KERNEL_TAPS, nch, hloc, part),
        preferred_element_type=jnp.float32,
    )
    wide_grad = extended(grad_mixed, border, pairs)
    back_taps = shifted_taps(wide_grad, wide_ids, own_ids, back_offsets, border)
    kernel_back = jnp.transpose(w_cv, (0, 2, 1)).reshape(KERNEL_TAPS * hid, hid)
    grad_hidden1 = jnp.einsum("oc,rol->rcl", kernel_back, back_taps, preferred_element_type=jnp.float32)
    grad_normed1 = gelu_back(normed1, grad_hidden1)
    grad_norm1_gain = jnp.sum(grad_normed1 * unit1, axis=(0, 2))
    grad_norm1_shift = jnp.sum(grad_normed1, axis=(0, 2))
    grad_inner = normalize_back(grad_normed1, unit1, scale1, g1).astype(jnp.bfloat16)
    grad_inner, _ = lax.optimization_barrier((grad_inner, part_outer))
    grad_b_inner = jnp.sum(grad_inner.astype(jnp.float32), axis=(0, 2))
    grad_w_inner = jnp.einsum("rdl,rhl->dh", hidden0, grad_inner, preferred_element_type=jnp.float32)
    grad_hidden0 = jnp.einsum("dh,rhl->rdl", w_in, grad_inner, preferred_element_type=jnp.float32)
    grad_normed0 = gelu_back(normed0, grad_hidden0)
    grad_norm0_gain = jnp.sum(grad_normed0 * unit0, axis=(0, 2))
    grad_norm0_shift = jnp.sum(grad_normed0, axis=(0, 2))
    input_grad = (cot.astype(jnp.float32) + normalize_back(grad_normed0, unit0, scale0, g0)).astype(jnp.bfloat16)

    output = to_channels(output, nch, q_count, rows)
    input_grad = to_channels(input_grad, nch, q_count, rows)

    vectors = [
        grad_norm0_gain,
        grad_norm0_shift,
        grad_b_inner,
        grad_norm1_gain,
        grad_norm1_shift,
        grad_b_conv,
        grad_norm2_gain,
        grad_norm2_shift,
        grad_b_outer,
    ]
    flat = jnp.concatenate([v.reshape(nch, -1) for v in vectors], axis=1)
    vec_len = flat.shape[1]
    vec_rows = -(-vec_len // hid)
    vec_rows = -(-(dloc + vec_rows) // 64) * 64 - dloc
    flat = jnp.pad(flat, ((0, 0), (0, vec_rows * hid - vec_len))).reshape(nch, vec_rows, hid)
    inner_plus = jnp.concatenate([grad_w_inner.reshape(nch, dloc, hid), flat], axis=1)
    inner_plus = inner_plus.reshape(nch, (dloc + vec_rows) * hid // 128, 128)

    conv_tail = grad_w_conv.shape[1:]
    part_conv = reduce_seq_batch(grad_w_conv.reshape(hid, math.prod(conv_tail) // 128, 128), 0, part_outer)
    part_conv = part_conv.reshape((part_conv.shape[0],) + conv_tail)
    part_inner = reduce_seq_batch(inner_plus, 1, part_conv)
    parts = [part_outer, part_conv, part_inner]
    parts = exchange(parts, ("ch",), 1, axes=(0, 2, 0), reduce=True)
    piece_shapes = [p.shape for p in parts]
    parts = [p.reshape(p.size // 128, 128) if p.size % 128 == 0 else p for p in parts]
    parts = [lax.all_gather(p, "batch", axis=0) for p in parts]
    parts = [
        lax.all_gather(p, "seq", axis=0, tiled=True).reshape((seqs * batches,) + shape)
        for p, shape in zip(parts, piece_shapes)
    ]
    red_w_outer = parts[0].reshape(hloc, dim)
    red_w_conv = parts[1].reshape(hid, KERNEL_TAPS, hloc).transpose(1, 2, 0)
    red_inner = parts[2].reshape(dloc + vec_rows, hid)
    red_w_inner = red_inner[:dloc]
    mine = red_inner[dloc:].reshape(-1)[:vec_len]
    reds = []
    cut = 0
    for v in vectors:
        n = v.shape[0] // nch
        reds.append(mine[cut : cut + n])
        cut += n
    return (
        output,
        input_grad,
        reds[0],
        reds[1],
        red_w_inner,
        reds[2],
        reds[3],
        reds[4],
        red_w_conv,
        reds[5],
        reds[6],
        reds[7],
        red_w_outer,
        reds[8],
    )


def solution(mesh):
    return jax.shard_map(
        local,
        mesh=mesh,
        in_specs=(
            P("batch", "ch", "seq"),
            P("batch", "seq"),
            P("ch"),
            P("ch"),
            P("ch", None),
            P("ch"),
            P("ch"),
            P("ch"),
            P(None, "ch", None),
            P("ch"),
            P("ch"),
            P("ch"),
            P("ch", None),
            P("ch"),
            P("batch", "ch", "seq"),
        ),
        out_specs=(
            P("batch", "ch", "seq"),
            P("batch", "ch", "seq"),
            P("ch"),
            P("ch"),
            P("ch", None),
            P("ch"),
            P("ch"),
            P("ch"),
            P(None, "ch", None),
            P("ch"),
            P("ch"),
            P("ch"),
            P("ch", None),
            P("ch"),
        ),
        check_vma=False,
    )
```

```python
import functools
import math

import jax
import jax.numpy as jnp
from jax import lax
from jax.experimental import pallas as pl
from jax.experimental.pallas import tpu as pltpu
from jax.sharding import PartitionSpec as P

KERNEL_TAPS = 5
DILATION_SPACING = 32


EPSILON = 1e-05


MESH_AXES = ("batch", "seq", "ch")
MESH_ID = pl.DeviceIdType.MESH


def _group_index(group, sizes, coords):
    me = 0
    for a in group:
        me = me * sizes[a] + coords[a]
    return me


def _exchange_kernel(sizes, group, gather, reduce, axes, *refs):
    count_arrays = len(axes)
    x_refs = refs[:count_arrays]
    o_refs = refs[count_arrays : 2 * count_arrays]
    send_sem, recv_sem = refs[2 * count_arrays :]
    coords = {a: lax.axis_index(a) for a in MESH_AXES}
    me = _group_index(group, sizes, coords)
    count = math.prod(sizes[a] for a in group)

    def device(index):
        where = dict(coords)
        rest = index
        for a in reversed(group):
            where[a] = lax.rem(rest, sizes[a])
            rest = rest // sizes[a]
        return tuple(where[a] for a in MESH_AXES)

    barrier = pltpu.get_barrier_semaphore()
    for j in range(1, count):
        pl.semaphore_signal(barrier, 1, device_id=device(lax.rem(me + j, count)), device_id_type=MESH_ID)
    pl.semaphore_wait(barrier, count - 1)
    copies = []
    for j in range(1, count):
        peer = lax.rem(me + j, count)
        for i in range(count_arrays):
            lead = (slice(None),) * axes[i]
            if gather[i]:
                src, dst = x_refs[i], o_refs[i].at[me]
            else:
                slot = (j - 1) if reduce else me
                src = x_refs[i].at[lead + (pl.ds(peer, 1),)]
                dst = o_refs[i].at[lead + (pl.ds(slot, 1),)]
            copy = pltpu.make_async_remote_copy(
                src_ref=src,
                dst_ref=dst,
                send_sem=send_sem.at[i, j - 1],
                recv_sem=recv_sem.at[i, j - 1],
                device_id=device(peer),
                device_id_type=MESH_ID,
            )
            copy.start()
            copies.append(copy)
    for copy in copies:
        copy.wait()


def exchange(xs, group, collective_id, gather=False, axes=None, reduce=False):
    sizes = {a: lax.axis_size(a) for a in MESH_AXES}
    count = math.prod(sizes[a] for a in group)
    axes = tuple(axes or (0,) * len(xs))
    if isinstance(gather, bool):
        gather = (gather,) * len(xs)
    gather = tuple(gather)
    if count == 1:
        return [x[None] if g else x for x, g in zip(xs, gather)]
    shapes = [jax.ShapeDtypeStruct((count,) + x.shape if g else x.shape, x.dtype) for x, g in zip(xs, gather)]
    if reduce:
        shapes = [
            jax.ShapeDtypeStruct(x.shape[:a] + (count - 1,) + x.shape[a + 1 :], x.dtype) for x, a in zip(xs, axes)
        ]
    moved = sum(x.size * x.dtype.itemsize * (count if g else 1) for x, g in zip(xs, gather))
    outs = pl.pallas_call(
        functools.partial(_exchange_kernel, sizes, group, gather, reduce, axes),
        out_shape=shapes,
        in_specs=[pl.BlockSpec(memory_space=pl.ANY)] * len(xs),
        out_specs=[pl.BlockSpec(memory_space=pl.ANY)] * len(xs),
        scratch_shapes=[
            pltpu.SemaphoreType.DMA((len(xs), count - 1)),
            pltpu.SemaphoreType.DMA((len(xs), count - 1)),
        ],
        compiler_params=pltpu.CompilerParams(collective_id=collective_id, has_side_effects=True),
        cost_estimate=pl.CostEstimate(flops=0, transcendentals=0, bytes_accessed=2 * moved),
    )(*xs)
    me = _group_index(group, sizes, {a: lax.axis_index(a) for a in group})
    placed = []
    if reduce:
        for x, out, axis in zip(xs, outs, axes):
            own = lax.dynamic_index_in_dim(x, me, axis, keepdims=False)
            placed.append(own + jnp.sum(out, axis=axis))
        return placed
    for x, out, axis, g in zip(xs, outs, axes, gather):
        own = x if g else lax.dynamic_index_in_dim(x, me, axis, keepdims=False)
        placed.append(lax.dynamic_update_index_in_dim(out, own, me, axis))
    return placed


def gelu_exact(values):
    return jax.nn.gelu(values, approximate=False)


def gelu_back(point, grad):
    return jax.vjp(gelu_exact, point)[1](grad)[0]


def normalize(values, gain, shift):
    center = jnp.mean(values, axis=1, keepdims=True)
    offset = values - center
    spread = jnp.mean(offset * offset, axis=1, keepdims=True)
    scale = lax.rsqrt(spread + EPSILON)
    unit = offset * scale
    return (unit * gain[:, None] + shift[:, None], unit, scale)


def normalize_back(grad, unit, scale, gain):
    scaled = grad * gain[:, None]
    first = jnp.mean(scaled, axis=1, keepdims=True)
    second = jnp.mean(scaled * unit, axis=1, keepdims=True)
    return scale * (scaled - first - unit * second)


def neighbour_pairs(seqs, nch, q_count):
    pairs = []
    for s in range(seqs):
        for c in range(nch):
            q = c % q_count
            if q < q_count - 1:
                pairs.append((s * nch + c, s * nch + c + 1))
            elif s < seqs - 1:
                pairs.append((s * nch + c, (s + 1) * nch + c - (q_count - 1)))
    return pairs


def extended(x, width, pairs):
    down = [(j, i) for i, j in pairs]
    length = x.shape[-1]
    before = lax.ppermute(x[..., length - width :], ("seq", "ch"), pairs)
    after = lax.ppermute(x[..., :width], ("seq", "ch"), down)
    return jnp.concatenate([before, x, after], axis=-1)


def shifted_taps(wide, wide_ids, own_ids, offsets, border):
    length = own_ids.shape[-1]
    pieces = []
    for offset in offsets:
        lower = border + offset
        shifted = wide[:, :, lower : lower + length]
        matching = wide_ids[:, lower : lower + length] == own_ids
        pieces.append(jnp.where(matching[:, None, :], shifted, jnp.zeros_like(shifted)))
    return jnp.concatenate(pieces, axis=1)


def to_positions(x, nch, q_count):
    rows, width, length = x.shape
    if q_count > 1:
        x = x.reshape(rows, width, q_count, length // q_count).transpose(0, 2, 1, 3)
        x = x.reshape(rows * q_count, width, length // q_count)
    x = lax.all_to_all(x, "ch", 0, 0, tiled=True)
    return _join(x, nch)


def _join(x, nch):
    total, width, length = x.shape
    p = total // nch
    return x.reshape(nch, p, width, length).transpose(1, 0, 2, 3).reshape(p, nch * width, length)


def to_channels(x, nch, q_count, rows):
    p, width, length = x.shape
    x = x.reshape(p, nch, width // nch, length).transpose(1, 0, 2, 3).reshape(nch * p, width // nch, length)
    x = lax.all_to_all(x, "ch", 0, 0, tiled=True)
    if q_count > 1:
        _, width, part = x.shape
        x = x.reshape(rows, q_count, width, part).transpose(0, 2, 1, 3).reshape(rows, width, q_count * part)
    return x


def local(
    inputs,
    segment_ids,
    norm0_gain,
    norm0_shift,
    w_inner,
    b_inner,
    norm1_gain,
    norm1_shift,
    w_conv,
    b_conv,
    norm2_gain,
    norm2_shift,
    w_outer,
    b_outer,
    cotangent,
):
    nch = lax.axis_size("ch")
    seqs = lax.axis_size("seq")
    batches = lax.axis_size("batch")
    rows, dloc, length = inputs.shape
    hloc = w_conv.shape[1]
    hid = hloc * nch
    dim = dloc * nch
    if rows % nch == 0:
        q_count = 1
    else:
        q_count = nch // rows
    part = length // q_count
    border = 2 * DILATION_SPACING
    offsets = [(k - KERNEL_TAPS // 2) * DILATION_SPACING for k in range(KERNEL_TAPS)]
    back_offsets = [-o for o in offsets]
    pairs = neighbour_pairs(seqs, nch, q_count)
    me = lax.axis_index("ch")

    smalls = [norm0_gain, norm0_shift, b_inner, norm1_gain, norm1_shift, b_conv, norm2_gain, norm2_shift, b_outer]
    sidx = lax.axis_index("seq")
    halves = [
        lax.dynamic_slice_in_dim(w_inner, sidx * (dloc // seqs), dloc // seqs, 0),
        lax.dynamic_slice_in_dim(w_conv, sidx * (hloc // seqs), hloc // seqs, 1),
        lax.dynamic_slice_in_dim(w_outer, sidx * (hloc // seqs), hloc // seqs, 0),
    ]
    if q_count == 1:
        small_all, w_in, w_cv, w_out, x = exchange(
            [jnp.concatenate(smalls)] + halves + [inputs], ("ch",), 0, gather=(True, True, True, True, False)
        )
        x = _join(x, nch)
    else:
        small_all, w_in, w_cv, w_out = exchange([jnp.concatenate(smalls)] + halves, ("ch",), 0, gather=True)
        x = to_positions(inputs, nch, q_count)
    cut = 0
    full = []
    for v in smalls:
        n = v.shape[0]
        full.append(small_all[:, cut : cut + n].reshape(n * nch))
        cut += n
    g0, s0, b_in, g1, s1, b_cv, g2, s2, b_out = full
    w_in = lax.all_gather(w_in, "seq", axis=1, tiled=True).reshape(dim, hid)
    w_cv = lax.all_gather(w_cv, "seq", axis=2, tiled=True).transpose(1, 0, 2, 3).reshape(KERNEL_TAPS, hid, hid)
    w_out = lax.all_gather(w_out, "seq", axis=1, tiled=True).reshape(hid, dim)

    cot = to_positions(cotangent, nch, q_count)
    prow = x.shape[0]
    if q_count == 1:
        ids = lax.dynamic_slice_in_dim(segment_ids, me * prow, prow, axis=0)
    else:
        ids = lax.dynamic_slice_in_dim(segment_ids, me // q_count, 1, axis=0)
        ids = lax.dynamic_slice_in_dim(ids, (me % q_count) * part, part, axis=1)
    own_ids = ids + 1
    wide_ids = extended(own_ids, border, pairs)

    residual = x.astype(jnp.float32)
    normed0, unit0, scale0 = normalize(residual, g0, s0)
    hidden0 = gelu_exact(normed0).astype(jnp.bfloat16)
    inner = jnp.einsum("dh,rdl->rhl", w_in, hidden0, preferred_element_type=jnp.float32) + b_in[:, None]
    normed1, unit1, scale1 = normalize(inner, g1, s1)
    hidden1 = gelu_exact(normed1).astype(jnp.bfloat16)
    wide_hidden = extended(hidden1, border, pairs)
    taps = shifted_taps(wide_hidden, wide_ids, own_ids, offsets, border)
    kernel_flat = w_cv.reshape(KERNEL_TAPS * hid, hid)
    mixed = jnp.einsum("co,rcl->rol", kernel_flat, taps, preferred_element_type=jnp.float32) + b_cv[:, None]
    normed2, unit2, scale2 = normalize(mixed, g2, s2)
    hidden2 = gelu_exact(normed2).astype(jnp.bfloat16)
    branch = jnp.einsum("hd,rhl->rdl", w_out, hidden2, preferred_element_type=jnp.float32)
    output = (residual + branch + b_out[:, None]).astype(jnp.bfloat16)

    grad_b_outer = jnp.sum(cot.astype(jnp.float32), axis=(0, 2))
    grad_w_outer = jnp.einsum("rhl,rdl->hd", hidden2, cot, preferred_element_type=jnp.float32)
    def reduce_seq_batch(g, split_dim, after=None):
        if after is not None:
            g, _ = lax.optimization_barrier((g, after))
        g = lax.psum_scatter(g, "seq", scatter_dimension=split_dim, tiled=True)
        return lax.psum_scatter(g, "batch", scatter_dimension=split_dim, tiled=True)

    part_outer = reduce_seq_batch(grad_w_outer.reshape(nch, hloc * dim // 128, 128), 1)
    grad_hidden2 = jnp.einsum("hd,rdl->rhl", w_out, cot, preferred_element_type=jnp.float32)
    grad_normed2 = gelu_back(normed2, grad_hidden2)
    grad_norm2_gain = jnp.sum(grad_normed2 * unit2, axis=(0, 2))
    grad_norm2_shift = jnp.sum(grad_normed2, axis=(0, 2))
    grad_mixed = normalize_back(grad_normed2, unit2, scale2, g2).astype(jnp.bfloat16)
    grad_b_conv = jnp.sum(grad_mixed.astype(jnp.float32), axis=(0, 2))
    grad_w_conv = jnp.einsum(
        "rol,rkcil->okci",
        grad_mixed,
        taps.reshape(prow, KERNEL_TAPS, nch, hloc, part),
        preferred_element_type=jnp.float32,
    )
    wide_grad = extended(grad_mixed, border, pairs)
    back_taps = shifted_taps(wide_grad, wide_ids, own_ids, back_offsets, border)
    kernel_back = jnp.transpose(w_cv, (0, 2, 1)).reshape(KERNEL_TAPS * hid, hid)
    grad_hidden1 = jnp.einsum("oc,rol->rcl", kernel_back, back_taps, preferred_element_type=jnp.float32)
    grad_normed1 = gelu_back(normed1, grad_hidden1)
    grad_norm1_gain = jnp.sum(grad_normed1 * unit1, axis=(0, 2))
    grad_norm1_shift = jnp.sum(grad_normed1, axis=(0, 2))
    grad_inner = normalize_back(grad_normed1, unit1, scale1, g1).astype(jnp.bfloat16)
    grad_inner, _ = lax.optimization_barrier((grad_inner, part_outer))
    grad_b_inner = jnp.sum(grad_inner.astype(jnp.float32), axis=(0, 2))
    grad_w_inner = jnp.einsum("rdl,rhl->dh", hidden0, grad_inner, preferred_element_type=jnp.float32)
    grad_hidden0 = jnp.einsum("dh,rhl->rdl", w_in, grad_inner, preferred_element_type=jnp.float32)
    grad_normed0 = gelu_back(normed0, grad_hidden0)
    grad_norm0_gain = jnp.sum(grad_normed0 * unit0, axis=(0, 2))
    grad_norm0_shift = jnp.sum(grad_normed0, axis=(0, 2))
    input_grad = (cot.astype(jnp.float32) + normalize_back(grad_normed0, unit0, scale0, g0)).astype(jnp.bfloat16)

    output = to_channels(output, nch, q_count, rows)
    input_grad = to_channels(input_grad, nch, q_count, rows)

    vectors = [
        grad_norm0_gain,
        grad_norm0_shift,
        grad_b_inner,
        grad_norm1_gain,
        grad_norm1_shift,
        grad_b_conv,
        grad_norm2_gain,
        grad_norm2_shift,
        grad_b_outer,
    ]
    flat = jnp.concatenate([v.reshape(nch, -1) for v in vectors], axis=1)
    vec_len = flat.shape[1]
    vec_rows = -(-vec_len // hid)
    vec_rows = -(-(dloc + vec_rows) // 64) * 64 - dloc
    flat = jnp.pad(flat, ((0, 0), (0, vec_rows * hid - vec_len))).reshape(nch, vec_rows, hid)
    inner_plus = jnp.concatenate([grad_w_inner.reshape(nch, dloc, hid), flat], axis=1)
    inner_plus = inner_plus.reshape(nch, (dloc + vec_rows) * hid // 128, 128)

    conv_tail = grad_w_conv.shape[1:]
    part_conv = reduce_seq_batch(grad_w_conv.reshape(hid, math.prod(conv_tail) // 128, 128), 0, part_outer)
    part_conv = part_conv.reshape((part_conv.shape[0],) + conv_tail)
    part_inner = reduce_seq_batch(inner_plus, 1, part_conv)
    parts = [part_outer, part_conv, part_inner]
    parts = exchange(parts, ("ch",), 1, axes=(0, 2, 0), reduce=True)
    piece_shapes = [p.shape for p in parts]
    parts = [p.reshape(p.size // 128, 128) if p.size % 128 == 0 else p for p in parts]
    parts = [lax.all_gather(p, "batch", axis=0) for p in parts]
    parts = [
        lax.all_gather(p, "seq", axis=0, tiled=True).reshape((seqs * batches,) + shape)
        for p, shape in zip(parts, piece_shapes)
    ]
    red_w_outer = parts[0].reshape(hloc, dim)
    red_w_conv = parts[1].reshape(hid, KERNEL_TAPS, hloc).transpose(1, 2, 0)
    red_inner = parts[2].reshape(dloc + vec_rows, hid)
    red_w_inner = red_inner[:dloc]
    mine = red_inner[dloc:].reshape(-1)[:vec_len]
    reds = []
    cut = 0
    for v in vectors:
        n = v.shape[0] // nch
        reds.append(mine[cut : cut + n])
        cut += n
    return (
        output,
        input_grad,
        reds[0],
        reds[1],
        red_w_inner,
        reds[2],
        reds[3],
        reds[4],
        red_w_conv,
        reds[5],
        reds[6],
        reds[7],
        red_w_outer,
        reds[8],
    )


def solution(mesh):
    return jax.shard_map(
        local,
        mesh=mesh,
        in_specs=(
            P("batch", "ch", "seq"),
            P("batch", "seq"),
            P("ch"),
            P("ch"),
            P("ch", None),
            P("ch"),
            P("ch"),
            P("ch"),
            P(None, "ch", None),
            P("ch"),
            P("ch"),
            P("ch"),
            P("ch", None),
            P("ch"),
            P("batch", "ch", "seq"),
        ),
        out_specs=(
            P("batch", "ch", "seq"),
            P("batch", "ch", "seq"),
            P("ch"),
            P("ch"),
            P("ch", None),
            P("ch"),
            P("ch"),
            P("ch"),
            P(None, "ch", None),
            P("ch"),
            P("ch"),
            P("ch"),
            P("ch", None),
            P("ch"),
        ),
        check_vma=False,
    )
```

```python
import functools
import math

import jax
import jax.numpy as jnp
from jax import lax
from jax.experimental import pallas as pl
from jax.experimental.pallas import tpu as pltpu
from jax.sharding import PartitionSpec as P

KERNEL_TAPS = 5
DILATION_SPACING = 32


EPSILON = 1e-05


MESH_AXES = ("batch", "seq", "ch")
MESH_ID = pl.DeviceIdType.MESH


def _group_index(group, sizes, coords):
    me = 0
    for a in group:
        me = me * sizes[a] + coords[a]
    return me


def _exchange_kernel(sizes, group, gather, reduce, axes, *refs):
    count_arrays = len(axes)
    x_refs = refs[:count_arrays]
    o_refs = refs[count_arrays : 2 * count_arrays]
    send_sem, recv_sem = refs[2 * count_arrays :]
    coords = {a: lax.axis_index(a) for a in MESH_AXES}
    me = _group_index(group, sizes, coords)
    count = math.prod(sizes[a] for a in group)

    def device(index):
        where = dict(coords)
        rest = index
        for a in reversed(group):
            where[a] = lax.rem(rest, sizes[a])
            rest = rest // sizes[a]
        return tuple(where[a] for a in MESH_AXES)

    barrier = pltpu.get_barrier_semaphore()
    for j in range(1, count):
        pl.semaphore_signal(barrier, 1, device_id=device(lax.rem(me + j, count)), device_id_type=MESH_ID)
    pl.semaphore_wait(barrier, count - 1)
    copies = []
    for j in range(1, count):
        peer = lax.rem(me + j, count)
        for i in range(count_arrays):
            lead = (slice(None),) * axes[i]
            if gather:
                src, dst = x_refs[i], o_refs[i].at[me]
            else:
                slot = (j - 1) if reduce else me
                src = x_refs[i].at[lead + (pl.ds(peer, 1),)]
                dst = o_refs[i].at[lead + (pl.ds(slot, 1),)]
            copy = pltpu.make_async_remote_copy(
                src_ref=src,
                dst_ref=dst,
                send_sem=send_sem.at[i, j - 1],
                recv_sem=recv_sem.at[i, j - 1],
                device_id=device(peer),
                device_id_type=MESH_ID,
            )
            copy.start()
            copies.append(copy)
    for copy in copies:
        copy.wait()


def exchange(xs, group, collective_id, gather=False, axes=None, reduce=False):
    sizes = {a: lax.axis_size(a) for a in MESH_AXES}
    count = math.prod(sizes[a] for a in group)
    axes = tuple(axes or (0,) * len(xs))
    if count == 1:
        return [x[None] if gather else x for x in xs]
    shapes = [jax.ShapeDtypeStruct((count,) + x.shape if gather else x.shape, x.dtype) for x in xs]
    if reduce:
        shapes = [
            jax.ShapeDtypeStruct(x.shape[:a] + (count - 1,) + x.shape[a + 1 :], x.dtype) for x, a in zip(xs, axes)
        ]
    moved = sum(x.size * x.dtype.itemsize * (count if gather else 1) for x in xs)
    outs = pl.pallas_call(
        functools.partial(_exchange_kernel, sizes, group, gather, reduce, axes),
        out_shape=shapes,
        in_specs=[pl.BlockSpec(memory_space=pl.ANY)] * len(xs),
        out_specs=[pl.BlockSpec(memory_space=pl.ANY)] * len(xs),
        scratch_shapes=[
            pltpu.SemaphoreType.DMA((len(xs), count - 1)),
            pltpu.SemaphoreType.DMA((len(xs), count - 1)),
        ],
        compiler_params=pltpu.CompilerParams(collective_id=collective_id, has_side_effects=True),
        cost_estimate=pl.CostEstimate(flops=0, transcendentals=0, bytes_accessed=2 * moved),
    )(*xs)
    me = _group_index(group, sizes, {a: lax.axis_index(a) for a in group})
    placed = []
    if reduce:
        for x, out, axis in zip(xs, outs, axes):
            own = lax.dynamic_index_in_dim(x, me, axis, keepdims=False)
            placed.append(own + jnp.sum(out, axis=axis))
        return placed
    for x, out, axis in zip(xs, outs, axes):
        own = x if gather else lax.dynamic_index_in_dim(x, me, axis, keepdims=False)
        placed.append(lax.dynamic_update_index_in_dim(out, own, me, axis))
    return placed


def gelu_exact(values):
    return jax.nn.gelu(values, approximate=False)


def gelu_back(point, grad):
    return jax.vjp(gelu_exact, point)[1](grad)[0]


def normalize(values, gain, shift):
    center = jnp.mean(values, axis=1, keepdims=True)
    offset = values - center
    spread = jnp.mean(offset * offset, axis=1, keepdims=True)
    scale = lax.rsqrt(spread + EPSILON)
    unit = offset * scale
    return (unit * gain[:, None] + shift[:, None], unit, scale)


def normalize_back(grad, unit, scale, gain):
    scaled = grad * gain[:, None]
    first = jnp.mean(scaled, axis=1, keepdims=True)
    second = jnp.mean(scaled * unit, axis=1, keepdims=True)
    return scale * (scaled - first - unit * second)


def neighbour_pairs(seqs, nch, q_count):
    pairs = []
    for s in range(seqs):
        for c in range(nch):
            q = c % q_count
            if q < q_count - 1:
                pairs.append((s * nch + c, s * nch + c + 1))
            elif s < seqs - 1:
                pairs.append((s * nch + c, (s + 1) * nch + c - (q_count - 1)))
    return pairs


def extended(x, width, pairs):
    down = [(j, i) for i, j in pairs]
    length = x.shape[-1]
    before = lax.ppermute(x[..., length - width :], ("seq", "ch"), pairs)
    after = lax.ppermute(x[..., :width], ("seq", "ch"), down)
    return jnp.concatenate([before, x, after], axis=-1)


def shifted_taps(wide, wide_ids, own_ids, offsets, border):
    length = own_ids.shape[-1]
    pieces = []
    for offset in offsets:
        lower = border + offset
        shifted = wide[:, :, lower : lower + length]
        matching = wide_ids[:, lower : lower + length] == own_ids
        pieces.append(jnp.where(matching[:, None, :], shifted, jnp.zeros_like(shifted)))
    return jnp.concatenate(pieces, axis=1)


def to_positions(x, nch, q_count):
    rows, width, length = x.shape
    if q_count > 1:
        x = x.reshape(rows, width, q_count, length // q_count).transpose(0, 2, 1, 3)
        x = x.reshape(rows * q_count, width, length // q_count)
    x = lax.all_to_all(x, "ch", 0, 0, tiled=True)
    return _join(x, nch)


def _join(x, nch):
    total, width, length = x.shape
    p = total // nch
    return x.reshape(nch, p, width, length).transpose(1, 0, 2, 3).reshape(p, nch * width, length)


def to_channels(x, nch, q_count, rows):
    p, width, length = x.shape
    x = x.reshape(p, nch, width // nch, length).transpose(1, 0, 2, 3).reshape(nch * p, width // nch, length)
    x = lax.all_to_all(x, "ch", 0, 0, tiled=True)
    if q_count > 1:
        _, width, part = x.shape
        x = x.reshape(rows, q_count, width, part).transpose(0, 2, 1, 3).reshape(rows, width, q_count * part)
    return x


def local(
    inputs,
    segment_ids,
    norm0_gain,
    norm0_shift,
    w_inner,
    b_inner,
    norm1_gain,
    norm1_shift,
    w_conv,
    b_conv,
    norm2_gain,
    norm2_shift,
    w_outer,
    b_outer,
    cotangent,
):
    nch = lax.axis_size("ch")
    seqs = lax.axis_size("seq")
    batches = lax.axis_size("batch")
    rows, dloc, length = inputs.shape
    hloc = w_conv.shape[1]
    hid = hloc * nch
    dim = dloc * nch
    if rows % nch == 0:
        q_count = 1
    else:
        q_count = nch // rows
    part = length // q_count
    border = 2 * DILATION_SPACING
    offsets = [(k - KERNEL_TAPS // 2) * DILATION_SPACING for k in range(KERNEL_TAPS)]
    back_offsets = [-o for o in offsets]
    pairs = neighbour_pairs(seqs, nch, q_count)
    me = lax.axis_index("ch")

    smalls = [norm0_gain, norm0_shift, b_inner, norm1_gain, norm1_shift, b_conv, norm2_gain, norm2_shift, b_outer]
    sidx = lax.axis_index("seq")
    halves = [
        lax.dynamic_slice_in_dim(w_inner, sidx * (dloc // seqs), dloc // seqs, 0),
        lax.dynamic_slice_in_dim(w_conv, sidx * (hloc // seqs), hloc // seqs, 1),
        lax.dynamic_slice_in_dim(w_outer, sidx * (hloc // seqs), hloc // seqs, 0),
    ]
    small_all, w_in, w_out = exchange([jnp.concatenate(smalls), halves[0], halves[2]], ("ch",), 0, gather=True)
    w_cv = lax.all_gather(halves[1], "ch", axis=0)
    cut = 0
    full = []
    for v in smalls:
        n = v.shape[0]
        full.append(small_all[:, cut : cut + n].reshape(n * nch))
        cut += n
    g0, s0, b_in, g1, s1, b_cv, g2, s2, b_out = full
    w_in = lax.all_gather(w_in, "seq", axis=1, tiled=True).reshape(dim, hid)
    w_cv = lax.all_gather(w_cv, "seq", axis=2, tiled=True).transpose(1, 0, 2, 3).reshape(KERNEL_TAPS, hid, hid)
    w_out = lax.all_gather(w_out, "seq", axis=1, tiled=True).reshape(hid, dim)

    x = to_positions(inputs, nch, q_count)
    cot = to_positions(cotangent, nch, q_count)
    prow = x.shape[0]
    if q_count == 1:
        ids = lax.dynamic_slice_in_dim(segment_ids, me * prow, prow, axis=0)
    else:
        ids = lax.dynamic_slice_in_dim(segment_ids, me // q_count, 1, axis=0)
        ids = lax.dynamic_slice_in_dim(ids, (me % q_count) * part, part, axis=1)
    own_ids = ids + 1
    wide_ids = extended(own_ids, border, pairs)

    residual = x.astype(jnp.float32)
    normed0, unit0, scale0 = normalize(residual, g0, s0)
    hidden0 = gelu_exact(normed0).astype(jnp.bfloat16)
    inner = jnp.einsum("dh,rdl->rhl", w_in, hidden0, preferred_element_type=jnp.float32) + b_in[:, None]
    normed1, unit1, scale1 = normalize(inner, g1, s1)
    hidden1 = gelu_exact(normed1).astype(jnp.bfloat16)
    wide_hidden = extended(hidden1, border, pairs)
    taps = shifted_taps(wide_hidden, wide_ids, own_ids, offsets, border)
    kernel_flat = w_cv.reshape(KERNEL_TAPS * hid, hid)
    mixed = jnp.einsum("co,rcl->rol", kernel_flat, taps, preferred_element_type=jnp.float32) + b_cv[:, None]
    normed2, unit2, scale2 = normalize(mixed, g2, s2)
    hidden2 = gelu_exact(normed2).astype(jnp.bfloat16)
    branch = jnp.einsum("hd,rhl->rdl", w_out, hidden2, preferred_element_type=jnp.float32)
    output = (residual + branch + b_out[:, None]).astype(jnp.bfloat16)

    grad_b_outer = jnp.sum(cot.astype(jnp.float32), axis=(0, 2))
    grad_w_outer = jnp.einsum("rhl,rdl->hd", hidden2, cot, preferred_element_type=jnp.float32)
    def reduce_seq_batch(g, split_dim, after=None):
        if after is not None:
            g, _ = lax.optimization_barrier((g, after))
        g = lax.psum_scatter(g, "seq", scatter_dimension=split_dim, tiled=True)
        return lax.psum_scatter(g, "batch", scatter_dimension=split_dim, tiled=True)

    part_outer = reduce_seq_batch(grad_w_outer.reshape(nch, hloc * dim // 128, 128), 1)
    grad_hidden2 = jnp.einsum("hd,rdl->rhl", w_out, cot, preferred_element_type=jnp.float32)
    grad_normed2 = gelu_back(normed2, grad_hidden2)
    grad_norm2_gain = jnp.sum(grad_normed2 * unit2, axis=(0, 2))
    grad_norm2_shift = jnp.sum(grad_normed2, axis=(0, 2))
    grad_mixed = normalize_back(grad_normed2, unit2, scale2, g2).astype(jnp.bfloat16)
    grad_b_conv = jnp.sum(grad_mixed.astype(jnp.float32), axis=(0, 2))
    grad_w_conv = jnp.einsum(
        "rol,rkcil->okci",
        grad_mixed,
        taps.reshape(prow, KERNEL_TAPS, nch, hloc, part),
        preferred_element_type=jnp.float32,
    )
    wide_grad = extended(grad_mixed, border, pairs)
    back_taps = shifted_taps(wide_grad, wide_ids, own_ids, back_offsets, border)
    kernel_back = jnp.transpose(w_cv, (0, 2, 1)).reshape(KERNEL_TAPS * hid, hid)
    grad_hidden1 = jnp.einsum("oc,rol->rcl", kernel_back, back_taps, preferred_element_type=jnp.float32)
    grad_normed1 = gelu_back(normed1, grad_hidden1)
    grad_norm1_gain = jnp.sum(grad_normed1 * unit1, axis=(0, 2))
    grad_norm1_shift = jnp.sum(grad_normed1, axis=(0, 2))
    grad_inner = normalize_back(grad_normed1, unit1, scale1, g1).astype(jnp.bfloat16)
    grad_inner, _ = lax.optimization_barrier((grad_inner, part_outer))
    grad_b_inner = jnp.sum(grad_inner.astype(jnp.float32), axis=(0, 2))
    grad_w_inner = jnp.einsum("rdl,rhl->dh", hidden0, grad_inner, preferred_element_type=jnp.float32)
    grad_hidden0 = jnp.einsum("dh,rhl->rdl", w_in, grad_inner, preferred_element_type=jnp.float32)
    grad_normed0 = gelu_back(normed0, grad_hidden0)
    grad_norm0_gain = jnp.sum(grad_normed0 * unit0, axis=(0, 2))
    grad_norm0_shift = jnp.sum(grad_normed0, axis=(0, 2))
    input_grad = (cot.astype(jnp.float32) + normalize_back(grad_normed0, unit0, scale0, g0)).astype(jnp.bfloat16)

    output = to_channels(output, nch, q_count, rows)
    input_grad = to_channels(input_grad, nch, q_count, rows)

    vectors = [
        grad_norm0_gain,
        grad_norm0_shift,
        grad_b_inner,
        grad_norm1_gain,
        grad_norm1_shift,
        grad_b_conv,
        grad_norm2_gain,
        grad_norm2_shift,
        grad_b_outer,
    ]
    flat = jnp.concatenate([v.reshape(nch, -1) for v in vectors], axis=1)
    vec_len = flat.shape[1]
    vec_rows = -(-vec_len // hid)
    vec_rows = -(-(dloc + vec_rows) // 64) * 64 - dloc
    flat = jnp.pad(flat, ((0, 0), (0, vec_rows * hid - vec_len))).reshape(nch, vec_rows, hid)
    inner_plus = jnp.concatenate([grad_w_inner.reshape(nch, dloc, hid), flat], axis=1)
    inner_plus = inner_plus.reshape(nch, (dloc + vec_rows) * hid // 128, 128)

    conv_tail = grad_w_conv.shape[1:]
    part_conv = reduce_seq_batch(grad_w_conv.reshape(hid, math.prod(conv_tail) // 128, 128), 0, part_outer)
    part_conv = part_conv.reshape((part_conv.shape[0],) + conv_tail)
    part_inner = reduce_seq_batch(inner_plus, 1, part_conv)
    parts = [part_outer, part_conv, part_inner]
    parts = exchange(parts, ("ch",), 1, axes=(0, 2, 0), reduce=True)
    piece_shapes = [p.shape for p in parts]
    piece_sizes = [p.size for p in parts]
    joined = jnp.concatenate([p.reshape(-1) for p in parts])
    joined_len = joined.shape[0]
    joined_pad = -(-joined_len // 1024) * 1024
    joined = jnp.pad(joined, (0, joined_pad - joined_len)).reshape(joined_pad // 128, 128)
    joined = lax.all_gather(joined, "batch", axis=0)
    joined = lax.all_gather(joined, "seq", axis=0, tiled=True).reshape(seqs * batches, joined_pad)
    parts = []
    cut = 0
    for size, shape in zip(piece_sizes, piece_shapes):
        parts.append(joined[:, cut : cut + size].reshape((seqs * batches,) + shape))
        cut += size
    red_w_outer = parts[0].reshape(hloc, dim)
    red_w_conv = parts[1].reshape(hid, KERNEL_TAPS, hloc).transpose(1, 2, 0)
    red_inner = parts[2].reshape(dloc + vec_rows, hid)
    red_w_inner = red_inner[:dloc]
    mine = red_inner[dloc:].reshape(-1)[:vec_len]
    reds = []
    cut = 0
    for v in vectors:
        n = v.shape[0] // nch
        reds.append(mine[cut : cut + n])
        cut += n
    return (
        output,
        input_grad,
        reds[0],
        reds[1],
        red_w_inner,
        reds[2],
        reds[3],
        reds[4],
        red_w_conv,
        reds[5],
        reds[6],
        reds[7],
        red_w_outer,
        reds[8],
    )


def solution(mesh):
    return jax.shard_map(
        local,
        mesh=mesh,
        in_specs=(
            P("batch", "ch", "seq"),
            P("batch", "seq"),
            P("ch"),
            P("ch"),
            P("ch", None),
            P("ch"),
            P("ch"),
            P("ch"),
            P(None, "ch", None),
            P("ch"),
            P("ch"),
            P("ch"),
            P("ch", None),
            P("ch"),
            P("batch", "ch", "seq"),
        ),
        out_specs=(
            P("batch", "ch", "seq"),
            P("batch", "ch", "seq"),
            P("ch"),
            P("ch"),
            P("ch", None),
            P("ch"),
            P("ch"),
            P("ch"),
            P(None, "ch", None),
            P("ch"),
            P("ch"),
            P("ch"),
            P("ch", None),
            P("ch"),
        ),
        check_vma=False,
    )
```

```python
import functools
import math

import jax
import jax.numpy as jnp
from jax import lax
from jax.experimental import pallas as pl
from jax.experimental.pallas import tpu as pltpu
from jax.sharding import PartitionSpec as P

KERNEL_TAPS = 5
DILATION_SPACING = 32


EPSILON = 1e-05


MESH_AXES = ("batch", "seq", "ch")
MESH_ID = pl.DeviceIdType.MESH


def _group_index(group, sizes, coords):
    me = 0
    for a in group:
        me = me * sizes[a] + coords[a]
    return me


def _exchange_kernel(sizes, group, gather, reduce, axes, *refs):
    count_arrays = len(axes)
    x_refs = refs[:count_arrays]
    o_refs = refs[count_arrays : 2 * count_arrays]
    send_sem, recv_sem = refs[2 * count_arrays :]
    coords = {a: lax.axis_index(a) for a in MESH_AXES}
    me = _group_index(group, sizes, coords)
    count = math.prod(sizes[a] for a in group)

    def device(index):
        where = dict(coords)
        rest = index
        for a in reversed(group):
            where[a] = lax.rem(rest, sizes[a])
            rest = rest // sizes[a]
        return tuple(where[a] for a in MESH_AXES)

    barrier = pltpu.get_barrier_semaphore()
    for j in range(1, count):
        pl.semaphore_signal(barrier, 1, device_id=device(lax.rem(me + j, count)), device_id_type=MESH_ID)
    pl.semaphore_wait(barrier, count - 1)
    copies = []
    for j in range(1, count):
        peer = lax.rem(me + j, count)
        for i in range(count_arrays):
            lead = (slice(None),) * axes[i]
            if gather:
                src, dst = x_refs[i], o_refs[i].at[me]
            else:
                slot = (j - 1) if reduce else me
                src = x_refs[i].at[lead + (pl.ds(peer, 1),)]
                dst = o_refs[i].at[lead + (pl.ds(slot, 1),)]
            copy = pltpu.make_async_remote_copy(
                src_ref=src,
                dst_ref=dst,
                send_sem=send_sem.at[i, j - 1],
                recv_sem=recv_sem.at[i, j - 1],
                device_id=device(peer),
                device_id_type=MESH_ID,
            )
            copy.start()
            copies.append(copy)
    for copy in copies:
        copy.wait()


def exchange(xs, group, collective_id, gather=False, axes=None, reduce=False):
    sizes = {a: lax.axis_size(a) for a in MESH_AXES}
    count = math.prod(sizes[a] for a in group)
    axes = tuple(axes or (0,) * len(xs))
    if count == 1:
        return [x[None] if gather else x for x in xs]
    shapes = [jax.ShapeDtypeStruct((count,) + x.shape if gather else x.shape, x.dtype) for x in xs]
    if reduce:
        shapes = [
            jax.ShapeDtypeStruct(x.shape[:a] + (count - 1,) + x.shape[a + 1 :], x.dtype) for x, a in zip(xs, axes)
        ]
    moved = sum(x.size * x.dtype.itemsize * (count if gather else 1) for x in xs)
    outs = pl.pallas_call(
        functools.partial(_exchange_kernel, sizes, group, gather, reduce, axes),
        out_shape=shapes,
        in_specs=[pl.BlockSpec(memory_space=pl.ANY)] * len(xs),
        out_specs=[pl.BlockSpec(memory_space=pl.ANY)] * len(xs),
        scratch_shapes=[
            pltpu.SemaphoreType.DMA((len(xs), count - 1)),
            pltpu.SemaphoreType.DMA((len(xs), count - 1)),
        ],
        compiler_params=pltpu.CompilerParams(collective_id=collective_id, has_side_effects=True),
        cost_estimate=pl.CostEstimate(flops=0, transcendentals=0, bytes_accessed=2 * moved),
    )(*xs)
    me = _group_index(group, sizes, {a: lax.axis_index(a) for a in group})
    placed = []
    if reduce:
        for x, out, axis in zip(xs, outs, axes):
            own = lax.dynamic_index_in_dim(x, me, axis, keepdims=False)
            placed.append(own + jnp.sum(out, axis=axis))
        return placed
    for x, out, axis in zip(xs, outs, axes):
        own = x if gather else lax.dynamic_index_in_dim(x, me, axis, keepdims=False)
        placed.append(lax.dynamic_update_index_in_dim(out, own, me, axis))
    return placed


def gelu_exact(values):
    return jax.nn.gelu(values, approximate=False)


def gelu_back(point, grad):
    return jax.vjp(gelu_exact, point)[1](grad)[0]


def normalize(values, gain, shift):
    center = jnp.mean(values, axis=1, keepdims=True)
    offset = values - center
    spread = jnp.mean(offset * offset, axis=1, keepdims=True)
    scale = lax.rsqrt(spread + EPSILON)
    unit = offset * scale
    return (unit * gain[:, None] + shift[:, None], unit, scale)


def normalize_back(grad, unit, scale, gain):
    scaled = grad * gain[:, None]
    first = jnp.mean(scaled, axis=1, keepdims=True)
    second = jnp.mean(scaled * unit, axis=1, keepdims=True)
    return scale * (scaled - first - unit * second)


def neighbour_pairs(seqs, nch, q_count):
    pairs = []
    for s in range(seqs):
        for c in range(nch):
            q = c % q_count
            if q < q_count - 1:
                pairs.append((s * nch + c, s * nch + c + 1))
            elif s < seqs - 1:
                pairs.append((s * nch + c, (s + 1) * nch + c - (q_count - 1)))
    return pairs


def extended(x, width, pairs):
    down = [(j, i) for i, j in pairs]
    length = x.shape[-1]
    before = lax.ppermute(x[..., length - width :], ("seq", "ch"), pairs)
    after = lax.ppermute(x[..., :width], ("seq", "ch"), down)
    return jnp.concatenate([before, x, after], axis=-1)


def shifted_taps(wide, wide_ids, own_ids, offsets, border):
    length = own_ids.shape[-1]
    pieces = []
    for offset in offsets:
        lower = border + offset
        shifted = wide[:, :, lower : lower + length]
        matching = wide_ids[:, lower : lower + length] == own_ids
        pieces.append(jnp.where(matching[:, None, :], shifted, jnp.zeros_like(shifted)))
    return jnp.concatenate(pieces, axis=1)


def to_positions(x, nch, q_count):
    rows, width, length = x.shape
    if q_count > 1:
        x = x.reshape(rows, width, q_count, length // q_count).transpose(0, 2, 1, 3)
        x = x.reshape(rows * q_count, width, length // q_count)
    x = lax.all_to_all(x, "ch", 0, 0, tiled=True)
    return _join(x, nch)


def _join(x, nch):
    total, width, length = x.shape
    p = total // nch
    return x.reshape(nch, p, width, length).transpose(1, 0, 2, 3).reshape(p, nch * width, length)


def to_channels(x, nch, q_count, rows):
    p, width, length = x.shape
    x = x.reshape(p, nch, width // nch, length).transpose(1, 0, 2, 3).reshape(nch * p, width // nch, length)
    x = lax.all_to_all(x, "ch", 0, 0, tiled=True)
    if q_count > 1:
        _, width, part = x.shape
        x = x.reshape(rows, q_count, width, part).transpose(0, 2, 1, 3).reshape(rows, width, q_count * part)
    return x


def local(
    inputs,
    segment_ids,
    norm0_gain,
    norm0_shift,
    w_inner,
    b_inner,
    norm1_gain,
    norm1_shift,
    w_conv,
    b_conv,
    norm2_gain,
    norm2_shift,
    w_outer,
    b_outer,
    cotangent,
):
    nch = lax.axis_size("ch")
    seqs = lax.axis_size("seq")
    batches = lax.axis_size("batch")
    rows, dloc, length = inputs.shape
    hloc = w_conv.shape[1]
    hid = hloc * nch
    dim = dloc * nch
    if rows % nch == 0:
        q_count = 1
    else:
        q_count = nch // rows
    part = length // q_count
    border = 2 * DILATION_SPACING
    offsets = [(k - KERNEL_TAPS // 2) * DILATION_SPACING for k in range(KERNEL_TAPS)]
    back_offsets = [-o for o in offsets]
    pairs = neighbour_pairs(seqs, nch, q_count)
    me = lax.axis_index("ch")

    smalls = [norm0_gain, norm0_shift, b_inner, norm1_gain, norm1_shift, b_conv, norm2_gain, norm2_shift, b_outer]
    sidx = lax.axis_index("seq")
    halves = [
        lax.dynamic_slice_in_dim(w_inner, sidx * (dloc // seqs), dloc // seqs, 0),
        lax.dynamic_slice_in_dim(w_conv, sidx * (hloc // seqs), hloc // seqs, 1),
        lax.dynamic_slice_in_dim(w_outer, sidx * (hloc // seqs), hloc // seqs, 0),
    ]
    small_all, w_in, w_out = exchange([jnp.concatenate(smalls), halves[0], halves[2]], ("ch",), 0, gather=True)
    w_cv = lax.all_gather(halves[1], "ch", axis=0)
    cut = 0
    full = []
    for v in smalls:
        n = v.shape[0]
        full.append(small_all[:, cut : cut + n].reshape(n * nch))
        cut += n
    g0, s0, b_in, g1, s1, b_cv, g2, s2, b_out = full
    w_in = lax.all_gather(w_in, "seq", axis=1, tiled=True).reshape(dim, hid)
    w_cv = lax.all_gather(w_cv, "seq", axis=2, tiled=True).transpose(1, 0, 2, 3).reshape(KERNEL_TAPS, hid, hid)
    w_out = lax.all_gather(w_out, "seq", axis=1, tiled=True).reshape(hid, dim)

    x = to_positions(inputs, nch, q_count)
    cot = to_positions(cotangent, nch, q_count)
    prow = x.shape[0]
    if q_count == 1:
        ids = lax.dynamic_slice_in_dim(segment_ids, me * prow, prow, axis=0)
    else:
        ids = lax.dynamic_slice_in_dim(segment_ids, me // q_count, 1, axis=0)
        ids = lax.dynamic_slice_in_dim(ids, (me % q_count) * part, part, axis=1)
    own_ids = ids + 1
    wide_ids = extended(own_ids, border, pairs)

    residual = x.astype(jnp.float32)
    normed0, unit0, scale0 = normalize(residual, g0, s0)
    hidden0 = gelu_exact(normed0).astype(jnp.bfloat16)
    inner = jnp.einsum("dh,rdl->rhl", w_in, hidden0, preferred_element_type=jnp.float32) + b_in[:, None]
    normed1, unit1, scale1 = normalize(inner, g1, s1)
    hidden1 = gelu_exact(normed1).astype(jnp.bfloat16)
    wide_hidden = extended(hidden1, border, pairs)
    taps = shifted_taps(wide_hidden, wide_ids, own_ids, offsets, border)
    kernel_flat = w_cv.reshape(KERNEL_TAPS * hid, hid)
    mixed = jnp.einsum("co,rcl->rol", kernel_flat, taps, preferred_element_type=jnp.float32) + b_cv[:, None]
    normed2, unit2, scale2 = normalize(mixed, g2, s2)
    hidden2 = gelu_exact(normed2).astype(jnp.bfloat16)
    branch = jnp.einsum("hd,rhl->rdl", w_out, hidden2, preferred_element_type=jnp.float32)
    output = (residual + branch + b_out[:, None]).astype(jnp.bfloat16)
    output = to_channels(output, nch, q_count, rows)

    grad_b_outer = jnp.sum(cot.astype(jnp.float32), axis=(0, 2))
    grad_w_outer = jnp.einsum("rhl,rdl->hd", hidden2, cot, preferred_element_type=jnp.float32)
    def reduce_seq_batch(g, split_dim, after=None):
        if after is not None:
            g, _ = lax.optimization_barrier((g, after))
        g = lax.psum_scatter(g, "seq", scatter_dimension=split_dim, tiled=True)
        return lax.psum_scatter(g, "batch", scatter_dimension=split_dim, tiled=True)

    part_outer = reduce_seq_batch(grad_w_outer.reshape(nch, hloc * dim // 128, 128), 1)
    grad_hidden2 = jnp.einsum("hd,rdl->rhl", w_out, cot, preferred_element_type=jnp.float32)
    grad_normed2 = gelu_back(normed2, grad_hidden2)
    grad_norm2_gain = jnp.sum(grad_normed2 * unit2, axis=(0, 2))
    grad_norm2_shift = jnp.sum(grad_normed2, axis=(0, 2))
    grad_mixed = normalize_back(grad_normed2, unit2, scale2, g2).astype(jnp.bfloat16)
    grad_b_conv = jnp.sum(grad_mixed.astype(jnp.float32), axis=(0, 2))
    grad_w_conv = jnp.einsum(
        "rol,rkcil->okci",
        grad_mixed,
        taps.reshape(prow, KERNEL_TAPS, nch, hloc, part),
        preferred_element_type=jnp.float32,
    )
    wide_grad = extended(grad_mixed, border, pairs)
    back_taps = shifted_taps(wide_grad, wide_ids, own_ids, back_offsets, border)
    kernel_back = jnp.transpose(w_cv, (0, 2, 1)).reshape(KERNEL_TAPS * hid, hid)
    grad_hidden1 = jnp.einsum("oc,rol->rcl", kernel_back, back_taps, preferred_element_type=jnp.float32)
    grad_normed1 = gelu_back(normed1, grad_hidden1)
    grad_norm1_gain = jnp.sum(grad_normed1 * unit1, axis=(0, 2))
    grad_norm1_shift = jnp.sum(grad_normed1, axis=(0, 2))
    grad_inner = normalize_back(grad_normed1, unit1, scale1, g1).astype(jnp.bfloat16)
    grad_inner, _, output = lax.optimization_barrier((grad_inner, part_outer, output))
    grad_b_inner = jnp.sum(grad_inner.astype(jnp.float32), axis=(0, 2))
    grad_w_inner = jnp.einsum("rdl,rhl->dh", hidden0, grad_inner, preferred_element_type=jnp.float32)
    grad_hidden0 = jnp.einsum("dh,rhl->rdl", w_in, grad_inner, preferred_element_type=jnp.float32)
    grad_normed0 = gelu_back(normed0, grad_hidden0)
    grad_norm0_gain = jnp.sum(grad_normed0 * unit0, axis=(0, 2))
    grad_norm0_shift = jnp.sum(grad_normed0, axis=(0, 2))
    input_grad = (cot.astype(jnp.float32) + normalize_back(grad_normed0, unit0, scale0, g0)).astype(jnp.bfloat16)

    input_grad = to_channels(input_grad, nch, q_count, rows)

    vectors = [
        grad_norm0_gain,
        grad_norm0_shift,
        grad_b_inner,
        grad_norm1_gain,
        grad_norm1_shift,
        grad_b_conv,
        grad_norm2_gain,
        grad_norm2_shift,
        grad_b_outer,
    ]
    flat = jnp.concatenate([v.reshape(nch, -1) for v in vectors], axis=1)
    vec_len = flat.shape[1]
    vec_rows = -(-vec_len // hid)
    vec_rows = -(-(dloc + vec_rows) // 64) * 64 - dloc
    flat = jnp.pad(flat, ((0, 0), (0, vec_rows * hid - vec_len))).reshape(nch, vec_rows, hid)
    inner_plus = jnp.concatenate([grad_w_inner.reshape(nch, dloc, hid), flat], axis=1)
    inner_plus = inner_plus.reshape(nch, (dloc + vec_rows) * hid // 128, 128)

    conv_tail = grad_w_conv.shape[1:]
    part_conv = reduce_seq_batch(grad_w_conv.reshape(hid, math.prod(conv_tail) // 128, 128), 0, part_outer)
    part_conv = part_conv.reshape((part_conv.shape[0],) + conv_tail)
    part_inner = reduce_seq_batch(inner_plus, 1, part_conv)
    parts = [part_outer, part_conv, part_inner]
    parts = exchange(parts, ("ch",), 1, axes=(0, 2, 0), reduce=True)
    piece_shapes = [p.shape for p in parts]
    parts = [p.reshape(p.size // 128, 128) if p.size % 128 == 0 else p for p in parts]
    parts = [lax.all_gather(p, "batch", axis=0) for p in parts]
    parts = [
        lax.all_gather(p, "seq", axis=0, tiled=True).reshape((seqs * batches,) + shape)
        for p, shape in zip(parts, piece_shapes)
    ]
    red_w_outer = parts[0].reshape(hloc, dim)
    red_w_conv = parts[1].reshape(hid, KERNEL_TAPS, hloc).transpose(1, 2, 0)
    red_inner = parts[2].reshape(dloc + vec_rows, hid)
    red_w_inner = red_inner[:dloc]
    mine = red_inner[dloc:].reshape(-1)[:vec_len]
    reds = []
    cut = 0
    for v in vectors:
        n = v.shape[0] // nch
        reds.append(mine[cut : cut + n])
        cut += n
    return (
        output,
        input_grad,
        reds[0],
        reds[1],
        red_w_inner,
        reds[2],
        reds[3],
        reds[4],
        red_w_conv,
        reds[5],
        reds[6],
        reds[7],
        red_w_outer,
        reds[8],
    )


def solution(mesh):
    return jax.shard_map(
        local,
        mesh=mesh,
        in_specs=(
            P("batch", "ch", "seq"),
            P("batch", "seq"),
            P("ch"),
            P("ch"),
            P("ch", None),
            P("ch"),
            P("ch"),
            P("ch"),
            P(None, "ch", None),
            P("ch"),
            P("ch"),
            P("ch"),
            P("ch", None),
            P("ch"),
            P("batch", "ch", "seq"),
        ),
        out_specs=(
            P("batch", "ch", "seq"),
            P("batch", "ch", "seq"),
            P("ch"),
            P("ch"),
            P("ch", None),
            P("ch"),
            P("ch"),
            P("ch"),
            P(None, "ch", None),
            P("ch"),
            P("ch"),
            P("ch"),
            P("ch", None),
            P("ch"),
        ),
        check_vma=False,
    )
```

```python
import functools
import math

import jax
import jax.numpy as jnp
from jax import lax
from jax.experimental import pallas as pl
from jax.experimental.pallas import tpu as pltpu
from jax.sharding import PartitionSpec as P

KERNEL_TAPS = 5
DILATION_SPACING = 32


EPSILON = 1e-05


MESH_AXES = ("batch", "seq", "ch")
MESH_ID = pl.DeviceIdType.MESH


def _group_index(group, sizes, coords):
    me = 0
    for a in group:
        me = me * sizes[a] + coords[a]
    return me


def _exchange_kernel(sizes, group, gather, reduce, axes, *refs):
    count_arrays = len(axes)
    x_refs = refs[:count_arrays]
    o_refs = refs[count_arrays : 2 * count_arrays]
    send_sem, recv_sem = refs[2 * count_arrays :]
    coords = {a: lax.axis_index(a) for a in MESH_AXES}
    me = _group_index(group, sizes, coords)
    count = math.prod(sizes[a] for a in group)

    def device(index):
        where = dict(coords)
        rest = index
        for a in reversed(group):
            where[a] = lax.rem(rest, sizes[a])
            rest = rest // sizes[a]
        return tuple(where[a] for a in MESH_AXES)

    barrier = pltpu.get_barrier_semaphore()
    for j in range(1, count):
        pl.semaphore_signal(barrier, 1, device_id=device(lax.rem(me + j, count)), device_id_type=MESH_ID)
    pl.semaphore_wait(barrier, count - 1)
    copies = []
    for j in range(1, count):
        peer = lax.rem(me + j, count)
        for i in range(count_arrays):
            lead = (slice(None),) * axes[i]
            if gather:
                src, dst = x_refs[i], o_refs[i].at[me]
            else:
                slot = (j - 1) if reduce else me
                src = x_refs[i].at[lead + (pl.ds(peer, 1),)]
                dst = o_refs[i].at[lead + (pl.ds(slot, 1),)]
            copy = pltpu.make_async_remote_copy(
                src_ref=src,
                dst_ref=dst,
                send_sem=send_sem.at[i, j - 1],
                recv_sem=recv_sem.at[i, j - 1],
                device_id=device(peer),
                device_id_type=MESH_ID,
            )
            copy.start()
            copies.append(copy)
    for copy in copies:
        copy.wait()


def exchange(xs, group, collective_id, gather=False, axes=None, reduce=False):
    sizes = {a: lax.axis_size(a) for a in MESH_AXES}
    count = math.prod(sizes[a] for a in group)
    axes = tuple(axes or (0,) * len(xs))
    if count == 1:
        return [x[None] if gather else x for x in xs]
    shapes = [jax.ShapeDtypeStruct((count,) + x.shape if gather else x.shape, x.dtype) for x in xs]
    if reduce:
        shapes = [
            jax.ShapeDtypeStruct(x.shape[:a] + (count - 1,) + x.shape[a + 1 :], x.dtype) for x, a in zip(xs, axes)
        ]
    moved = sum(x.size * x.dtype.itemsize * (count if gather else 1) for x in xs)
    outs = pl.pallas_call(
        functools.partial(_exchange_kernel, sizes, group, gather, reduce, axes),
        out_shape=shapes,
        in_specs=[pl.BlockSpec(memory_space=pl.ANY)] * len(xs),
        out_specs=[pl.BlockSpec(memory_space=pl.ANY)] * len(xs),
        scratch_shapes=[
            pltpu.SemaphoreType.DMA((len(xs), count - 1)),
            pltpu.SemaphoreType.DMA((len(xs), count - 1)),
        ],
        compiler_params=pltpu.CompilerParams(collective_id=collective_id, has_side_effects=True),
        cost_estimate=pl.CostEstimate(flops=0, transcendentals=0, bytes_accessed=2 * moved),
    )(*xs)
    me = _group_index(group, sizes, {a: lax.axis_index(a) for a in group})
    placed = []
    if reduce:
        for x, out, axis in zip(xs, outs, axes):
            own = lax.dynamic_index_in_dim(x, me, axis, keepdims=False)
            placed.append(own + jnp.sum(out, axis=axis))
        return placed
    for x, out, axis in zip(xs, outs, axes):
        own = x if gather else lax.dynamic_index_in_dim(x, me, axis, keepdims=False)
        placed.append(lax.dynamic_update_index_in_dim(out, own, me, axis))
    return placed


def gelu_exact(values):
    return jax.nn.gelu(values, approximate=False)


def gelu_back(point, grad):
    return jax.vjp(gelu_exact, point)[1](grad)[0]


def normalize(values, gain, shift):
    center = jnp.mean(values, axis=1, keepdims=True)
    offset = values - center
    spread = jnp.mean(offset * offset, axis=1, keepdims=True)
    scale = lax.rsqrt(spread + EPSILON)
    unit = offset * scale
    return (unit * gain[:, None] + shift[:, None], unit, scale)


def normalize_back(grad, unit, scale, gain):
    scaled = grad * gain[:, None]
    first = jnp.mean(scaled, axis=1, keepdims=True)
    second = jnp.mean(scaled * unit, axis=1, keepdims=True)
    return scale * (scaled - first - unit * second)


def neighbour_pairs(seqs, nch, q_count):
    pairs = []
    for s in range(seqs):
        for c in range(nch):
            q = c % q_count
            if q < q_count - 1:
                pairs.append((s * nch + c, s * nch + c + 1))
            elif s < seqs - 1:
                pairs.append((s * nch + c, (s + 1) * nch + c - (q_count - 1)))
    return pairs


def extended(x, width, pairs):
    down = [(j, i) for i, j in pairs]
    length = x.shape[-1]
    before = lax.ppermute(x[..., length - width :], ("seq", "ch"), pairs)
    after = lax.ppermute(x[..., :width], ("seq", "ch"), down)
    return jnp.concatenate([before, x, after], axis=-1)


def shifted_taps(wide, wide_ids, own_ids, offsets, border):
    length = own_ids.shape[-1]
    pieces = []
    for offset in offsets:
        lower = border + offset
        shifted = wide[:, :, lower : lower + length]
        matching = wide_ids[:, lower : lower + length] == own_ids
        pieces.append(jnp.where(matching[:, None, :], shifted, jnp.zeros_like(shifted)))
    return jnp.concatenate(pieces, axis=1)


def to_positions(x, nch, q_count):
    rows, width, length = x.shape
    if q_count > 1:
        x = x.reshape(rows, width, q_count, length // q_count).transpose(0, 2, 1, 3)
        x = x.reshape(rows * q_count, width, length // q_count)
    x = lax.all_to_all(x, "ch", 0, 0, tiled=True)
    return _join(x, nch)


def _join(x, nch):
    total, width, length = x.shape
    p = total // nch
    return x.reshape(nch, p, width, length).transpose(1, 0, 2, 3).reshape(p, nch * width, length)


def to_channels(x, nch, q_count, rows):
    p, width, length = x.shape
    x = x.reshape(p, nch, width // nch, length).transpose(1, 0, 2, 3).reshape(nch * p, width // nch, length)
    x = lax.all_to_all(x, "ch", 0, 0, tiled=True)
    if q_count > 1:
        _, width, part = x.shape
        x = x.reshape(rows, q_count, width, part).transpose(0, 2, 1, 3).reshape(rows, width, q_count * part)
    return x


def local(
    inputs,
    segment_ids,
    norm0_gain,
    norm0_shift,
    w_inner,
    b_inner,
    norm1_gain,
    norm1_shift,
    w_conv,
    b_conv,
    norm2_gain,
    norm2_shift,
    w_outer,
    b_outer,
    cotangent,
):
    nch = lax.axis_size("ch")
    seqs = lax.axis_size("seq")
    batches = lax.axis_size("batch")
    rows, dloc, length = inputs.shape
    hloc = w_conv.shape[1]
    hid = hloc * nch
    dim = dloc * nch
    if rows % nch == 0:
        q_count = 1
    else:
        q_count = nch // rows
    part = length // q_count
    border = 2 * DILATION_SPACING
    offsets = [(k - KERNEL_TAPS // 2) * DILATION_SPACING for k in range(KERNEL_TAPS)]
    back_offsets = [-o for o in offsets]
    pairs = neighbour_pairs(seqs, nch, q_count)
    me = lax.axis_index("ch")

    smalls = [norm0_gain, norm0_shift, b_inner, norm1_gain, norm1_shift, b_conv, norm2_gain, norm2_shift, b_outer]
    sidx = lax.axis_index("seq")
    halves = [
        lax.dynamic_slice_in_dim(w_inner, sidx * (dloc // seqs), dloc // seqs, 0),
        lax.dynamic_slice_in_dim(w_conv, sidx * (hloc // seqs), hloc // seqs, 1),
        lax.dynamic_slice_in_dim(w_outer, sidx * (hloc // seqs), hloc // seqs, 0),
    ]
    small_all, w_in, w_out = exchange([jnp.concatenate(smalls), halves[0], halves[2]], ("ch",), 0, gather=True)
    w_cv = lax.all_gather(halves[1], "ch", axis=0)
    cut = 0
    full = []
    for v in smalls:
        n = v.shape[0]
        full.append(small_all[:, cut : cut + n].reshape(n * nch))
        cut += n
    g0, s0, b_in, g1, s1, b_cv, g2, s2, b_out = full
    w_in = lax.all_gather(w_in, "seq", axis=1, tiled=True).reshape(dim, hid)
    w_cv = lax.all_gather(w_cv, "seq", axis=2, tiled=True).transpose(1, 0, 2, 3).reshape(KERNEL_TAPS, hid, hid)
    w_out = lax.all_gather(w_out, "seq", axis=1, tiled=True).reshape(hid, dim)

    x = to_positions(inputs, nch, q_count)
    cot = to_positions(cotangent, nch, q_count)
    prow = x.shape[0]
    if q_count == 1:
        ids = lax.dynamic_slice_in_dim(segment_ids, me * prow, prow, axis=0)
    else:
        ids = lax.dynamic_slice_in_dim(segment_ids, me // q_count, 1, axis=0)
        ids = lax.dynamic_slice_in_dim(ids, (me % q_count) * part, part, axis=1)
    own_ids = ids + 1
    wide_ids = extended(own_ids, border, pairs)

    residual = x.astype(jnp.float32)
    normed0, unit0, scale0 = normalize(residual, g0, s0)
    hidden0 = gelu_exact(normed0).astype(jnp.bfloat16)
    inner = jnp.einsum("dh,rdl->rhl", w_in, hidden0, preferred_element_type=jnp.float32) + b_in[:, None]
    normed1, unit1, scale1 = normalize(inner, g1, s1)
    hidden1 = gelu_exact(normed1).astype(jnp.bfloat16)
    wide_hidden = extended(hidden1, border, pairs)
    taps = shifted_taps(wide_hidden, wide_ids, own_ids, offsets, border)
    kernel_flat = w_cv.reshape(KERNEL_TAPS * hid, hid)
    mixed = jnp.einsum("co,rcl->rol", kernel_flat, taps, preferred_element_type=jnp.float32) + b_cv[:, None]
    normed2, unit2, scale2 = normalize(mixed, g2, s2)
    hidden2 = gelu_exact(normed2).astype(jnp.bfloat16)
    branch = jnp.einsum("hd,rhl->rdl", w_out, hidden2, preferred_element_type=jnp.float32)
    output = (residual + branch + b_out[:, None]).astype(jnp.bfloat16)
    output = to_channels(output, nch, q_count, rows)

    grad_b_outer = jnp.sum(cot.astype(jnp.float32), axis=(0, 2))
    grad_w_outer = jnp.einsum("rhl,rdl->hd", hidden2, cot, preferred_element_type=jnp.float32)
    def reduce_seq_batch(g, split_dim, after=None):
        if after is not None:
            g, _ = lax.optimization_barrier((g, after))
        g = lax.psum_scatter(g, "seq", scatter_dimension=split_dim, tiled=True)
        return lax.psum_scatter(g, "batch", scatter_dimension=split_dim, tiled=True)

    part_outer = reduce_seq_batch(grad_w_outer.reshape(nch, hloc * dim // 128, 128), 1)
    grad_hidden2 = jnp.einsum("hd,rdl->rhl", w_out, cot, preferred_element_type=jnp.float32)
    grad_normed2 = gelu_back(normed2, grad_hidden2)
    grad_norm2_gain = jnp.sum(grad_normed2 * unit2, axis=(0, 2))
    grad_norm2_shift = jnp.sum(grad_normed2, axis=(0, 2))
    grad_mixed = normalize_back(grad_normed2, unit2, scale2, g2).astype(jnp.bfloat16)
    grad_b_conv = jnp.sum(grad_mixed.astype(jnp.float32), axis=(0, 2))
    grad_w_conv = jnp.einsum(
        "rol,rkcil->okci",
        grad_mixed,
        taps.reshape(prow, KERNEL_TAPS, nch, hloc, part),
        preferred_element_type=jnp.float32,
    )
    wide_grad = extended(grad_mixed, border, pairs)
    back_taps = shifted_taps(wide_grad, wide_ids, own_ids, back_offsets, border)
    kernel_back = jnp.transpose(w_cv, (0, 2, 1)).reshape(KERNEL_TAPS * hid, hid)
    grad_hidden1 = jnp.einsum("oc,rol->rcl", kernel_back, back_taps, preferred_element_type=jnp.float32)
    grad_normed1 = gelu_back(normed1, grad_hidden1)
    grad_norm1_gain = jnp.sum(grad_normed1 * unit1, axis=(0, 2))
    grad_norm1_shift = jnp.sum(grad_normed1, axis=(0, 2))
    grad_inner = normalize_back(grad_normed1, unit1, scale1, g1).astype(jnp.bfloat16)
    grad_inner, _, output = lax.optimization_barrier((grad_inner, part_outer, output))
    grad_b_inner = jnp.sum(grad_inner.astype(jnp.float32), axis=(0, 2))
    grad_w_inner = jnp.einsum("rdl,rhl->dh", hidden0, grad_inner, preferred_element_type=jnp.float32)
    grad_hidden0 = jnp.einsum("dh,rhl->rdl", w_in, grad_inner, preferred_element_type=jnp.float32)
    grad_normed0 = gelu_back(normed0, grad_hidden0)
    grad_norm0_gain = jnp.sum(grad_normed0 * unit0, axis=(0, 2))
    grad_norm0_shift = jnp.sum(grad_normed0, axis=(0, 2))
    input_grad = (cot.astype(jnp.float32) + normalize_back(grad_normed0, unit0, scale0, g0)).astype(jnp.bfloat16)

    input_grad = to_channels(input_grad, nch, q_count, rows)

    vectors = [
        grad_norm0_gain,
        grad_norm0_shift,
        grad_b_inner,
        grad_norm1_gain,
        grad_norm1_shift,
        grad_b_conv,
        grad_norm2_gain,
        grad_norm2_shift,
        grad_b_outer,
    ]
    flat = jnp.concatenate([v.reshape(nch, -1) for v in vectors], axis=1)
    vec_len = flat.shape[1]
    vec_rows = -(-vec_len // hid)
    vec_rows = -(-(dloc + vec_rows) // 64) * 64 - dloc
    flat = jnp.pad(flat, ((0, 0), (0, vec_rows * hid - vec_len))).reshape(nch, vec_rows, hid)
    inner_plus = jnp.concatenate([grad_w_inner.reshape(nch, dloc, hid), flat], axis=1)
    inner_plus = inner_plus.reshape(nch, (dloc + vec_rows) * hid // 128, 128)

    conv_tail = grad_w_conv.shape[1:]
    part_conv = reduce_seq_batch(grad_w_conv.reshape(hid, math.prod(conv_tail) // 128, 128), 0, part_outer)
    part_conv = part_conv.reshape((part_conv.shape[0],) + conv_tail)
    part_inner = reduce_seq_batch(inner_plus, 1, part_conv)
    parts = [part_outer, part_conv, part_inner]
    parts = exchange(parts, ("ch",), 1, axes=(0, 2, 0), reduce=True)
    piece_shapes = [p.shape for p in parts]
    piece_sizes = [p.size for p in parts]
    joined = jnp.concatenate([p.reshape(-1) for p in parts])
    joined_len = joined.shape[0]
    joined_pad = -(-joined_len // 1024) * 1024
    joined = jnp.pad(joined, (0, joined_pad - joined_len)).reshape(joined_pad // 128, 128)
    joined = lax.all_gather(joined, "batch", axis=0)
    joined = lax.all_gather(joined, "seq", axis=0, tiled=True).reshape(seqs * batches, joined_pad)
    parts = []
    cut = 0
    for size, shape in zip(piece_sizes, piece_shapes):
        parts.append(joined[:, cut : cut + size].reshape((seqs * batches,) + shape))
        cut += size
    red_w_outer = parts[0].reshape(hloc, dim)
    red_w_conv = parts[1].reshape(hid, KERNEL_TAPS, hloc).transpose(1, 2, 0)
    red_inner = parts[2].reshape(dloc + vec_rows, hid)
    red_w_inner = red_inner[:dloc]
    mine = red_inner[dloc:].reshape(-1)[:vec_len]
    reds = []
    cut = 0
    for v in vectors:
        n = v.shape[0] // nch
        reds.append(mine[cut : cut + n])
        cut += n
    return (
        output,
        input_grad,
        reds[0],
        reds[1],
        red_w_inner,
        reds[2],
        reds[3],
        reds[4],
        red_w_conv,
        reds[5],
        reds[6],
        reds[7],
        red_w_outer,
        reds[8],
    )


def solution(mesh):
    return jax.shard_map(
        local,
        mesh=mesh,
        in_specs=(
            P("batch", "ch", "seq"),
            P("batch", "seq"),
            P("ch"),
            P("ch"),
            P("ch", None),
            P("ch"),
            P("ch"),
            P("ch"),
            P(None, "ch", None),
            P("ch"),
            P("ch"),
            P("ch"),
            P("ch", None),
            P("ch"),
            P("batch", "ch", "seq"),
        ),
        out_specs=(
            P("batch", "ch", "seq"),
            P("batch", "ch", "seq"),
            P("ch"),
            P("ch"),
            P("ch", None),
            P("ch"),
            P("ch"),
            P("ch"),
            P(None, "ch", None),
            P("ch"),
            P("ch"),
            P("ch"),
            P("ch", None),
            P("ch"),
        ),
        check_vma=False,
    )
```

```python
import functools
import math

import jax
import jax.numpy as jnp
from jax import lax
from jax.experimental import pallas as pl
from jax.experimental.pallas import tpu as pltpu
from jax.sharding import PartitionSpec as P

KERNEL_TAPS = 5
DILATION_SPACING = 32


EPSILON = 1e-05


MESH_AXES = ("batch", "seq", "ch")
MESH_ID = pl.DeviceIdType.MESH


def _group_index(group, sizes, coords):
    me = 0
    for a in group:
        me = me * sizes[a] + coords[a]
    return me


def _exchange_kernel(sizes, group, gather, reduce, axes, *refs):
    count_arrays = len(axes)
    x_refs = refs[:count_arrays]
    o_refs = refs[count_arrays : 2 * count_arrays]
    send_sem, recv_sem = refs[2 * count_arrays :]
    coords = {a: lax.axis_index(a) for a in MESH_AXES}
    me = _group_index(group, sizes, coords)
    count = math.prod(sizes[a] for a in group)

    def device(index):
        where = dict(coords)
        rest = index
        for a in reversed(group):
            where[a] = lax.rem(rest, sizes[a])
            rest = rest // sizes[a]
        return tuple(where[a] for a in MESH_AXES)

    barrier = pltpu.get_barrier_semaphore()
    for j in range(1, count):
        pl.semaphore_signal(barrier, 1, device_id=device(lax.rem(me + j, count)), device_id_type=MESH_ID)
    pl.semaphore_wait(barrier, count - 1)
    copies = []
    for j in range(1, count):
        peer = lax.rem(me + j, count)
        for i in range(count_arrays):
            lead = (slice(None),) * axes[i]
            if gather:
                src, dst = x_refs[i], o_refs[i].at[me]
            else:
                slot = (j - 1) if reduce else me
                src = x_refs[i].at[lead + (pl.ds(peer, 1),)]
                dst = o_refs[i].at[lead + (pl.ds(slot, 1),)]
            copy = pltpu.make_async_remote_copy(
                src_ref=src,
                dst_ref=dst,
                send_sem=send_sem.at[i, j - 1],
                recv_sem=recv_sem.at[i, j - 1],
                device_id=device(peer),
                device_id_type=MESH_ID,
            )
            copy.start()
            copies.append(copy)
    for copy in copies:
        copy.wait()


def exchange(xs, group, collective_id, gather=False, axes=None, reduce=False):
    sizes = {a: lax.axis_size(a) for a in MESH_AXES}
    count = math.prod(sizes[a] for a in group)
    axes = tuple(axes or (0,) * len(xs))
    if count == 1:
        return [x[None] if gather else x for x in xs]
    shapes = [jax.ShapeDtypeStruct((count,) + x.shape if gather else x.shape, x.dtype) for x in xs]
    if reduce:
        shapes = [
            jax.ShapeDtypeStruct(x.shape[:a] + (count - 1,) + x.shape[a + 1 :], x.dtype) for x, a in zip(xs, axes)
        ]
    moved = sum(x.size * x.dtype.itemsize * (count if gather else 1) for x in xs)
    outs = pl.pallas_call(
        functools.partial(_exchange_kernel, sizes, group, gather, reduce, axes),
        out_shape=shapes,
        in_specs=[pl.BlockSpec(memory_space=pl.ANY)] * len(xs),
        out_specs=[pl.BlockSpec(memory_space=pl.ANY)] * len(xs),
        scratch_shapes=[
            pltpu.SemaphoreType.DMA((len(xs), count - 1)),
            pltpu.SemaphoreType.DMA((len(xs), count - 1)),
        ],
        compiler_params=pltpu.CompilerParams(collective_id=collective_id, has_side_effects=True),
        cost_estimate=pl.CostEstimate(flops=0, transcendentals=0, bytes_accessed=2 * moved),
    )(*xs)
    me = _group_index(group, sizes, {a: lax.axis_index(a) for a in group})
    placed = []
    if reduce:
        for x, out, axis in zip(xs, outs, axes):
            own = lax.dynamic_index_in_dim(x, me, axis, keepdims=False)
            placed.append(own + jnp.sum(out, axis=axis))
        return placed
    for x, out, axis in zip(xs, outs, axes):
        own = x if gather else lax.dynamic_index_in_dim(x, me, axis, keepdims=False)
        placed.append(lax.dynamic_update_index_in_dim(out, own, me, axis))
    return placed


def gelu_exact(values):
    return jax.nn.gelu(values, approximate=False)


def gelu_back(point, grad):
    return jax.vjp(gelu_exact, point)[1](grad)[0]


def normalize(values, gain, shift):
    center = jnp.mean(values, axis=1, keepdims=True)
    offset = values - center
    spread = jnp.mean(offset * offset, axis=1, keepdims=True)
    scale = lax.rsqrt(spread + EPSILON)
    unit = offset * scale
    return (unit * gain[:, None] + shift[:, None], unit, scale)


def normalize_back(grad, unit, scale, gain):
    scaled = grad * gain[:, None]
    first = jnp.mean(scaled, axis=1, keepdims=True)
    second = jnp.mean(scaled * unit, axis=1, keepdims=True)
    return scale * (scaled - first - unit * second)


def neighbour_pairs(seqs, nch, q_count):
    pairs = []
    for s in range(seqs):
        for c in range(nch):
            q = c % q_count
            if q < q_count - 1:
                pairs.append((s * nch + c, s * nch + c + 1))
            elif s < seqs - 1:
                pairs.append((s * nch + c, (s + 1) * nch + c - (q_count - 1)))
    return pairs


def extended(x, width, pairs):
    down = [(j, i) for i, j in pairs]
    length = x.shape[-1]
    before = lax.ppermute(x[..., length - width :], ("seq", "ch"), pairs)
    after = lax.ppermute(x[..., :width], ("seq", "ch"), down)
    return jnp.concatenate([before, x, after], axis=-1)


def shifted_taps(wide, wide_ids, own_ids, offsets, border):
    length = own_ids.shape[-1]
    pieces = []
    for offset in offsets:
        lower = border + offset
        shifted = wide[:, :, lower : lower + length]
        matching = wide_ids[:, lower : lower + length] == own_ids
        pieces.append(jnp.where(matching[:, None, :], shifted, jnp.zeros_like(shifted)))
    return jnp.concatenate(pieces, axis=1)


def to_positions(x, nch, q_count):
    rows, width, length = x.shape
    if q_count > 1:
        x = x.reshape(rows, width, q_count, length // q_count).transpose(0, 2, 1, 3)
        x = x.reshape(rows * q_count, width, length // q_count)
    x = lax.all_to_all(x, "ch", 0, 0, tiled=True)
    return _join(x, nch)


def _join(x, nch):
    total, width, length = x.shape
    p = total // nch
    return x.reshape(nch, p, width, length).transpose(1, 0, 2, 3).reshape(p, nch * width, length)


def to_channels(x, nch, q_count, rows):
    p, width, length = x.shape
    x = x.reshape(p, nch, width // nch, length).transpose(1, 0, 2, 3).reshape(nch * p, width // nch, length)
    x = lax.all_to_all(x, "ch", 0, 0, tiled=True)
    if q_count > 1:
        _, width, part = x.shape
        x = x.reshape(rows, q_count, width, part).transpose(0, 2, 1, 3).reshape(rows, width, q_count * part)
    return x


def local(
    inputs,
    segment_ids,
    norm0_gain,
    norm0_shift,
    w_inner,
    b_inner,
    norm1_gain,
    norm1_shift,
    w_conv,
    b_conv,
    norm2_gain,
    norm2_shift,
    w_outer,
    b_outer,
    cotangent,
):
    nch = lax.axis_size("ch")
    seqs = lax.axis_size("seq")
    batches = lax.axis_size("batch")
    rows, dloc, length = inputs.shape
    hloc = w_conv.shape[1]
    hid = hloc * nch
    dim = dloc * nch
    if rows % nch == 0:
        q_count = 1
    else:
        q_count = nch // rows
    part = length // q_count
    border = 2 * DILATION_SPACING
    offsets = [(k - KERNEL_TAPS // 2) * DILATION_SPACING for k in range(KERNEL_TAPS)]
    back_offsets = [-o for o in offsets]
    pairs = neighbour_pairs(seqs, nch, q_count)
    me = lax.axis_index("ch")

    smalls = [norm0_gain, norm0_shift, b_inner, norm1_gain, norm1_shift, b_conv, norm2_gain, norm2_shift, b_outer]
    sidx = lax.axis_index("seq")
    halves = [
        lax.dynamic_slice_in_dim(w_inner, sidx * (dloc // seqs), dloc // seqs, 0),
        lax.dynamic_slice_in_dim(w_conv, sidx * (hloc // seqs), hloc // seqs, 1),
        lax.dynamic_slice_in_dim(w_outer, sidx * (hloc // seqs), hloc // seqs, 0),
    ]
    small_all, w_in, w_out = exchange([jnp.concatenate(smalls), halves[0], halves[2]], ("ch",), 0, gather=True)
    w_cv = lax.all_gather(halves[1], "ch", axis=0)
    cut = 0
    full = []
    for v in smalls:
        n = v.shape[0]
        full.append(small_all[:, cut : cut + n].reshape(n * nch))
        cut += n
    g0, s0, b_in, g1, s1, b_cv, g2, s2, b_out = full
    w_in = lax.all_gather(w_in, "seq", axis=1, tiled=True).reshape(dim, hid)
    w_cv = lax.all_gather(w_cv, "seq", axis=2, tiled=True).transpose(1, 0, 2, 3).reshape(KERNEL_TAPS, hid, hid)
    w_out = lax.all_gather(w_out, "seq", axis=1, tiled=True).reshape(hid, dim)

    x = to_positions(inputs, nch, q_count)
    cot = to_positions(cotangent, nch, q_count)
    prow = x.shape[0]
    if q_count == 1:
        ids = lax.dynamic_slice_in_dim(segment_ids, me * prow, prow, axis=0)
    else:
        ids = lax.dynamic_slice_in_dim(segment_ids, me // q_count, 1, axis=0)
        ids = lax.dynamic_slice_in_dim(ids, (me % q_count) * part, part, axis=1)
    own_ids = ids + 1
    wide_ids = extended(own_ids, border, pairs)

    residual = x.astype(jnp.float32)
    normed0, unit0, scale0 = normalize(residual, g0, s0)
    hidden0 = gelu_exact(normed0).astype(jnp.bfloat16)
    inner = jnp.einsum("dh,rdl->rhl", w_in, hidden0, preferred_element_type=jnp.float32) + b_in[:, None]
    normed1, unit1, scale1 = normalize(inner, g1, s1)
    hidden1 = gelu_exact(normed1).astype(jnp.bfloat16)
    wide_hidden = extended(hidden1, border, pairs)
    taps = shifted_taps(wide_hidden, wide_ids, own_ids, offsets, border)
    kernel_flat = w_cv.reshape(KERNEL_TAPS * hid, hid)
    mixed = jnp.einsum("co,rcl->rol", kernel_flat, taps, preferred_element_type=jnp.float32) + b_cv[:, None]
    normed2, unit2, scale2 = normalize(mixed, g2, s2)
    hidden2 = gelu_exact(normed2).astype(jnp.bfloat16)
    branch = jnp.einsum("hd,rhl->rdl", w_out, hidden2, preferred_element_type=jnp.float32)
    output = (residual + branch + b_out[:, None]).astype(jnp.bfloat16)
    output = to_channels(output, nch, q_count, rows)

    grad_b_outer = jnp.sum(cot.astype(jnp.float32), axis=(0, 2))
    grad_w_outer = jnp.einsum("rhl,rdl->hd", hidden2, cot, preferred_element_type=jnp.float32)
    def reduce_seq_batch(g, split_dim, after=None):
        if after is not None:
            g, _ = lax.optimization_barrier((g, after))
        g = lax.psum_scatter(g, "seq", scatter_dimension=split_dim, tiled=True)
        return lax.psum_scatter(g, "batch", scatter_dimension=split_dim, tiled=True)

    part_outer = reduce_seq_batch(grad_w_outer.reshape(nch, hloc * dim // 128, 128), 1)
    grad_hidden2 = jnp.einsum("hd,rdl->rhl", w_out, cot, preferred_element_type=jnp.float32)
    grad_normed2 = gelu_back(normed2, grad_hidden2)
    grad_norm2_gain = jnp.sum(grad_normed2 * unit2, axis=(0, 2))
    grad_norm2_shift = jnp.sum(grad_normed2, axis=(0, 2))
    grad_mixed = normalize_back(grad_normed2, unit2, scale2, g2).astype(jnp.bfloat16)
    grad_b_conv = jnp.sum(grad_mixed.astype(jnp.float32), axis=(0, 2))
    grad_w_conv = jnp.einsum(
        "rol,rkcil->okci",
        grad_mixed,
        taps.reshape(prow, KERNEL_TAPS, nch, hloc, part),
        preferred_element_type=jnp.float32,
    )
    wide_grad = extended(grad_mixed, border, pairs)
    back_taps = shifted_taps(wide_grad, wide_ids, own_ids, back_offsets, border)
    kernel_back = jnp.transpose(w_cv, (0, 2, 1)).reshape(KERNEL_TAPS * hid, hid)
    grad_hidden1 = jnp.einsum("oc,rol->rcl", kernel_back, back_taps, preferred_element_type=jnp.float32)
    grad_normed1 = gelu_back(normed1, grad_hidden1)
    grad_norm1_gain = jnp.sum(grad_normed1 * unit1, axis=(0, 2))
    grad_norm1_shift = jnp.sum(grad_normed1, axis=(0, 2))
    grad_inner = normalize_back(grad_normed1, unit1, scale1, g1).astype(jnp.bfloat16)
    grad_inner, _, output = lax.optimization_barrier((grad_inner, part_outer, output))
    grad_b_inner = jnp.sum(grad_inner.astype(jnp.float32), axis=(0, 2))
    grad_w_inner = jnp.einsum("rdl,rhl->dh", hidden0, grad_inner, preferred_element_type=jnp.float32)
    grad_hidden0 = jnp.einsum("dh,rhl->rdl", w_in, grad_inner, preferred_element_type=jnp.float32)
    grad_normed0 = gelu_back(normed0, grad_hidden0)
    grad_norm0_gain = jnp.sum(grad_normed0 * unit0, axis=(0, 2))
    grad_norm0_shift = jnp.sum(grad_normed0, axis=(0, 2))
    input_grad = (cot.astype(jnp.float32) + normalize_back(grad_normed0, unit0, scale0, g0)).astype(jnp.bfloat16)


    vectors = [
        grad_norm0_gain,
        grad_norm0_shift,
        grad_b_inner,
        grad_norm1_gain,
        grad_norm1_shift,
        grad_b_conv,
        grad_norm2_gain,
        grad_norm2_shift,
        grad_b_outer,
    ]
    flat = jnp.concatenate([v.reshape(nch, -1) for v in vectors], axis=1)
    vec_len = flat.shape[1]
    vec_rows = -(-vec_len // hid)
    vec_rows = -(-(dloc + vec_rows) // 64) * 64 - dloc
    flat = jnp.pad(flat, ((0, 0), (0, vec_rows * hid - vec_len))).reshape(nch, vec_rows, hid)
    inner_plus = jnp.concatenate([grad_w_inner.reshape(nch, dloc, hid), flat], axis=1)
    inner_plus = inner_plus.reshape(nch, (dloc + vec_rows) * hid // 128, 128)

    conv_tail = grad_w_conv.shape[1:]
    def finish(part, axis, cid):
        part = exchange([part], ("ch",), cid, axes=(axis,), reduce=True)[0]
        shape = part.shape
        if part.size % 128 == 0:
            part = part.reshape(part.size // 128, 128)
        part = lax.all_gather(part, "batch", axis=0)
        return lax.all_gather(part, "seq", axis=0, tiled=True).reshape((seqs * batches,) + shape)

    part_conv = reduce_seq_batch(grad_w_conv.reshape(hid, math.prod(conv_tail) // 128, 128), 0, part_outer)
    part_conv = part_conv.reshape((part_conv.shape[0],) + conv_tail)
    red_outer = finish(part_outer, 0, 1)
    inner_plus, red_outer = lax.optimization_barrier((inner_plus, red_outer))
    part_inner = reduce_seq_batch(inner_plus, 1, part_conv)
    red_conv = finish(part_conv, 2, 2)
    input_grad, red_conv = lax.optimization_barrier((input_grad, red_conv))
    input_grad = to_channels(input_grad, nch, q_count, rows)
    red_inner = finish(part_inner, 0, 3)
    red_w_outer = red_outer.reshape(hloc, dim)
    red_w_conv = red_conv.reshape(hid, KERNEL_TAPS, hloc).transpose(1, 2, 0)
    red_inner = red_inner.reshape(dloc + vec_rows, hid)
    red_w_inner = red_inner[:dloc]
    mine = red_inner[dloc:].reshape(-1)[:vec_len]
    reds = []
    cut = 0
    for v in vectors:
        n = v.shape[0] // nch
        reds.append(mine[cut : cut + n])
        cut += n
    return (
        output,
        input_grad,
        reds[0],
        reds[1],
        red_w_inner,
        reds[2],
        reds[3],
        reds[4],
        red_w_conv,
        reds[5],
        reds[6],
        reds[7],
        red_w_outer,
        reds[8],
    )


def solution(mesh):
    return jax.shard_map(
        local,
        mesh=mesh,
        in_specs=(
            P("batch", "ch", "seq"),
            P("batch", "seq"),
            P("ch"),
            P("ch"),
            P("ch", None),
            P("ch"),
            P("ch"),
            P("ch"),
            P(None, "ch", None),
            P("ch"),
            P("ch"),
            P("ch"),
            P("ch", None),
            P("ch"),
            P("batch", "ch", "seq"),
        ),
        out_specs=(
            P("batch", "ch", "seq"),
            P("batch", "ch", "seq"),
            P("ch"),
            P("ch"),
            P("ch", None),
            P("ch"),
            P("ch"),
            P("ch"),
            P(None, "ch", None),
            P("ch"),
            P("ch"),
            P("ch"),
            P("ch", None),
            P("ch"),
        ),
        check_vma=False,
    )
```

```python
import functools
import math

import jax
import jax.numpy as jnp
from jax import lax
from jax.experimental import pallas as pl
from jax.experimental.pallas import tpu as pltpu
from jax.sharding import PartitionSpec as P

KERNEL_TAPS = 5
DILATION_SPACING = 32


EPSILON = 1e-05


MESH_AXES = ("batch", "seq", "ch")
MESH_ID = pl.DeviceIdType.MESH


def _group_index(group, sizes, coords):
    me = 0
    for a in group:
        me = me * sizes[a] + coords[a]
    return me


def _exchange_kernel(sizes, group, gather, reduce, axes, *refs):
    count_arrays = len(axes)
    x_refs = refs[:count_arrays]
    o_refs = refs[count_arrays : 2 * count_arrays]
    send_sem, recv_sem = refs[2 * count_arrays :]
    coords = {a: lax.axis_index(a) for a in MESH_AXES}
    me = _group_index(group, sizes, coords)
    count = math.prod(sizes[a] for a in group)

    def device(index):
        where = dict(coords)
        rest = index
        for a in reversed(group):
            where[a] = lax.rem(rest, sizes[a])
            rest = rest // sizes[a]
        return tuple(where[a] for a in MESH_AXES)

    barrier = pltpu.get_barrier_semaphore()
    for j in range(1, count):
        pl.semaphore_signal(barrier, 1, device_id=device(lax.rem(me + j, count)), device_id_type=MESH_ID)
    pl.semaphore_wait(barrier, count - 1)
    copies = []
    for j in range(1, count):
        peer = lax.rem(me + j, count)
        for i in range(count_arrays):
            lead = (slice(None),) * axes[i]
            if gather:
                src, dst = x_refs[i], o_refs[i].at[me]
            else:
                slot = (j - 1) if reduce else me
                src = x_refs[i].at[lead + (pl.ds(peer, 1),)]
                dst = o_refs[i].at[lead + (pl.ds(slot, 1),)]
            copy = pltpu.make_async_remote_copy(
                src_ref=src,
                dst_ref=dst,
                send_sem=send_sem.at[i, j - 1],
                recv_sem=recv_sem.at[i, j - 1],
                device_id=device(peer),
                device_id_type=MESH_ID,
            )
            copy.start()
            copies.append(copy)
    for copy in copies:
        copy.wait()


def exchange(xs, group, collective_id, gather=False, axes=None, reduce=False):
    sizes = {a: lax.axis_size(a) for a in MESH_AXES}
    count = math.prod(sizes[a] for a in group)
    axes = tuple(axes or (0,) * len(xs))
    if count == 1:
        return [x[None] if gather else x for x in xs]
    shapes = [jax.ShapeDtypeStruct((count,) + x.shape if gather else x.shape, x.dtype) for x in xs]
    if reduce:
        shapes = [
            jax.ShapeDtypeStruct(x.shape[:a] + (count - 1,) + x.shape[a + 1 :], x.dtype) for x, a in zip(xs, axes)
        ]
    moved = sum(x.size * x.dtype.itemsize * (count if gather else 1) for x in xs)
    outs = pl.pallas_call(
        functools.partial(_exchange_kernel, sizes, group, gather, reduce, axes),
        out_shape=shapes,
        in_specs=[pl.BlockSpec(memory_space=pl.ANY)] * len(xs),
        out_specs=[pl.BlockSpec(memory_space=pl.ANY)] * len(xs),
        scratch_shapes=[
            pltpu.SemaphoreType.DMA((len(xs), count - 1)),
            pltpu.SemaphoreType.DMA((len(xs), count - 1)),
        ],
        compiler_params=pltpu.CompilerParams(collective_id=collective_id, has_side_effects=True),
        cost_estimate=pl.CostEstimate(flops=0, transcendentals=0, bytes_accessed=2 * moved),
    )(*xs)
    me = _group_index(group, sizes, {a: lax.axis_index(a) for a in group})
    placed = []
    if reduce:
        for x, out, axis in zip(xs, outs, axes):
            own = lax.dynamic_index_in_dim(x, me, axis, keepdims=False)
            placed.append(own + jnp.sum(out, axis=axis))
        return placed
    for x, out, axis in zip(xs, outs, axes):
        own = x if gather else lax.dynamic_index_in_dim(x, me, axis, keepdims=False)
        placed.append(lax.dynamic_update_index_in_dim(out, own, me, axis))
    return placed


def gelu_exact(values):
    return jax.nn.gelu(values, approximate=False)


def gelu_back(point, grad):
    return jax.vjp(gelu_exact, point)[1](grad)[0]


def normalize(values, gain, shift):
    center = jnp.mean(values, axis=1, keepdims=True)
    offset = values - center
    spread = jnp.mean(offset * offset, axis=1, keepdims=True)
    scale = lax.rsqrt(spread + EPSILON)
    unit = offset * scale
    return (unit * gain[:, None] + shift[:, None], unit, scale)


def normalize_back(grad, unit, scale, gain):
    scaled = grad * gain[:, None]
    first = jnp.mean(scaled, axis=1, keepdims=True)
    second = jnp.mean(scaled * unit, axis=1, keepdims=True)
    return scale * (scaled - first - unit * second)


def neighbour_pairs(seqs, nch, q_count):
    pairs = []
    for s in range(seqs):
        for c in range(nch):
            q = c % q_count
            if q < q_count - 1:
                pairs.append((s * nch + c, s * nch + c + 1))
            elif s < seqs - 1:
                pairs.append((s * nch + c, (s + 1) * nch + c - (q_count - 1)))
    return pairs


def extended(x, width, pairs):
    down = [(j, i) for i, j in pairs]
    length = x.shape[-1]
    before = lax.ppermute(x[..., length - width :], ("seq", "ch"), pairs)
    after = lax.ppermute(x[..., :width], ("seq", "ch"), down)
    return jnp.concatenate([before, x, after], axis=-1)


def shifted_taps(wide, wide_ids, own_ids, offsets, border):
    length = own_ids.shape[-1]
    pieces = []
    for offset in offsets:
        lower = border + offset
        shifted = wide[:, :, lower : lower + length]
        matching = wide_ids[:, lower : lower + length] == own_ids
        pieces.append(jnp.where(matching[:, None, :], shifted, jnp.zeros_like(shifted)))
    return jnp.concatenate(pieces, axis=1)


def to_positions(x, nch, q_count):
    rows, width, length = x.shape
    if q_count > 1:
        x = x.reshape(rows, width, q_count, length // q_count).transpose(0, 2, 1, 3)
        x = x.reshape(rows * q_count, width, length // q_count)
    x = lax.all_to_all(x, "ch", 0, 0, tiled=True)
    return _join(x, nch)


def _join(x, nch):
    total, width, length = x.shape
    p = total // nch
    return x.reshape(nch, p, width, length).transpose(1, 0, 2, 3).reshape(p, nch * width, length)


def to_channels(x, nch, q_count, rows):
    p, width, length = x.shape
    x = x.reshape(p, nch, width // nch, length).transpose(1, 0, 2, 3).reshape(nch * p, width // nch, length)
    x = lax.all_to_all(x, "ch", 0, 0, tiled=True)
    if q_count > 1:
        _, width, part = x.shape
        x = x.reshape(rows, q_count, width, part).transpose(0, 2, 1, 3).reshape(rows, width, q_count * part)
    return x


def local(
    inputs,
    segment_ids,
    norm0_gain,
    norm0_shift,
    w_inner,
    b_inner,
    norm1_gain,
    norm1_shift,
    w_conv,
    b_conv,
    norm2_gain,
    norm2_shift,
    w_outer,
    b_outer,
    cotangent,
):
    nch = lax.axis_size("ch")
    seqs = lax.axis_size("seq")
    batches = lax.axis_size("batch")
    rows, dloc, length = inputs.shape
    hloc = w_conv.shape[1]
    hid = hloc * nch
    dim = dloc * nch
    if rows % nch == 0:
        q_count = 1
    else:
        q_count = nch // rows
    part = length // q_count
    border = 2 * DILATION_SPACING
    offsets = [(k - KERNEL_TAPS // 2) * DILATION_SPACING for k in range(KERNEL_TAPS)]
    back_offsets = [-o for o in offsets]
    pairs = neighbour_pairs(seqs, nch, q_count)
    me = lax.axis_index("ch")

    smalls = [norm0_gain, norm0_shift, b_inner, norm1_gain, norm1_shift, b_conv, norm2_gain, norm2_shift, b_outer]
    sidx = lax.axis_index("seq")
    halves = [
        lax.dynamic_slice_in_dim(w_inner, sidx * (dloc // seqs), dloc // seqs, 0),
        lax.dynamic_slice_in_dim(w_conv, sidx * (hloc // seqs), hloc // seqs, 1),
        lax.dynamic_slice_in_dim(w_outer, sidx * (hloc // seqs), hloc // seqs, 0),
    ]
    small_all, w_in, w_out = exchange([jnp.concatenate(smalls), halves[0], halves[2]], ("ch",), 0, gather=True)
    w_cv = lax.all_gather(halves[1], "ch", axis=0)
    cut = 0
    full = []
    for v in smalls:
        n = v.shape[0]
        full.append(small_all[:, cut : cut + n].reshape(n * nch))
        cut += n
    g0, s0, b_in, g1, s1, b_cv, g2, s2, b_out = full
    w_in = lax.all_gather(w_in, "seq", axis=1, tiled=True).reshape(dim, hid)
    w_cv = lax.all_gather(w_cv, "seq", axis=2, tiled=True).transpose(1, 0, 2, 3).reshape(KERNEL_TAPS, hid, hid)
    w_out = lax.all_gather(w_out, "seq", axis=1, tiled=True).reshape(hid, dim)

    x = to_positions(inputs, nch, q_count)
    cot = to_positions(cotangent, nch, q_count)
    prow = x.shape[0]
    if q_count == 1:
        ids = lax.dynamic_slice_in_dim(segment_ids, me * prow, prow, axis=0)
    else:
        ids = lax.dynamic_slice_in_dim(segment_ids, me // q_count, 1, axis=0)
        ids = lax.dynamic_slice_in_dim(ids, (me % q_count) * part, part, axis=1)
    own_ids = ids + 1
    wide_ids = extended(own_ids, border, pairs)

    residual = x.astype(jnp.float32)
    normed0, unit0, scale0 = normalize(residual, g0, s0)
    hidden0 = gelu_exact(normed0).astype(jnp.bfloat16)
    inner = jnp.einsum("dh,rdl->rhl", w_in, hidden0, preferred_element_type=jnp.float32) + b_in[:, None]
    normed1, unit1, scale1 = normalize(inner, g1, s1)
    hidden1 = gelu_exact(normed1).astype(jnp.bfloat16)
    wide_hidden = extended(hidden1, border, pairs)
    taps = shifted_taps(wide_hidden, wide_ids, own_ids, offsets, border)
    kernel_flat = w_cv.reshape(KERNEL_TAPS * hid, hid)
    mixed = jnp.einsum("co,rcl->rol", kernel_flat, taps, preferred_element_type=jnp.float32) + b_cv[:, None]
    normed2, unit2, scale2 = normalize(mixed, g2, s2)
    hidden2 = gelu_exact(normed2).astype(jnp.bfloat16)
    branch = jnp.einsum("hd,rhl->rdl", w_out, hidden2, preferred_element_type=jnp.float32)
    output = (residual + branch + b_out[:, None]).astype(jnp.bfloat16)

    grad_b_outer = jnp.sum(cot.astype(jnp.float32), axis=(0, 2))
    grad_w_outer = jnp.einsum("rhl,rdl->hd", hidden2, cot, preferred_element_type=jnp.float32)
    def reduce_seq_batch(g, split_dim, after=None):
        if after is not None:
            g, _ = lax.optimization_barrier((g, after))
        g = lax.psum_scatter(g, "seq", scatter_dimension=split_dim, tiled=True)
        return lax.psum_scatter(g, "batch", scatter_dimension=split_dim, tiled=True)

    part_outer = reduce_seq_batch(grad_w_outer.reshape(nch, hloc * dim // 128, 128), 1)
    grad_hidden2 = jnp.einsum("hd,rdl->rhl", w_out, cot, preferred_element_type=jnp.float32)
    grad_normed2 = gelu_back(normed2, grad_hidden2)
    grad_norm2_gain = jnp.sum(grad_normed2 * unit2, axis=(0, 2))
    grad_norm2_shift = jnp.sum(grad_normed2, axis=(0, 2))
    grad_mixed = normalize_back(grad_normed2, unit2, scale2, g2).astype(jnp.bfloat16)
    grad_b_conv = jnp.sum(grad_mixed.astype(jnp.float32), axis=(0, 2))
    grad_w_conv = jnp.einsum(
        "rol,rkcil->okci",
        grad_mixed,
        taps.reshape(prow, KERNEL_TAPS, nch, hloc, part),
        preferred_element_type=jnp.float32,
    )
    conv_tail = grad_w_conv.shape[1:]
    conv_flat, _ = lax.optimization_barrier(
        (grad_w_conv.reshape(hid, math.prod(conv_tail) // 128, 128), part_outer)
    )
    conv_seq = lax.psum_scatter(conv_flat, "seq", scatter_dimension=0, tiled=True)
    output, conv_seq = lax.optimization_barrier((output, conv_seq))
    output = to_channels(output, nch, q_count, rows)
    wide_grad = extended(grad_mixed, border, pairs)
    back_taps = shifted_taps(wide_grad, wide_ids, own_ids, back_offsets, border)
    kernel_back = jnp.transpose(w_cv, (0, 2, 1)).reshape(KERNEL_TAPS * hid, hid)
    grad_hidden1 = jnp.einsum("oc,rol->rcl", kernel_back, back_taps, preferred_element_type=jnp.float32)
    grad_normed1 = gelu_back(normed1, grad_hidden1)
    grad_norm1_gain = jnp.sum(grad_normed1 * unit1, axis=(0, 2))
    grad_norm1_shift = jnp.sum(grad_normed1, axis=(0, 2))
    grad_inner = normalize_back(grad_normed1, unit1, scale1, g1).astype(jnp.bfloat16)
    grad_inner, _, output = lax.optimization_barrier((grad_inner, part_outer, output))
    grad_b_inner = jnp.sum(grad_inner.astype(jnp.float32), axis=(0, 2))
    grad_w_inner = jnp.einsum("rdl,rhl->dh", hidden0, grad_inner, preferred_element_type=jnp.float32)
    grad_hidden0 = jnp.einsum("dh,rhl->rdl", w_in, grad_inner, preferred_element_type=jnp.float32)
    grad_normed0 = gelu_back(normed0, grad_hidden0)
    grad_norm0_gain = jnp.sum(grad_normed0 * unit0, axis=(0, 2))
    grad_norm0_shift = jnp.sum(grad_normed0, axis=(0, 2))
    input_grad = (cot.astype(jnp.float32) + normalize_back(grad_normed0, unit0, scale0, g0)).astype(jnp.bfloat16)


    vectors = [
        grad_norm0_gain,
        grad_norm0_shift,
        grad_b_inner,
        grad_norm1_gain,
        grad_norm1_shift,
        grad_b_conv,
        grad_norm2_gain,
        grad_norm2_shift,
        grad_b_outer,
    ]
    flat = jnp.concatenate([v.reshape(nch, -1) for v in vectors], axis=1)
    vec_len = flat.shape[1]
    vec_rows = -(-vec_len // hid)
    vec_rows = -(-(dloc + vec_rows) // 64) * 64 - dloc
    flat = jnp.pad(flat, ((0, 0), (0, vec_rows * hid - vec_len))).reshape(nch, vec_rows, hid)
    inner_plus = jnp.concatenate([grad_w_inner.reshape(nch, dloc, hid), flat], axis=1)
    inner_plus = inner_plus.reshape(nch, (dloc + vec_rows) * hid // 128, 128)

    conv_tail = grad_w_conv.shape[1:]
    def finish(part, axis, cid):
        part = exchange([part], ("ch",), cid, axes=(axis,), reduce=True)[0]
        shape = part.shape
        if part.size % 128 == 0:
            part = part.reshape(part.size // 128, 128)
        part = lax.all_gather(part, "batch", axis=0)
        return lax.all_gather(part, "seq", axis=0, tiled=True).reshape((seqs * batches,) + shape)

    part_conv = lax.psum_scatter(conv_seq, "batch", scatter_dimension=0, tiled=True)
    part_conv = part_conv.reshape((part_conv.shape[0],) + conv_tail)
    red_outer = finish(part_outer, 0, 1)
    inner_plus, red_outer = lax.optimization_barrier((inner_plus, red_outer))
    part_inner = reduce_seq_batch(inner_plus, 1, part_conv)
    red_conv = finish(part_conv, 2, 2)
    input_grad, red_conv = lax.optimization_barrier((input_grad, red_conv))
    input_grad = to_channels(input_grad, nch, q_count, rows)
    red_inner = finish(part_inner, 0, 3)
    red_w_outer = red_outer.reshape(hloc, dim)
    red_w_conv = red_conv.reshape(hid, KERNEL_TAPS, hloc).transpose(1, 2, 0)
    red_inner = red_inner.reshape(dloc + vec_rows, hid)
    red_w_inner = red_inner[:dloc]
    mine = red_inner[dloc:].reshape(-1)[:vec_len]
    reds = []
    cut = 0
    for v in vectors:
        n = v.shape[0] // nch
        reds.append(mine[cut : cut + n])
        cut += n
    return (
        output,
        input_grad,
        reds[0],
        reds[1],
        red_w_inner,
        reds[2],
        reds[3],
        reds[4],
        red_w_conv,
        reds[5],
        reds[6],
        reds[7],
        red_w_outer,
        reds[8],
    )


def solution(mesh):
    return jax.shard_map(
        local,
        mesh=mesh,
        in_specs=(
            P("batch", "ch", "seq"),
            P("batch", "seq"),
            P("ch"),
            P("ch"),
            P("ch", None),
            P("ch"),
            P("ch"),
            P("ch"),
            P(None, "ch", None),
            P("ch"),
            P("ch"),
            P("ch"),
            P("ch", None),
            P("ch"),
            P("batch", "ch", "seq"),
        ),
        out_specs=(
            P("batch", "ch", "seq"),
            P("batch", "ch", "seq"),
            P("ch"),
            P("ch"),
            P("ch", None),
            P("ch"),
            P("ch"),
            P("ch"),
            P(None, "ch", None),
            P("ch"),
            P("ch"),
            P("ch"),
            P("ch", None),
            P("ch"),
        ),
        check_vma=False,
    )
```

```python
import functools
import math

import jax
import jax.numpy as jnp
from jax import lax
from jax.experimental import pallas as pl
from jax.experimental.pallas import tpu as pltpu
from jax.sharding import PartitionSpec as P

KERNEL_TAPS = 5
DILATION_SPACING = 32


EPSILON = 1e-05


MESH_AXES = ("batch", "seq", "ch")
MESH_ID = pl.DeviceIdType.MESH


def _group_index(group, sizes, coords):
    me = 0
    for a in group:
        me = me * sizes[a] + coords[a]
    return me


def _exchange_kernel(sizes, group, gather, reduce, axes, *refs):
    count_arrays = len(axes)
    x_refs = refs[:count_arrays]
    o_refs = refs[count_arrays : 2 * count_arrays]
    send_sem, recv_sem = refs[2 * count_arrays :]
    coords = {a: lax.axis_index(a) for a in MESH_AXES}
    me = _group_index(group, sizes, coords)
    count = math.prod(sizes[a] for a in group)

    def device(index):
        where = dict(coords)
        rest = index
        for a in reversed(group):
            where[a] = lax.rem(rest, sizes[a])
            rest = rest // sizes[a]
        return tuple(where[a] for a in MESH_AXES)

    barrier = pltpu.get_barrier_semaphore()
    for j in range(1, count):
        pl.semaphore_signal(barrier, 1, device_id=device(lax.rem(me + j, count)), device_id_type=MESH_ID)
    pl.semaphore_wait(barrier, count - 1)
    copies = []
    for j in range(1, count):
        peer = lax.rem(me + j, count)
        for i in range(count_arrays):
            lead = (slice(None),) * axes[i]
            if gather:
                src, dst = x_refs[i], o_refs[i].at[me]
            else:
                slot = (j - 1) if reduce else me
                src = x_refs[i].at[lead + (pl.ds(peer, 1),)]
                dst = o_refs[i].at[lead + (pl.ds(slot, 1),)]
            copy = pltpu.make_async_remote_copy(
                src_ref=src,
                dst_ref=dst,
                send_sem=send_sem.at[i, j - 1],
                recv_sem=recv_sem.at[i, j - 1],
                device_id=device(peer),
                device_id_type=MESH_ID,
            )
            copy.start()
            copies.append(copy)
    for copy in copies:
        copy.wait()


def exchange(xs, group, collective_id, gather=False, axes=None, reduce=False):
    sizes = {a: lax.axis_size(a) for a in MESH_AXES}
    count = math.prod(sizes[a] for a in group)
    axes = tuple(axes or (0,) * len(xs))
    if count == 1:
        return [x[None] if gather else x for x in xs]
    shapes = [jax.ShapeDtypeStruct((count,) + x.shape if gather else x.shape, x.dtype) for x in xs]
    if reduce:
        shapes = [
            jax.ShapeDtypeStruct(x.shape[:a] + (count - 1,) + x.shape[a + 1 :], x.dtype) for x, a in zip(xs, axes)
        ]
    moved = sum(x.size * x.dtype.itemsize * (count if gather else 1) for x in xs)
    outs = pl.pallas_call(
        functools.partial(_exchange_kernel, sizes, group, gather, reduce, axes),
        out_shape=shapes,
        in_specs=[pl.BlockSpec(memory_space=pl.ANY)] * len(xs),
        out_specs=[pl.BlockSpec(memory_space=pl.ANY)] * len(xs),
        scratch_shapes=[
            pltpu.SemaphoreType.DMA((len(xs), count - 1)),
            pltpu.SemaphoreType.DMA((len(xs), count - 1)),
        ],
        compiler_params=pltpu.CompilerParams(collective_id=collective_id, has_side_effects=True),
        cost_estimate=pl.CostEstimate(flops=0, transcendentals=0, bytes_accessed=2 * moved),
    )(*xs)
    me = _group_index(group, sizes, {a: lax.axis_index(a) for a in group})
    placed = []
    if reduce:
        for x, out, axis in zip(xs, outs, axes):
            own = lax.dynamic_index_in_dim(x, me, axis, keepdims=False)
            placed.append(own + jnp.sum(out, axis=axis))
        return placed
    for x, out, axis in zip(xs, outs, axes):
        own = x if gather else lax.dynamic_index_in_dim(x, me, axis, keepdims=False)
        placed.append(lax.dynamic_update_index_in_dim(out, own, me, axis))
    return placed


def gelu_exact(values):
    return jax.nn.gelu(values, approximate=False)


def gelu_back(point, grad):
    return jax.vjp(gelu_exact, point)[1](grad)[0]


def normalize(values, gain, shift):
    center = jnp.mean(values, axis=1, keepdims=True)
    offset = values - center
    spread = jnp.mean(offset * offset, axis=1, keepdims=True)
    scale = lax.rsqrt(spread + EPSILON)
    unit = offset * scale
    return (unit * gain[:, None] + shift[:, None], unit, scale)


def normalize_back(grad, unit, scale, gain):
    scaled = grad * gain[:, None]
    first = jnp.mean(scaled, axis=1, keepdims=True)
    second = jnp.mean(scaled * unit, axis=1, keepdims=True)
    return scale * (scaled - first - unit * second)


def neighbour_pairs(seqs, nch, q_count):
    pairs = []
    for s in range(seqs):
        for c in range(nch):
            q = c % q_count
            if q < q_count - 1:
                pairs.append((s * nch + c, s * nch + c + 1))
            elif s < seqs - 1:
                pairs.append((s * nch + c, (s + 1) * nch + c - (q_count - 1)))
    return pairs


def extended(x, width, pairs):
    down = [(j, i) for i, j in pairs]
    length = x.shape[-1]
    before = lax.ppermute(x[..., length - width :], ("seq", "ch"), pairs)
    after = lax.ppermute(x[..., :width], ("seq", "ch"), down)
    return jnp.concatenate([before, x, after], axis=-1)


def shifted_taps(wide, wide_ids, own_ids, offsets, border):
    length = own_ids.shape[-1]
    pieces = []
    for offset in offsets:
        lower = border + offset
        shifted = wide[:, :, lower : lower + length]
        matching = wide_ids[:, lower : lower + length] == own_ids
        pieces.append(jnp.where(matching[:, None, :], shifted, jnp.zeros_like(shifted)))
    return jnp.concatenate(pieces, axis=1)


def to_positions(x, nch, q_count):
    rows, width, length = x.shape
    if q_count > 1:
        x = x.reshape(rows, width, q_count, length // q_count).transpose(0, 2, 1, 3)
        x = x.reshape(rows * q_count, width, length // q_count)
    x = lax.all_to_all(x, "ch", 0, 0, tiled=True)
    return _join(x, nch)


def _join(x, nch):
    total, width, length = x.shape
    p = total // nch
    return x.reshape(nch, p, width, length).transpose(1, 0, 2, 3).reshape(p, nch * width, length)


def to_channels(x, nch, q_count, rows):
    p, width, length = x.shape
    x = x.reshape(p, nch, width // nch, length).transpose(1, 0, 2, 3).reshape(nch * p, width // nch, length)
    x = lax.all_to_all(x, "ch", 0, 0, tiled=True)
    if q_count > 1:
        _, width, part = x.shape
        x = x.reshape(rows, q_count, width, part).transpose(0, 2, 1, 3).reshape(rows, width, q_count * part)
    return x


def local(
    inputs,
    segment_ids,
    norm0_gain,
    norm0_shift,
    w_inner,
    b_inner,
    norm1_gain,
    norm1_shift,
    w_conv,
    b_conv,
    norm2_gain,
    norm2_shift,
    w_outer,
    b_outer,
    cotangent,
):
    nch = lax.axis_size("ch")
    seqs = lax.axis_size("seq")
    batches = lax.axis_size("batch")
    rows, dloc, length = inputs.shape
    hloc = w_conv.shape[1]
    hid = hloc * nch
    dim = dloc * nch
    if rows % nch == 0:
        q_count = 1
    else:
        q_count = nch // rows
    part = length // q_count
    border = 2 * DILATION_SPACING
    offsets = [(k - KERNEL_TAPS // 2) * DILATION_SPACING for k in range(KERNEL_TAPS)]
    back_offsets = [-o for o in offsets]
    pairs = neighbour_pairs(seqs, nch, q_count)
    me = lax.axis_index("ch")

    smalls = [norm0_gain, norm0_shift, b_inner, norm1_gain, norm1_shift, b_conv, norm2_gain, norm2_shift, b_outer]
    sidx = lax.axis_index("seq")
    halves = [
        lax.dynamic_slice_in_dim(w_inner, sidx * (dloc // seqs), dloc // seqs, 0),
        lax.dynamic_slice_in_dim(w_conv, sidx * (hloc // seqs), hloc // seqs, 1),
        lax.dynamic_slice_in_dim(w_outer, sidx * (hloc // seqs), hloc // seqs, 0),
    ]
    small_all, w_in, w_out = exchange([jnp.concatenate(smalls), halves[0], halves[2]], ("ch",), 0, gather=True)
    w_cv = lax.all_gather(halves[1], "ch", axis=0)
    cut = 0
    full = []
    for v in smalls:
        n = v.shape[0]
        full.append(small_all[:, cut : cut + n].reshape(n * nch))
        cut += n
    g0, s0, b_in, g1, s1, b_cv, g2, s2, b_out = full
    w_in = lax.all_gather(w_in, "seq", axis=1, tiled=True).reshape(dim, hid)
    w_cv = lax.all_gather(w_cv, "seq", axis=2, tiled=True).transpose(1, 0, 2, 3).reshape(KERNEL_TAPS, hid, hid)
    w_out = lax.all_gather(w_out, "seq", axis=1, tiled=True).reshape(hid, dim)

    x = to_positions(inputs, nch, q_count)
    cot = to_positions(cotangent, nch, q_count)
    prow = x.shape[0]
    if q_count == 1:
        ids = lax.dynamic_slice_in_dim(segment_ids, me * prow, prow, axis=0)
    else:
        ids = lax.dynamic_slice_in_dim(segment_ids, me // q_count, 1, axis=0)
        ids = lax.dynamic_slice_in_dim(ids, (me % q_count) * part, part, axis=1)
    own_ids = ids + 1
    wide_ids = extended(own_ids, border, pairs)

    residual = x.astype(jnp.float32)
    normed0, unit0, scale0 = normalize(residual, g0, s0)
    hidden0 = gelu_exact(normed0).astype(jnp.bfloat16)
    inner = jnp.einsum("dh,rdl->rhl", w_in, hidden0, preferred_element_type=jnp.float32) + b_in[:, None]
    normed1, unit1, scale1 = normalize(inner, g1, s1)
    hidden1 = gelu_exact(normed1).astype(jnp.bfloat16)
    wide_hidden = extended(hidden1, border, pairs)
    taps = shifted_taps(wide_hidden, wide_ids, own_ids, offsets, border)
    kernel_flat = w_cv.reshape(KERNEL_TAPS * hid, hid)
    mixed = jnp.einsum("co,rcl->rol", kernel_flat, taps, preferred_element_type=jnp.float32) + b_cv[:, None]
    normed2, unit2, scale2 = normalize(mixed, g2, s2)
    hidden2 = gelu_exact(normed2).astype(jnp.bfloat16)
    branch = jnp.einsum("hd,rhl->rdl", w_out, hidden2, preferred_element_type=jnp.float32)
    output = (residual + branch + b_out[:, None]).astype(jnp.bfloat16)
    output = to_channels(output, nch, q_count, rows)

    grad_b_outer = jnp.sum(cot.astype(jnp.float32), axis=(0, 2))
    grad_w_outer = jnp.einsum("rhl,rdl->hd", hidden2, cot, preferred_element_type=jnp.float32)
    def reduce_seq_batch(g, split_dim, after=None):
        if after is not None:
            g, _ = lax.optimization_barrier((g, after))
        g = lax.psum_scatter(g, "seq", scatter_dimension=split_dim, tiled=True)
        return lax.psum_scatter(g, "batch", scatter_dimension=split_dim, tiled=True)

    part_outer = reduce_seq_batch(grad_w_outer.reshape(nch, hloc * dim // 128, 128), 1)
    grad_hidden2 = jnp.einsum("hd,rdl->rhl", w_out, cot, preferred_element_type=jnp.float32)
    grad_normed2 = gelu_back(normed2, grad_hidden2)
    grad_norm2_gain = jnp.sum(grad_normed2 * unit2, axis=(0, 2))
    grad_norm2_shift = jnp.sum(grad_normed2, axis=(0, 2))
    grad_mixed = normalize_back(grad_normed2, unit2, scale2, g2).astype(jnp.bfloat16)
    grad_b_conv = jnp.sum(grad_mixed.astype(jnp.float32), axis=(0, 2))
    grad_w_conv = jnp.einsum(
        "rol,rkcil->okci",
        grad_mixed,
        taps.reshape(prow, KERNEL_TAPS, nch, hloc, part),
        preferred_element_type=jnp.float32,
    )
    conv_tail = grad_w_conv.shape[1:]
    conv_flat, _ = lax.optimization_barrier(
        (grad_w_conv.reshape(hid, math.prod(conv_tail) // 128, 128), part_outer)
    )
    conv_seq = lax.psum_scatter(conv_flat, "seq", scatter_dimension=0, tiled=True)
    wide_grad = extended(grad_mixed, border, pairs)
    back_taps = shifted_taps(wide_grad, wide_ids, own_ids, back_offsets, border)
    back_taps, conv_seq = lax.optimization_barrier((back_taps, conv_seq))
    kernel_back = jnp.transpose(w_cv, (0, 2, 1)).reshape(KERNEL_TAPS * hid, hid)
    grad_hidden1 = jnp.einsum("oc,rol->rcl", kernel_back, back_taps, preferred_element_type=jnp.float32)
    grad_normed1 = gelu_back(normed1, grad_hidden1)
    grad_norm1_gain = jnp.sum(grad_normed1 * unit1, axis=(0, 2))
    grad_norm1_shift = jnp.sum(grad_normed1, axis=(0, 2))
    grad_inner = normalize_back(grad_normed1, unit1, scale1, g1).astype(jnp.bfloat16)
    grad_inner, _, output = lax.optimization_barrier((grad_inner, part_outer, output))
    grad_b_inner = jnp.sum(grad_inner.astype(jnp.float32), axis=(0, 2))
    grad_w_inner = jnp.einsum("rdl,rhl->dh", hidden0, grad_inner, preferred_element_type=jnp.float32)
    grad_hidden0 = jnp.einsum("dh,rhl->rdl", w_in, grad_inner, preferred_element_type=jnp.float32)
    grad_normed0 = gelu_back(normed0, grad_hidden0)
    grad_norm0_gain = jnp.sum(grad_normed0 * unit0, axis=(0, 2))
    grad_norm0_shift = jnp.sum(grad_normed0, axis=(0, 2))
    input_grad = (cot.astype(jnp.float32) + normalize_back(grad_normed0, unit0, scale0, g0)).astype(jnp.bfloat16)


    vectors = [
        grad_norm0_gain,
        grad_norm0_shift,
        grad_b_inner,
        grad_norm1_gain,
        grad_norm1_shift,
        grad_b_conv,
        grad_norm2_gain,
        grad_norm2_shift,
        grad_b_outer,
    ]
    flat = jnp.concatenate([v.reshape(nch, -1) for v in vectors], axis=1)
    vec_len = flat.shape[1]
    vec_rows = -(-vec_len // hid)
    vec_rows = -(-(dloc + vec_rows) // 64) * 64 - dloc
    flat = jnp.pad(flat, ((0, 0), (0, vec_rows * hid - vec_len))).reshape(nch, vec_rows, hid)
    inner_plus = jnp.concatenate([grad_w_inner.reshape(nch, dloc, hid), flat], axis=1)
    inner_plus = inner_plus.reshape(nch, (dloc + vec_rows) * hid // 128, 128)

    conv_tail = grad_w_conv.shape[1:]
    def finish(part, axis, cid):
        part = exchange([part], ("ch",), cid, axes=(axis,), reduce=True)[0]
        shape = part.shape
        if part.size % 128 == 0:
            part = part.reshape(part.size // 128, 128)
        part = lax.all_gather(part, "batch", axis=0)
        return lax.all_gather(part, "seq", axis=0, tiled=True).reshape((seqs * batches,) + shape)

    part_conv = lax.psum_scatter(conv_seq, "batch", scatter_dimension=0, tiled=True)
    part_conv = part_conv.reshape((part_conv.shape[0],) + conv_tail)
    red_outer = finish(part_outer, 0, 1)
    inner_plus, red_outer = lax.optimization_barrier((inner_plus, red_outer))
    part_inner = reduce_seq_batch(inner_plus, 1, part_conv)
    red_conv = finish(part_conv, 2, 2)
    input_grad, red_conv = lax.optimization_barrier((input_grad, red_conv))
    input_grad = to_channels(input_grad, nch, q_count, rows)
    red_inner = finish(part_inner, 0, 3)
    red_w_outer = red_outer.reshape(hloc, dim)
    red_w_conv = red_conv.reshape(hid, KERNEL_TAPS, hloc).transpose(1, 2, 0)
    red_inner = red_inner.reshape(dloc + vec_rows, hid)
    red_w_inner = red_inner[:dloc]
    mine = red_inner[dloc:].reshape(-1)[:vec_len]
    reds = []
    cut = 0
    for v in vectors:
        n = v.shape[0] // nch
        reds.append(mine[cut : cut + n])
        cut += n
    return (
        output,
        input_grad,
        reds[0],
        reds[1],
        red_w_inner,
        reds[2],
        reds[3],
        reds[4],
        red_w_conv,
        reds[5],
        reds[6],
        reds[7],
        red_w_outer,
        reds[8],
    )


def solution(mesh):
    return jax.shard_map(
        local,
        mesh=mesh,
        in_specs=(
            P("batch", "ch", "seq"),
            P("batch", "seq"),
            P("ch"),
            P("ch"),
            P("ch", None),
            P("ch"),
            P("ch"),
            P("ch"),
            P(None, "ch", None),
            P("ch"),
            P("ch"),
            P("ch"),
            P("ch", None),
            P("ch"),
            P("batch", "ch", "seq"),
        ),
        out_specs=(
            P("batch", "ch", "seq"),
            P("batch", "ch", "seq"),
            P("ch"),
            P("ch"),
            P("ch", None),
            P("ch"),
            P("ch"),
            P("ch"),
            P(None, "ch", None),
            P("ch"),
            P("ch"),
            P("ch"),
            P("ch", None),
            P("ch"),
        ),
        check_vma=False,
    )
```

```python
import functools
import math

import jax
import jax.numpy as jnp
from jax import lax
from jax.experimental import pallas as pl
from jax.experimental.pallas import tpu as pltpu
from jax.sharding import PartitionSpec as P

KERNEL_TAPS = 5
DILATION_SPACING = 32


EPSILON = 1e-05


MESH_AXES = ("batch", "seq", "ch")
MESH_ID = pl.DeviceIdType.MESH


def _group_index(group, sizes, coords):
    me = 0
    for a in group:
        me = me * sizes[a] + coords[a]
    return me


def _exchange_kernel(sizes, group, gather, reduce, axes, *refs):
    count_arrays = len(axes)
    x_refs = refs[:count_arrays]
    o_refs = refs[count_arrays : 2 * count_arrays]
    send_sem, recv_sem = refs[2 * count_arrays :]
    coords = {a: lax.axis_index(a) for a in MESH_AXES}
    me = _group_index(group, sizes, coords)
    count = math.prod(sizes[a] for a in group)

    def device(index):
        where = dict(coords)
        rest = index
        for a in reversed(group):
            where[a] = lax.rem(rest, sizes[a])
            rest = rest // sizes[a]
        return tuple(where[a] for a in MESH_AXES)

    barrier = pltpu.get_barrier_semaphore()
    for j in range(1, count):
        pl.semaphore_signal(barrier, 1, device_id=device(lax.rem(me + j, count)), device_id_type=MESH_ID)
    pl.semaphore_wait(barrier, count - 1)
    copies = []
    for j in range(1, count):
        peer = lax.rem(me + j, count)
        for i in range(count_arrays):
            lead = (slice(None),) * axes[i]
            if gather:
                src, dst = x_refs[i], o_refs[i].at[me]
            else:
                slot = (j - 1) if reduce else me
                src = x_refs[i].at[lead + (pl.ds(peer, 1),)]
                dst = o_refs[i].at[lead + (pl.ds(slot, 1),)]
            copy = pltpu.make_async_remote_copy(
                src_ref=src,
                dst_ref=dst,
                send_sem=send_sem.at[i, j - 1],
                recv_sem=recv_sem.at[i, j - 1],
                device_id=device(peer),
                device_id_type=MESH_ID,
            )
            copy.start()
            copies.append(copy)
    for copy in copies:
        copy.wait()


def exchange(xs, group, collective_id, gather=False, axes=None, reduce=False):
    sizes = {a: lax.axis_size(a) for a in MESH_AXES}
    count = math.prod(sizes[a] for a in group)
    axes = tuple(axes or (0,) * len(xs))
    if count == 1:
        return [x[None] if gather else x for x in xs]
    shapes = [jax.ShapeDtypeStruct((count,) + x.shape if gather else x.shape, x.dtype) for x in xs]
    if reduce:
        shapes = [
            jax.ShapeDtypeStruct(x.shape[:a] + (count - 1,) + x.shape[a + 1 :], x.dtype) for x, a in zip(xs, axes)
        ]
    moved = sum(x.size * x.dtype.itemsize * (count if gather else 1) for x in xs)
    outs = pl.pallas_call(
        functools.partial(_exchange_kernel, sizes, group, gather, reduce, axes),
        out_shape=shapes,
        in_specs=[pl.BlockSpec(memory_space=pl.ANY)] * len(xs),
        out_specs=[pl.BlockSpec(memory_space=pl.ANY)] * len(xs),
        scratch_shapes=[
            pltpu.SemaphoreType.DMA((len(xs), count - 1)),
            pltpu.SemaphoreType.DMA((len(xs), count - 1)),
        ],
        compiler_params=pltpu.CompilerParams(collective_id=collective_id, has_side_effects=True),
        cost_estimate=pl.CostEstimate(flops=0, transcendentals=0, bytes_accessed=2 * moved),
    )(*xs)
    me = _group_index(group, sizes, {a: lax.axis_index(a) for a in group})
    placed = []
    if reduce:
        for x, out, axis in zip(xs, outs, axes):
            own = lax.dynamic_index_in_dim(x, me, axis, keepdims=False)
            placed.append(own + jnp.sum(out, axis=axis))
        return placed
    for x, out, axis in zip(xs, outs, axes):
        own = x if gather else lax.dynamic_index_in_dim(x, me, axis, keepdims=False)
        placed.append(lax.dynamic_update_index_in_dim(out, own, me, axis))
    return placed


def gelu_exact(values):
    return jax.nn.gelu(values, approximate=False)


def gelu_back(point, grad):
    return jax.vjp(gelu_exact, point)[1](grad)[0]


def normalize(values, gain, shift):
    center = jnp.mean(values, axis=1, keepdims=True)
    offset = values - center
    spread = jnp.mean(offset * offset, axis=1, keepdims=True)
    scale = lax.rsqrt(spread + EPSILON)
    unit = offset * scale
    return (unit * gain[:, None] + shift[:, None], unit, scale)


def normalize_back(grad, unit, scale, gain):
    scaled = grad * gain[:, None]
    first = jnp.mean(scaled, axis=1, keepdims=True)
    second = jnp.mean(scaled * unit, axis=1, keepdims=True)
    return scale * (scaled - first - unit * second)


def neighbour_pairs(seqs, nch, q_count):
    pairs = []
    for s in range(seqs):
        for c in range(nch):
            q = c % q_count
            if q < q_count - 1:
                pairs.append((s * nch + c, s * nch + c + 1))
            elif s < seqs - 1:
                pairs.append((s * nch + c, (s + 1) * nch + c - (q_count - 1)))
    return pairs


def extended(x, width, pairs):
    down = [(j, i) for i, j in pairs]
    length = x.shape[-1]
    before = lax.ppermute(x[..., length - width :], ("seq", "ch"), pairs)
    after = lax.ppermute(x[..., :width], ("seq", "ch"), down)
    return jnp.concatenate([before, x, after], axis=-1)


def shifted_taps(wide, wide_ids, own_ids, offsets, border):
    length = own_ids.shape[-1]
    pieces = []
    for offset in offsets:
        lower = border + offset
        shifted = wide[:, :, lower : lower + length]
        matching = wide_ids[:, lower : lower + length] == own_ids
        pieces.append(jnp.where(matching[:, None, :], shifted, jnp.zeros_like(shifted)))
    return jnp.concatenate(pieces, axis=1)


def to_positions(x, nch, q_count):
    rows, width, length = x.shape
    if q_count > 1:
        x = x.reshape(rows, width, q_count, length // q_count).transpose(0, 2, 1, 3)
        x = x.reshape(rows * q_count, width, length // q_count)
    x = lax.all_to_all(x, "ch", 0, 0, tiled=True)
    return _join(x, nch)


def _join(x, nch):
    total, width, length = x.shape
    p = total // nch
    return x.reshape(nch, p, width, length).transpose(1, 0, 2, 3).reshape(p, nch * width, length)


def to_channels(x, nch, q_count, rows):
    p, width, length = x.shape
    x = x.reshape(p, nch, width // nch, length).transpose(1, 0, 2, 3).reshape(nch * p, width // nch, length)
    x = lax.all_to_all(x, "ch", 0, 0, tiled=True)
    if q_count > 1:
        _, width, part = x.shape
        x = x.reshape(rows, q_count, width, part).transpose(0, 2, 1, 3).reshape(rows, width, q_count * part)
    return x


def local(
    inputs,
    segment_ids,
    norm0_gain,
    norm0_shift,
    w_inner,
    b_inner,
    norm1_gain,
    norm1_shift,
    w_conv,
    b_conv,
    norm2_gain,
    norm2_shift,
    w_outer,
    b_outer,
    cotangent,
):
    nch = lax.axis_size("ch")
    seqs = lax.axis_size("seq")
    batches = lax.axis_size("batch")
    rows, dloc, length = inputs.shape
    hloc = w_conv.shape[1]
    hid = hloc * nch
    dim = dloc * nch
    if rows % nch == 0:
        q_count = 1
    else:
        q_count = nch // rows
    part = length // q_count
    border = 2 * DILATION_SPACING
    offsets = [(k - KERNEL_TAPS // 2) * DILATION_SPACING for k in range(KERNEL_TAPS)]
    back_offsets = [-o for o in offsets]
    pairs = neighbour_pairs(seqs, nch, q_count)
    me = lax.axis_index("ch")

    smalls = [norm0_gain, norm0_shift, b_inner, norm1_gain, norm1_shift, b_conv, norm2_gain, norm2_shift, b_outer]
    sidx = lax.axis_index("seq")
    halves = [
        lax.dynamic_slice_in_dim(w_inner, sidx * (dloc // seqs), dloc // seqs, 0),
        lax.dynamic_slice_in_dim(w_conv, sidx * (hloc // seqs), hloc // seqs, 1),
        lax.dynamic_slice_in_dim(w_outer, sidx * (hloc // seqs), hloc // seqs, 0),
    ]
    small_all, w_in, w_out = exchange([jnp.concatenate(smalls), halves[0], halves[2]], ("ch",), 0, gather=True)
    w_cv = lax.all_gather(halves[1], "ch", axis=0)
    cut = 0
    full = []
    for v in smalls:
        n = v.shape[0]
        full.append(small_all[:, cut : cut + n].reshape(n * nch))
        cut += n
    g0, s0, b_in, g1, s1, b_cv, g2, s2, b_out = full
    w_in = lax.all_gather(w_in, "seq", axis=1, tiled=True).reshape(dim, hid)
    w_cv = lax.all_gather(w_cv, "seq", axis=2, tiled=True).transpose(1, 0, 2, 3).reshape(KERNEL_TAPS, hid, hid)
    w_out = lax.all_gather(w_out, "seq", axis=1, tiled=True).reshape(hid, dim)

    x = to_positions(inputs, nch, q_count)
    cot = to_positions(cotangent, nch, q_count)
    prow = x.shape[0]
    if q_count == 1:
        ids = lax.dynamic_slice_in_dim(segment_ids, me * prow, prow, axis=0)
    else:
        ids = lax.dynamic_slice_in_dim(segment_ids, me // q_count, 1, axis=0)
        ids = lax.dynamic_slice_in_dim(ids, (me % q_count) * part, part, axis=1)
    own_ids = ids + 1
    wide_ids = extended(own_ids, border, pairs)

    residual = x.astype(jnp.float32)
    normed0, unit0, scale0 = normalize(residual, g0, s0)
    hidden0 = gelu_exact(normed0).astype(jnp.bfloat16)
    inner = jnp.einsum("dh,rdl->rhl", w_in, hidden0, preferred_element_type=jnp.float32) + b_in[:, None]
    normed1, unit1, scale1 = normalize(inner, g1, s1)
    hidden1 = gelu_exact(normed1).astype(jnp.bfloat16)
    wide_hidden = extended(hidden1, border, pairs)
    taps = shifted_taps(wide_hidden, wide_ids, own_ids, offsets, border)
    kernel_flat = w_cv.reshape(KERNEL_TAPS * hid, hid)
    mixed = jnp.einsum("co,rcl->rol", kernel_flat, taps, preferred_element_type=jnp.float32) + b_cv[:, None]
    normed2, unit2, scale2 = normalize(mixed, g2, s2)
    hidden2 = gelu_exact(normed2).astype(jnp.bfloat16)
    branch = jnp.einsum("hd,rhl->rdl", w_out, hidden2, preferred_element_type=jnp.float32)
    output = (residual + branch + b_out[:, None]).astype(jnp.bfloat16)
    output = to_channels(output, nch, q_count, rows)

    grad_b_outer = jnp.sum(cot.astype(jnp.float32), axis=(0, 2))
    grad_w_outer = jnp.einsum("rhl,rdl->hd", hidden2, cot, preferred_element_type=jnp.float32)
    def reduce_seq_batch(g, split_dim, after=None):
        if after is not None:
            g, _ = lax.optimization_barrier((g, after))
        g = lax.psum_scatter(g, "seq", scatter_dimension=split_dim, tiled=True)
        return lax.psum_scatter(g, "batch", scatter_dimension=split_dim, tiled=True)

    part_outer = reduce_seq_batch(grad_w_outer.reshape(nch, hloc * dim // 128, 128), 1)
    grad_hidden2 = jnp.einsum("hd,rdl->rhl", w_out, cot, preferred_element_type=jnp.float32)
    grad_normed2 = gelu_back(normed2, grad_hidden2)
    grad_norm2_gain = jnp.sum(grad_normed2 * unit2, axis=(0, 2))
    grad_norm2_shift = jnp.sum(grad_normed2, axis=(0, 2))
    grad_mixed = normalize_back(grad_normed2, unit2, scale2, g2).astype(jnp.bfloat16)
    grad_b_conv = jnp.sum(grad_mixed.astype(jnp.float32), axis=(0, 2))
    grad_w_conv = jnp.einsum(
        "rol,rkcil->okci",
        grad_mixed,
        taps.reshape(prow, KERNEL_TAPS, nch, hloc, part),
        preferred_element_type=jnp.float32,
    )
    conv_tail = grad_w_conv.shape[1:]
    conv_flat, _ = lax.optimization_barrier(
        (grad_w_conv.reshape(hid, math.prod(conv_tail) // 128, 128), part_outer)
    )
    conv_seq = lax.psum_scatter(conv_flat, "seq", scatter_dimension=0, tiled=True)
    wide_grad = extended(grad_mixed, border, pairs)
    back_taps = shifted_taps(wide_grad, wide_ids, own_ids, back_offsets, border)
    back_taps, conv_seq = lax.optimization_barrier((back_taps, conv_seq))
    kernel_back = jnp.transpose(w_cv, (0, 2, 1)).reshape(KERNEL_TAPS * hid, hid)
    grad_hidden1 = jnp.einsum("oc,rol->rcl", kernel_back, back_taps, preferred_element_type=jnp.float32)
    grad_normed1 = gelu_back(normed1, grad_hidden1)
    grad_norm1_gain = jnp.sum(grad_normed1 * unit1, axis=(0, 2))
    grad_norm1_shift = jnp.sum(grad_normed1, axis=(0, 2))
    grad_inner = normalize_back(grad_normed1, unit1, scale1, g1).astype(jnp.bfloat16)
    grad_inner, _, output = lax.optimization_barrier((grad_inner, part_outer, output))
    grad_b_inner = jnp.sum(grad_inner.astype(jnp.float32), axis=(0, 2))
    grad_w_inner = jnp.einsum("rdl,rhl->dh", hidden0, grad_inner, preferred_element_type=jnp.float32)
    grad_hidden0 = jnp.einsum("dh,rhl->rdl", w_in, grad_inner, preferred_element_type=jnp.float32)
    grad_normed0 = gelu_back(normed0, grad_hidden0)
    grad_norm0_gain = jnp.sum(grad_normed0 * unit0, axis=(0, 2))
    grad_norm0_shift = jnp.sum(grad_normed0, axis=(0, 2))
    input_grad = (cot.astype(jnp.float32) + normalize_back(grad_normed0, unit0, scale0, g0)).astype(jnp.bfloat16)


    vectors = [
        grad_norm0_gain,
        grad_norm0_shift,
        grad_b_inner,
        grad_norm1_gain,
        grad_norm1_shift,
        grad_b_conv,
        grad_norm2_gain,
        grad_norm2_shift,
        grad_b_outer,
    ]
    flat = jnp.concatenate([v.reshape(nch, -1) for v in vectors], axis=1)
    vec_len = flat.shape[1]
    vec_rows = -(-vec_len // hid)
    vec_rows = -(-(dloc + vec_rows) // 64) * 64 - dloc
    flat = jnp.pad(flat, ((0, 0), (0, vec_rows * hid - vec_len))).reshape(nch, vec_rows, hid)
    inner_plus = jnp.concatenate([grad_w_inner.reshape(nch, dloc, hid), flat], axis=1)
    inner_plus = inner_plus.reshape(nch, (dloc + vec_rows) * hid // 128, 128)

    conv_tail = grad_w_conv.shape[1:]
    def finish(part, axis, cid):
        part = exchange([part], ("ch",), cid, axes=(axis,), reduce=True)[0]
        shape = part.shape
        if part.size % 128 == 0:
            part = part.reshape(part.size // 128, 128)
        part = lax.all_gather(part, "batch", axis=0)
        return lax.all_gather(part, "seq", axis=0, tiled=True).reshape((seqs * batches,) + shape)

    part_conv = lax.psum_scatter(conv_seq, "batch", scatter_dimension=0, tiled=True)
    part_conv = part_conv.reshape((part_conv.shape[0],) + conv_tail)
    part_conv_issued = part_conv
    part_outer, _ = lax.optimization_barrier((part_outer, part_conv_issued))
    red_outer = finish(part_outer, 0, 1)
    inner_plus, red_outer = lax.optimization_barrier((inner_plus, red_outer))
    part_inner = reduce_seq_batch(inner_plus, 1, part_conv)
    red_conv = finish(part_conv, 2, 2)
    input_grad, red_conv = lax.optimization_barrier((input_grad, red_conv))
    input_grad = to_channels(input_grad, nch, q_count, rows)
    red_inner = finish(part_inner, 0, 3)
    red_w_outer = red_outer.reshape(hloc, dim)
    red_w_conv = red_conv.reshape(hid, KERNEL_TAPS, hloc).transpose(1, 2, 0)
    red_inner = red_inner.reshape(dloc + vec_rows, hid)
    red_w_inner = red_inner[:dloc]
    mine = red_inner[dloc:].reshape(-1)[:vec_len]
    reds = []
    cut = 0
    for v in vectors:
        n = v.shape[0] // nch
        reds.append(mine[cut : cut + n])
        cut += n
    return (
        output,
        input_grad,
        reds[0],
        reds[1],
        red_w_inner,
        reds[2],
        reds[3],
        reds[4],
        red_w_conv,
        reds[5],
        reds[6],
        reds[7],
        red_w_outer,
        reds[8],
    )


def solution(mesh):
    return jax.shard_map(
        local,
        mesh=mesh,
        in_specs=(
            P("batch", "ch", "seq"),
            P("batch", "seq"),
            P("ch"),
            P("ch"),
            P("ch", None),
            P("ch"),
            P("ch"),
            P("ch"),
            P(None, "ch", None),
            P("ch"),
            P("ch"),
            P("ch"),
            P("ch", None),
            P("ch"),
            P("batch", "ch", "seq"),
        ),
        out_specs=(
            P("batch", "ch", "seq"),
            P("batch", "ch", "seq"),
            P("ch"),
            P("ch"),
            P("ch", None),
            P("ch"),
            P("ch"),
            P("ch"),
            P(None, "ch", None),
            P("ch"),
            P("ch"),
            P("ch"),
            P("ch", None),
            P("ch"),
        ),
        check_vma=False,
    )
```

```python
import functools
import math

import jax
import jax.numpy as jnp
from jax import lax
from jax.experimental import pallas as pl
from jax.experimental.pallas import tpu as pltpu
from jax.sharding import PartitionSpec as P

KERNEL_TAPS = 5
DILATION_SPACING = 32


EPSILON = 1e-05


MESH_AXES = ("batch", "seq", "ch")
MESH_ID = pl.DeviceIdType.MESH


def _group_index(group, sizes, coords):
    me = 0
    for a in group:
        me = me * sizes[a] + coords[a]
    return me


def _exchange_kernel(sizes, group, gather, reduce, axes, *refs):
    count_arrays = len(axes)
    x_refs = refs[:count_arrays]
    o_refs = refs[count_arrays : 2 * count_arrays]
    send_sem, recv_sem = refs[2 * count_arrays :]
    coords = {a: lax.axis_index(a) for a in MESH_AXES}
    me = _group_index(group, sizes, coords)
    count = math.prod(sizes[a] for a in group)

    def device(index):
        where = dict(coords)
        rest = index
        for a in reversed(group):
            where[a] = lax.rem(rest, sizes[a])
            rest = rest // sizes[a]
        return tuple(where[a] for a in MESH_AXES)

    barrier = pltpu.get_barrier_semaphore()
    for j in range(1, count):
        pl.semaphore_signal(barrier, 1, device_id=device(lax.rem(me + j, count)), device_id_type=MESH_ID)
    pl.semaphore_wait(barrier, count - 1)
    copies = []
    for j in range(1, count):
        peer = lax.rem(me + j, count)
        for i in range(count_arrays):
            lead = (slice(None),) * axes[i]
            if gather:
                src, dst = x_refs[i], o_refs[i].at[me]
            else:
                slot = (j - 1) if reduce else me
                src = x_refs[i].at[lead + (pl.ds(peer, 1),)]
                dst = o_refs[i].at[lead + (pl.ds(slot, 1),)]
            copy = pltpu.make_async_remote_copy(
                src_ref=src,
                dst_ref=dst,
                send_sem=send_sem.at[i, j - 1],
                recv_sem=recv_sem.at[i, j - 1],
                device_id=device(peer),
                device_id_type=MESH_ID,
            )
            copy.start()
            copies.append(copy)
    for copy in copies:
        copy.wait()


def exchange(xs, group, collective_id, gather=False, axes=None, reduce=False):
    sizes = {a: lax.axis_size(a) for a in MESH_AXES}
    count = math.prod(sizes[a] for a in group)
    axes = tuple(axes or (0,) * len(xs))
    if count == 1:
        return [x[None] if gather else x for x in xs]
    shapes = [jax.ShapeDtypeStruct((count,) + x.shape if gather else x.shape, x.dtype) for x in xs]
    if reduce:
        shapes = [
            jax.ShapeDtypeStruct(x.shape[:a] + (count - 1,) + x.shape[a + 1 :], x.dtype) for x, a in zip(xs, axes)
        ]
    moved = sum(x.size * x.dtype.itemsize * (count if gather else 1) for x in xs)
    outs = pl.pallas_call(
        functools.partial(_exchange_kernel, sizes, group, gather, reduce, axes),
        out_shape=shapes,
        in_specs=[pl.BlockSpec(memory_space=pl.ANY)] * len(xs),
        out_specs=[pl.BlockSpec(memory_space=pl.ANY)] * len(xs),
        scratch_shapes=[
            pltpu.SemaphoreType.DMA((len(xs), count - 1)),
            pltpu.SemaphoreType.DMA((len(xs), count - 1)),
        ],
        compiler_params=pltpu.CompilerParams(collective_id=collective_id, has_side_effects=True),
        cost_estimate=pl.CostEstimate(flops=0, transcendentals=0, bytes_accessed=2 * moved),
    )(*xs)
    me = _group_index(group, sizes, {a: lax.axis_index(a) for a in group})
    placed = []
    if reduce:
        for x, out, axis in zip(xs, outs, axes):
            own = lax.dynamic_index_in_dim(x, me, axis, keepdims=False)
            placed.append(own + jnp.sum(out, axis=axis))
        return placed
    for x, out, axis in zip(xs, outs, axes):
        own = x if gather else lax.dynamic_index_in_dim(x, me, axis, keepdims=False)
        placed.append(lax.dynamic_update_index_in_dim(out, own, me, axis))
    return placed


def gelu_exact(values):
    return jax.nn.gelu(values, approximate=False)


def gelu_back(point, grad):
    return jax.vjp(gelu_exact, point)[1](grad)[0]


def normalize(values, gain, shift):
    center = jnp.mean(values, axis=1, keepdims=True)
    offset = values - center
    spread = jnp.mean(offset * offset, axis=1, keepdims=True)
    scale = lax.rsqrt(spread + EPSILON)
    unit = offset * scale
    return (unit * gain[:, None] + shift[:, None], unit, scale)


def normalize_back(grad, unit, scale, gain):
    scaled = grad * gain[:, None]
    first = jnp.mean(scaled, axis=1, keepdims=True)
    second = jnp.mean(scaled * unit, axis=1, keepdims=True)
    return scale * (scaled - first - unit * second)


def neighbour_pairs(seqs, nch, q_count):
    pairs = []
    for s in range(seqs):
        for c in range(nch):
            q = c % q_count
            if q < q_count - 1:
                pairs.append((s * nch + c, s * nch + c + 1))
            elif s < seqs - 1:
                pairs.append((s * nch + c, (s + 1) * nch + c - (q_count - 1)))
    return pairs


def extended(x, width, pairs):
    down = [(j, i) for i, j in pairs]
    length = x.shape[-1]
    before = lax.ppermute(x[..., length - width :], ("seq", "ch"), pairs)
    after = lax.ppermute(x[..., :width], ("seq", "ch"), down)
    return jnp.concatenate([before, x, after], axis=-1)


def shifted_taps(wide, wide_ids, own_ids, offsets, border):
    length = own_ids.shape[-1]
    pieces = []
    for offset in offsets:
        lower = border + offset
        shifted = wide[:, :, lower : lower + length]
        matching = wide_ids[:, lower : lower + length] == own_ids
        pieces.append(jnp.where(matching[:, None, :], shifted, jnp.zeros_like(shifted)))
    return jnp.concatenate(pieces, axis=1)


def to_positions(x, nch, q_count):
    rows, width, length = x.shape
    if q_count > 1:
        x = x.reshape(rows, width, q_count, length // q_count).transpose(0, 2, 1, 3)
        x = x.reshape(rows * q_count, width, length // q_count)
    x = lax.all_to_all(x, "ch", 0, 0, tiled=True)
    return _join(x, nch)


def _join(x, nch):
    total, width, length = x.shape
    p = total // nch
    return x.reshape(nch, p, width, length).transpose(1, 0, 2, 3).reshape(p, nch * width, length)


def to_channels(x, nch, q_count, rows):
    p, width, length = x.shape
    x = x.reshape(p, nch, width // nch, length).transpose(1, 0, 2, 3).reshape(nch * p, width // nch, length)
    x = lax.all_to_all(x, "ch", 0, 0, tiled=True)
    if q_count > 1:
        _, width, part = x.shape
        x = x.reshape(rows, q_count, width, part).transpose(0, 2, 1, 3).reshape(rows, width, q_count * part)
    return x


def local(
    inputs,
    segment_ids,
    norm0_gain,
    norm0_shift,
    w_inner,
    b_inner,
    norm1_gain,
    norm1_shift,
    w_conv,
    b_conv,
    norm2_gain,
    norm2_shift,
    w_outer,
    b_outer,
    cotangent,
):
    nch = lax.axis_size("ch")
    seqs = lax.axis_size("seq")
    batches = lax.axis_size("batch")
    rows, dloc, length = inputs.shape
    hloc = w_conv.shape[1]
    hid = hloc * nch
    dim = dloc * nch
    if rows % nch == 0:
        q_count = 1
    else:
        q_count = nch // rows
    part = length // q_count
    border = 2 * DILATION_SPACING
    offsets = [(k - KERNEL_TAPS // 2) * DILATION_SPACING for k in range(KERNEL_TAPS)]
    back_offsets = [-o for o in offsets]
    pairs = neighbour_pairs(seqs, nch, q_count)
    me = lax.axis_index("ch")

    smalls = [norm0_gain, norm0_shift, b_inner, norm1_gain, norm1_shift, b_conv, norm2_gain, norm2_shift, b_outer]
    sidx = lax.axis_index("seq")
    halves = [
        lax.dynamic_slice_in_dim(w_inner, sidx * (dloc // seqs), dloc // seqs, 0),
        lax.dynamic_slice_in_dim(w_conv, sidx * (hloc // seqs), hloc // seqs, 1),
        lax.dynamic_slice_in_dim(w_outer, sidx * (hloc // seqs), hloc // seqs, 0),
    ]
    small_all, w_in, w_out = exchange([jnp.concatenate(smalls), halves[0], halves[2]], ("ch",), 0, gather=True)
    w_cv = lax.all_gather(halves[1], "ch", axis=0)
    cut = 0
    full = []
    for v in smalls:
        n = v.shape[0]
        full.append(small_all[:, cut : cut + n].reshape(n * nch))
        cut += n
    g0, s0, b_in, g1, s1, b_cv, g2, s2, b_out = full
    w_in = lax.all_gather(w_in, "seq", axis=1, tiled=True).reshape(dim, hid)
    w_cv = lax.all_gather(w_cv, "seq", axis=2, tiled=True).transpose(1, 0, 2, 3).reshape(KERNEL_TAPS, hid, hid)
    w_out = lax.all_gather(w_out, "seq", axis=1, tiled=True).reshape(hid, dim)

    x = to_positions(inputs, nch, q_count)
    cot = to_positions(cotangent, nch, q_count)
    prow = x.shape[0]
    if q_count == 1:
        ids = lax.dynamic_slice_in_dim(segment_ids, me * prow, prow, axis=0)
    else:
        ids = lax.dynamic_slice_in_dim(segment_ids, me // q_count, 1, axis=0)
        ids = lax.dynamic_slice_in_dim(ids, (me % q_count) * part, part, axis=1)
    own_ids = ids + 1
    wide_ids = extended(own_ids, border, pairs)

    residual = x.astype(jnp.float32)
    normed0, unit0, scale0 = normalize(residual, g0, s0)
    hidden0 = gelu_exact(normed0).astype(jnp.bfloat16)
    inner = jnp.einsum("dh,rdl->rhl", w_in, hidden0, preferred_element_type=jnp.float32) + b_in[:, None]
    normed1, unit1, scale1 = normalize(inner, g1, s1)
    hidden1 = gelu_exact(normed1).astype(jnp.bfloat16)
    wide_hidden = extended(hidden1, border, pairs)
    taps = shifted_taps(wide_hidden, wide_ids, own_ids, offsets, border)
    kernel_flat = w_cv.reshape(KERNEL_TAPS * hid, hid)
    mixed = jnp.einsum("co,rcl->rol", kernel_flat, taps, preferred_element_type=jnp.float32) + b_cv[:, None]
    normed2, unit2, scale2 = normalize(mixed, g2, s2)
    hidden2 = gelu_exact(normed2).astype(jnp.bfloat16)
    branch = jnp.einsum("hd,rhl->rdl", w_out, hidden2, preferred_element_type=jnp.float32)
    output = (residual + branch + b_out[:, None]).astype(jnp.bfloat16)
    output = to_channels(output, nch, q_count, rows)

    grad_b_outer = jnp.sum(cot.astype(jnp.float32), axis=(0, 2))
    grad_w_outer = jnp.einsum("rhl,rdl->hd", hidden2, cot, preferred_element_type=jnp.float32)
    def reduce_seq_batch(g, split_dim, after=None):
        if after is not None:
            g, _ = lax.optimization_barrier((g, after))
        g = lax.psum_scatter(g, "seq", scatter_dimension=split_dim, tiled=True)
        return lax.psum_scatter(g, "batch", scatter_dimension=split_dim, tiled=True)

    part_outer = reduce_seq_batch(grad_w_outer.reshape(nch, hloc * dim // 128, 128), 1)
    grad_hidden2 = jnp.einsum("hd,rdl->rhl", w_out, cot, preferred_element_type=jnp.float32)
    grad_normed2 = gelu_back(normed2, grad_hidden2)
    grad_norm2_gain = jnp.sum(grad_normed2 * unit2, axis=(0, 2))
    grad_norm2_shift = jnp.sum(grad_normed2, axis=(0, 2))
    grad_mixed = normalize_back(grad_normed2, unit2, scale2, g2).astype(jnp.bfloat16)
    grad_b_conv = jnp.sum(grad_mixed.astype(jnp.float32), axis=(0, 2))
    grad_w_conv = jnp.einsum(
        "rol,rkcil->okci",
        grad_mixed,
        taps.reshape(prow, KERNEL_TAPS, nch, hloc, part),
        preferred_element_type=jnp.float32,
    )
    wide_grad = extended(grad_mixed, border, pairs)
    back_taps = shifted_taps(wide_grad, wide_ids, own_ids, back_offsets, border)
    kernel_back = jnp.transpose(w_cv, (0, 2, 1)).reshape(KERNEL_TAPS * hid, hid)
    grad_hidden1 = jnp.einsum("oc,rol->rcl", kernel_back, back_taps, preferred_element_type=jnp.float32)
    grad_normed1 = gelu_back(normed1, grad_hidden1)
    grad_norm1_gain = jnp.sum(grad_normed1 * unit1, axis=(0, 2))
    grad_norm1_shift = jnp.sum(grad_normed1, axis=(0, 2))
    grad_inner = normalize_back(grad_normed1, unit1, scale1, g1).astype(jnp.bfloat16)
    grad_inner, _, output = lax.optimization_barrier((grad_inner, part_outer, output))
    grad_b_inner = jnp.sum(grad_inner.astype(jnp.float32), axis=(0, 2))
    grad_w_inner = jnp.einsum("rdl,rhl->dh", hidden0, grad_inner, preferred_element_type=jnp.float32)
    grad_hidden0 = jnp.einsum("dh,rhl->rdl", w_in, grad_inner, preferred_element_type=jnp.float32)
    grad_normed0 = gelu_back(normed0, grad_hidden0)
    grad_norm0_gain = jnp.sum(grad_normed0 * unit0, axis=(0, 2))
    grad_norm0_shift = jnp.sum(grad_normed0, axis=(0, 2))
    input_grad = (cot.astype(jnp.float32) + normalize_back(grad_normed0, unit0, scale0, g0)).astype(jnp.bfloat16)


    vectors = [
        grad_norm0_gain,
        grad_norm0_shift,
        grad_b_inner,
        grad_norm1_gain,
        grad_norm1_shift,
        grad_b_conv,
        grad_norm2_gain,
        grad_norm2_shift,
        grad_b_outer,
    ]
    flat = jnp.concatenate([v.reshape(nch, -1) for v in vectors], axis=1)
    vec_len = flat.shape[1]
    inner_rows = dloc * hid // 128
    stack_rows = -(-(inner_rows + -(-vec_len // 128)) // (seqs * batches * 8)) * (seqs * batches * 8)
    vec_rows = stack_rows - inner_rows
    flat = jnp.pad(flat, ((0, 0), (0, vec_rows * 128 - vec_len))).reshape(nch, vec_rows, 128)
    inner_plus = jnp.concatenate([grad_w_inner.reshape(nch, inner_rows, 128), flat], axis=1)

    conv_tail = grad_w_conv.shape[1:]
    def finish(part, axis, cid):
        part = exchange([part], ("ch",), cid, axes=(axis,), reduce=True)[0]
        shape = part.shape
        if part.size % 128 == 0:
            part = part.reshape(part.size // 128, 128)
        part = lax.all_gather(part, "batch", axis=0)
        return lax.all_gather(part, "seq", axis=0, tiled=True).reshape((seqs * batches,) + shape)

    part_conv = reduce_seq_batch(grad_w_conv.reshape(hid, math.prod(conv_tail) // 128, 128), 0, part_outer)
    part_conv = part_conv.reshape((part_conv.shape[0],) + conv_tail)
    red_outer = finish(part_outer, 0, 1)
    inner_plus, red_outer = lax.optimization_barrier((inner_plus, red_outer))
    part_inner = reduce_seq_batch(inner_plus, 1, part_conv)
    red_conv = finish(part_conv, 2, 2)
    input_grad, red_conv = lax.optimization_barrier((input_grad, red_conv))
    input_grad = to_channels(input_grad, nch, q_count, rows)
    red_inner = finish(part_inner, 0, 3)
    red_w_outer = red_outer.reshape(hloc, dim)
    red_w_conv = red_conv.reshape(hid, KERNEL_TAPS, hloc).transpose(1, 2, 0)
    red_inner = red_inner.reshape(-1)
    red_w_inner = red_inner[: dloc * hid].reshape(dloc, hid)
    mine = red_inner[dloc * hid : dloc * hid + vec_len]
    reds = []
    cut = 0
    for v in vectors:
        n = v.shape[0] // nch
        reds.append(mine[cut : cut + n])
        cut += n
    return (
        output,
        input_grad,
        reds[0],
        reds[1],
        red_w_inner,
        reds[2],
        reds[3],
        reds[4],
        red_w_conv,
        reds[5],
        reds[6],
        reds[7],
        red_w_outer,
        reds[8],
    )


def solution(mesh):
    return jax.shard_map(
        local,
        mesh=mesh,
        in_specs=(
            P("batch", "ch", "seq"),
            P("batch", "seq"),
            P("ch"),
            P("ch"),
            P("ch", None),
            P("ch"),
            P("ch"),
            P("ch"),
            P(None, "ch", None),
            P("ch"),
            P("ch"),
            P("ch"),
            P("ch", None),
            P("ch"),
            P("batch", "ch", "seq"),
        ),
        out_specs=(
            P("batch", "ch", "seq"),
            P("batch", "ch", "seq"),
            P("ch"),
            P("ch"),
            P("ch", None),
            P("ch"),
            P("ch"),
            P("ch"),
            P(None, "ch", None),
            P("ch"),
            P("ch"),
            P("ch"),
            P("ch", None),
            P("ch"),
        ),
        check_vma=False,
    )
```

```python
import functools
import math

import jax
import jax.numpy as jnp
from jax import lax
from jax.experimental import pallas as pl
from jax.experimental.pallas import tpu as pltpu
from jax.sharding import PartitionSpec as P

KERNEL_TAPS = 5
DILATION_SPACING = 32


EPSILON = 1e-05


MESH_AXES = ("batch", "seq", "ch")
MESH_ID = pl.DeviceIdType.MESH


def _group_index(group, sizes, coords):
    me = 0
    for a in group:
        me = me * sizes[a] + coords[a]
    return me


def _exchange_kernel(sizes, group, gather, reduce, axes, *refs):
    count_arrays = len(axes)
    x_refs = refs[:count_arrays]
    o_refs = refs[count_arrays : 2 * count_arrays]
    send_sem, recv_sem = refs[2 * count_arrays :]
    coords = {a: lax.axis_index(a) for a in MESH_AXES}
    me = _group_index(group, sizes, coords)
    count = math.prod(sizes[a] for a in group)

    def device(index):
        where = dict(coords)
        rest = index
        for a in reversed(group):
            where[a] = lax.rem(rest, sizes[a])
            rest = rest // sizes[a]
        return tuple(where[a] for a in MESH_AXES)

    barrier = pltpu.get_barrier_semaphore()
    for j in range(1, count):
        pl.semaphore_signal(barrier, 1, device_id=device(lax.rem(me + j, count)), device_id_type=MESH_ID)
    pl.semaphore_wait(barrier, count - 1)
    copies = []
    for j in range(1, count):
        peer = lax.rem(me + j, count)
        for i in range(count_arrays):
            lead = (slice(None),) * axes[i]
            if gather:
                src, dst = x_refs[i], o_refs[i].at[me]
            else:
                slot = (j - 1) if reduce else me
                src = x_refs[i].at[lead + (pl.ds(peer, 1),)]
                dst = o_refs[i].at[lead + (pl.ds(slot, 1),)]
            copy = pltpu.make_async_remote_copy(
                src_ref=src,
                dst_ref=dst,
                send_sem=send_sem.at[i, j - 1],
                recv_sem=recv_sem.at[i, j - 1],
                device_id=device(peer),
                device_id_type=MESH_ID,
            )
            copy.start()
            copies.append(copy)
    for copy in copies:
        copy.wait()


def exchange(xs, group, collective_id, gather=False, axes=None, reduce=False):
    sizes = {a: lax.axis_size(a) for a in MESH_AXES}
    count = math.prod(sizes[a] for a in group)
    axes = tuple(axes or (0,) * len(xs))
    if count == 1:
        return [x[None] if gather else x for x in xs]
    shapes = [jax.ShapeDtypeStruct((count,) + x.shape if gather else x.shape, x.dtype) for x in xs]
    if reduce:
        shapes = [
            jax.ShapeDtypeStruct(x.shape[:a] + (count - 1,) + x.shape[a + 1 :], x.dtype) for x, a in zip(xs, axes)
        ]
    moved = sum(x.size * x.dtype.itemsize * (count if gather else 1) for x in xs)
    outs = pl.pallas_call(
        functools.partial(_exchange_kernel, sizes, group, gather, reduce, axes),
        out_shape=shapes,
        in_specs=[pl.BlockSpec(memory_space=pl.ANY)] * len(xs),
        out_specs=[pl.BlockSpec(memory_space=pl.ANY)] * len(xs),
        scratch_shapes=[
            pltpu.SemaphoreType.DMA((len(xs), count - 1)),
            pltpu.SemaphoreType.DMA((len(xs), count - 1)),
        ],
        compiler_params=pltpu.CompilerParams(collective_id=collective_id, has_side_effects=True),
        cost_estimate=pl.CostEstimate(flops=0, transcendentals=0, bytes_accessed=2 * moved),
    )(*xs)
    me = _group_index(group, sizes, {a: lax.axis_index(a) for a in group})
    placed = []
    if reduce:
        for x, out, axis in zip(xs, outs, axes):
            own = lax.dynamic_index_in_dim(x, me, axis, keepdims=False)
            placed.append(own + jnp.sum(out, axis=axis))
        return placed
    for x, out, axis in zip(xs, outs, axes):
        own = x if gather else lax.dynamic_index_in_dim(x, me, axis, keepdims=False)
        placed.append(lax.dynamic_update_index_in_dim(out, own, me, axis))
    return placed


def gelu_exact(values):
    return jax.nn.gelu(values, approximate=False)


def gelu_back(point, grad):
    return jax.vjp(gelu_exact, point)[1](grad)[0]


def normalize(values, gain, shift):
    center = jnp.mean(values, axis=1, keepdims=True)
    offset = values - center
    spread = jnp.mean(offset * offset, axis=1, keepdims=True)
    scale = lax.rsqrt(spread + EPSILON)
    unit = offset * scale
    return (unit * gain[:, None] + shift[:, None], unit, scale)


def normalize_back(grad, unit, scale, gain):
    scaled = grad * gain[:, None]
    first = jnp.mean(scaled, axis=1, keepdims=True)
    second = jnp.mean(scaled * unit, axis=1, keepdims=True)
    return scale * (scaled - first - unit * second)


def neighbour_pairs(seqs, nch, q_count):
    pairs = []
    for s in range(seqs):
        for c in range(nch):
            q = c % q_count
            if q < q_count - 1:
                pairs.append((s * nch + c, s * nch + c + 1))
            elif s < seqs - 1:
                pairs.append((s * nch + c, (s + 1) * nch + c - (q_count - 1)))
    return pairs


def extended(x, width, pairs):
    down = [(j, i) for i, j in pairs]
    length = x.shape[-1]
    before = lax.ppermute(x[..., length - width :], ("seq", "ch"), pairs)
    after = lax.ppermute(x[..., :width], ("seq", "ch"), down)
    return jnp.concatenate([before, x, after], axis=-1)


def shifted_taps(wide, wide_ids, own_ids, offsets, border):
    length = own_ids.shape[-1]
    pieces = []
    for offset in offsets:
        lower = border + offset
        shifted = wide[:, :, lower : lower + length]
        matching = wide_ids[:, lower : lower + length] == own_ids
        pieces.append(jnp.where(matching[:, None, :], shifted, jnp.zeros_like(shifted)))
    return jnp.concatenate(pieces, axis=1)


def to_positions(x, nch, q_count):
    rows, width, length = x.shape
    if q_count > 1:
        x = x.reshape(rows, width, q_count, length // q_count).transpose(0, 2, 1, 3)
        x = x.reshape(rows * q_count, width, length // q_count)
    x = lax.all_to_all(x, "ch", 0, 0, tiled=True)
    return _join(x, nch)


def _join(x, nch):
    total, width, length = x.shape
    p = total // nch
    return x.reshape(nch, p, width, length).transpose(1, 0, 2, 3).reshape(p, nch * width, length)


def to_channels(x, nch, q_count, rows):
    p, width, length = x.shape
    x = x.reshape(p, nch, width // nch, length).transpose(1, 0, 2, 3).reshape(nch * p, width // nch, length)
    x = lax.all_to_all(x, "ch", 0, 0, tiled=True)
    if q_count > 1:
        _, width, part = x.shape
        x = x.reshape(rows, q_count, width, part).transpose(0, 2, 1, 3).reshape(rows, width, q_count * part)
    return x


def local(
    inputs,
    segment_ids,
    norm0_gain,
    norm0_shift,
    w_inner,
    b_inner,
    norm1_gain,
    norm1_shift,
    w_conv,
    b_conv,
    norm2_gain,
    norm2_shift,
    w_outer,
    b_outer,
    cotangent,
):
    nch = lax.axis_size("ch")
    seqs = lax.axis_size("seq")
    batches = lax.axis_size("batch")
    rows, dloc, length = inputs.shape
    hloc = w_conv.shape[1]
    hid = hloc * nch
    dim = dloc * nch
    if rows % nch == 0:
        q_count = 1
    else:
        q_count = nch // rows
    part = length // q_count
    border = 2 * DILATION_SPACING
    offsets = [(k - KERNEL_TAPS // 2) * DILATION_SPACING for k in range(KERNEL_TAPS)]
    back_offsets = [-o for o in offsets]
    pairs = neighbour_pairs(seqs, nch, q_count)
    me = lax.axis_index("ch")

    smalls = [norm0_gain, norm0_shift, b_inner, norm1_gain, norm1_shift, b_conv, norm2_gain, norm2_shift, b_outer]
    sidx = lax.axis_index("seq")
    halves = [
        lax.dynamic_slice_in_dim(w_inner, sidx * (dloc // seqs), dloc // seqs, 0),
        lax.dynamic_slice_in_dim(w_conv, sidx * (hloc // seqs), hloc // seqs, 1),
        lax.dynamic_slice_in_dim(w_outer, sidx * (hloc // seqs), hloc // seqs, 0),
    ]
    small_all, w_in, w_out = exchange([jnp.concatenate(smalls), halves[0], halves[2]], ("ch",), 0, gather=True)
    w_cv = lax.all_gather(halves[1], "ch", axis=0)
    cut = 0
    full = []
    for v in smalls:
        n = v.shape[0]
        full.append(small_all[:, cut : cut + n].reshape(n * nch))
        cut += n
    g0, s0, b_in, g1, s1, b_cv, g2, s2, b_out = full
    w_in = lax.all_gather(w_in, "seq", axis=1, tiled=True).reshape(dim, hid)
    w_cv = lax.all_gather(w_cv, "seq", axis=2, tiled=True).transpose(1, 0, 2, 3).reshape(KERNEL_TAPS, hid, hid)
    w_out = lax.all_gather(w_out, "seq", axis=1, tiled=True).reshape(hid, dim)

    x = to_positions(inputs, nch, q_count)
    cot = to_positions(cotangent, nch, q_count)
    prow = x.shape[0]
    if q_count == 1:
        ids = lax.dynamic_slice_in_dim(segment_ids, me * prow, prow, axis=0)
    else:
        ids = lax.dynamic_slice_in_dim(segment_ids, me // q_count, 1, axis=0)
        ids = lax.dynamic_slice_in_dim(ids, (me % q_count) * part, part, axis=1)
    own_ids = ids + 1
    wide_ids = extended(own_ids, border, pairs)

    residual = x.astype(jnp.float32)
    normed0, unit0, scale0 = normalize(residual, g0, s0)
    hidden0 = gelu_exact(normed0).astype(jnp.bfloat16)
    inner = jnp.einsum("dh,rdl->rhl", w_in, hidden0, preferred_element_type=jnp.float32) + b_in[:, None]
    normed1, unit1, scale1 = normalize(inner, g1, s1)
    hidden1 = gelu_exact(normed1).astype(jnp.bfloat16)
    wide_hidden = extended(hidden1, border, pairs)
    taps = shifted_taps(wide_hidden, wide_ids, own_ids, offsets, border)
    kernel_flat = w_cv.reshape(KERNEL_TAPS * hid, hid)
    mixed = jnp.einsum("co,rcl->rol", kernel_flat, taps, preferred_element_type=jnp.float32) + b_cv[:, None]
    normed2, unit2, scale2 = normalize(mixed, g2, s2)
    hidden2 = gelu_exact(normed2).astype(jnp.bfloat16)
    branch = jnp.einsum("hd,rhl->rdl", w_out, hidden2, preferred_element_type=jnp.float32)
    output = (residual + branch + b_out[:, None]).astype(jnp.bfloat16)
    output = to_channels(output, nch, q_count, rows)

    grad_b_outer = jnp.sum(cot.astype(jnp.float32), axis=(0, 2))
    grad_w_outer = jnp.einsum("rhl,rdl->hd", hidden2, cot, preferred_element_type=jnp.float32)
    def reduce_seq_batch(g, split_dim, after=None):
        if after is not None:
            g, _ = lax.optimization_barrier((g, after))
        g = lax.psum_scatter(g, "seq", scatter_dimension=split_dim, tiled=True)
        return lax.psum_scatter(g, "batch", scatter_dimension=split_dim, tiled=True)

    part_outer = reduce_seq_batch(grad_w_outer.reshape(nch, hloc, dim), 2)
    grad_hidden2 = jnp.einsum("hd,rdl->rhl", w_out, cot, preferred_element_type=jnp.float32)
    grad_normed2 = gelu_back(normed2, grad_hidden2)
    grad_norm2_gain = jnp.sum(grad_normed2 * unit2, axis=(0, 2))
    grad_norm2_shift = jnp.sum(grad_normed2, axis=(0, 2))
    grad_mixed = normalize_back(grad_normed2, unit2, scale2, g2).astype(jnp.bfloat16)
    grad_b_conv = jnp.sum(grad_mixed.astype(jnp.float32), axis=(0, 2))
    grad_w_conv = jnp.einsum(
        "rol,rkcil->okci",
        grad_mixed,
        taps.reshape(prow, KERNEL_TAPS, nch, hloc, part),
        preferred_element_type=jnp.float32,
    )
    wide_grad = extended(grad_mixed, border, pairs)
    back_taps = shifted_taps(wide_grad, wide_ids, own_ids, back_offsets, border)
    kernel_back = jnp.transpose(w_cv, (0, 2, 1)).reshape(KERNEL_TAPS * hid, hid)
    grad_hidden1 = jnp.einsum("oc,rol->rcl", kernel_back, back_taps, preferred_element_type=jnp.float32)
    grad_normed1 = gelu_back(normed1, grad_hidden1)
    grad_norm1_gain = jnp.sum(grad_normed1 * unit1, axis=(0, 2))
    grad_norm1_shift = jnp.sum(grad_normed1, axis=(0, 2))
    grad_inner = normalize_back(grad_normed1, unit1, scale1, g1).astype(jnp.bfloat16)
    grad_inner, _, output = lax.optimization_barrier((grad_inner, part_outer, output))
    grad_b_inner = jnp.sum(grad_inner.astype(jnp.float32), axis=(0, 2))
    grad_w_inner = jnp.einsum("rdl,rhl->dh", hidden0, grad_inner, preferred_element_type=jnp.float32)
    grad_hidden0 = jnp.einsum("dh,rhl->rdl", w_in, grad_inner, preferred_element_type=jnp.float32)
    grad_normed0 = gelu_back(normed0, grad_hidden0)
    grad_norm0_gain = jnp.sum(grad_normed0 * unit0, axis=(0, 2))
    grad_norm0_shift = jnp.sum(grad_normed0, axis=(0, 2))
    input_grad = (cot.astype(jnp.float32) + normalize_back(grad_normed0, unit0, scale0, g0)).astype(jnp.bfloat16)


    vectors = [
        grad_norm0_gain,
        grad_norm0_shift,
        grad_b_inner,
        grad_norm1_gain,
        grad_norm1_shift,
        grad_b_conv,
        grad_norm2_gain,
        grad_norm2_shift,
        grad_b_outer,
    ]
    flat = jnp.concatenate([v.reshape(nch, -1) for v in vectors], axis=1)
    vec_len = flat.shape[1]
    inner_rows = dloc * hid // 128
    stack_rows = -(-(inner_rows + -(-vec_len // 128)) // (seqs * batches * 8)) * (seqs * batches * 8)
    vec_rows = stack_rows - inner_rows
    flat = jnp.pad(flat, ((0, 0), (0, vec_rows * 128 - vec_len))).reshape(nch, vec_rows, 128)
    inner_plus = jnp.concatenate([grad_w_inner.reshape(nch, inner_rows, 128), flat], axis=1)

    conv_tail = grad_w_conv.shape[1:]
    def finish(part, axis, cid):
        part = exchange([part], ("ch",), cid, axes=(axis,), reduce=True)[0]
        shape = part.shape
        if part.size % 128 == 0:
            part = part.reshape(part.size // 128, 128)
        part = lax.all_gather(part, "batch", axis=0)
        return lax.all_gather(part, "seq", axis=0, tiled=True).reshape((seqs * batches,) + shape)

    part_conv = reduce_seq_batch(grad_w_conv.reshape(hid, math.prod(conv_tail) // 128, 128), 0, part_outer)
    part_conv = part_conv.reshape((part_conv.shape[0],) + conv_tail)
    red_outer = finish(part_outer, 0, 1)
    inner_plus, red_outer = lax.optimization_barrier((inner_plus, red_outer))
    part_inner = reduce_seq_batch(inner_plus, 1, part_conv)
    red_conv = finish(part_conv, 2, 2)
    input_grad, red_conv = lax.optimization_barrier((input_grad, red_conv))
    input_grad = to_channels(input_grad, nch, q_count, rows)
    red_inner = finish(part_inner, 0, 3)
    red_w_outer = jnp.moveaxis(red_outer, 0, 1).reshape(hloc, dim)
    red_w_conv = red_conv.reshape(hid, KERNEL_TAPS, hloc).transpose(1, 2, 0)
    red_inner = red_inner.reshape(-1)
    red_w_inner = red_inner[: dloc * hid].reshape(dloc, hid)
    mine = red_inner[dloc * hid : dloc * hid + vec_len]
    reds = []
    cut = 0
    for v in vectors:
        n = v.shape[0] // nch
        reds.append(mine[cut : cut + n])
        cut += n
    return (
        output,
        input_grad,
        reds[0],
        reds[1],
        red_w_inner,
        reds[2],
        reds[3],
        reds[4],
        red_w_conv,
        reds[5],
        reds[6],
        reds[7],
        red_w_outer,
        reds[8],
    )


def solution(mesh):
    return jax.shard_map(
        local,
        mesh=mesh,
        in_specs=(
            P("batch", "ch", "seq"),
            P("batch", "seq"),
            P("ch"),
            P("ch"),
            P("ch", None),
            P("ch"),
            P("ch"),
            P("ch"),
            P(None, "ch", None),
            P("ch"),
            P("ch"),
            P("ch"),
            P("ch", None),
            P("ch"),
            P("batch", "ch", "seq"),
        ),
        out_specs=(
            P("batch", "ch", "seq"),
            P("batch", "ch", "seq"),
            P("ch"),
            P("ch"),
            P("ch", None),
            P("ch"),
            P("ch"),
            P("ch"),
            P(None, "ch", None),
            P("ch"),
            P("ch"),
            P("ch"),
            P("ch", None),
            P("ch"),
        ),
        check_vma=False,
    )
```

```python
import functools
import math

import jax
import jax.numpy as jnp
from jax import lax
from jax.experimental import pallas as pl
from jax.experimental.pallas import tpu as pltpu
from jax.sharding import PartitionSpec as P

KERNEL_TAPS = 5
DILATION_SPACING = 32


EPSILON = 1e-05


MESH_AXES = ("batch", "seq", "ch")
MESH_ID = pl.DeviceIdType.MESH


def _group_index(group, sizes, coords):
    me = 0
    for a in group:
        me = me * sizes[a] + coords[a]
    return me


def _exchange_kernel(sizes, group, gather, reduce, axes, *refs):
    count_arrays = len(axes)
    x_refs = refs[:count_arrays]
    o_refs = refs[count_arrays : 2 * count_arrays]
    send_sem, recv_sem = refs[2 * count_arrays :]
    coords = {a: lax.axis_index(a) for a in MESH_AXES}
    me = _group_index(group, sizes, coords)
    count = math.prod(sizes[a] for a in group)

    def device(index):
        where = dict(coords)
        rest = index
        for a in reversed(group):
            where[a] = lax.rem(rest, sizes[a])
            rest = rest // sizes[a]
        return tuple(where[a] for a in MESH_AXES)

    barrier = pltpu.get_barrier_semaphore()
    for j in range(1, count):
        pl.semaphore_signal(barrier, 1, device_id=device(lax.rem(me + j, count)), device_id_type=MESH_ID)
    pl.semaphore_wait(barrier, count - 1)
    copies = []
    for j in range(1, count):
        peer = lax.rem(me + j, count)
        for i in range(count_arrays):
            lead = (slice(None),) * axes[i]
            if gather:
                src, dst = x_refs[i], o_refs[i].at[me]
            else:
                slot = (j - 1) if reduce else me
                src = x_refs[i].at[lead + (pl.ds(peer, 1),)]
                dst = o_refs[i].at[lead + (pl.ds(slot, 1),)]
            copy = pltpu.make_async_remote_copy(
                src_ref=src,
                dst_ref=dst,
                send_sem=send_sem.at[i, j - 1],
                recv_sem=recv_sem.at[i, j - 1],
                device_id=device(peer),
                device_id_type=MESH_ID,
            )
            copy.start()
            copies.append(copy)
    for copy in copies:
        copy.wait()


def exchange(xs, group, collective_id, gather=False, axes=None, reduce=False):
    sizes = {a: lax.axis_size(a) for a in MESH_AXES}
    count = math.prod(sizes[a] for a in group)
    axes = tuple(axes or (0,) * len(xs))
    if count == 1:
        return [x[None] if gather else x for x in xs]
    shapes = [jax.ShapeDtypeStruct((count,) + x.shape if gather else x.shape, x.dtype) for x in xs]
    if reduce:
        shapes = [
            jax.ShapeDtypeStruct(x.shape[:a] + (count - 1,) + x.shape[a + 1 :], x.dtype) for x, a in zip(xs, axes)
        ]
    moved = sum(x.size * x.dtype.itemsize * (count if gather else 1) for x in xs)
    outs = pl.pallas_call(
        functools.partial(_exchange_kernel, sizes, group, gather, reduce, axes),
        out_shape=shapes,
        in_specs=[pl.BlockSpec(memory_space=pl.ANY)] * len(xs),
        out_specs=[pl.BlockSpec(memory_space=pl.ANY)] * len(xs),
        scratch_shapes=[
            pltpu.SemaphoreType.DMA((len(xs), count - 1)),
            pltpu.SemaphoreType.DMA((len(xs), count - 1)),
        ],
        compiler_params=pltpu.CompilerParams(collective_id=collective_id, has_side_effects=True),
        cost_estimate=pl.CostEstimate(flops=0, transcendentals=0, bytes_accessed=2 * moved),
    )(*xs)
    me = _group_index(group, sizes, {a: lax.axis_index(a) for a in group})
    placed = []
    if reduce:
        for x, out, axis in zip(xs, outs, axes):
            own = lax.dynamic_index_in_dim(x, me, axis, keepdims=False)
            placed.append(own + jnp.sum(out, axis=axis))
        return placed
    for x, out, axis in zip(xs, outs, axes):
        own = x if gather else lax.dynamic_index_in_dim(x, me, axis, keepdims=False)
        placed.append(lax.dynamic_update_index_in_dim(out, own, me, axis))
    return placed


def gelu_exact(values):
    return jax.nn.gelu(values, approximate=False)


def gelu_back(point, grad):
    return jax.vjp(gelu_exact, point)[1](grad)[0]


def normalize(values, gain, shift):
    center = jnp.mean(values, axis=1, keepdims=True)
    offset = values - center
    spread = jnp.mean(offset * offset, axis=1, keepdims=True)
    scale = lax.rsqrt(spread + EPSILON)
    unit = offset * scale
    return (unit * gain[:, None] + shift[:, None], unit, scale)


def normalize_back(grad, unit, scale, gain):
    scaled = grad * gain[:, None]
    first = jnp.mean(scaled, axis=1, keepdims=True)
    second = jnp.mean(scaled * unit, axis=1, keepdims=True)
    return scale * (scaled - first - unit * second)


def neighbour_pairs(seqs, nch, q_count):
    pairs = []
    for s in range(seqs):
        for c in range(nch):
            q = c % q_count
            if q < q_count - 1:
                pairs.append((s * nch + c, s * nch + c + 1))
            elif s < seqs - 1:
                pairs.append((s * nch + c, (s + 1) * nch + c - (q_count - 1)))
    return pairs


def extended(x, width, pairs):
    down = [(j, i) for i, j in pairs]
    length = x.shape[-1]
    before = lax.ppermute(x[..., length - width :], ("seq", "ch"), pairs)
    after = lax.ppermute(x[..., :width], ("seq", "ch"), down)
    return jnp.concatenate([before, x, after], axis=-1)


def shifted_taps(wide, wide_ids, own_ids, offsets, border):
    length = own_ids.shape[-1]
    pieces = []
    for offset in offsets:
        lower = border + offset
        shifted = wide[:, :, lower : lower + length]
        matching = wide_ids[:, lower : lower + length] == own_ids
        pieces.append(jnp.where(matching[:, None, :], shifted, jnp.zeros_like(shifted)))
    return jnp.concatenate(pieces, axis=1)


def to_positions(x, nch, q_count):
    rows, width, length = x.shape
    if q_count > 1:
        x = x.reshape(rows, width, q_count, length // q_count).transpose(0, 2, 1, 3)
        x = x.reshape(rows * q_count, width, length // q_count)
    x = lax.all_to_all(x, "ch", 0, 0, tiled=True)
    return _join(x, nch)


def _join(x, nch):
    total, width, length = x.shape
    p = total // nch
    return x.reshape(nch, p, width, length).transpose(1, 0, 2, 3).reshape(p, nch * width, length)


def to_channels(x, nch, q_count, rows):
    p, width, length = x.shape
    x = x.reshape(p, nch, width // nch, length).transpose(1, 0, 2, 3).reshape(nch * p, width // nch, length)
    x = lax.all_to_all(x, "ch", 0, 0, tiled=True)
    if q_count > 1:
        _, width, part = x.shape
        x = x.reshape(rows, q_count, width, part).transpose(0, 2, 1, 3).reshape(rows, width, q_count * part)
    return x


def local(
    inputs,
    segment_ids,
    norm0_gain,
    norm0_shift,
    w_inner,
    b_inner,
    norm1_gain,
    norm1_shift,
    w_conv,
    b_conv,
    norm2_gain,
    norm2_shift,
    w_outer,
    b_outer,
    cotangent,
):
    nch = lax.axis_size("ch")
    seqs = lax.axis_size("seq")
    batches = lax.axis_size("batch")
    rows, dloc, length = inputs.shape
    hloc = w_conv.shape[1]
    hid = hloc * nch
    dim = dloc * nch
    if rows % nch == 0:
        q_count = 1
    else:
        q_count = nch // rows
    part = length // q_count
    border = 2 * DILATION_SPACING
    offsets = [(k - KERNEL_TAPS // 2) * DILATION_SPACING for k in range(KERNEL_TAPS)]
    back_offsets = [-o for o in offsets]
    pairs = neighbour_pairs(seqs, nch, q_count)
    me = lax.axis_index("ch")

    smalls = [norm0_gain, norm0_shift, b_inner, norm1_gain, norm1_shift, b_conv, norm2_gain, norm2_shift, b_outer]
    sidx = lax.axis_index("seq")
    halves = [
        lax.dynamic_slice_in_dim(w_inner, sidx * (dloc // seqs), dloc // seqs, 0),
        lax.dynamic_slice_in_dim(w_conv, sidx * (hloc // seqs), hloc // seqs, 1),
        lax.dynamic_slice_in_dim(w_outer, sidx * (hloc // seqs), hloc // seqs, 0),
    ]
    small_all, w_in, w_cv, w_out = exchange([jnp.concatenate(smalls)] + halves, ("ch",), 0, gather=True)
    cut = 0
    full = []
    for v in smalls:
        n = v.shape[0]
        full.append(small_all[:, cut : cut + n].reshape(n * nch))
        cut += n
    g0, s0, b_in, g1, s1, b_cv, g2, s2, b_out = full
    w_in = lax.all_gather(w_in, "seq", axis=1, tiled=True).reshape(dim, hid)
    w_cv = lax.all_gather(w_cv, "seq", axis=2, tiled=True).transpose(1, 0, 2, 3).reshape(KERNEL_TAPS, hid, hid)
    w_out = lax.all_gather(w_out, "seq", axis=1, tiled=True).reshape(hid, dim)

    x = to_positions(inputs, nch, q_count)
    cot = to_positions(cotangent, nch, q_count)
    prow = x.shape[0]
    if q_count == 1:
        ids = lax.dynamic_slice_in_dim(segment_ids, me * prow, prow, axis=0)
    else:
        ids = lax.dynamic_slice_in_dim(segment_ids, me // q_count, 1, axis=0)
        ids = lax.dynamic_slice_in_dim(ids, (me % q_count) * part, part, axis=1)
    own_ids = ids + 1
    wide_ids = extended(own_ids, border, pairs)

    residual = x.astype(jnp.float32)
    normed0, unit0, scale0 = normalize(residual, g0, s0)
    hidden0 = gelu_exact(normed0).astype(jnp.bfloat16)
    inner = jnp.einsum("dh,rdl->rhl", w_in, hidden0, preferred_element_type=jnp.float32) + b_in[:, None]
    normed1, unit1, scale1 = normalize(inner, g1, s1)
    hidden1 = gelu_exact(normed1).astype(jnp.bfloat16)
    wide_hidden = extended(hidden1, border, pairs)
    taps = shifted_taps(wide_hidden, wide_ids, own_ids, offsets, border)
    kernel_flat = w_cv.reshape(KERNEL_TAPS * hid, hid)
    mixed = jnp.einsum("co,rcl->rol", kernel_flat, taps, preferred_element_type=jnp.float32) + b_cv[:, None]
    normed2, unit2, scale2 = normalize(mixed, g2, s2)
    hidden2 = gelu_exact(normed2).astype(jnp.bfloat16)
    branch = jnp.einsum("hd,rhl->rdl", w_out, hidden2, preferred_element_type=jnp.float32)
    output = (residual + branch + b_out[:, None]).astype(jnp.bfloat16)
    output = to_channels(output, nch, q_count, rows)

    grad_b_outer = jnp.sum(cot.astype(jnp.float32), axis=(0, 2))
    grad_w_outer = jnp.einsum("rhl,rdl->hd", hidden2, cot, preferred_element_type=jnp.float32)
    def reduce_seq_batch(g, split_dim, after=None):
        if after is not None:
            g, _ = lax.optimization_barrier((g, after))
        g = lax.psum_scatter(g, "seq", scatter_dimension=split_dim, tiled=True)
        return lax.psum_scatter(g, "batch", scatter_dimension=split_dim, tiled=True)

    part_outer = reduce_seq_batch(grad_w_outer.reshape(nch, hloc * dim // 128, 128), 1)
    grad_hidden2 = jnp.einsum("hd,rdl->rhl", w_out, cot, preferred_element_type=jnp.float32)
    grad_normed2 = gelu_back(normed2, grad_hidden2)
    grad_norm2_gain = jnp.sum(grad_normed2 * unit2, axis=(0, 2))
    grad_norm2_shift = jnp.sum(grad_normed2, axis=(0, 2))
    grad_mixed = normalize_back(grad_normed2, unit2, scale2, g2).astype(jnp.bfloat16)
    grad_b_conv = jnp.sum(grad_mixed.astype(jnp.float32), axis=(0, 2))
    grad_w_conv = jnp.einsum(
        "rol,rkcil->okci",
        grad_mixed,
        taps.reshape(prow, KERNEL_TAPS, nch, hloc, part),
        preferred_element_type=jnp.float32,
    )
    wide_grad = extended(grad_mixed, border, pairs)
    back_taps = shifted_taps(wide_grad, wide_ids, own_ids, back_offsets, border)
    kernel_back = jnp.transpose(w_cv, (0, 2, 1)).reshape(KERNEL_TAPS * hid, hid)
    grad_hidden1 = jnp.einsum("oc,rol->rcl", kernel_back, back_taps, preferred_element_type=jnp.float32)
    grad_normed1 = gelu_back(normed1, grad_hidden1)
    grad_norm1_gain = jnp.sum(grad_normed1 * unit1, axis=(0, 2))
    grad_norm1_shift = jnp.sum(grad_normed1, axis=(0, 2))
    grad_inner = normalize_back(grad_normed1, unit1, scale1, g1).astype(jnp.bfloat16)
    grad_inner, _, output = lax.optimization_barrier((grad_inner, part_outer, output))
    grad_b_inner = jnp.sum(grad_inner.astype(jnp.float32), axis=(0, 2))
    grad_w_inner = jnp.einsum("rdl,rhl->dh", hidden0, grad_inner, preferred_element_type=jnp.float32)
    grad_hidden0 = jnp.einsum("dh,rhl->rdl", w_in, grad_inner, preferred_element_type=jnp.float32)
    grad_normed0 = gelu_back(normed0, grad_hidden0)
    grad_norm0_gain = jnp.sum(grad_normed0 * unit0, axis=(0, 2))
    grad_norm0_shift = jnp.sum(grad_normed0, axis=(0, 2))
    input_grad = (cot.astype(jnp.float32) + normalize_back(grad_normed0, unit0, scale0, g0)).astype(jnp.bfloat16)


    vectors = [
        grad_norm0_gain,
        grad_norm0_shift,
        grad_b_inner,
        grad_norm1_gain,
        grad_norm1_shift,
        grad_b_conv,
        grad_norm2_gain,
        grad_norm2_shift,
        grad_b_outer,
    ]
    flat = jnp.concatenate([v.reshape(nch, -1) for v in vectors], axis=1)
    vec_len = flat.shape[1]
    inner_rows = dloc * hid // 128
    stack_rows = -(-(inner_rows + -(-vec_len // 128)) // (seqs * batches * 8)) * (seqs * batches * 8)
    vec_rows = stack_rows - inner_rows
    flat = jnp.pad(flat, ((0, 0), (0, vec_rows * 128 - vec_len))).reshape(nch, vec_rows, 128)
    inner_plus = jnp.concatenate([grad_w_inner.reshape(nch, inner_rows, 128), flat], axis=1)

    conv_tail = grad_w_conv.shape[1:]
    def finish(part, axis, cid):
        part = exchange([part], ("ch",), cid, axes=(axis,), reduce=True)[0]
        shape = part.shape
        if part.size % 128 == 0:
            part = part.reshape(part.size // 128, 128)
        part = lax.all_gather(part, "batch", axis=0)
        return lax.all_gather(part, "seq", axis=0, tiled=True).reshape((seqs * batches,) + shape)

    part_conv = reduce_seq_batch(grad_w_conv.reshape(hid, math.prod(conv_tail) // 128, 128), 0, part_outer)
    part_conv = part_conv.reshape((part_conv.shape[0],) + conv_tail)
    red_outer = finish(part_outer, 0, 1)
    inner_plus, red_outer = lax.optimization_barrier((inner_plus, red_outer))
    part_inner = reduce_seq_batch(inner_plus, 1, part_conv)
    red_conv = finish(part_conv, 2, 2)
    input_grad, red_conv = lax.optimization_barrier((input_grad, red_conv))
    input_grad = to_channels(input_grad, nch, q_count, rows)
    red_inner = finish(part_inner, 0, 3)
    red_w_outer = red_outer.reshape(hloc, dim)
    red_w_conv = red_conv.reshape(hid, KERNEL_TAPS, hloc).transpose(1, 2, 0)
    red_inner = red_inner.reshape(-1)
    red_w_inner = red_inner[: dloc * hid].reshape(dloc, hid)
    mine = red_inner[dloc * hid : dloc * hid + vec_len]
    reds = []
    cut = 0
    for v in vectors:
        n = v.shape[0] // nch
        reds.append(mine[cut : cut + n])
        cut += n
    return (
        output,
        input_grad,
        reds[0],
        reds[1],
        red_w_inner,
        reds[2],
        reds[3],
        reds[4],
        red_w_conv,
        reds[5],
        reds[6],
        reds[7],
        red_w_outer,
        reds[8],
    )


def solution(mesh):
    return jax.shard_map(
        local,
        mesh=mesh,
        in_specs=(
            P("batch", "ch", "seq"),
            P("batch", "seq"),
            P("ch"),
            P("ch"),
            P("ch", None),
            P("ch"),
            P("ch"),
            P("ch"),
            P(None, "ch", None),
            P("ch"),
            P("ch"),
            P("ch"),
            P("ch", None),
            P("ch"),
            P("batch", "ch", "seq"),
        ),
        out_specs=(
            P("batch", "ch", "seq"),
            P("batch", "ch", "seq"),
            P("ch"),
            P("ch"),
            P("ch", None),
            P("ch"),
            P("ch"),
            P("ch"),
            P(None, "ch", None),
            P("ch"),
            P("ch"),
            P("ch"),
            P("ch", None),
            P("ch"),
        ),
        check_vma=False,
    )
```

```python
import functools
import math

import jax
import jax.numpy as jnp
from jax import lax
from jax.experimental import pallas as pl
from jax.experimental.pallas import tpu as pltpu
from jax.sharding import PartitionSpec as P

KERNEL_TAPS = 5
DILATION_SPACING = 32


EPSILON = 1e-05


MESH_AXES = ("batch", "seq", "ch")
MESH_ID = pl.DeviceIdType.MESH


def _group_index(group, sizes, coords):
    me = 0
    for a in group:
        me = me * sizes[a] + coords[a]
    return me


def _exchange_kernel(sizes, group, gather, reduce, axes, *refs):
    count_arrays = len(axes)
    x_refs = refs[:count_arrays]
    o_refs = refs[count_arrays : 2 * count_arrays]
    send_sem, recv_sem = refs[2 * count_arrays :]
    coords = {a: lax.axis_index(a) for a in MESH_AXES}
    me = _group_index(group, sizes, coords)
    count = math.prod(sizes[a] for a in group)

    def device(index):
        where = dict(coords)
        rest = index
        for a in reversed(group):
            where[a] = lax.rem(rest, sizes[a])
            rest = rest // sizes[a]
        return tuple(where[a] for a in MESH_AXES)

    barrier = pltpu.get_barrier_semaphore()
    for j in range(1, count):
        pl.semaphore_signal(barrier, 1, device_id=device(lax.rem(me + j, count)), device_id_type=MESH_ID)
    pl.semaphore_wait(barrier, count - 1)
    copies = []
    for j in range(1, count):
        peer = lax.rem(me + j, count)
        for i in range(count_arrays):
            lead = (slice(None),) * axes[i]
            if gather:
                src, dst = x_refs[i], o_refs[i].at[me]
            else:
                slot = (j - 1) if reduce else me
                src = x_refs[i].at[lead + (pl.ds(peer, 1),)]
                dst = o_refs[i].at[lead + (pl.ds(slot, 1),)]
            copy = pltpu.make_async_remote_copy(
                src_ref=src,
                dst_ref=dst,
                send_sem=send_sem.at[i, j - 1],
                recv_sem=recv_sem.at[i, j - 1],
                device_id=device(peer),
                device_id_type=MESH_ID,
            )
            copy.start()
            copies.append(copy)
    for copy in copies:
        copy.wait()


def exchange(xs, group, collective_id, gather=False, axes=None, reduce=False):
    sizes = {a: lax.axis_size(a) for a in MESH_AXES}
    count = math.prod(sizes[a] for a in group)
    axes = tuple(axes or (0,) * len(xs))
    if count == 1:
        return [x[None] if gather else x for x in xs]
    shapes = [jax.ShapeDtypeStruct((count,) + x.shape if gather else x.shape, x.dtype) for x in xs]
    if reduce:
        shapes = [
            jax.ShapeDtypeStruct(x.shape[:a] + (count - 1,) + x.shape[a + 1 :], x.dtype) for x, a in zip(xs, axes)
        ]
    moved = sum(x.size * x.dtype.itemsize * (count if gather else 1) for x in xs)
    outs = pl.pallas_call(
        functools.partial(_exchange_kernel, sizes, group, gather, reduce, axes),
        out_shape=shapes,
        in_specs=[pl.BlockSpec(memory_space=pl.ANY)] * len(xs),
        out_specs=[pl.BlockSpec(memory_space=pl.ANY)] * len(xs),
        scratch_shapes=[
            pltpu.SemaphoreType.DMA((len(xs), count - 1)),
            pltpu.SemaphoreType.DMA((len(xs), count - 1)),
        ],
        compiler_params=pltpu.CompilerParams(collective_id=collective_id, has_side_effects=True),
        cost_estimate=pl.CostEstimate(flops=0, transcendentals=0, bytes_accessed=2 * moved),
    )(*xs)
    me = _group_index(group, sizes, {a: lax.axis_index(a) for a in group})
    placed = []
    if reduce:
        for x, out, axis in zip(xs, outs, axes):
            own = lax.dynamic_index_in_dim(x, me, axis, keepdims=False)
            placed.append(own + jnp.sum(out, axis=axis))
        return placed
    for x, out, axis in zip(xs, outs, axes):
        own = x if gather else lax.dynamic_index_in_dim(x, me, axis, keepdims=False)
        placed.append(lax.dynamic_update_index_in_dim(out, own, me, axis))
    return placed


def gelu_exact(values):
    return jax.nn.gelu(values, approximate=False)


def gelu_back(point, grad):
    return jax.vjp(gelu_exact, point)[1](grad)[0]


def normalize(values, gain, shift):
    center = jnp.mean(values, axis=1, keepdims=True)
    offset = values - center
    spread = jnp.mean(offset * offset, axis=1, keepdims=True)
    scale = lax.rsqrt(spread + EPSILON)
    unit = offset * scale
    return (unit * gain[:, None] + shift[:, None], unit, scale)


def normalize_back(grad, unit, scale, gain):
    scaled = grad * gain[:, None]
    first = jnp.mean(scaled, axis=1, keepdims=True)
    second = jnp.mean(scaled * unit, axis=1, keepdims=True)
    return scale * (scaled - first - unit * second)


def neighbour_pairs(seqs, nch, q_count):
    pairs = []
    for s in range(seqs):
        for c in range(nch):
            q = c % q_count
            if q < q_count - 1:
                pairs.append((s * nch + c, s * nch + c + 1))
            elif s < seqs - 1:
                pairs.append((s * nch + c, (s + 1) * nch + c - (q_count - 1)))
    return pairs


def extended(x, width, pairs):
    down = [(j, i) for i, j in pairs]
    length = x.shape[-1]
    before = lax.ppermute(x[..., length - width :], ("seq", "ch"), pairs)
    after = lax.ppermute(x[..., :width], ("seq", "ch"), down)
    return jnp.concatenate([before, x, after], axis=-1)


def shifted_taps(wide, wide_ids, own_ids, offsets, border):
    length = own_ids.shape[-1]
    pieces = []
    for offset in offsets:
        lower = border + offset
        shifted = wide[:, :, lower : lower + length]
        matching = wide_ids[:, lower : lower + length] == own_ids
        pieces.append(jnp.where(matching[:, None, :], shifted, jnp.zeros_like(shifted)))
    return jnp.concatenate(pieces, axis=1)


def to_positions(x, nch, q_count):
    rows, width, length = x.shape
    if q_count > 1:
        x = x.reshape(rows, width, q_count, length // q_count).transpose(0, 2, 1, 3)
        x = x.reshape(rows * q_count, width, length // q_count)
    x = lax.all_to_all(x, "ch", 0, 0, tiled=True)
    return _join(x, nch)


def _join(x, nch):
    total, width, length = x.shape
    p = total // nch
    return x.reshape(nch, p, width, length).transpose(1, 0, 2, 3).reshape(p, nch * width, length)


def to_channels(x, nch, q_count, rows):
    p, width, length = x.shape
    x = x.reshape(p, nch, width // nch, length).transpose(1, 0, 2, 3).reshape(nch * p, width // nch, length)
    x = lax.all_to_all(x, "ch", 0, 0, tiled=True)
    if q_count > 1:
        _, width, part = x.shape
        x = x.reshape(rows, q_count, width, part).transpose(0, 2, 1, 3).reshape(rows, width, q_count * part)
    return x


def local(
    inputs,
    segment_ids,
    norm0_gain,
    norm0_shift,
    w_inner,
    b_inner,
    norm1_gain,
    norm1_shift,
    w_conv,
    b_conv,
    norm2_gain,
    norm2_shift,
    w_outer,
    b_outer,
    cotangent,
):
    nch = lax.axis_size("ch")
    seqs = lax.axis_size("seq")
    batches = lax.axis_size("batch")
    rows, dloc, length = inputs.shape
    hloc = w_conv.shape[1]
    hid = hloc * nch
    dim = dloc * nch
    if rows % nch == 0:
        q_count = 1
    else:
        q_count = nch // rows
    part = length // q_count
    border = 2 * DILATION_SPACING
    offsets = [(k - KERNEL_TAPS // 2) * DILATION_SPACING for k in range(KERNEL_TAPS)]
    back_offsets = [-o for o in offsets]
    pairs = neighbour_pairs(seqs, nch, q_count)
    me = lax.axis_index("ch")

    smalls = [norm0_gain, norm0_shift, b_inner, norm1_gain, norm1_shift, b_conv, norm2_gain, norm2_shift, b_outer]
    sidx = lax.axis_index("seq")
    halves = [
        lax.dynamic_slice_in_dim(w_inner, sidx * (dloc // seqs), dloc // seqs, 0),
        lax.dynamic_slice_in_dim(w_conv, sidx * (hloc // seqs), hloc // seqs, 1),
        lax.dynamic_slice_in_dim(w_outer, sidx * (hloc // seqs), hloc // seqs, 0),
    ]
    small_all, w_in, w_cv, w_out = exchange([jnp.concatenate(smalls)] + halves, ("ch",), 0, gather=True)
    cut = 0
    full = []
    for v in smalls:
        n = v.shape[0]
        full.append(small_all[:, cut : cut + n].reshape(n * nch))
        cut += n
    g0, s0, b_in, g1, s1, b_cv, g2, s2, b_out = full
    w_in, w_cv, w_out = exchange([w_in, w_cv, w_out], ("seq",), 4, gather=True)
    w_in = w_in.transpose(1, 0, 2, 3).reshape(dim, hid)
    w_cv = w_cv.transpose(2, 1, 0, 3, 4).reshape(KERNEL_TAPS, hid, hid)
    w_out = w_out.transpose(1, 0, 2, 3).reshape(hid, dim)

    x = to_positions(inputs, nch, q_count)
    cot = to_positions(cotangent, nch, q_count)
    prow = x.shape[0]
    if q_count == 1:
        ids = lax.dynamic_slice_in_dim(segment_ids, me * prow, prow, axis=0)
    else:
        ids = lax.dynamic_slice_in_dim(segment_ids, me // q_count, 1, axis=0)
        ids = lax.dynamic_slice_in_dim(ids, (me % q_count) * part, part, axis=1)
    own_ids = ids + 1
    wide_ids = extended(own_ids, border, pairs)

    residual = x.astype(jnp.float32)
    normed0, unit0, scale0 = normalize(residual, g0, s0)
    hidden0 = gelu_exact(normed0).astype(jnp.bfloat16)
    inner = jnp.einsum("dh,rdl->rhl", w_in, hidden0, preferred_element_type=jnp.float32) + b_in[:, None]
    normed1, unit1, scale1 = normalize(inner, g1, s1)
    hidden1 = gelu_exact(normed1).astype(jnp.bfloat16)
    wide_hidden = extended(hidden1, border, pairs)
    taps = shifted_taps(wide_hidden, wide_ids, own_ids, offsets, border)
    kernel_flat = w_cv.reshape(KERNEL_TAPS * hid, hid)
    mixed = jnp.einsum("co,rcl->rol", kernel_flat, taps, preferred_element_type=jnp.float32) + b_cv[:, None]
    normed2, unit2, scale2 = normalize(mixed, g2, s2)
    hidden2 = gelu_exact(normed2).astype(jnp.bfloat16)
    branch = jnp.einsum("hd,rhl->rdl", w_out, hidden2, preferred_element_type=jnp.float32)
    output = (residual + branch + b_out[:, None]).astype(jnp.bfloat16)
    output = to_channels(output, nch, q_count, rows)

    grad_b_outer = jnp.sum(cot.astype(jnp.float32), axis=(0, 2))
    grad_w_outer = jnp.einsum("rhl,rdl->hd", hidden2, cot, preferred_element_type=jnp.float32)
    def reduce_seq_batch(g, split_dim, after=None):
        if after is not None:
            g, _ = lax.optimization_barrier((g, after))
        g = lax.psum_scatter(g, "seq", scatter_dimension=split_dim, tiled=True)
        return lax.psum_scatter(g, "batch", scatter_dimension=split_dim, tiled=True)

    part_outer = reduce_seq_batch(grad_w_outer.reshape(nch, hloc * dim // 128, 128), 1)
    grad_hidden2 = jnp.einsum("hd,rdl->rhl", w_out, cot, preferred_element_type=jnp.float32)
    grad_normed2 = gelu_back(normed2, grad_hidden2)
    grad_norm2_gain = jnp.sum(grad_normed2 * unit2, axis=(0, 2))
    grad_norm2_shift = jnp.sum(grad_normed2, axis=(0, 2))
    grad_mixed = normalize_back(grad_normed2, unit2, scale2, g2).astype(jnp.bfloat16)
    grad_b_conv = jnp.sum(grad_mixed.astype(jnp.float32), axis=(0, 2))
    grad_w_conv = jnp.einsum(
        "rol,rkcil->okci",
        grad_mixed,
        taps.reshape(prow, KERNEL_TAPS, nch, hloc, part),
        preferred_element_type=jnp.float32,
    )
    wide_grad = extended(grad_mixed, border, pairs)
    back_taps = shifted_taps(wide_grad, wide_ids, own_ids, back_offsets, border)
    kernel_back = jnp.transpose(w_cv, (0, 2, 1)).reshape(KERNEL_TAPS * hid, hid)
    grad_hidden1 = jnp.einsum("oc,rol->rcl", kernel_back, back_taps, preferred_element_type=jnp.float32)
    grad_normed1 = gelu_back(normed1, grad_hidden1)
    grad_norm1_gain = jnp.sum(grad_normed1 * unit1, axis=(0, 2))
    grad_norm1_shift = jnp.sum(grad_normed1, axis=(0, 2))
    grad_inner = normalize_back(grad_normed1, unit1, scale1, g1).astype(jnp.bfloat16)
    grad_inner, _, output = lax.optimization_barrier((grad_inner, part_outer, output))
    grad_b_inner = jnp.sum(grad_inner.astype(jnp.float32), axis=(0, 2))
    grad_w_inner = jnp.einsum("rdl,rhl->dh", hidden0, grad_inner, preferred_element_type=jnp.float32)
    grad_hidden0 = jnp.einsum("dh,rhl->rdl", w_in, grad_inner, preferred_element_type=jnp.float32)
    grad_normed0 = gelu_back(normed0, grad_hidden0)
    grad_norm0_gain = jnp.sum(grad_normed0 * unit0, axis=(0, 2))
    grad_norm0_shift = jnp.sum(grad_normed0, axis=(0, 2))
    input_grad = (cot.astype(jnp.float32) + normalize_back(grad_normed0, unit0, scale0, g0)).astype(jnp.bfloat16)


    vectors = [
        grad_norm0_gain,
        grad_norm0_shift,
        grad_b_inner,
        grad_norm1_gain,
        grad_norm1_shift,
        grad_b_conv,
        grad_norm2_gain,
        grad_norm2_shift,
        grad_b_outer,
    ]
    flat = jnp.concatenate([v.reshape(nch, -1) for v in vectors], axis=1)
    vec_len = flat.shape[1]
    inner_rows = dloc * hid // 128
    stack_rows = -(-(inner_rows + -(-vec_len // 128)) // (seqs * batches * 8)) * (seqs * batches * 8)
    vec_rows = stack_rows - inner_rows
    flat = jnp.pad(flat, ((0, 0), (0, vec_rows * 128 - vec_len))).reshape(nch, vec_rows, 128)
    inner_plus = jnp.concatenate([grad_w_inner.reshape(nch, inner_rows, 128), flat], axis=1)

    conv_tail = grad_w_conv.shape[1:]
    def finish(part, axis, cid):
        part = exchange([part], ("ch",), cid, axes=(axis,), reduce=True)[0]
        shape = part.shape
        if part.size % 128 == 0:
            part = part.reshape(part.size // 128, 128)
        part = lax.all_gather(part, "batch", axis=0)
        return lax.all_gather(part, "seq", axis=0, tiled=True).reshape((seqs * batches,) + shape)

    part_conv = reduce_seq_batch(grad_w_conv.reshape(hid, math.prod(conv_tail) // 128, 128), 0, part_outer)
    part_conv = part_conv.reshape((part_conv.shape[0],) + conv_tail)
    red_outer = finish(part_outer, 0, 1)
    inner_plus, red_outer = lax.optimization_barrier((inner_plus, red_outer))
    part_inner = reduce_seq_batch(inner_plus, 1, part_conv)
    red_conv = finish(part_conv, 2, 2)
    input_grad, red_conv = lax.optimization_barrier((input_grad, red_conv))
    input_grad = to_channels(input_grad, nch, q_count, rows)
    red_inner = finish(part_inner, 0, 3)
    red_w_outer = red_outer.reshape(hloc, dim)
    red_w_conv = red_conv.reshape(hid, KERNEL_TAPS, hloc).transpose(1, 2, 0)
    red_inner = red_inner.reshape(-1)
    red_w_inner = red_inner[: dloc * hid].reshape(dloc, hid)
    mine = red_inner[dloc * hid : dloc * hid + vec_len]
    reds = []
    cut = 0
    for v in vectors:
        n = v.shape[0] // nch
        reds.append(mine[cut : cut + n])
        cut += n
    return (
        output,
        input_grad,
        reds[0],
        reds[1],
        red_w_inner,
        reds[2],
        reds[3],
        reds[4],
        red_w_conv,
        reds[5],
        reds[6],
        reds[7],
        red_w_outer,
        reds[8],
    )


def solution(mesh):
    return jax.shard_map(
        local,
        mesh=mesh,
        in_specs=(
            P("batch", "ch", "seq"),
            P("batch", "seq"),
            P("ch"),
            P("ch"),
            P("ch", None),
            P("ch"),
            P("ch"),
            P("ch"),
            P(None, "ch", None),
            P("ch"),
            P("ch"),
            P("ch"),
            P("ch", None),
            P("ch"),
            P("batch", "ch", "seq"),
        ),
        out_specs=(
            P("batch", "ch", "seq"),
            P("batch", "ch", "seq"),
            P("ch"),
            P("ch"),
            P("ch", None),
            P("ch"),
            P("ch"),
            P("ch"),
            P(None, "ch", None),
            P("ch"),
            P("ch"),
            P("ch"),
            P("ch", None),
            P("ch"),
        ),
        check_vma=False,
    )
```
